32 devices in a mesh: leaf: 8 (over z, y), fsdp: 4 (over x, core).
Axes of the slice: x: 2, y: 2, z: 4, core: 2. Of those that a mesh axis runs over, the one named last changes fastest.
Arguments:
- hidden: bfloat16 [4, 2048, 768], P('fsdp', 'leaf'), may hold values from -6 to 6
- noise_mask: int32 [4, 2048], P('fsdp', 'leaf'), may hold values 0 or 1
- seg_blocks: int32 [4, 128], P('fsdp'), may hold values from 0 to 12, as said below
- parents: int32 [4, 13], P('fsdp'), may hold values from 0 to 4, as said below
- ln1_gain: bfloat16 [768], P(('leaf', 'fsdp')), may hold values from 0.099609375 to 1.8984375
- w_qkv: bfloat16 [768, 2304], P(('leaf', 'fsdp')), may hold values from -0.21875 to 0.21875
- w_out: bfloat16 [768, 768], P(('leaf', 'fsdp')), may hold values from -3.5 to 3.5
- ln2_gain: bfloat16 [768], P(('leaf', 'fsdp')), may hold values from 0.099609375 to 1.8984375
- w_up: bfloat16 [768, 3072], P(('leaf', 'fsdp')), may hold values from -0.21875 to 0.21875
- up_bias: bfloat16 [3072], P(('leaf', 'fsdp')), may hold values from -3 to 3
- w_down: bfloat16 [3072, 768], P(('leaf', 'fsdp')), may hold values from -0.109375 to 0.109375
- down_bias: bfloat16 [768], P(('leaf', 'fsdp')), may hold values from -2 to 2
- mask_embed: bfloat16 [768], P(('leaf', 'fsdp')), may hold values from -5 to 5
- cotangent: bfloat16 [4, 2, 2048, 768], P('fsdp', None, 'leaf'), may hold values from -6 to 6
Outputs:
- output: bfloat16 [4, 2, 2048, 768], P('fsdp', None, 'leaf')
- grad_hidden: bfloat16 [4, 2048, 768], P('fsdp', 'leaf')
- grad_ln1_gain: float32 [768], P(('leaf', 'fsdp'))
- grad_w_qkv: float32 [768, 2304], P(('leaf', 'fsdp'))
- grad_w_out: float32 [768, 768], P(('leaf', 'fsdp'))
- grad_ln2_gain: float32 [768], P(('leaf', 'fsdp'))
- grad_w_up: float32 [768, 3072], P(('leaf', 'fsdp'))
- grad_up_bias: float32 [3072], P(('leaf', 'fsdp'))
- grad_w_down: float32 [3072, 768], P(('leaf', 'fsdp'))
- grad_down_bias: float32 [768], P(('leaf', 'fsdp'))
- grad_mask_embed: float32 [768], P(('leaf', 'fsdp'))
The draws below stay inside these ranges and needn't reach their ends.
Inputs may be any that keep to these rules, and one draw needn't show every extreme that they name: `seg_blocks`: segment numbers never fall along a tree; segment 0 holds the first 64 blocks (rounded down); every other segment has one block or more; the last segment ends the tree. `parents`: segment 0 is the trunk with parent 0; segments 1 to 4 have parent 0; each of them is the parent of exactly 2 of the segments above 4.
All inputs are finite; a program needn't handle non-finite values. No bound on the sum of `noise_mask` on one device may be relied on, other than what follows from the above.
Results may differ from the reference program's by a relative error of at most 0.015.
Values may be sent and summed in bfloat16 or wider, within the bound.
No kernel may reach another device: no remote copies, remote signals or barrier semaphores. Data moves between devices by JAX's collectives and lax.ppermute only.
A program may use at most 256 MiB of HBM per device.

```python
import math
import jax
import jax.numpy as jnp
from jax import lax

D = 768
HEAD_DIM = 64
FF = 3072
BLOCK = 16
BRANCHES = 4
LEAVES = 2
SEGS = 13
TREE_TOK = 2048
TREE_BLK = 128
TREES = 4


def draw_parents(key, part):
    tree_keys = jax.random.split(key, TREES)

    def one_tree(tree_key):
        order = jax.random.permutation(tree_key, BRANCHES * LEAVES)
        leaf_parent = (1 + order // LEAVES).astype(jnp.int32)
        return jnp.concatenate([jnp.zeros((1 + BRANCHES,), jnp.int32), leaf_parent])
    return jax.vmap(one_tree)(tree_keys)


def draw_seg_blocks(key, part):
    tree_keys = jax.random.split(jax.random.fold_in(key, 7), TREES)
    trunk = TREE_BLK // 2
    others = SEGS - 1
    rest = TREE_BLK - trunk
    spare = rest - others

    def one_tree(tree_key):
        picks = jax.random.randint(tree_key, (max(spare, 1),), 0, others).astype(jnp.int32)
        slots = jnp.arange(others, dtype=jnp.int32)
        hits = (picks[:, None] == slots[None, :]).astype(jnp.int32)
        hits = hits * (jnp.arange(max(spare, 1), dtype=jnp.int32) < spare).astype(jnp.int32)[:, None]
        lengths = 1 + jnp.sum(hits, axis=0).astype(jnp.int32)
        all_lengths = jnp.concatenate([jnp.full((1,), trunk, jnp.int32), lengths])
        ends = jnp.cumsum(all_lengths)
        block_ids = jnp.arange(TREE_BLK, dtype=jnp.int32)
        return jnp.sum((block_ids[:, None] >= ends[None, :-1]).astype(jnp.int32), axis=1).astype(jnp.int32)
    return jax.vmap(one_tree)(tree_keys)


def touch_ends(entries, own_key, low, largest):
    longest = entries.shape.index(max(entries.shape))
    spots = []
    for shift in (0, 1):
        where = [jax.random.randint(jax.random.fold_in(own_key, axis), (), 0, length) for axis, length in enumerate(entries.shape)]
        where[longest] = (where[longest] + shift) % entries.shape[longest]
        spots.append(tuple(where))
    return entries.at[spots[0]].set(low).at[spots[1]].set(largest)


def steps_of(own_key, shape, shards, low, top_value):
    factor_of, own = 1.0, jax.random.fold_in(own_key, 6)
    for dim, parts in shards:
        steps = jnp.exp(jax.random.uniform(jax.random.fold_in(own, dim), (parts,), jnp.float32, low / len(shards), top_value / len(shards)))
        factor_of = factor_of * jnp.repeat(steps, shape[dim] // parts).reshape([-1 if axis == dim else 1 for axis in range(len(shape))])
    return factor_of


def gaussian(key, dims, scale, reach, pieces=(), kind=jnp.bfloat16):
    array = jax.random.normal(key, dims, jnp.float32) * scale
    if len(pieces) > 0:
        array = steps_of(key, dims, pieces, -0.22, 0.18) * array
    return jnp.clip(array, min=-reach, max=reach).astype(kind)


def setup_inputs(seed: int = 0) -> dict:
    key_of = jax.random.split(jax.random.key(seed), 15)
    hidden = gaussian(key_of[0], (TREES, TREE_TOK, D), 1.0, 6.0, ((0, 4), (1, 8)))
    noise_mask = touch_ends((jax.random.randint(key_of[1], (TREES, TREE_TOK), 0, 2) < 1).astype(jnp.int32), jax.random.fold_in(key_of[1], 1), 0, 1)
    seg_blocks = draw_seg_blocks(jax.random.fold_in(key_of[14], 71), 0)
    parents = draw_parents(jax.random.fold_in(key_of[14], 71), 0)
    ln1_gain = jnp.clip(1.0 + 0.18 * jax.random.normal(key_of[4], (D,), jnp.float32), 0.099609375, 1.8984375).astype(jnp.bfloat16)
    w_qkv = gaussian(key_of[5], (D, 3 * D), D ** -0.5, 0.21875, ((0, 32),))
    w_out = gaussian(key_of[6], (D, D), (max(1, 8 * D // TREE_TOK)) ** -0.5, 3.5, ((0, 32),))
    ln2_gain = jnp.clip(1.0 + 0.18 * jax.random.normal(key_of[7], (D,), jnp.float32), 0.099609375, 1.8984375).astype(jnp.bfloat16)
    w_up = gaussian(key_of[8], (D, FF), D ** -0.5, 0.21875, ((0, 32),))
    up_bias = gaussian(key_of[9], (FF,), 0.5, 3.0, ((0, 32),))
    w_down = gaussian(key_of[10], (FF, D), FF ** -0.5, 0.109375, ((0, 32),))
    down_bias = gaussian(key_of[11], (D,), 0.3, 2.0, ((0, 32),))
    mask_embed = gaussian(key_of[12], (D,), 1.0, 5.0, ((0, 32),))
    cotangent = gaussian(key_of[13], (TREES, 2, TREE_TOK, D), 1.0, 6.0, ((0, 4), (2, 8)))
    return {"hidden": hidden, "noise_mask": noise_mask, "seg_blocks": seg_blocks, "parents": parents, "ln1_gain": ln1_gain, "w_qkv": w_qkv, "w_out": w_out, "ln2_gain": ln2_gain, "w_up": w_up, "up_bias": up_bias, "w_down": w_down, "down_bias": down_bias, "mask_embed": mask_embed, "cotangent": cotangent}


HIGH = lax.Precision.HIGHEST
NEG_FILL = -1000000000.0
EPSILON = 1e-05

@jax.custom_vjp
def low(v):
    return lax.optimization_barrier(v.astype(jnp.bfloat16)).astype(jnp.float32)

@jax.custom_vjp
def low_back(v):
    return v

def low_keep(v):
    return (low(v), None)

def low_pass(kept, grad):
    return (grad,)

def back_keep(v):
    return (v, None)

def back_low(kept, grad):
    return (low(grad),)
low.defvjp(low_keep, low_pass)
low_back.defvjp(back_keep, back_low)

def look_up(table, indices):
    slots = jnp.arange(table.shape[0], dtype=jnp.int32)
    hits = indices[..., None] == slots
    return lax.optimization_barrier(jnp.sum(jnp.where(hits, table, 0), axis=-1)).astype(jnp.int32)

def tree_layout(seg_row, parent_row):
    slots = jnp.arange(parent_row.shape[0], dtype=jnp.int32)
    seg_lengths = lax.optimization_barrier(jnp.sum((seg_row[:, None] == slots).astype(jnp.int32), axis=0))
    seg_starts = jnp.cumsum(seg_lengths) - seg_lengths
    grand_parent = look_up(parent_row, parent_row)
    offsets = jnp.where(slots > 0, look_up(seg_lengths, parent_row), 0) + jnp.where(parent_row > 0, look_up(seg_lengths, grand_parent), 0)
    block_ids = jnp.arange(seg_row.shape[0], dtype=jnp.int32)
    path_block = look_up(offsets, seg_row) + block_ids - look_up(seg_starts, seg_row)
    return (path_block, look_up(parent_row, seg_row), look_up(grand_parent, seg_row))

def block_mask(seg_row, parent_row):
    path_block, first_up, second_up = tree_layout(seg_row, parent_row)
    related = (seg_row[None, :] == seg_row[:, None]) | (seg_row[None, :] == first_up[:, None]) | (seg_row[None, :] == second_up[:, None])
    clean_ok = related & (path_block[None, :] <= path_block[:, None])
    noisy_ok = related & (path_block[None, :] < path_block[:, None])
    total = seg_row.shape[0]
    same_block = jnp.arange(total)[:, None] == jnp.arange(total)[None, :]
    upper = jnp.concatenate([clean_ok, jnp.zeros_like(clean_ok)], axis=1)
    lower = jnp.concatenate([noisy_ok, same_block], axis=1)
    return jnp.concatenate([upper, lower], axis=0)

def layer_norm(values, gain):
    centred = values - lax.optimization_barrier(jnp.mean(values, axis=-1, keepdims=True))
    spread = lax.optimization_barrier(jnp.mean(centred * centred, axis=-1, keepdims=True))
    return centred * lax.rsqrt(spread + EPSILON) * gain

def rotate(values, cosine, sine):
    half = values.shape[-1] // 2
    first = values[..., :half]
    second = values[..., half:]
    return jnp.concatenate([first * cosine - second * sine, second * cosine + first * sine], axis=-1)

def project(left, right):
    return jnp.matmul(left, right, precision=HIGH)

def reference(hidden, noise_mask, seg_blocks, parents, ln1_gain, w_qkv, w_out, ln2_gain, w_up, up_bias, w_down, down_bias, mask_embed, cotangent):
    trees = hidden.shape[0]
    tree_tok = hidden.shape[1]
    width = hidden.shape[2]
    heads = width // HEAD_DIM
    rows = 2 * tree_tok
    query_rows = math.gcd(rows, 512)
    path_block = jax.vmap(tree_layout)(seg_blocks, parents)[0]
    offsets_in = jnp.arange(BLOCK, dtype=jnp.int32)
    positions = (path_block[:, :, None] * BLOCK + offsets_in).reshape(trees, tree_tok).astype(jnp.float32)
    positions = jnp.concatenate([positions, positions], axis=1)
    freqs = jnp.exp(jnp.arange(HEAD_DIM // 2, dtype=jnp.float32) * (-math.log(10000.0) / (HEAD_DIM // 2)))
    angles = positions[:, :, None, None] * freqs
    cosine = jnp.cos(angles)
    sine = jnp.sin(angles)
    masks = jax.vmap(block_mask)(seg_blocks, parents)
    masked = (noise_mask == 1)[:, :, None]

    def forward(hid, gain_one, qkv_w, out_w, gain_two, up_w, up_b, down_w, down_b, embed):
        noisy = jnp.where(masked, embed, hid)
        stream = jnp.concatenate([hid, noisy], axis=1)
        normed = low(layer_norm(stream, gain_one))
        projected = low_back(project(normed, qkv_w))
        query = projected[..., :width].reshape(trees, rows, heads, HEAD_DIM)
        keyed = projected[..., width:2 * width].reshape(trees, rows, heads, HEAD_DIM)
        valued = projected[..., 2 * width:].reshape(trees, rows, heads, HEAD_DIM)
        query = low(rotate(query, cosine, sine))
        keyed = low(rotate(keyed, cosine, sine))
        valued = low(valued)

        def tree_attend(operands):
            q_tree, k_tree, v_tree, mask_tree = operands
            q_blocks = q_tree.reshape(rows // query_rows, query_rows, heads, HEAD_DIM)
            m_blocks = mask_tree.reshape(rows // query_rows, query_rows // BLOCK, mask_tree.shape[1])

            def one_block(pair):
                q_part, m_part = pair
                token_mask = jnp.repeat(jnp.repeat(m_part, BLOCK, axis=0), BLOCK, axis=1)
                raw = jnp.einsum('qhd,khd->hqk', q_part, k_tree, precision=HIGH) * 0.125
                scores = low_back(jnp.where(token_mask[None], raw, NEG_FILL))
                probs = low(jax.nn.softmax(scores, axis=-1))
                return jnp.einsum('hqk,khd->qhd', probs, v_tree, precision=HIGH)
            return lax.map(jax.checkpoint(one_block), (q_blocks, m_blocks)).reshape(rows, heads, HEAD_DIM)
        attended = lax.map(tree_attend, (query, keyed, valued, masks))
        mixed = low(low_back(attended.reshape(trees, rows, width)))
        after = stream + low_back(project(mixed, out_w))
        normed_two = low(layer_norm(after, gain_two))
        pre_act = low_back(project(normed_two, up_w) + up_b)
        activated = low(jax.nn.gelu(pre_act, approximate=True))
        return after + low_back(project(activated, down_w) + down_b)
    inputs = tuple((item.astype(jnp.float32) for item in (hidden, ln1_gain, w_qkv, w_out, ln2_gain, w_up, up_bias, w_down, down_bias, mask_embed)))
    result, backward = jax.vjp(forward, *inputs)
    grads = backward(cotangent.astype(jnp.float32).reshape(trees, rows, width))
    return (result.reshape(trees, 2, tree_tok, width).astype(jnp.bfloat16), grads[0].astype(jnp.bfloat16), grads[1], grads[2], grads[3], grads[4], grads[5], grads[6], grads[7], grads[8], grads[9])
```

```python
import functools
import math

import jax
import jax.numpy as jnp
from jax import lax
from jax.experimental import pallas as pl
from jax.experimental.pallas import tpu as pltpu
from jax.sharding import PartitionSpec as P

HEAD_DIM = 64
BLOCK = 16
NEG_FILL = -1000000000.0
EPSILON = 1e-05
VMEM_LIMIT = 56 * 1024 * 1024
BF = jnp.bfloat16
F32 = jnp.float32


def look_up(table, indices):
    slots = jnp.arange(table.shape[0], dtype=jnp.int32)
    hits = indices[..., None] == slots
    return jnp.sum(jnp.where(hits, table, 0), axis=-1)


def tree_layout(seg_row, parent_row):
    slots = jnp.arange(parent_row.shape[0], dtype=jnp.int32)
    seg_lengths = jnp.sum((seg_row[:, None] == slots).astype(jnp.int32), axis=0)
    seg_starts = jnp.sum((seg_row[:, None] < slots).astype(jnp.int32), axis=0)
    grand_parent = look_up(parent_row, parent_row)
    offsets = jnp.where(slots > 0, look_up(seg_lengths, parent_row), 0) + jnp.where(
        parent_row > 0, look_up(seg_lengths, grand_parent), 0
    )
    block_ids = jnp.arange(seg_row.shape[0], dtype=jnp.int32)
    path_block = look_up(offsets, seg_row) + block_ids - look_up(seg_starts, seg_row)
    return (path_block, look_up(parent_row, seg_row), look_up(grand_parent, seg_row))


class Links:
    def __init__(self):
        leaf = lax.axis_index("leaf")
        fsdp = lax.axis_index("fsdp")
        self.z, self.y = leaf // 2, leaf % 2
        self.x, self.core = fsdp // 2, fsdp % 2

    def swap_core(self, v):
        return lax.ppermute(v, "fsdp", [(i, i ^ 1) for i in range(4)])

    def swap_x(self, v):
        return lax.ppermute(v, "fsdp", [(i, i ^ 2) for i in range(4)])

    def swap_y(self, v, pairs=None):
        return lax.ppermute(v, "leaf", pairs or [(i, i ^ 1) for i in range(8)])

    def up(self, v, first, last):
        return lax.ppermute(v, "leaf", [(i, i + 2) for i in range(2 * first, 2 * last + 2)])

    def down(self, v, first, last):
        return lax.ppermute(v, "leaf", [(i, i - 2) for i in range(2 * first, 2 * last + 2)])


def both(bit, own, other, axis):
    return jnp.where(
        bit == 0, jnp.stack([own, other], axis), jnp.stack([other, own], axis)
    )


def gather_rows(at, block):
    ups, downs = [], []
    cur = block
    for s in (1, 2, 3):
        cur = at.up(cur, s - 1, 2)
        ups.append(cur)
    cur = block
    for s in (1, 2, 3):
        cur = at.down(cur, 1, 4 - s)
        downs.append(cur)
    places = []
    for p in range(4):
        value = block
        for z in range(4):
            if z != p:
                value = jnp.where(at.z == z, ups[z - p - 1] if z > p else downs[p - z - 1], value)
        places.append(value)
    line = jnp.stack(places)
    plane = both(at.y, line, at.swap_y(line), 1)
    plane = plane.reshape((8,) + block.shape)
    return both(at.x, plane, at.swap_x(plane), 1)


def pick(v, index, axis):
    return lax.dynamic_index_in_dim(v, index, axis, keepdims=False)


def choose(bit, v, axis):
    first, second = pick(v, 0, axis), pick(v, 1, axis)
    return jnp.where(bit == 0, first, second), jnp.where(bit == 0, second, first)


def plus(a, b):
    return a.astype(F32) + b.astype(F32)


def reduce_rows(at, own, other):
    g = plus(own, at.swap_core(other)).astype(BF)
    keep, send = choose(at.x, g, 1)
    g = plus(keep, at.swap_x(send)).astype(BF)
    g = g.reshape((4, 2) + g.shape[1:])
    keep, send = choose(at.y, g, 1)
    g = plus(keep, at.swap_y(send)).astype(BF)
    high = None
    for s in (1, 2, 3):
        part = pick(g, jnp.minimum(at.z + 4 - s, 3), 0)
        part = part if high is None else plus(part, high).astype(BF)
        high = at.up(part, 0, s - 1)
    low = None
    for s in (1, 2, 3):
        part = pick(g, jnp.maximum(at.z - 4 + s, 0), 0)
        part = part if low is None else plus(part, low).astype(BF)
        low = at.down(part, 4 - s, 3)
    return plus(pick(g, at.z, 0), high) + low.astype(F32)


def to_column_half(at, half_a, half_b):
    keep = jnp.where(at.core == 0, half_a, half_b)
    send = jnp.where(at.core == 0, half_b, half_a)
    got = at.swap_core(send)
    return both(at.core, keep, got, 0).reshape(2 * keep.shape[0], keep.shape[1])


def from_column_half(at, g):
    g = g.reshape(2, g.shape[0] // 2, g.shape[1])
    keep, send = choose(at.core, g, 0)
    got = at.swap_core(send)
    return jnp.where(at.core == 0, keep, got), jnp.where(at.core == 0, got, keep)


def spec(shape, index_map):
    return pl.BlockSpec(shape, index_map)


def turn(values, cosine, sine):
    lane = lax.broadcasted_iota(jnp.int32, (values.shape[0], 128), 1)
    low_half = (lane % HEAD_DIM) < HEAD_DIM // 2
    groups = []
    for n in range(values.shape[1] // 128):
        part = values[:, n * 128 : (n + 1) * 128]
        swapped = jnp.where(low_half, pltpu.roll(part, 96, 1), pltpu.roll(part, 32, 1))
        groups.append(part * cosine + swapped * sine)
    return groups


def project_kernel(x_ref, gain_ref, own_ref, other_ref, cos_ref, sin_ref, a_ref, q_ref, k_ref, v_ref):
    tile = pl.program_id(0)
    x = x_ref[...].astype(F32)
    centred = x - jnp.mean(x, axis=-1, keepdims=True)
    spread = jnp.mean(centred * centred, axis=-1, keepdims=True)
    a = (centred * lax.rsqrt(spread + EPSILON) * gain_ref[...]).astype(BF)
    a_ref[...] = a
    cosine, sine = cos_ref[...], sin_ref[...]
    half = own_ref.shape[1] // 3
    for n, w_ref in enumerate((own_ref, other_ref)):
        base = n * half
        kv = jnp.dot(a, w_ref[:, half:], preferred_element_type=F32)
        for g, part in enumerate(turn(kv[:, :half], cosine, sine)):
            k_ref[:, base + g * 128 : base + (g + 1) * 128] = part.astype(BF)
        v_ref[:, base : base + half] = kv[:, half:].astype(BF)

        @pl.when(tile < 2)
        def _():
            q = jnp.dot(a, w_ref[:, :half], preferred_element_type=F32)
            for g, part in enumerate(turn(q, cosine, sine)):
                q_ref[:, base + g * 128 : base + (g + 1) * 128] = part.astype(BF)


def project(x_all, gain, own, other, cosine, sine, rows):
    total, width = x_all.shape
    tiles = total // rows
    whole = lambda shape: spec(shape, lambda t: (0, 0))
    out = lambda n: jax.ShapeDtypeStruct((n, width), BF)
    return pl.pallas_call(
        project_kernel,
        grid=(tiles,),
        in_specs=[
            spec((rows, width), lambda t: (t, 0)),
            whole((1, width)),
            whole(own.shape),
            whole(other.shape),
            spec((rows, 128), lambda t: (t, 0)),
            spec((rows, 128), lambda t: (t, 0)),
        ],
        out_specs=[
            spec((rows, width), lambda t: (t, 0)),
            spec((rows, width), lambda t: (jnp.minimum(t, 1), 0)),
            spec((rows, width), lambda t: (t, 0)),
            spec((rows, width), lambda t: (t, 0)),
        ],
        out_shape=[out(total), out(2 * rows), out(total), out(total)],
        compiler_params=pltpu.CompilerParams(vmem_limit_bytes=VMEM_LIMIT),
        cost_estimate=pl.CostEstimate(
            flops=2 * total * width * 2 * width,
            bytes_accessed=2 * (4 * total * width + 3 * width * width),
            transcendentals=0,
        ),
    )(x_all, gain, own, other, cosine, sine)


def matmul_t(a, b):
    return lax.dot_general(a, b, (((1,), (1,)), ((), ())), preferred_element_type=F32)


def attend_kernel(
    rows, tiles, flag_ref, qcol_ref, krow_ref, q_ref, k_ref, v_ref, o_ref, lse_ref,
    bias_ref, s_ref, top_ref, sum_ref, acc_ref,
):
    pair = pl.program_id(0)
    both_rows = 2 * rows

    def span(t):
        return slice(t * rows, (t + 1) * rows)

    def lines(t):
        return slice(rows, both_rows) if t == 1 else slice(0, both_rows)

    @pl.when(pair == 0)
    def _():
        lse_ref[...] = jnp.zeros_like(lse_ref)
        own = qcol_ref[:, 0:1]
        up_one = qcol_ref[:, 1:2]
        up_two = qcol_ref[:, 2:3]
        limit = qcol_ref[:, 3:4]
        for t in range(tiles):
            if t == 1:
                r = lax.broadcasted_iota(jnp.int32, (rows, rows), 0) // BLOCK
                c = lax.broadcasted_iota(jnp.int32, (rows, rows), 1) // BLOCK
                bias_ref[rows:, span(t)] = jnp.where(r == c, 0.0, NEG_FILL)
            else:
                seg = krow_ref[0:1, span(t)]
                index = krow_ref[1:2, span(t)]
                ok = ((seg == own) | (seg == up_one) | (seg == up_two)) & (index < limit)
                bias_ref[:, span(t)] = jnp.where(ok, 0.0, NEG_FILL)

    lane = lax.broadcasted_iota(jnp.int32, (both_rows, 128), 1)
    result = None
    for h in range(2):
        mine = (lane // HEAD_DIM) == h
        q = jnp.where(mine, q_ref[...] * 0.125, 0).astype(BF)
        top_ref[...] = jnp.full_like(top_ref, -3.0e38)
        for t in range(tiles):

            @pl.when(flag_ref[t] > 0)
            def _():
                at = lines(t)
                s = matmul_t(q[at], k_ref[span(t), :]) + bias_ref[at, span(t)]
                s_ref[at, span(t)] = s
                best = top_ref[at, :]
                for c in range(rows // 128):
                    best = jnp.maximum(best, s[:, c * 128 : (c + 1) * 128])
                top_ref[at, :] = best

        top = jnp.max(top_ref[...], axis=-1, keepdims=True)
        sum_ref[...] = jnp.zeros_like(sum_ref)
        acc_ref[...] = jnp.zeros_like(acc_ref)
        for t in range(tiles):

            @pl.when(flag_ref[t] > 0)
            def _():
                at = lines(t)
                p = jnp.exp(s_ref[at, span(t)] - top[at])
                part = sum_ref[at, :]
                for c in range(rows // 128):
                    part = part + p[:, c * 128 : (c + 1) * 128]
                sum_ref[at, :] = part
                acc_ref[at, :] += jnp.dot(p.astype(BF), v_ref[span(t), :], preferred_element_type=F32)

        total = jnp.sum(sum_ref[...], axis=-1, keepdims=True)
        o = acc_ref[...] / total
        lse_ref[...] = jnp.where(lane == 2 * pair + h, top + jnp.log(total), lse_ref[...])
        result = o if result is None else jnp.where(mine, o, result)
    o_ref[...] = result.astype(BF)


def attend(flags, qcol, krow, q, k, v, rows):
    width = q.shape[1]
    total = k.shape[0]
    tiles = total // rows
    pair = lambda n: spec((n, 128), lambda p, f: (0, p))
    fixed = lambda shape: spec(shape, lambda p, f: (0, 0))
    return pl.pallas_call(
        functools.partial(attend_kernel, rows, tiles),
        grid_spec=pltpu.PrefetchScalarGridSpec(
            num_scalar_prefetch=1,
            grid=(width // 128,),
            in_specs=[fixed(qcol.shape), fixed(krow.shape), pair(2 * rows), pair(total), pair(total)],
            out_specs=[pair(2 * rows), fixed((2 * rows, 128))],
            scratch_shapes=[
                pltpu.VMEM((2 * rows, total), F32),
                pltpu.VMEM((2 * rows, total), F32),
                pltpu.VMEM((2 * rows, 128), F32),
                pltpu.VMEM((2 * rows, 128), F32),
                pltpu.VMEM((2 * rows, 128), F32),
            ],
        ),
        out_shape=[
            jax.ShapeDtypeStruct((2 * rows, width), BF),
            jax.ShapeDtypeStruct((2 * rows, 128), F32),
        ],
        compiler_params=pltpu.CompilerParams(vmem_limit_bytes=VMEM_LIMIT),
        cost_estimate=pl.CostEstimate(
            flops=16 * rows * total * width,
            bytes_accessed=4 * (total + rows) * width,
            transcendentals=2 * rows * total * width // HEAD_DIM,
        ),
    )(flags, qcol, krow, q, k, v)


def attend_back_kernel(
    rows, tiles, flag_ref, qrow_ref, kcol_ref, q_ref, k_ref, v_ref, o_ref, g_ref, lse_ref,
    cos_ref, sin_ref, dq_ref, dk_ref, dv_ref, bias_ref, acc_ref,
):
    pair = pl.program_id(0)
    both_rows = 2 * rows

    def span(t):
        return slice(t * rows, (t + 1) * rows)

    def lines(t):
        return slice(rows, both_rows) if t == 1 else slice(0, both_rows)

    @pl.when(pair == 0)
    def _():
        own = qrow_ref[0:1, :]
        up_one = qrow_ref[1:2, :]
        up_two = qrow_ref[2:3, :]
        limit = qrow_ref[3:4, :]
        for t in range(tiles):
            if t == 1:
                r = lax.broadcasted_iota(jnp.int32, (rows, rows), 0) // BLOCK
                c = lax.broadcasted_iota(jnp.int32, (rows, rows), 1) // BLOCK
                bias_ref[span(t), rows:] = jnp.where(r == c, 0.0, NEG_FILL)
            else:
                seg = kcol_ref[span(t), 0:1]
                index = kcol_ref[span(t), 1:2]
                ok = ((seg == own) | (seg == up_one) | (seg == up_two)) & (index < limit)
                bias_ref[span(t), :] = jnp.where(ok, 0.0, NEG_FILL)

    lane = lax.broadcasted_iota(jnp.int32, (both_rows, 128), 1)
    acc_ref[...] = jnp.zeros_like(acc_ref)
    queries, grads, deltas, norms = [], [], [], []
    product = (o_ref[...].astype(F32) * g_ref[...].astype(F32)).T
    for h in range(2):
        mine = (lane // HEAD_DIM) == h
        queries.append(jnp.where(mine, q_ref[...] * 0.125, 0).astype(BF))
        grads.append(jnp.where(mine, g_ref[...], 0).astype(BF))
        deltas.append(jnp.sum(product[h * HEAD_DIM : (h + 1) * HEAD_DIM], axis=0, keepdims=True))
        norms.append(lse_ref[pl.ds(2 * pair + h, 1), :])
    for t in range(tiles):

        @pl.when(flag_ref[t] == 0)
        def _():
            dk_ref[span(t), :] = jnp.zeros((rows, 128), BF)
            dv_ref[span(t), :] = jnp.zeros((rows, 128), BF)

        @pl.when(flag_ref[t] > 0)
        def _():
            at = lines(t)
            keys, values = k_ref[span(t), :], v_ref[span(t), :]
            keys_t = keys.astype(F32).T.astype(BF)
            dk = dv = None
            for h in range(2):
                q, g = queries[h][at], grads[h][at]
                s = matmul_t(keys, q) + bias_ref[span(t), at]
                p = jnp.exp(s - norms[h][:, at])
                dp = matmul_t(values, g)
                ds = (p * (dp - deltas[h][:, at])).astype(BF)
                part_v = jnp.dot(p.astype(BF), g, preferred_element_type=F32)
                part_k = jnp.dot(ds, q, preferred_element_type=F32)
                dv = part_v if dv is None else dv + part_v
                dk = part_k if dk is None else dk + part_k
                half = slice(h * HEAD_DIM, (h + 1) * HEAD_DIM)
                acc_ref[half, at] += jnp.dot(keys_t[half], ds, preferred_element_type=F32)
            [dk] = turn(dk, cos_ref[span(t), :], -sin_ref[span(t), :])
            dk_ref[span(t), :] = dk.astype(BF)
            dv_ref[span(t), :] = dv.astype(BF)

    dq = acc_ref[...].T * 0.125
    [dq] = turn(dq, cos_ref[:both_rows, :], -sin_ref[:both_rows, :])
    dq_ref[...] = dq.astype(BF)


def attend_back(flags, qrow, kcol, q, k, v, o, g, lse, cosine, sine, rows):
    width = q.shape[1]
    total = k.shape[0]
    tiles = total // rows
    pair = lambda n: spec((n, 128), lambda p, f: (0, p))
    fixed = lambda shape: spec(shape, lambda p, f: (0, 0))
    out = lambda n: jax.ShapeDtypeStruct((n, width), BF)
    return pl.pallas_call(
        functools.partial(attend_back_kernel, rows, tiles),
        grid_spec=pltpu.PrefetchScalarGridSpec(
            num_scalar_prefetch=1,
            grid=(width // 128,),
            in_specs=[
                fixed(qrow.shape), fixed(kcol.shape), pair(2 * rows), pair(total), pair(total),
                pair(2 * rows), pair(2 * rows), fixed(lse.shape), fixed(cosine.shape), fixed(sine.shape),
            ],
            out_specs=[pair(2 * rows), pair(total), pair(total)],
            scratch_shapes=[
                pltpu.VMEM((total, 2 * rows), F32),
                pltpu.VMEM((128, 2 * rows), F32),
            ],
        ),
        out_shape=[out(2 * rows), out(total), out(total)],
        compiler_params=pltpu.CompilerParams(vmem_limit_bytes=VMEM_LIMIT),
        cost_estimate=pl.CostEstimate(
            flops=40 * rows * total * width,
            bytes_accessed=8 * (total + rows) * width,
            transcendentals=2 * rows * total * width // HEAD_DIM,
        ),
    )(flags, qrow, kcol, q, k, v, o, g, lse, cosine, sine)


def normalise(values):
    centred = values - jnp.mean(values, axis=-1, keepdims=True)
    spread = jnp.mean(centred * centred, axis=-1, keepdims=True)
    scale = lax.rsqrt(spread + EPSILON)
    return centred * scale, scale


def norm_back(hat, scale, gain, grad):
    scaled = grad * gain
    return scale * (
        scaled
        - jnp.mean(scaled, axis=-1, keepdims=True)
        - hat * jnp.mean(scaled * hat, axis=-1, keepdims=True)
    )


ROOT = math.sqrt(2.0 / math.pi)


def gelu_parts(u):
    t = jnp.tanh(ROOT * (u + 0.044715 * (u * u * u)))
    slope = 0.5 * (1.0 + t) + 0.5 * u * (1.0 - t * t) * (ROOT * (1.0 + 3 * 0.044715 * (u * u)))
    return 0.5 * u * (1.0 + t), slope


def mm(a, b):
    return jnp.dot(a, b, preferred_element_type=F32)


def mm_t(a, b):
    return lax.dot_general(a, b, (((1,), (1,)), ((), ())), preferred_element_type=F32)


def t_mm(a, b):
    return lax.dot_general(a, b, (((0,), (0,)), ((), ())), preferred_element_type=F32)


def halves_of_heads(w):
    w = w.reshape(w.shape[0], 3, 2, -1)
    return w[:, :, 0].reshape(w.shape[0], -1), w[:, :, 1].reshape(w.shape[0], -1)


def heads_of_halves(a, b):
    a, b = a.reshape(a.shape[0], 3, -1), b.reshape(b.shape[0], 3, -1)
    return jnp.stack([a, b], 2).reshape(a.shape[0], -1)


def halves_of_units(w, chunk):
    w = w.reshape(w.shape[0], -1, 2, chunk)
    return w[:, :, 0].reshape(w.shape[0], -1), w[:, :, 1].reshape(w.shape[0], -1)


def units_of_halves(a, b, chunk):
    a, b = a.reshape(a.shape[0], -1, chunk), b.reshape(b.shape[0], -1, chunk)
    return jnp.stack([a, b], 2).reshape(a.shape[0], -1)


class Chain:
    def __init__(self, rows):
        self.at = Links()
        self.rows = rows
        self.core = self.at.core

    def tree(self, hid):
        at = self.at
        chain = []
        cur = hid
        for s in (1, 2, 3):
            cur = at.up(cur, s - 1, 2)
            pairs = [(i, i ^ 1) for i in range(2 * s, 8)]
            chain += [cur, at.swap_y(cur, pairs)]
        chain.append(at.swap_y(hid, [(i, i + 1) for i in range(0, 8, 2)]))
        return chain

    def tile_leaves(self):
        z, y = self.at.z, self.at.y
        found = []
        for s in (1, 2, 3):
            found += [(2 * (z - s) + y, z >= s), (2 * (z - s) + 1 - y, z >= s)]
        found.append((2 * z, y == 1))
        return found

    def tree_sum(self, own, parts):
        at = self.at
        low = [at.swap_y(parts[6], [(i, i - 1) for i in range(1, 8, 2)])]
        for s in (1, 2, 3):
            pairs = [(i, i ^ 1) for i in range(2 * s, 8)]
            low.append(at.swap_y(parts[2 * s - 1], pairs))
        cur = plus(parts[4], low[3])
        for s in (2, 1):
            cur = at.down(cur.astype(BF), s + 1, 3).astype(F32) + plus(parts[2 * s - 2], low[s])
        return own + at.down(cur.astype(BF), 1, 3).astype(F32) + low[0].astype(F32)

    def weights(self, w_qkv, w_out, w_up, w_down, vectors):
        at = self.at
        block = to_column_half(at, *halves_of_heads(w_qkv))
        mine = at.swap_core(vectors)
        row = both(at.core, vectors, mine, 0).reshape(1, -1)
        row = jnp.pad(row, ((0, 7), (0, block.shape[1] - row.shape[1])))
        first = gather_rows(at, jnp.concatenate([block, row], axis=0))
        m = block.shape[0]
        qkv = first[:, :, :m].reshape(16 * m, -1)
        vec = first[:, :, m, : 2 * vectors.shape[0]].reshape(32, -1)
        out_up = jnp.concatenate(
            [
                to_column_half(at, w_out[:, : w_out.shape[1] // 2], w_out[:, w_out.shape[1] // 2 :]),
                to_column_half(at, *halves_of_units(w_up, w_down.shape[0])),
            ],
            axis=1,
        )
        second = gather_rows(at, out_up).reshape(16 * m, -1)
        down = gather_rows(at, w_down).reshape(16 * w_down.shape[0], -1)
        cut = w_out.shape[1] // 2
        out_own = second[:, :cut]
        up_own = second[:, cut:]
        qkv_both = (qkv, at.swap_core(qkv))
        up_both = (up_own, at.swap_core(up_own))
        down_both = (down, at.swap_core(down))
        out = both(at.core, out_own, at.swap_core(out_own), 1).reshape(16 * m, -1)
        half = out.shape[0] // 2
        out = jnp.where(at.core == 0, out, jnp.concatenate([out[half:], out[:half]], axis=0))
        return qkv_both, out, up_both, down_both, vec

    def unit_bias(self, bias, chunk):
        a, b = halves_of_units(bias[None], chunk)
        return jnp.where(self.core == 0, a, b), jnp.where(self.core == 0, b, a)

    def unit_bias_back(self, own, other, chunk):
        a = jnp.where(self.core == 0, own, other)
        b = jnp.where(self.core == 0, other, own)
        return units_of_halves(a, b, chunk)[0]

    def sum_down(self, own, other):
        shape = (8, 2, own.shape[0] // 16, own.shape[1])
        return reduce_rows(self.at, own.reshape(shape), other.reshape(shape))

    def sum_up(self, own, other, chunk):
        shape = (8, 2, own.shape[0] // 16, own.shape[1])
        g = reduce_rows(self.at, own.reshape(shape), other.reshape(shape))
        return units_of_halves(*from_column_half(self.at, g), chunk)

    def sum_out(self, g):
        at = self.at
        half = g.shape[0] // 2
        g = jnp.where(at.core == 0, g, jnp.concatenate([g[half:], g[:half]], axis=0))
        g = g.reshape(8, 2, g.shape[0] // 16, 2, g.shape[1] // 2)
        own, other = choose(at.core, g, 3)
        a, b = from_column_half(at, reduce_rows(at, own, other))
        return jnp.concatenate([a, b], axis=1)

    def sum_qkv(self, own, other, vec):
        at = self.at
        m = own.shape[0] // 16
        shape = (8, 2, m, own.shape[1])
        n = vec.shape[1]
        rows = jnp.pad(vec.astype(BF).reshape(8, 2, 2, 1, n), ((0, 0),) * 3 + ((0, 7), (0, own.shape[1] - n)))
        mine, its = choose(at.core, rows, 2)
        g = reduce_rows(
            at,
            jnp.concatenate([own.reshape(shape), mine], axis=2),
            jnp.concatenate([other.reshape(shape), its], axis=2),
        )
        return heads_of_halves(*from_column_half(at, g[:m])), g[m, :n]


AXES = ("leaf", "fsdp")


class Whole:
    def __init__(self, rows, leaves, devices):
        self.rows, self.leaves, self.devices = rows, leaves, devices
        self.leaf = lax.axis_index("leaf")

    def tree(self, hid):
        every = lax.all_gather(hid, "leaf", axis=0, tiled=False)
        return [pick(every, leaf, 0) for leaf, _ in self.tile_leaves()]

    def tile_leaves(self):
        found = []
        for s in range(1, self.leaves):
            place = self.leaf - s
            found.append((jnp.maximum(place, 0), place >= 0))
        return found

    def tree_sum(self, own, parts):
        every = jnp.stack([own.astype(BF)] + [p for p in parts])
        order = [pick(every, (self.leaf - t) % self.leaves, 0) for t in range(self.leaves)]
        every = jnp.concatenate(order, axis=0)
        return lax.psum_scatter(every, "leaf", scatter_dimension=0, tiled=True).astype(F32)

    def weights(self, w_qkv, w_out, w_up, w_down, vectors):
        every = lambda w: lax.all_gather(w, AXES, axis=0, tiled=True)
        up_w, down_w = every(w_up), every(w_down)
        half = down_w.shape[0] // 2
        return (
            halves_of_heads(every(w_qkv)),
            every(w_out),
            (up_w[:, :half], up_w[:, half:]),
            (down_w[:half], down_w[half:]),
            every(vectors[None]),
        )

    def unit_bias(self, bias, chunk):
        half = bias.shape[0] // 2
        return bias[None, :half], bias[None, half:]

    def unit_bias_back(self, own, other, chunk):
        return jnp.concatenate([own, other], axis=1)[0]

    def scatter(self, g):
        return lax.psum_scatter(g.astype(F32), AXES, scatter_dimension=0, tiled=True)

    def sum_down(self, own, other):
        return self.scatter(jnp.concatenate([own, other], axis=0))

    def sum_up(self, own, other, chunk):
        return self.scatter(jnp.concatenate([own, other], axis=1))

    def sum_out(self, g):
        return self.scatter(g)

    def sum_qkv(self, own, other, vec):
        return self.scatter(heads_of_halves(own, other)), self.scatter(vec)[0]


def shards(
    leaves,
    groups,
    hidden,
    noise_mask,
    seg_blocks,
    parents,
    ln1_gain,
    w_qkv,
    w_out,
    ln2_gain,
    w_up,
    up_bias,
    w_down,
    down_bias,
    mask_embed,
    cotangent,
):
    rows = hidden.shape[1]
    width = hidden.shape[2]
    devices = leaves * groups
    net = Chain(rows) if (leaves, groups) == (8, 4) else Whole(rows, leaves, devices)
    chunk = w_down.shape[0]
    few = ln1_gain.shape[0]

    hid = hidden[0]
    lower = net.tree(hid)
    vectors = jnp.concatenate([ln1_gain, ln2_gain, down_bias, mask_embed, up_bias])
    qkv_w, out_w, up_w, down_w, vec = net.weights(w_qkv, w_out, w_up, w_down, vectors)
    gain_one, gain_two, down_b, embed = (
        vec[:, n * few : (n + 1) * few].reshape(1, width).astype(F32) for n in range(4)
    )
    up_b = net.unit_bias(vec[:, 4 * few :].reshape(-1).astype(F32), chunk)

    blocks = rows // BLOCK
    leaf = lax.axis_index("leaf")
    seg_row = seg_blocks[0]
    path_block, first_up, second_up = tree_layout(seg_row, parents[0])
    table = jnp.stack([seg_row, path_block, jnp.arange(seg_row.shape[0], dtype=jnp.int32), first_up, second_up])
    table = table.reshape(5, leaves, blocks)
    own = pick(table, leaf, 1)
    tiles = [own, own.at[0].set(-1)]
    for place, valid in net.tile_leaves():
        tile = pick(table, jnp.maximum(place, 0), 1)
        tiles.append(tile.at[0].set(jnp.where(valid, tile[0], -1)))
    keys = jnp.stack(tiles, axis=1)
    limit = jnp.concatenate([own[2] + 1, own[2]])
    queries = [jnp.tile(own[n], 2) for n in (0, 3, 4)] + [limit]
    seg_k, index_k = keys[0].reshape(1, -1), keys[2].reshape(1, -1)
    allowed = (
        (seg_k == queries[0][:, None]) | (seg_k == queries[1][:, None]) | (seg_k == queries[2][:, None])
    ) & (index_k < limit[:, None])
    flags = jnp.any(allowed.reshape(2 * blocks, -1, blocks), axis=(0, 2)).astype(jnp.int32)
    flags = flags.at[:2].set(1)
    per_token = lambda v: jnp.repeat(v, BLOCK, axis=-1)
    query_rows = per_token(jnp.stack(queries + queries))
    key_rows = per_token(jnp.concatenate([seg_k, index_k] * 4))
    query_cols = query_rows.T
    key_cols = key_rows.T

    lanes = jnp.arange(128, dtype=jnp.int32)
    exponent = (lanes % (HEAD_DIM // 2)).astype(F32) * (-math.log(10000.0) / (HEAD_DIM // 2))
    positions = (keys[1][:, :, None] * BLOCK + jnp.arange(BLOCK, dtype=jnp.int32)).reshape(-1, 1)
    angles = positions.astype(F32) * jnp.exp(exponent)
    cosine = jnp.cos(angles)
    sine = jnp.sin(angles) * jnp.where((lanes % HEAD_DIM) < HEAD_DIM // 2, -1.0, 1.0)

    masked = (noise_mask[0] == 1)[:, None]
    noisy = jnp.where(masked, embed.astype(BF), hid)
    x_all = jnp.concatenate([hid, noisy] + lower, axis=0)
    stream = jnp.concatenate([hid, noisy], axis=0).astype(F32)
    a_all, query, key, value = project(x_all, gain_one, qkv_w[0], qkv_w[1], cosine, sine, rows)
    mixed, log_norm = attend(flags, query_cols, key_rows, query, key, value, rows)
    after = stream + mm(mixed, out_w)
    hat_two, scale_two = normalise(after)
    normed_two = (hat_two * gain_two).astype(BF)
    act, slope = [], []
    for n in range(2):
        g, s = gelu_parts(mm(normed_two, up_w[n]) + up_b[n])
        act.append(g.astype(BF))
        slope.append(s)
    result = after + (mm(act[0], down_w[0]) + mm(act[1], down_w[1])) + down_b
    output = result.astype(BF).reshape(1, 2, rows, width)

    grad_two = cotangent[0].reshape(2 * rows, width)
    grad_out = grad_two.astype(F32)
    grad_down_b = jnp.sum(grad_out, axis=0)
    grad_down_w = [t_mm(act[n], grad_two).astype(BF) for n in range(2)]
    grad_pre = [(mm_t(grad_two, down_w[n]) * slope[n]).astype(BF) for n in range(2)]
    grad_up_b = [jnp.sum(g.astype(F32), axis=0, keepdims=True) for g in grad_pre]
    grad_up_w = [t_mm(normed_two, g).astype(BF) for g in grad_pre]
    grad_normed = mm_t(grad_pre[0], up_w[0]) + mm_t(grad_pre[1], up_w[1])
    grad_gain_two = jnp.sum(grad_normed * hat_two, axis=0)
    grad_after = grad_out + norm_back(hat_two, scale_two, gain_two, grad_normed)
    sum_down = net.sum_down(*grad_down_w)
    sum_up = net.sum_up(*grad_up_w, chunk)

    grad_one = grad_after.astype(BF)
    grad_out_w = t_mm(mixed, grad_one).astype(BF)
    grad_mixed = mm_t(grad_one, out_w).astype(BF)
    sum_out = net.sum_out(grad_out_w)
    grad_q, grad_k, grad_v = attend_back(
        flags, query_rows, key_cols, query, key, value, mixed, grad_mixed, log_norm.T, cosine, sine, rows
    )
    half = width // 2
    grad_a_kv = None
    grad_a_q = None
    grad_qkv_w = []
    for n in range(2):
        cut = slice(n * half, (n + 1) * half)
        pieces = (grad_k[:, cut], grad_v[:, cut])
        kv = jnp.concatenate(pieces, axis=1)
        part = mm_t(kv, qkv_w[n][:, half:])
        grad_a_kv = part if grad_a_kv is None else grad_a_kv + part
        part = mm_t(grad_q[:, cut], qkv_w[n][:, :half])
        grad_a_q = part if grad_a_q is None else grad_a_q + part
        grad_qkv_w.append(
            jnp.concatenate(
                [t_mm(a_all[: 2 * rows], grad_q[:, cut]).astype(BF), t_mm(a_all, kv).astype(BF)], axis=1
            )
        )
    hat_all, _ = normalise(x_all.astype(F32))
    grad_gain_one = jnp.sum(grad_a_kv * hat_all, axis=0) + jnp.sum(grad_a_q * hat_all[: 2 * rows], axis=0)
    mine = grad_a_kv[: 2 * rows] + grad_a_q
    parts = [grad_a_kv[t * rows : (t + 1) * rows].astype(BF) for t in range(2, len(tiles))]
    hat_noisy, scale_noisy = normalise(stream[rows:])
    stream_noisy = grad_after[rows:] + norm_back(hat_noisy, scale_noisy, gain_one, mine[rows:])
    grad_embed = jnp.sum(jnp.where(masked, stream_noisy, 0.0), axis=0)
    grad_vec = jnp.concatenate(
        [
            v.reshape(devices, -1)
            for v in (
                grad_gain_one, grad_gain_two, grad_down_b, grad_embed,
                net.unit_bias_back(grad_up_b[0], grad_up_b[1], chunk),
            )
        ],
        axis=1,
    )
    sum_qkv, sum_vec = net.sum_qkv(*grad_qkv_w, grad_vec)
    clean = net.tree_sum(mine[:rows], parts)
    hat_clean, scale_clean = normalise(stream[:rows])
    stream_clean = grad_after[:rows] + norm_back(hat_clean, scale_clean, gain_one, clean)
    grad_hidden = (stream_clean + jnp.where(masked, 0.0, stream_noisy)).astype(BF)[None]
    piece = lambda n: sum_vec[n * few : (n + 1) * few]
    return (
        output,
        grad_hidden,
        piece(0),
        sum_qkv,
        sum_out,
        piece(1),
        sum_up,
        sum_vec[4 * few :],
        sum_down,
        piece(2),
        piece(3),
    )


def solution(mesh):
    split = ("leaf", "fsdp")
    in_specs = (
        P("fsdp", "leaf", None),
        P("fsdp", "leaf"),
        P("fsdp", None),
        P("fsdp", None),
        P(split),
        P(split, None),
        P(split, None),
        P(split),
        P(split, None),
        P(split),
        P(split, None),
        P(split),
        P(split),
        P("fsdp", None, "leaf", None),
    )
    out_specs = (
        P("fsdp", None, "leaf", None),
        P("fsdp", "leaf", None),
        P(split),
        P(split, None),
        P(split, None),
        P(split),
        P(split, None),
        P(split),
        P(split, None),
        P(split),
        P(split),
    )
    body = functools.partial(shards, mesh.shape["leaf"], mesh.shape["fsdp"])
    return jax.shard_map(body, mesh=mesh, in_specs=in_specs, out_specs=out_specs, check_vma=False)
```

```python
import functools
import math

import jax
import jax.numpy as jnp
from jax import lax
from jax.experimental import pallas as pl
from jax.experimental.pallas import tpu as pltpu
from jax.sharding import PartitionSpec as P

HEAD_DIM = 64
BLOCK = 16
NEG_FILL = -1000000000.0
EPSILON = 1e-05
VMEM_LIMIT = 56 * 1024 * 1024
BF = jnp.bfloat16
F32 = jnp.float32


def look_up(table, indices):
    slots = jnp.arange(table.shape[0], dtype=jnp.int32)
    hits = indices[..., None] == slots
    return jnp.sum(jnp.where(hits, table, 0), axis=-1)


def tree_layout(seg_row, parent_row):
    slots = jnp.arange(parent_row.shape[0], dtype=jnp.int32)
    seg_lengths = jnp.sum((seg_row[:, None] == slots).astype(jnp.int32), axis=0)
    seg_starts = jnp.sum((seg_row[:, None] < slots).astype(jnp.int32), axis=0)
    grand_parent = look_up(parent_row, parent_row)
    offsets = jnp.where(slots > 0, look_up(seg_lengths, parent_row), 0) + jnp.where(
        parent_row > 0, look_up(seg_lengths, grand_parent), 0
    )
    block_ids = jnp.arange(seg_row.shape[0], dtype=jnp.int32)
    path_block = look_up(offsets, seg_row) + block_ids - look_up(seg_starts, seg_row)
    return (path_block, look_up(parent_row, seg_row), look_up(grand_parent, seg_row))


class Links:
    def __init__(self):
        leaf = lax.axis_index("leaf")
        fsdp = lax.axis_index("fsdp")
        self.z, self.y = leaf // 2, leaf % 2
        self.x, self.core = fsdp // 2, fsdp % 2

    def swap_core(self, v):
        return lax.ppermute(v, "fsdp", [(i, i ^ 1) for i in range(4)])

    def swap_x(self, v):
        return lax.ppermute(v, "fsdp", [(i, i ^ 2) for i in range(4)])

    def swap_y(self, v, pairs=None):
        return lax.ppermute(v, "leaf", pairs or [(i, i ^ 1) for i in range(8)])

    def swap_z(self, v, n):
        return lax.ppermute(v, "leaf", [(i, i ^ (2 * n)) for i in range(8)])

    def up(self, v, first, last):
        return lax.ppermute(v, "leaf", [(i, i + 2) for i in range(2 * first, 2 * last + 2)])

    def down(self, v, first, last):
        return lax.ppermute(v, "leaf", [(i, i - 2) for i in range(2 * first, 2 * last + 2)])


def both(bit, own, other, axis):
    return jnp.where(
        bit == 0, jnp.stack([own, other], axis), jnp.stack([other, own], axis)
    )


def after(values, done):
    values, done = list(values), list(done)
    return lax.optimization_barrier(tuple(values + done))[: len(values)]


def z_gather(at, block):
    return jnp.concatenate([block] + [at.swap_z(block, n) for n in (1, 2, 3)], axis=0)


def pick(v, index, axis):
    return lax.dynamic_index_in_dim(v, index, axis, keepdims=False)


def choose(bit, v, axis):
    first, second = pick(v, 0, axis), pick(v, 1, axis)
    return jnp.where(bit == 0, first, second), jnp.where(bit == 0, second, first)


def plus(a, b):
    return a.astype(F32) + b.astype(F32)


def z_reduce(at, g):
    got = [at.swap_z(pick(g, at.z ^ n, 0), n) for n in (1, 2, 3)]
    return plus(pick(g, at.z, 0), got[0]) + plus(got[1], got[2])


def reduce_x_first(at, own, other):
    g = plus(own, at.swap_core(other)).astype(BF)
    keep, send = choose(at.x, g, 1)
    g = plus(keep, at.swap_x(send)).astype(BF)
    g = g.reshape((4, 2) + g.shape[1:])
    keep, send = choose(at.y, g, 1)
    return z_reduce(at, plus(keep, at.swap_y(send)).astype(BF))


def reduce_y_first(at, own, other):
    g = plus(own, at.swap_core(other)).astype(BF)
    g = g.reshape((4, 2) + g.shape[1:])
    keep, send = choose(at.y, g, 1)
    g = z_reduce(at, plus(keep, at.swap_y(send)).astype(BF)).astype(BF)
    keep, send = choose(at.x, g, 0)
    return plus(keep, at.swap_x(send))


def to_column_half(at, half_a, half_b):
    keep = jnp.where(at.core == 0, half_a, half_b)
    send = jnp.where(at.core == 0, half_b, half_a)
    got = at.swap_core(send)
    return both(at.core, keep, got, 0).reshape(2 * keep.shape[0], keep.shape[1])


def from_column_half(at, g):
    g = g.reshape(2, g.shape[0] // 2, g.shape[1])
    keep, send = choose(at.core, g, 0)
    got = at.swap_core(send)
    return jnp.where(at.core == 0, keep, got), jnp.where(at.core == 0, got, keep)


def spec(shape, index_map):
    return pl.BlockSpec(shape, index_map)


def turn(values, cosine, sine):
    lane = lax.broadcasted_iota(jnp.int32, (values.shape[0], 128), 1)
    low_half = (lane % HEAD_DIM) < HEAD_DIM // 2
    groups = []
    for n in range(values.shape[1] // 128):
        part = values[:, n * 128 : (n + 1) * 128]
        swapped = jnp.where(low_half, pltpu.roll(part, 96, 1), pltpu.roll(part, 32, 1))
        groups.append(part * cosine + swapped * sine)
    return groups


def fetch(pieces, sems):
    copies = [pltpu.make_async_copy(src, dst, sems.at[n]) for n, (src, dst) in enumerate(pieces)]
    for copy in copies:
        copy.start()
    return copies


def placed(ref, count, size, table, row):
    return [
        ref.at[pl.ds(pl.multiple_of(table[row, n] * size, size), size), :] for n in range(count)
    ]


def project_kernel(
    count, size, first_rows, table_ref, x_ref, mask_ref, embed_ref, gain_ref, own_hbm, other_hbm, cos_ref, sin_ref,
    a_ref, q_ref, k_ref, v_ref, own_ref, other_ref, sems,
):
    tile = pl.program_id(0)

    @pl.when(tile == 0)
    def _():
        pieces = []
        for hbm, ref in ((own_hbm, own_ref), (other_hbm, other_ref)):
            spots = placed(ref, count, size, table_ref, 0)
            pieces += [(hbm.at[n, pl.ds(0, size), :], spots[n]) for n in range(count)]
        for copy in fetch(pieces, sems):
            copy.wait()

    x = jnp.where(mask_ref[...] > 0, embed_ref[...], x_ref[...].astype(F32))
    centred = x - jnp.mean(x, axis=-1, keepdims=True)
    spread = jnp.mean(centred * centred, axis=-1, keepdims=True)
    a = (centred * lax.rsqrt(spread + EPSILON) * gain_ref[...]).astype(BF)
    a_ref[...] = a
    cosine, sine = cos_ref[...], sin_ref[...]
    half = own_ref.shape[1] // 3
    for n, w_ref in enumerate((own_ref, other_ref)):
        base = n * half
        keys = jnp.dot(a, w_ref[:, half : 2 * half], preferred_element_type=F32)
        for g, part in enumerate(turn(keys, cosine, sine)):
            k_ref[:, base + g * 128 : base + (g + 1) * 128] = part.astype(BF)
        values = jnp.dot(a, w_ref[:, 2 * half :], preferred_element_type=F32)
        v_ref[:, base : base + half] = values.astype(BF)

    @pl.when(tile * x_ref.shape[0] < first_rows)
    def _():
        rows = q_ref.shape[0]
        for n, w_ref in enumerate((own_ref, other_ref)):
            base = n * half
            q = jnp.dot(a[:rows], w_ref[:, :half], preferred_element_type=F32)
            for g, part in enumerate(turn(q, cosine[:rows], sine[:rows])):
                q_ref[:, base + g * 128 : base + (g + 1) * 128] = part.astype(BF)


def project(table, x_all, mask, embed, gain, own, other, cosine, sine, rows):
    total, width = x_all.shape
    step = next(n for n in (3 * rows, 2 * rows, rows) if total % n == 0)
    q_step = min(step, 2 * rows)
    last_q = 2 * rows // q_step - 1
    count = own.shape[0]
    size = width // count
    columns = own.shape[2]
    whole = lambda shape: spec(shape, lambda t, i: (0, 0))
    moved = lambda n: spec((step, n), lambda t, i: (t, 0))
    out = lambda n: jax.ShapeDtypeStruct((n, width), BF)
    anywhere = pl.BlockSpec(memory_space=pl.ANY)
    return pl.pallas_call(
        functools.partial(project_kernel, count, size, 2 * rows),
        grid_spec=pltpu.PrefetchScalarGridSpec(
            num_scalar_prefetch=1,
            grid=(total // step,),
            in_specs=[
                moved(width), moved(1), whole((1, width)), whole((1, width)), anywhere, anywhere, moved(128), moved(128),
            ],
            out_specs=[
                moved(width),
                spec((q_step, width), lambda t, i: (jnp.minimum(t, last_q), 0)),
                moved(width),
                moved(width),
            ],
            scratch_shapes=[
                pltpu.VMEM((width, columns), BF),
                pltpu.VMEM((width, columns), BF),
                pltpu.SemaphoreType.DMA((2 * count,)),
            ],
        ),
        out_shape=[out(total), out(2 * rows), out(total), out(total)],
        compiler_params=pltpu.CompilerParams(vmem_limit_bytes=VMEM_LIMIT),
        cost_estimate=pl.CostEstimate(
            flops=2 * total * width * 2 * width + 4 * rows * width * width,
            bytes_accessed=2 * (4 * total * width + 3 * width * width),
            transcendentals=0,
        ),
    )(table, x_all, mask, embed, gain, own, other, cosine, sine)


def middle_kernel(
    count, size, chunk, table_ref, o_ref, x_ref, dy_ref, gain_ref, up_b_ref, down_b_ref,
    one_own, one_other, two_own, two_other,
    y_ref, b_ref, g_ref, du_ref, dh_low_ref, do_ref, dh_ref, dgain_ref, dup_b_ref, ddown_b_ref,
    out_ref, up_ref, down_ref, sems,
):
    cut = out_ref.shape[1] // 2
    units = up_ref.shape[2]
    pieces_out, pieces_up, pieces_down = [], [], []
    for n, (one, two) in enumerate(((one_own, two_own), (one_other, two_other))):
        column = pl.multiple_of(table_ref[3, n] * cut, cut)
        for j in range(count):
            spot = pl.multiple_of(table_ref[1, j] * size, size)
            pieces_out.append(
                (one.at[j, :, pl.ds(0, cut)], out_ref.at[pl.ds(spot, size), pl.ds(column, cut)])
            )
            spot = pl.multiple_of(table_ref[0, j] * size, size)
            pieces_up.append((one.at[j, :, pl.ds(cut, units)], up_ref.at[n, pl.ds(spot, size), :]))
            spot = pl.multiple_of(table_ref[2, j] * chunk, chunk)
            pieces_down.append((two.at[j], down_ref.at[n, pl.ds(spot, chunk), :]))
    copies = fetch(pieces_out + pieces_up + pieces_down, sems)
    for copy in copies[: 2 * count]:
        copy.wait()
    h = x_ref[...].astype(F32) + jnp.dot(o_ref[...], out_ref[...], preferred_element_type=F32)
    centred = h - jnp.mean(h, axis=-1, keepdims=True)
    spread = jnp.mean(centred * centred, axis=-1, keepdims=True)
    scale = lax.rsqrt(spread + EPSILON)
    hat = centred * scale
    b = (hat * gain_ref[...]).astype(BF)
    b_ref[...] = b
    dy = dy_ref[...]
    ddown_b_ref[...] = jnp.sum(dy.astype(F32), axis=0, keepdims=True)
    for copy in copies[2 * count :]:
        copy.wait()
    y = h + down_b_ref[...]
    db = None
    wide = next(n for n in (768, 512, 384, 256, 128) if units % n == 0)
    for n in range(2):
        for c in range(0, units, wide):
            at = slice(c, c + wide)
            to = slice(n * units + c, n * units + c + wide)
            u = jnp.dot(b, up_ref[n, :, at], preferred_element_type=F32) + up_b_ref[n : n + 1, at]
            g, slope = gelu_parts(u)
            g = g.astype(BF)
            g_ref[:, to] = g
            y = y + jnp.dot(g, down_ref[n, at, :], preferred_element_type=F32)
            du = (matmul_t(dy, down_ref[n, at, :]) * slope).astype(BF)
            du_ref[:, to] = du
            dup_b_ref[n : n + 1, at] = jnp.sum(du.astype(F32), axis=0, keepdims=True)
            part = matmul_t(du, up_ref[n, :, at])
            db = part if db is None else db + part
    y_ref[...] = y.astype(BF)
    dgain_ref[...] = jnp.sum(db * hat, axis=0, keepdims=True)
    dh = dy.astype(F32) + norm_back(hat, scale, gain_ref[...], db)
    dh_ref[...] = dh
    low = dh.astype(BF)
    dh_low_ref[...] = low
    do_ref[...] = matmul_t(low, out_ref[...]).astype(BF)


def middle(table, o, x, dy, gain, up_b, down_b, one, two):
    rows, width = o.shape
    count, size, columns = one[0].shape
    chunk = two[0].shape[1]
    units = columns - width // 2
    anywhere = pl.BlockSpec(memory_space=pl.ANY)
    full = lambda shape: spec(shape, lambda t, i: (0, 0))
    shapes = [
        ((rows, width), BF), ((rows, width), BF), ((rows, 2 * units), BF), ((rows, 2 * units), BF), ((rows, width), BF),
        ((rows, width), BF), ((rows, width), F32), ((1, width), F32), ((2, units), F32), ((1, width), F32),
    ]
    return pl.pallas_call(
        functools.partial(middle_kernel, count, size, chunk),
        grid_spec=pltpu.PrefetchScalarGridSpec(
            num_scalar_prefetch=1,
            grid=(1,),
            in_specs=[full(v.shape) for v in (o, x, dy, gain, up_b, down_b)] + [anywhere] * 4,
            out_specs=[full(shape) for shape, _ in shapes],
            scratch_shapes=[
                pltpu.VMEM((width, width), BF),
                pltpu.VMEM((2, width, units), BF),
                pltpu.VMEM((2, units, width), BF),
                pltpu.SemaphoreType.DMA((6 * count,)),
            ],
        ),
        out_shape=[jax.ShapeDtypeStruct(shape, kind) for shape, kind in shapes],
        compiler_params=pltpu.CompilerParams(vmem_limit_bytes=VMEM_LIMIT),
        cost_estimate=pl.CostEstimate(
            flops=2 * rows * width * (2 * width + 8 * units),
            bytes_accessed=4 * (width * width + 4 * units * width),
            transcendentals=2 * rows * units,
        ),
    )(table, o, x, dy, gain, up_b, down_b, one[0], one[1], two[0], two[1])


def matmul_t(a, b):
    return lax.dot_general(a, b, (((1,), (1,)), ((), ())), preferred_element_type=F32)


def attend_kernel(
    rows, tiles, flag_ref, qcol_ref, krow_ref, q_ref, k_ref, v_ref, o_ref, lse_ref,
    bias_ref, s_ref, top_ref, sum_ref, acc_ref,
):
    pair = pl.program_id(0)
    both_rows = 2 * rows

    def span(t):
        return slice(t * rows, (t + 1) * rows)

    def lines(t):
        return slice(rows, both_rows) if t == 1 else slice(0, both_rows)

    @pl.when(pair == 0)
    def _():
        lse_ref[...] = jnp.zeros_like(lse_ref)
        own = qcol_ref[:, 0:1]
        up_one = qcol_ref[:, 1:2]
        up_two = qcol_ref[:, 2:3]
        limit = qcol_ref[:, 3:4]
        for t in range(tiles):
            if t == 1:
                r = lax.broadcasted_iota(jnp.int32, (rows, rows), 0) // BLOCK
                c = lax.broadcasted_iota(jnp.int32, (rows, rows), 1) // BLOCK
                bias_ref[rows:, span(t)] = jnp.where(r == c, 0.0, NEG_FILL)
            else:
                seg = krow_ref[0:1, span(t)]
                index = krow_ref[1:2, span(t)]
                ok = ((seg == own) | (seg == up_one) | (seg == up_two)) & (index < limit)
                bias_ref[:, span(t)] = jnp.where(ok, 0.0, NEG_FILL)

    lane = lax.broadcasted_iota(jnp.int32, (both_rows, 128), 1)
    queries = [jnp.where((lane // HEAD_DIM) == h, q_ref[...] * 0.125, 0).astype(BF) for h in range(2)]
    top_ref[...] = jnp.full_like(top_ref, -3.0e38)
    for t in range(tiles):

        @pl.when(flag_ref[t] > 0)
        def _():
            at = lines(t)
            keys, bias = k_ref[span(t), :], bias_ref[at, span(t)]
            for h in range(2):
                s = matmul_t(queries[h][at], keys) + bias
                s_ref[h, at, span(t)] = s
                best = top_ref[h, at, :]
                for c in range(rows // 128):
                    best = jnp.maximum(best, s[:, c * 128 : (c + 1) * 128])
                top_ref[h, at, :] = best

    tops = [jnp.max(top_ref[h], axis=-1, keepdims=True) for h in range(2)]
    sum_ref[...] = jnp.zeros_like(sum_ref)
    acc_ref[...] = jnp.zeros_like(acc_ref)
    for t in range(tiles):

        @pl.when(flag_ref[t] > 0)
        def _():
            at = lines(t)
            values = v_ref[span(t), :]
            for h in range(2):
                p = jnp.exp(s_ref[h, at, span(t)] - tops[h][at])
                part = sum_ref[h, at, :]
                for c in range(rows // 128):
                    part = part + p[:, c * 128 : (c + 1) * 128]
                sum_ref[h, at, :] = part
                acc_ref[h, at, :] += jnp.dot(p.astype(BF), values, preferred_element_type=F32)

    outs, norms = [], lse_ref[...]
    for h in range(2):
        total = jnp.sum(sum_ref[h], axis=-1, keepdims=True)
        outs.append(acc_ref[h] / total)
        norms = jnp.where(lane == 2 * pair + h, tops[h] + jnp.log(total), norms)
    lse_ref[...] = norms
    o_ref[...] = jnp.where(lane < HEAD_DIM, outs[0], outs[1]).astype(BF)


def attend(flags, qcol, krow, q, k, v, rows):
    width = q.shape[1]
    total = k.shape[0]
    tiles = total // rows
    pair = lambda n: spec((n, 128), lambda p, f: (0, p))
    fixed = lambda shape: spec(shape, lambda p, f: (0, 0))
    return pl.pallas_call(
        functools.partial(attend_kernel, rows, tiles),
        grid_spec=pltpu.PrefetchScalarGridSpec(
            num_scalar_prefetch=1,
            grid=(width // 128,),
            in_specs=[fixed(qcol.shape), fixed(krow.shape), pair(2 * rows), pair(total), pair(total)],
            out_specs=[pair(2 * rows), fixed((2 * rows, 128))],
            scratch_shapes=[
                pltpu.VMEM((2 * rows, total), F32),
                pltpu.VMEM((2, 2 * rows, total), F32),
                pltpu.VMEM((2, 2 * rows, 128), F32),
                pltpu.VMEM((2, 2 * rows, 128), F32),
                pltpu.VMEM((2, 2 * rows, 128), F32),
            ],
        ),
        out_shape=[
            jax.ShapeDtypeStruct((2 * rows, width), BF),
            jax.ShapeDtypeStruct((2 * rows, 128), F32),
        ],
        compiler_params=pltpu.CompilerParams(vmem_limit_bytes=VMEM_LIMIT),
        cost_estimate=pl.CostEstimate(
            flops=16 * rows * total * width,
            bytes_accessed=4 * (total + rows) * width,
            transcendentals=2 * rows * total * width // HEAD_DIM,
        ),
    )(flags, qcol, krow, q, k, v)


def attend_back_kernel(
    rows, tiles, flag_ref, qrow_ref, kcol_ref, q_ref, k_ref, v_ref, o_ref, g_ref, lse_ref,
    cos_ref, sin_ref, dq_ref, dk_ref, dv_ref, bias_ref, acc_ref,
):
    pair = pl.program_id(0)
    both_rows = 2 * rows

    def span(t):
        return slice(t * rows, (t + 1) * rows)

    def lines(t):
        return slice(rows, both_rows) if t == 1 else slice(0, both_rows)

    @pl.when(pair == 0)
    def _():
        own = qrow_ref[0:1, :]
        up_one = qrow_ref[1:2, :]
        up_two = qrow_ref[2:3, :]
        limit = qrow_ref[3:4, :]
        for t in range(tiles):
            if t == 1:
                r = lax.broadcasted_iota(jnp.int32, (rows, rows), 0) // BLOCK
                c = lax.broadcasted_iota(jnp.int32, (rows, rows), 1) // BLOCK
                bias_ref[span(t), rows:] = jnp.where(r == c, 0.0, NEG_FILL)
            else:
                seg = kcol_ref[span(t), 0:1]
                index = kcol_ref[span(t), 1:2]
                ok = ((seg == own) | (seg == up_one) | (seg == up_two)) & (index < limit)
                bias_ref[span(t), :] = jnp.where(ok, 0.0, NEG_FILL)

    lane = lax.broadcasted_iota(jnp.int32, (both_rows, 128), 1)
    acc_ref[...] = jnp.zeros_like(acc_ref)
    queries, grads, deltas, norms = [], [], [], []
    product = (o_ref[...].astype(F32) * g_ref[...].astype(F32)).T
    for h in range(2):
        mine = (lane // HEAD_DIM) == h
        queries.append(jnp.where(mine, q_ref[...] * 0.125, 0).astype(BF))
        grads.append(jnp.where(mine, g_ref[...], 0).astype(BF))
        deltas.append(jnp.sum(product[h * HEAD_DIM : (h + 1) * HEAD_DIM], axis=0, keepdims=True))
        norms.append(lse_ref[pl.ds(2 * pair + h, 1), :])
    for t in range(tiles):

        @pl.when(flag_ref[t] == 0)
        def _():
            dk_ref[span(t), :] = jnp.zeros((rows, 128), BF)
            dv_ref[span(t), :] = jnp.zeros((rows, 128), BF)

        @pl.when(flag_ref[t] > 0)
        def _():
            at = lines(t)
            keys, values = k_ref[span(t), :], v_ref[span(t), :]
            keys_t = keys.astype(F32).T.astype(BF)
            dk = dv = None
            for h in range(2):
                q, g = queries[h][at], grads[h][at]
                s = matmul_t(keys, q) + bias_ref[span(t), at]
                p = jnp.exp(s - norms[h][:, at])
                dp = matmul_t(values, g)
                ds = (p * (dp - deltas[h][:, at])).astype(BF)
                part_v = jnp.dot(p.astype(BF), g, preferred_element_type=F32)
                part_k = jnp.dot(ds, q, preferred_element_type=F32)
                dv = part_v if dv is None else dv + part_v
                dk = part_k if dk is None else dk + part_k
                half = slice(h * HEAD_DIM, (h + 1) * HEAD_DIM)
                acc_ref[half, at] += jnp.dot(keys_t[half], ds, preferred_element_type=F32)
            [dk] = turn(dk, cos_ref[span(t), :], -sin_ref[span(t), :])
            dk_ref[span(t), :] = dk.astype(BF)
            dv_ref[span(t), :] = dv.astype(BF)

    dq = acc_ref[...].T * 0.125
    [dq] = turn(dq, cos_ref[:both_rows, :], -sin_ref[:both_rows, :])
    dq_ref[...] = dq.astype(BF)


def attend_back(flags, qrow, kcol, q, k, v, o, g, lse, cosine, sine, rows):
    width = q.shape[1]
    total = k.shape[0]
    tiles = total // rows
    pair = lambda n: spec((n, 128), lambda p, f: (0, p))
    fixed = lambda shape: spec(shape, lambda p, f: (0, 0))
    out = lambda n: jax.ShapeDtypeStruct((n, width), BF)
    return pl.pallas_call(
        functools.partial(attend_back_kernel, rows, tiles),
        grid_spec=pltpu.PrefetchScalarGridSpec(
            num_scalar_prefetch=1,
            grid=(width // 128,),
            in_specs=[
                fixed(qrow.shape), fixed(kcol.shape), pair(2 * rows), pair(total), pair(total),
                pair(2 * rows), pair(2 * rows), fixed(lse.shape), fixed(cosine.shape), fixed(sine.shape),
            ],
            out_specs=[pair(2 * rows), pair(total), pair(total)],
            scratch_shapes=[
                pltpu.VMEM((total, 2 * rows), F32),
                pltpu.VMEM((128, 2 * rows), F32),
            ],
        ),
        out_shape=[out(2 * rows), out(total), out(total)],
        compiler_params=pltpu.CompilerParams(vmem_limit_bytes=VMEM_LIMIT),
        cost_estimate=pl.CostEstimate(
            flops=40 * rows * total * width,
            bytes_accessed=8 * (total + rows) * width,
            transcendentals=2 * rows * total * width // HEAD_DIM,
        ),
    )(flags, qrow, kcol, q, k, v, o, g, lse, cosine, sine)


def normalise(values):
    centred = values - jnp.mean(values, axis=-1, keepdims=True)
    spread = jnp.mean(centred * centred, axis=-1, keepdims=True)
    scale = lax.rsqrt(spread + EPSILON)
    return centred * scale, scale


def norm_back(hat, scale, gain, grad):
    scaled = grad * gain
    return scale * (
        scaled
        - jnp.mean(scaled, axis=-1, keepdims=True)
        - hat * jnp.mean(scaled * hat, axis=-1, keepdims=True)
    )


ROOT = math.sqrt(2.0 / math.pi)


def gelu_parts(u):
    t = jnp.tanh(ROOT * (u + 0.044715 * (u * u * u)))
    slope = 0.5 * (1.0 + t) + 0.5 * u * (1.0 - t * t) * (ROOT * (1.0 + 3 * 0.044715 * (u * u)))
    return 0.5 * u * (1.0 + t), slope


def mm(a, b):
    return jnp.dot(a, b, preferred_element_type=F32)


def mm_t(a, b):
    return lax.dot_general(a, b, (((1,), (1,)), ((), ())), preferred_element_type=F32)


def t_mm(a, b):
    return lax.dot_general(a, b, (((0,), (0,)), ((), ())), preferred_element_type=F32)


def halves_of_heads(w):
    w = w.reshape(w.shape[0], 3, 2, -1)
    return w[:, :, 0].reshape(w.shape[0], -1), w[:, :, 1].reshape(w.shape[0], -1)


def heads_of_halves(a, b):
    a, b = a.reshape(a.shape[0], 3, -1), b.reshape(b.shape[0], 3, -1)
    return jnp.stack([a, b], 2).reshape(a.shape[0], -1)


def halves_of_units(w, chunk):
    w = w.reshape(w.shape[0], -1, 2, chunk)
    return w[:, :, 0].reshape(w.shape[0], -1), w[:, :, 1].reshape(w.shape[0], -1)


def units_of_halves(a, b, chunk):
    a, b = a.reshape(a.shape[0], -1, chunk), b.reshape(b.shape[0], -1, chunk)
    return jnp.stack([a, b], 2).reshape(a.shape[0], -1)


class Chain:
    def __init__(self, rows):
        self.at = Links()
        self.rows = rows
        self.core = self.at.core

    def places(self):
        at = self.at
        n = jnp.arange(4)
        zyx = ((at.z ^ n)[None, None, :] * 2 + (at.y ^ n[:2])[None, :, None]) * 2 + (at.x ^ n[:2])[:, None, None]
        yzx = ((at.z ^ n)[None, :, None] * 2 + (at.y ^ n[:2])[:, None, None]) * 2 + (at.x ^ n[:2])[None, None, :]
        first = zyx.reshape(16)
        columns = jnp.where(jnp.arange(16) % 2 == 0, at.core, 1 - at.core)
        return jnp.stack([first, first ^ (8 * at.core), yzx.reshape(16), columns]).astype(jnp.int32)

    def gather(self, hid, w_qkv, w_out, w_up, w_down, vectors):
        at = self.at
        chunk, cut = w_down.shape[0], w_out.shape[1] // 2
        up_a, up_b = halves_of_units(w_up, chunk)
        one_a = jnp.concatenate([w_out[:, :cut], up_a], axis=1)
        one_b = jnp.concatenate([w_out[:, cut:], up_b], axis=1)
        qkv_a, qkv_b = halves_of_heads(w_qkv)
        row = jnp.pad(vectors[None], ((0, 7), (0, qkv_a.shape[1] - vectors.shape[0])))
        qkv_a, qkv_b = (jnp.concatenate([v, row], axis=0) for v in (qkv_a, qkv_b))
        block = to_column_half(at, qkv_a, qkv_b)
        few = w_qkv.shape[0]
        block = jnp.concatenate(
            [block[:few], block[few + 8 : 2 * few + 8], block[few : few + 8], block[2 * few + 8 :]], axis=0
        )[None]
        beside = at.swap_y(hid, [(i, i + 1) for i in range(0, 8, 2)])
        down_two = jnp.stack([w_down, at.swap_x(w_down)])[None]
        one = to_column_half(at, one_a, one_b)[None]
        line = z_gather(at, block)
        [cur] = after([hid], [line])
        hops = [at.up(cur, 0, 2)]
        plane = jnp.concatenate([line, at.swap_y(line)], axis=0)
        [cur, plane] = after([hops[0], plane], [beside])
        hops.append(at.up(cur, 1, 2))
        across = [at.swap_y(cur, [(i, i ^ 1) for i in range(2, 8)])]
        qkv = jnp.concatenate([plane, at.swap_x(plane)], axis=0)
        [cur] = after([hops[1]], [across[0]])
        hops.append(at.up(cur, 2, 2))
        across.append(at.swap_y(cur, [(i, i ^ 1) for i in range(4, 8)]))
        [last, one, qkv] = after([hops[2], one, qkv], [across[1]])
        across.append(at.swap_y(last, [(i, i ^ 1) for i in range(6, 8)]))
        qkv_both = (qkv, at.swap_core(qkv))
        line = z_gather(at, one)
        [line, down_two] = after([line, down_two], [across[2], qkv_both[1]])
        plane = jnp.concatenate([line, at.swap_y(line)], axis=0)
        down_line = z_gather(at, down_two)
        [plane, down_line] = after([plane, down_line], [plane, down_line])
        one = jnp.concatenate([plane, at.swap_x(plane)], axis=0)
        down = jnp.concatenate([down_line, at.swap_y(down_line)], axis=0)
        down = down.reshape((16,) + w_down.shape)
        one_both = (one, at.swap_core(one))
        down_both = (down, at.swap_core(down))
        m = 2 * few
        vec = jnp.concatenate([qkv[:, m, : vectors.shape[0]], qkv[:, m + 8, : vectors.shape[0]]], axis=1)
        order = (self.places()[0][None, :] == jnp.arange(16)[:, None]).astype(BF)
        vec = mm(order, vec).reshape(32, -1)
        lower = []
        for n in range(3):
            lower += [hops[n], across[n]]
        return lower + [beside], qkv_both, one_both, down_both, vec

    def tile_leaves(self):
        z, y = self.at.z, self.at.y
        found = []
        for s in (1, 2, 3):
            found += [(2 * (z - s) + y, z >= s), (2 * (z - s) + 1 - y, z >= s)]
        found.append((2 * z, y == 1))
        return found

    def tree_sum(self, own, parts):
        at = self.at
        low = [at.swap_y(parts[6], [(i, i - 1) for i in range(1, 8, 2)])]
        for s in (1, 2, 3):
            pairs = [(i, i ^ 1) for i in range(2 * s, 8)]
            low.append(at.swap_y(parts[2 * s - 1], pairs))
        cur = plus(parts[4], low[3])
        for s in (2, 1):
            cur = at.down(cur.astype(BF), s + 1, 3).astype(F32) + plus(parts[2 * s - 2], low[s])
        return own + at.down(cur.astype(BF), 1, 3).astype(F32) + low[0].astype(F32)

    def unit_bias(self, bias, chunk):
        a, b = halves_of_units(bias[None], chunk)
        return jnp.where(self.core == 0, a, b), jnp.where(self.core == 0, b, a)

    def unit_bias_back(self, own, other, chunk):
        a = jnp.where(self.core == 0, own, other)
        b = jnp.where(self.core == 0, other, own)
        return units_of_halves(a, b, chunk)[0]

    def sum_down(self, own, other):
        shape = (8, 2, own.shape[0] // 16, own.shape[1])
        return reduce_x_first(self.at, own.reshape(shape), other.reshape(shape))

    def sum_up(self, own, other, chunk):
        shape = (8, 2, own.shape[0] // 16, own.shape[1])
        g = reduce_y_first(self.at, own.reshape(shape), other.reshape(shape))
        return units_of_halves(*from_column_half(self.at, g), chunk)

    def sum_out(self, g):
        at = self.at
        half = g.shape[0] // 2
        g = jnp.where(at.core == 0, g, jnp.concatenate([g[half:], g[:half]], axis=0))
        g = g.reshape(8, 2, g.shape[0] // 16, 2, g.shape[1] // 2)
        own, other = choose(at.core, g, 3)
        a, b = from_column_half(at, reduce_x_first(at, own, other))
        return jnp.concatenate([a, b], axis=1)

    def sum_qkv(self, own, other, vec):
        at = self.at
        m = own.shape[0] // 16
        shape = (8, 2, m, own.shape[1])
        n = vec.shape[1]
        rows = jnp.pad(vec.astype(BF).reshape(8, 2, 2, 1, n), ((0, 0),) * 3 + ((0, 7), (0, own.shape[1] - n)))
        mine, its = choose(at.core, rows, 2)
        g = reduce_x_first(
            at,
            jnp.concatenate([own.reshape(shape), mine], axis=2),
            jnp.concatenate([other.reshape(shape), its], axis=2),
        )
        return heads_of_halves(*from_column_half(at, g[:m])), g[m, :n]


AXES = ("leaf", "fsdp")


def in_place(places, w, rows):
    count = w.shape[0]
    if count == 1:
        return w[0]
    size = rows // count
    out = jnp.zeros((rows, w.shape[2]), w.dtype)
    for n in range(count):
        out = lax.dynamic_update_slice(out, w[n, :size], (places[n] * size, 0))
    return out


class Whole:
    def __init__(self, rows, leaves, devices):
        self.rows, self.leaves, self.devices = rows, leaves, devices
        self.leaf = lax.axis_index("leaf")

    def places(self):
        return jnp.array([[0, 0], [0, 0], [0, 0], [0, 1]], jnp.int32)

    def tile_leaves(self):
        found = []
        for s in range(1, self.leaves):
            place = self.leaf - s
            found.append((jnp.maximum(place, 0), place >= 0))
        return found

    def tree_sum(self, own, parts):
        every = jnp.stack([own.astype(BF)] + [p for p in parts])
        order = [pick(every, (self.leaf - t) % self.leaves, 0) for t in range(self.leaves)]
        every = jnp.concatenate(order, axis=0)
        return lax.psum_scatter(every, "leaf", scatter_dimension=0, tiled=True).astype(F32)

    def gather(self, hid, w_qkv, w_out, w_up, w_down, vectors):
        tree = lax.all_gather(hid, "leaf", axis=0, tiled=False)
        lower = [pick(tree, leaf, 0) for leaf, _ in self.tile_leaves()]
        every = lambda w: lax.all_gather(w, AXES, axis=0, tiled=True)
        up_w, down_w, out_w = every(w_up), every(w_down), every(w_out)
        half, cut = down_w.shape[0] // 2, out_w.shape[1] // 2
        return (
            lower,
            tuple(v[None] for v in halves_of_heads(every(w_qkv))),
            tuple(
                jnp.concatenate([out_w[:, n * cut : (n + 1) * cut], up_w[:, n * half : (n + 1) * half]], axis=1)[None]
                for n in range(2)
            ),
            tuple(down_w[None, n * half : (n + 1) * half] for n in range(2)),
            every(vectors[None]),
        )

    def unit_bias(self, bias, chunk):
        half = bias.shape[0] // 2
        return bias[None, :half], bias[None, half:]

    def unit_bias_back(self, own, other, chunk):
        return jnp.concatenate([own, other], axis=1)[0]

    def scatter(self, g):
        return lax.psum_scatter(g.astype(F32), AXES, scatter_dimension=0, tiled=True)

    def sum_down(self, own, other):
        return self.scatter(jnp.concatenate([own, other], axis=0))

    def sum_up(self, own, other, chunk):
        return self.scatter(jnp.concatenate([own, other], axis=1))

    def sum_out(self, g):
        return self.scatter(g)

    def sum_qkv(self, own, other, vec):
        return self.scatter(heads_of_halves(own, other)), self.scatter(vec)[0]


def shards(
    leaves,
    groups,
    hidden,
    noise_mask,
    seg_blocks,
    parents,
    ln1_gain,
    w_qkv,
    w_out,
    ln2_gain,
    w_up,
    up_bias,
    w_down,
    down_bias,
    mask_embed,
    cotangent,
):
    rows = hidden.shape[1]
    width = hidden.shape[2]
    devices = leaves * groups
    net = Chain(rows) if (leaves, groups) == (8, 4) else Whole(rows, leaves, devices)
    chunk = w_down.shape[0]
    few = ln1_gain.shape[0]

    hid = hidden[0]
    vectors = jnp.concatenate([ln1_gain, ln2_gain, down_bias, mask_embed, up_bias])
    lower, qkv_w, one_w, down_w, vec = net.gather(hid, w_qkv, w_out, w_up, w_down, vectors)
    places = net.places()
    gain_one, gain_two, down_b, embed = (
        vec[:, n * few : (n + 1) * few].reshape(1, width).astype(F32) for n in range(4)
    )
    up_b = net.unit_bias(vec[:, 4 * few :].reshape(-1).astype(F32), chunk)

    blocks = rows // BLOCK
    leaf = lax.axis_index("leaf")
    seg_row = seg_blocks[0]
    path_block, first_up, second_up = tree_layout(seg_row, parents[0])
    table = jnp.stack([seg_row, path_block, jnp.arange(seg_row.shape[0], dtype=jnp.int32), first_up, second_up])
    table = table.reshape(5, leaves, blocks)
    own = pick(table, leaf, 1)
    tiles = [own, own.at[0].set(-1)]
    for place, valid in net.tile_leaves():
        tile = pick(table, jnp.maximum(place, 0), 1)
        tiles.append(tile.at[0].set(jnp.where(valid, tile[0], -1)))
    keys = jnp.stack(tiles, axis=1)
    limit = jnp.concatenate([own[2] + 1, own[2]])
    queries = [jnp.tile(own[n], 2) for n in (0, 3, 4)] + [limit]
    seg_k, index_k = keys[0].reshape(1, -1), keys[2].reshape(1, -1)
    allowed = (
        (seg_k == queries[0][:, None]) | (seg_k == queries[1][:, None]) | (seg_k == queries[2][:, None])
    ) & (index_k < limit[:, None])
    flags = jnp.any(allowed.reshape(2 * blocks, -1, blocks), axis=(0, 2)).astype(jnp.int32)
    flags = flags.at[:2].set(1)
    per_token = lambda v: jnp.repeat(v, BLOCK, axis=-1)
    query_rows = per_token(jnp.stack(queries + queries))
    key_rows = per_token(jnp.concatenate([seg_k, index_k] * 4))
    query_cols = query_rows.T
    key_cols = key_rows.T

    lanes = jnp.arange(128, dtype=jnp.int32)
    exponent = (lanes % (HEAD_DIM // 2)).astype(F32) * (-math.log(10000.0) / (HEAD_DIM // 2))
    positions = (keys[1][:, :, None] * BLOCK + jnp.arange(BLOCK, dtype=jnp.int32)).reshape(-1, 1)
    angles = positions.astype(F32) * jnp.exp(exponent)
    cosine = jnp.cos(angles)
    sine = jnp.sin(angles) * jnp.where((lanes % HEAD_DIM) < HEAD_DIM // 2, -1.0, 1.0)

    masked = (noise_mask[0] == 1)[:, None]
    x_all = jnp.concatenate([hid, hid] + lower, axis=0)
    swapped = jnp.pad(noise_mask[0][:, None], ((rows, x_all.shape[0] - 2 * rows), (0, 0)))
    a_all, query, key, value = project(
        places, x_all, swapped, embed, gain_one, qkv_w[0], qkv_w[1], cosine, sine, rows
    )
    mixed, log_norm = attend(flags, query_cols, key_rows, query, key, value, rows)
    noisy = jnp.where(masked, embed.astype(BF), hid)
    stream_low = jnp.concatenate([hid, noisy], axis=0)
    stream = stream_low.astype(F32)
    grad_two = cotangent[0].reshape(2 * rows, width)
    (
        output, normed_two, act, grad_pre, grad_one, grad_mixed, grad_after, grad_gain_two, grad_up_b, grad_down_b,
    ) = middle(places, mixed, stream_low, grad_two, gain_two, jnp.concatenate(up_b, axis=0), down_b, one_w, down_w)
    output = output.reshape(1, 2, rows, width)
    units = act.shape[1] // 2
    two = lambda v: (v[:, :units], v[:, units:])
    grad_down_w = [t_mm(v, grad_two).astype(BF) for v in two(act)]
    grad_up_w = [t_mm(normed_two, v).astype(BF) for v in two(grad_pre)]
    sum_down = net.sum_down(*grad_down_w)
    sum_up = net.sum_up(*grad_up_w, chunk)

    grad_out_w = t_mm(mixed, grad_one).astype(BF)
    sum_out = net.sum_out(grad_out_w)
    grad_q, grad_k, grad_v = attend_back(
        flags, query_rows, key_cols, query, key, value, mixed, grad_mixed, log_norm.T, cosine, sine, rows
    )
    half = width // 2
    qkv_w = [in_place(places[0], w, width) for w in qkv_w]
    grad_a_kv = None
    grad_a_q = None
    grad_qkv_w = []
    for n in range(2):
        cut = slice(n * half, (n + 1) * half)
        pieces = (grad_k[:, cut], grad_v[:, cut])
        kv = jnp.concatenate(pieces, axis=1)
        part = mm_t(kv, qkv_w[n][:, half:])
        grad_a_kv = part if grad_a_kv is None else grad_a_kv + part
        part = mm_t(grad_q[:, cut], qkv_w[n][:, :half])
        grad_a_q = part if grad_a_q is None else grad_a_q + part
        grad_qkv_w.append(
            jnp.concatenate(
                [t_mm(a_all[: 2 * rows], grad_q[:, cut]).astype(BF), t_mm(a_all, kv).astype(BF)], axis=1
            )
        )
    hat_all, _ = normalise(jnp.concatenate([stream_low] + lower, axis=0).astype(F32))
    grad_gain_one = jnp.sum(grad_a_kv * hat_all, axis=0) + jnp.sum(grad_a_q * hat_all[: 2 * rows], axis=0)
    mine = grad_a_kv[: 2 * rows] + grad_a_q
    parts = [grad_a_kv[t * rows : (t + 1) * rows].astype(BF) for t in range(2, len(tiles))]
    hat_noisy, scale_noisy = normalise(stream[rows:])
    stream_noisy = grad_after[rows:] + norm_back(hat_noisy, scale_noisy, gain_one, mine[rows:])
    grad_embed = jnp.sum(jnp.where(masked, stream_noisy, 0.0), axis=0)
    grad_vec = jnp.concatenate(
        [
            v.reshape(devices, -1)
            for v in (
                grad_gain_one, grad_gain_two, grad_down_b, grad_embed,
                net.unit_bias_back(grad_up_b[:1], grad_up_b[1:], chunk),
            )
        ],
        axis=1,
    )
    sum_qkv, sum_vec = net.sum_qkv(*grad_qkv_w, grad_vec)
    clean = net.tree_sum(mine[:rows], parts)
    hat_clean, scale_clean = normalise(stream[:rows])
    stream_clean = grad_after[:rows] + norm_back(hat_clean, scale_clean, gain_one, clean)
    grad_hidden = (stream_clean + jnp.where(masked, 0.0, stream_noisy)).astype(BF)[None]
    piece = lambda n: sum_vec[n * few : (n + 1) * few]
    return (
        output,
        grad_hidden,
        piece(0),
        sum_qkv,
        sum_out,
        piece(1),
        sum_up,
        sum_vec[4 * few :],
        sum_down,
        piece(2),
        piece(3),
    )


def solution(mesh):
    split = ("leaf", "fsdp")
    in_specs = (
        P("fsdp", "leaf", None),
        P("fsdp", "leaf"),
        P("fsdp", None),
        P("fsdp", None),
        P(split),
        P(split, None),
        P(split, None),
        P(split),
        P(split, None),
        P(split),
        P(split, None),
        P(split),
        P(split),
        P("fsdp", None, "leaf", None),
    )
    out_specs = (
        P("fsdp", None, "leaf", None),
        P("fsdp", "leaf", None),
        P(split),
        P(split, None),
        P(split, None),
        P(split),
        P(split, None),
        P(split),
        P(split, None),
        P(split),
        P(split),
    )
    body = functools.partial(shards, mesh.shape["leaf"], mesh.shape["fsdp"])
    return jax.shard_map(body, mesh=mesh, in_specs=in_specs, out_specs=out_specs, check_vma=False)
```

```python
import functools
import math

import jax
import jax.numpy as jnp
from jax import lax
from jax.experimental import pallas as pl
from jax.experimental.pallas import tpu as pltpu
from jax.sharding import PartitionSpec as P

HEAD_DIM = 64
BLOCK = 16
NEG_FILL = -1000000000.0
EPSILON = 1e-05
VMEM_LIMIT = 56 * 1024 * 1024
BF = jnp.bfloat16
F32 = jnp.float32


class Links:
    def __init__(self):
        leaf = lax.axis_index("leaf")
        fsdp = lax.axis_index("fsdp")
        self.z, self.y = leaf // 2, leaf % 2
        self.x, self.core = fsdp // 2, fsdp % 2

    def swap_core(self, v):
        return lax.ppermute(v, "fsdp", [(i, i ^ 1) for i in range(4)])

    def swap_x(self, v):
        return lax.ppermute(v, "fsdp", [(i, i ^ 2) for i in range(4)])

    def swap_y(self, v, pairs=None):
        return lax.ppermute(v, "leaf", pairs or [(i, i ^ 1) for i in range(8)])

    def swap_z(self, v, n):
        return lax.ppermute(v, "leaf", [(i, i ^ (2 * n)) for i in range(8)])

    def up(self, v, first, last):
        return lax.ppermute(v, "leaf", [(i, i + 2) for i in range(2 * first, 2 * last + 2)])

    def down(self, v, first, last):
        return lax.ppermute(v, "leaf", [(i, i - 2) for i in range(2 * first, 2 * last + 2)])


def both(bit, own, other, axis):
    return jnp.where(
        bit == 0, jnp.stack([own, other], axis), jnp.stack([other, own], axis)
    )


def tie(*values):
    flat, tree = jax.tree.flatten(values)
    return jax.tree.unflatten(tree, lax.optimization_barrier(tuple(flat)))


def z_gather(at, block):
    return jnp.concatenate([block] + [at.swap_z(block, n) for n in (1, 2, 3)], axis=0)


def pick(v, index, axis):
    return lax.dynamic_index_in_dim(v, index, axis, keepdims=False)


def choose(bit, v, axis):
    return pick(v, bit, axis), pick(v, 1 - bit, axis)


def plus(a, b):
    return a.astype(F32) + b.astype(F32)


def z_parts(at, g):
    return pick(g, at.z, 0), [pick(g, at.z ^ n, 0) for n in (1, 2, 3)]


def z_move(at, parts):
    return [at.swap_z(part, n) for n, part in zip((1, 2, 3), parts)]


def z_total(keep, got):
    return plus(keep, got[0]) + plus(got[1], got[2])


def to_column_half(at, half_a, half_b):
    keep = jnp.where(at.core == 0, half_a, half_b)
    send = jnp.where(at.core == 0, half_b, half_a)
    got = at.swap_core(send)
    return both(at.core, keep, got, 0).reshape(2 * keep.shape[0], keep.shape[1])


def from_column_half(at, g):
    g = g.reshape(2, g.shape[0] // 2, g.shape[1])
    keep, send = choose(at.core, g, 0)
    got = at.swap_core(send)
    return jnp.where(at.core == 0, keep, got), jnp.where(at.core == 0, got, keep)


def spec(shape, index_map):
    return pl.BlockSpec(shape, index_map)


def turn(values, cosine, sine):
    lane = lax.broadcasted_iota(jnp.int32, (values.shape[0], 128), 1)
    low_half = (lane % HEAD_DIM) < HEAD_DIM // 2
    groups = []
    for n in range(values.shape[1] // 128):
        part = values[:, n * 128 : (n + 1) * 128]
        swapped = jnp.where(low_half, pltpu.roll(part, 96, 1), pltpu.roll(part, 32, 1))
        groups.append(part * cosine + swapped * sine)
    return groups


def column(row):
    return jnp.broadcast_to(row, (8, row.shape[1])).T[:, :1]


def tables_kernel(places, rows, leaf_ref, seg_ref, parent_ref, qcol_ref, qrow_ref, kcol_ref, krow_ref, flag_ref, pad_ref):
    leaf = leaf_ref[0]
    blocks = rows // BLOCK
    slots = 16
    seg = column(seg_ref[...].astype(F32))
    lane = lax.broadcasted_iota(jnp.int32, (seg.shape[0], 128), 1).astype(F32)
    length = jnp.sum(jnp.where(seg == lane, 1.0, 0.0), axis=0, keepdims=True)
    start = jnp.sum(jnp.where(seg < lane, 1.0, 0.0), axis=0, keepdims=True)
    pad_ref[...] = jnp.zeros_like(pad_ref)
    pad_ref[0:1, 0 : parent_ref.shape[1]] = parent_ref[...].astype(F32)
    parent_row = pad_ref[0:1, :]
    lane = lax.broadcasted_iota(jnp.int32, (slots, 128), 1).astype(F32)
    slot = lax.broadcasted_iota(jnp.int32, (slots, 1), 0).astype(F32)
    parent = column(parent_row)[:slots]
    look = lambda index, row: jnp.sum(jnp.where(index == lane, row, 0.0), axis=1, keepdims=True)
    grand = look(parent, parent_row)
    start = look(slot, start)
    shift = jnp.where(slot > 0, look(parent, length), 0.0) + jnp.where(parent > 0, look(grand, length), 0.0) - start

    def facts(block):
        own = jnp.sum(jnp.where(block >= start, 1.0, 0.0), axis=0, keepdims=True) - 1.0
        take = lambda col: jnp.sum(jnp.where(slot == own, col, 0.0), axis=0, keepdims=True)
        return own, take(parent), take(grand), take(shift)

    token = lax.broadcasted_iota(jnp.int32, (1, rows), 1)
    zero = jnp.zeros((1, rows), F32)
    tiles = [(leaf, leaf >= 0), (leaf, leaf < 0)] + places(leaf)
    for t, (place, valid) in enumerate(tiles):
        first = jnp.maximum(place, 0) * blocks
        block = (first + lax.shift_right_logical(token, 4)).astype(F32)
        own, one, two, move = facts(block)
        position = (move + block) * BLOCK + (token & (BLOCK - 1)).astype(F32)
        at = slice(t * rows, (t + 1) * rows)
        if t < 2:
            limit = block + (1.0 if t == 0 else 0.0)
            lines = jnp.concatenate([own, one, two, limit, zero, zero, zero, zero], axis=0)
            qrow_ref[:, at] = lines
            qcol_ref[at, :] = lines.T
        lines = jnp.concatenate(
            [jnp.where(valid, own, -1.0), block, position, zero, zero, zero, zero, zero], axis=0
        )
        krow_ref[:, at] = lines
        kcol_ref[at, :] = lines.T
    queries = qcol_ref[pl.ds(0, 2 * blocks, stride=BLOCK), :]
    lane = lax.broadcasted_iota(jnp.int32, (1, 128), 1)
    for t, (place, valid) in enumerate(tiles):
        if t < 2:
            flag_ref[t] = 1
            continue
        block = (jnp.maximum(place, 0) * blocks + lane).astype(F32)
        own = facts(block)[0]
        allowed = (
            ((own == queries[:, 0:1]) | (own == queries[:, 1:2]) | (own == queries[:, 2:3]))
            & (block < queries[:, 3:4])
            & (lane < blocks)
            & valid
        )
        flag_ref[t] = jnp.max(jnp.where(allowed, 1.0, 0.0)).astype(jnp.int32)


def tables(places, leaf, seg, parent, rows):
    tiles = 2 + len(places(leaf))
    total = tiles * rows
    smem = pl.BlockSpec(memory_space=pltpu.SMEM)
    vmem = pl.BlockSpec(memory_space=pltpu.VMEM)
    shapes = [(2 * rows, 8), (8, 2 * rows), (total, 8), (8, total)]
    return pl.pallas_call(
        functools.partial(tables_kernel, places, rows),
        in_specs=[smem, vmem, vmem],
        out_specs=[vmem] * 4 + [smem],
        out_shape=[jax.ShapeDtypeStruct(shape, F32) for shape in shapes] + [jax.ShapeDtypeStruct((tiles,), jnp.int32)],
        scratch_shapes=[pltpu.VMEM((8, 128), F32)],
    )(leaf.reshape(1), seg, parent)


def fetch(pieces, sems):
    copies = [pltpu.make_async_copy(src, dst, sems.at[n]) for n, (src, dst) in enumerate(pieces)]
    for copy in copies:
        copy.start()
    return copies


def placed(ref, count, size, table, row):
    return [
        ref.at[pl.ds(pl.multiple_of(table[row, n] * size, size), size), :] for n in range(count)
    ]


def project_kernel(
    count, size, first_rows, table_ref, x_ref, mask_ref, embed_ref, gain_ref, own_hbm, other_hbm, cos_ref, sin_ref,
    a_ref, q_ref, k_ref, v_ref, own_ref, other_ref, sems,
):
    tile = pl.program_id(0)

    @pl.when(tile == 0)
    def _():
        pieces = []
        for hbm, ref in ((own_hbm, own_ref), (other_hbm, other_ref)):
            spots = placed(ref, count, size, table_ref, 0)
            pieces += [(hbm.at[n, pl.ds(0, size), :], spots[n]) for n in range(count)]
        for copy in fetch(pieces, sems):
            copy.wait()

    x = jnp.where(mask_ref[...] > 0, embed_ref[...], x_ref[...].astype(F32))
    centred = x - jnp.mean(x, axis=-1, keepdims=True)
    spread = jnp.mean(centred * centred, axis=-1, keepdims=True)
    a = (centred * lax.rsqrt(spread + EPSILON) * gain_ref[...]).astype(BF)
    a_ref[...] = a
    cosine, sine = cos_ref[...], sin_ref[...]
    half = own_ref.shape[1] // 3
    for n, w_ref in enumerate((own_ref, other_ref)):
        base = n * half
        keys = jnp.dot(a, w_ref[:, half : 2 * half], preferred_element_type=F32)
        for g, part in enumerate(turn(keys, cosine, sine)):
            k_ref[:, base + g * 128 : base + (g + 1) * 128] = part.astype(BF)
        values = jnp.dot(a, w_ref[:, 2 * half :], preferred_element_type=F32)
        v_ref[:, base : base + half] = values.astype(BF)

    @pl.when(tile * x_ref.shape[0] < first_rows)
    def _():
        rows = q_ref.shape[0]
        for n, w_ref in enumerate((own_ref, other_ref)):
            base = n * half
            q = jnp.dot(a[:rows], w_ref[:, :half], preferred_element_type=F32)
            for g, part in enumerate(turn(q, cosine[:rows], sine[:rows])):
                q_ref[:, base + g * 128 : base + (g + 1) * 128] = part.astype(BF)


def project(table, x_all, mask, embed, gain, own, other, cosine, sine, rows):
    total, width = x_all.shape
    step = next(n for n in (3 * rows, 2 * rows, rows) if total % n == 0)
    q_step = min(step, 2 * rows)
    last_q = 2 * rows // q_step - 1
    count = own.shape[0]
    size = width // count
    columns = own.shape[2]
    whole = lambda shape: spec(shape, lambda t, i: (0, 0))
    moved = lambda n: spec((step, n), lambda t, i: (t, 0))
    out = lambda n: jax.ShapeDtypeStruct((n, width), BF)
    anywhere = pl.BlockSpec(memory_space=pl.ANY)
    return pl.pallas_call(
        functools.partial(project_kernel, count, size, 2 * rows),
        grid_spec=pltpu.PrefetchScalarGridSpec(
            num_scalar_prefetch=1,
            grid=(total // step,),
            in_specs=[
                moved(width), moved(1), whole((1, width)), whole((1, width)), anywhere, anywhere, moved(128), moved(128),
            ],
            out_specs=[
                moved(width),
                spec((q_step, width), lambda t, i: (jnp.minimum(t, last_q), 0)),
                moved(width),
                moved(width),
            ],
            scratch_shapes=[
                pltpu.VMEM((width, columns), BF),
                pltpu.VMEM((width, columns), BF),
                pltpu.SemaphoreType.DMA((2 * count,)),
            ],
        ),
        out_shape=[out(total), out(2 * rows), out(total), out(total)],
        compiler_params=pltpu.CompilerParams(vmem_limit_bytes=VMEM_LIMIT),
        cost_estimate=pl.CostEstimate(
            flops=2 * total * width * 2 * width + 4 * rows * width * width,
            bytes_accessed=2 * (4 * total * width + 3 * width * width),
            transcendentals=0,
        ),
    )(table, x_all, mask, embed, gain, own, other, cosine, sine)


def middle_kernel(
    count, size, chunk, table_ref, o_ref, x_ref, mask_ref, embed_ref, dy_ref, gain_ref, up_b_ref, down_b_ref,
    one_own, one_other, two_own, two_other,
    y_ref, b_ref, g_ref, du_ref, dh_low_ref, do_ref, dh_ref, dgain_ref, dup_b_ref, ddown_b_ref,
    out_ref, up_ref, down_ref, sems,
):
    cut = out_ref.shape[1] // 2
    units = up_ref.shape[2]
    pieces_out, pieces_up, pieces_down = [], [], []
    for n, (one, two) in enumerate(((one_own, two_own), (one_other, two_other))):
        column = pl.multiple_of(table_ref[3, n] * cut, cut)
        for j in range(count):
            spot = pl.multiple_of(table_ref[1, j] * size, size)
            pieces_out.append(
                (one.at[j, :, pl.ds(0, cut)], out_ref.at[pl.ds(spot, size), pl.ds(column, cut)])
            )
            spot = pl.multiple_of(table_ref[0, j] * size, size)
            pieces_up.append((one.at[j, :, pl.ds(cut, units)], up_ref.at[n, pl.ds(spot, size), :]))
            spot = pl.multiple_of(table_ref[2, j] * chunk, chunk)
            pieces_down.append((two.at[j], down_ref.at[n, pl.ds(spot, chunk), :]))
    copies = fetch(pieces_out + pieces_up + pieces_down, sems)
    for copy in copies[: 2 * count]:
        copy.wait()
    x = jnp.where(mask_ref[...] > 0, embed_ref[...], x_ref[...].astype(F32))
    h = x + jnp.dot(o_ref[...], out_ref[...], preferred_element_type=F32)
    centred = h - jnp.mean(h, axis=-1, keepdims=True)
    spread = jnp.mean(centred * centred, axis=-1, keepdims=True)
    scale = lax.rsqrt(spread + EPSILON)
    hat = centred * scale
    b = (hat * gain_ref[...]).astype(BF)
    b_ref[...] = b
    dy = dy_ref[...]
    ddown_b_ref[...] = jnp.sum(dy.astype(F32), axis=0, keepdims=True)
    for copy in copies[2 * count :]:
        copy.wait()
    y = h + down_b_ref[...]
    db = None
    wide = next(n for n in (768, 512, 384, 256, 128) if units % n == 0)
    for n in range(2):
        for c in range(0, units, wide):
            at = slice(c, c + wide)
            to = slice(n * units + c, n * units + c + wide)
            u = jnp.dot(b, up_ref[n, :, at], preferred_element_type=F32) + up_b_ref[n : n + 1, at]
            g, slope = gelu_parts(u)
            g = g.astype(BF)
            g_ref[:, to] = g
            y = y + jnp.dot(g, down_ref[n, at, :], preferred_element_type=F32)
            du = (matmul_t(dy, down_ref[n, at, :]) * slope).astype(BF)
            du_ref[:, to] = du
            dup_b_ref[n : n + 1, at] = jnp.sum(du.astype(F32), axis=0, keepdims=True)
            part = matmul_t(du, up_ref[n, :, at])
            db = part if db is None else db + part
    y_ref[...] = y.astype(BF)
    dgain_ref[...] = jnp.sum(db * hat, axis=0, keepdims=True)
    dh = dy.astype(F32) + norm_back(hat, scale, gain_ref[...], db)
    dh_ref[...] = dh
    low = dh.astype(BF)
    dh_low_ref[...] = low
    do_ref[...] = matmul_t(low, out_ref[...]).astype(BF)


def middle(table, o, x, mask, embed, dy, gain, up_b, down_b, one, two):
    rows, width = o.shape
    count, size, columns = one[0].shape
    chunk = two[0].shape[1]
    units = columns - width // 2
    anywhere = pl.BlockSpec(memory_space=pl.ANY)
    full = lambda shape: spec(shape, lambda t, i: (0, 0))
    shapes = [
        ((rows, width), BF), ((rows, width), BF), ((rows, 2 * units), BF), ((rows, 2 * units), BF), ((rows, width), BF),
        ((rows, width), BF), ((rows, width), F32), ((1, width), F32), ((2, units), F32), ((1, width), F32),
    ]
    return pl.pallas_call(
        functools.partial(middle_kernel, count, size, chunk),
        grid_spec=pltpu.PrefetchScalarGridSpec(
            num_scalar_prefetch=1,
            grid=(1,),
            in_specs=[full((rows, v.shape[1]) if v is x or v is mask else v.shape) for v in (o, x, mask, embed, dy, gain, up_b, down_b)]
            + [anywhere] * 4,
            out_specs=[full(shape) for shape, _ in shapes],
            scratch_shapes=[
                pltpu.VMEM((width, width), BF),
                pltpu.VMEM((2, width, units), BF),
                pltpu.VMEM((2, units, width), BF),
                pltpu.SemaphoreType.DMA((6 * count,)),
            ],
        ),
        out_shape=[jax.ShapeDtypeStruct(shape, kind) for shape, kind in shapes],
        compiler_params=pltpu.CompilerParams(vmem_limit_bytes=VMEM_LIMIT),
        cost_estimate=pl.CostEstimate(
            flops=2 * rows * width * (2 * width + 8 * units),
            bytes_accessed=4 * (width * width + 4 * units * width),
            transcendentals=2 * rows * units,
        ),
    )(table, o, x, mask, embed, dy, gain, up_b, down_b, one[0], one[1], two[0], two[1])


def matmul_t(a, b):
    return lax.dot_general(a, b, (((1,), (1,)), ((), ())), preferred_element_type=F32)


def attend_kernel(
    rows, tiles, flag_ref, qcol_ref, krow_ref, q_ref, k_ref, v_ref, o_ref, lse_ref,
    bias_ref, s_ref, top_ref, sum_ref, acc_ref,
):
    pair = pl.program_id(0)
    both_rows = 2 * rows

    def span(t):
        return slice(t * rows, (t + 1) * rows)

    def lines(t):
        return slice(rows, both_rows) if t == 1 else slice(0, both_rows)

    @pl.when(pair == 0)
    def _():
        lse_ref[...] = jnp.zeros_like(lse_ref)
        own = qcol_ref[:, 0:1]
        up_one = qcol_ref[:, 1:2]
        up_two = qcol_ref[:, 2:3]
        limit = qcol_ref[:, 3:4]
        for t in range(tiles):
            if t == 1:
                r = lax.broadcasted_iota(jnp.int32, (rows, rows), 0) // BLOCK
                c = lax.broadcasted_iota(jnp.int32, (rows, rows), 1) // BLOCK
                bias_ref[rows:, span(t)] = jnp.where(r == c, 0.0, NEG_FILL)
            else:
                seg = krow_ref[0:1, span(t)]
                index = krow_ref[1:2, span(t)]
                ok = ((seg == own) | (seg == up_one) | (seg == up_two)) & (index < limit)
                bias_ref[:, span(t)] = jnp.where(ok, 0.0, NEG_FILL)

    lane = lax.broadcasted_iota(jnp.int32, (both_rows, 128), 1)
    queries = [jnp.where((lane // HEAD_DIM) == h, q_ref[...] * 0.125, 0).astype(BF) for h in range(2)]
    top_ref[...] = jnp.full_like(top_ref, -3.0e38)
    for t in range(tiles):

        @pl.when(flag_ref[t] > 0)
        def _():
            at = lines(t)
            keys, bias = k_ref[span(t), :], bias_ref[at, span(t)]
            for h in range(2):
                s = matmul_t(queries[h][at], keys) + bias
                s_ref[h, at, span(t)] = s
                best = top_ref[h, at, :]
                for c in range(rows // 128):
                    best = jnp.maximum(best, s[:, c * 128 : (c + 1) * 128])
                top_ref[h, at, :] = best

    tops = [jnp.max(top_ref[h], axis=-1, keepdims=True) for h in range(2)]
    sum_ref[...] = jnp.zeros_like(sum_ref)
    acc_ref[...] = jnp.zeros_like(acc_ref)
    for t in range(tiles):

        @pl.when(flag_ref[t] > 0)
        def _():
            at = lines(t)
            values = v_ref[span(t), :]
            for h in range(2):
                p = jnp.exp(s_ref[h, at, span(t)] - tops[h][at])
                part = sum_ref[h, at, :]
                for c in range(rows // 128):
                    part = part + p[:, c * 128 : (c + 1) * 128]
                sum_ref[h, at, :] = part
                acc_ref[h, at, :] += jnp.dot(p.astype(BF), values, preferred_element_type=F32)

    outs, norms = [], lse_ref[...]
    for h in range(2):
        total = jnp.sum(sum_ref[h], axis=-1, keepdims=True)
        outs.append(acc_ref[h] / total)
        norms = jnp.where(lane == 2 * pair + h, tops[h] + jnp.log(total), norms)
    lse_ref[...] = norms
    o_ref[...] = jnp.where(lane < HEAD_DIM, outs[0], outs[1]).astype(BF)


def attend(flags, qcol, krow, q, k, v, rows):
    width = q.shape[1]
    total = k.shape[0]
    tiles = total // rows
    pair = lambda n: spec((n, 128), lambda p, f: (0, p))
    fixed = lambda shape: spec(shape, lambda p, f: (0, 0))
    return pl.pallas_call(
        functools.partial(attend_kernel, rows, tiles),
        grid_spec=pltpu.PrefetchScalarGridSpec(
            num_scalar_prefetch=1,
            grid=(width // 128,),
            in_specs=[fixed(qcol.shape), fixed(krow.shape), pair(2 * rows), pair(total), pair(total)],
            out_specs=[pair(2 * rows), fixed((2 * rows, 128))],
            scratch_shapes=[
                pltpu.VMEM((2 * rows, total), F32),
                pltpu.VMEM((2, 2 * rows, total), F32),
                pltpu.VMEM((2, 2 * rows, 128), F32),
                pltpu.VMEM((2, 2 * rows, 128), F32),
                pltpu.VMEM((2, 2 * rows, 128), F32),
            ],
        ),
        out_shape=[
            jax.ShapeDtypeStruct((2 * rows, width), BF),
            jax.ShapeDtypeStruct((2 * rows, 128), F32),
        ],
        compiler_params=pltpu.CompilerParams(vmem_limit_bytes=VMEM_LIMIT),
        cost_estimate=pl.CostEstimate(
            flops=16 * rows * total * width,
            bytes_accessed=4 * (total + rows) * width,
            transcendentals=2 * rows * total * width // HEAD_DIM,
        ),
    )(flags, qcol, krow, q, k, v)


def attend_back_kernel(
    rows, first, last, flag_ref, qrow_ref, kcol_ref, q_ref, k_ref, v_ref, o_ref, g_ref, lse_ref, *refs,
):
    refs = list(refs)
    near = first == 0
    cos_ref, sin_ref = refs[:2]
    part_ref = refs[2] if near else None
    dq_ref, dk_ref, dv_ref, bias_ref, acc_ref = refs[-5:]
    pair = pl.program_id(0)
    both_rows = 2 * rows

    def span(t):
        return slice(t * rows, (t + 1) * rows)

    def lines(t):
        return slice(rows, both_rows) if t == 1 else slice(0, both_rows)

    @pl.when(pair == 0)
    def _():
        own = qrow_ref[0:1, :]
        up_one = qrow_ref[1:2, :]
        up_two = qrow_ref[2:3, :]
        limit = qrow_ref[3:4, :]
        for t in range(first, last):
            if t == 1:
                r = lax.broadcasted_iota(jnp.int32, (rows, rows), 0) // BLOCK
                c = lax.broadcasted_iota(jnp.int32, (rows, rows), 1) // BLOCK
                bias_ref[span(t - first), rows:] = jnp.where(r == c, 0.0, NEG_FILL)
            else:
                seg = kcol_ref[span(t), 0:1]
                index = kcol_ref[span(t), 1:2]
                ok = ((seg == own) | (seg == up_one) | (seg == up_two)) & (index < limit)
                bias_ref[span(t - first), :] = jnp.where(ok, 0.0, NEG_FILL)

    lane = lax.broadcasted_iota(jnp.int32, (both_rows, 128), 1)
    acc_ref[...] = part_ref[...] if near else jnp.zeros_like(acc_ref)
    queries, grads, deltas, norms = [], [], [], []
    product = (o_ref[...].astype(F32) * g_ref[...].astype(F32)).T
    for h in range(2):
        mine = (lane // HEAD_DIM) == h
        queries.append(jnp.where(mine, q_ref[...] * 0.125, 0).astype(BF))
        grads.append(jnp.where(mine, g_ref[...], 0).astype(BF))
        deltas.append(jnp.sum(product[h * HEAD_DIM : (h + 1) * HEAD_DIM], axis=0, keepdims=True))
        norms.append(lse_ref[pl.ds(2 * pair + h, 1), :])
    for t in range(first, last):
        to = span(t - first)

        @pl.when(flag_ref[t] == 0)
        def _():
            dk_ref[to, :] = jnp.zeros((rows, 128), BF)
            dv_ref[to, :] = jnp.zeros((rows, 128), BF)

        @pl.when(flag_ref[t] > 0)
        def _():
            at = lines(t)
            keys, values = k_ref[span(t), :], v_ref[span(t), :]
            keys_t = keys.astype(F32).T.astype(BF)
            dk = dv = None
            for h in range(2):
                q, g = queries[h][at], grads[h][at]
                s = matmul_t(keys, q) + bias_ref[to, at]
                p = jnp.exp(s - norms[h][:, at])
                dp = matmul_t(values, g)
                ds = (p * (dp - deltas[h][:, at])).astype(BF)
                part_v = jnp.dot(p.astype(BF), g, preferred_element_type=F32)
                part_k = jnp.dot(ds, q, preferred_element_type=F32)
                dv = part_v if dv is None else dv + part_v
                dk = part_k if dk is None else dk + part_k
                half = slice(h * HEAD_DIM, (h + 1) * HEAD_DIM)
                acc_ref[half, at] += jnp.dot(keys_t[half], ds, preferred_element_type=F32)
            [dk] = turn(dk, cos_ref[span(t), :], -sin_ref[span(t), :])
            dk_ref[to, :] = dk.astype(BF)
            dv_ref[to, :] = dv.astype(BF)

    if near:
        dq = acc_ref[...].T * 0.125
        [dq] = turn(dq, cos_ref[:both_rows, :], -sin_ref[:both_rows, :])
        dq_ref[...] = dq.astype(BF)
    else:
        dq_ref[...] = acc_ref[...]


def attend_back(first, last, flags, qrow, kcol, q, k, v, o, g, lse, cosine, sine, rows, part=None):
    width = q.shape[1]
    total = k.shape[0]
    there = (last - first) * rows
    near = first == 0
    pair = lambda n: spec((n, 128), lambda p, f: (0, p))
    turned = spec((128, 2 * rows), lambda p, f: (p, 0))
    fixed = lambda shape: spec(shape, lambda p, f: (0, 0))
    out = lambda n: jax.ShapeDtypeStruct((n, width), BF)
    return pl.pallas_call(
        functools.partial(attend_back_kernel, rows, first, last),
        grid_spec=pltpu.PrefetchScalarGridSpec(
            num_scalar_prefetch=1,
            grid=(width // 128,),
            in_specs=[
                fixed(qrow.shape), fixed(kcol.shape), pair(2 * rows), pair(total), pair(total),
                pair(2 * rows), pair(2 * rows), fixed(lse.shape), fixed(cosine.shape), fixed(sine.shape),
            ] + ([turned] if near else []),
            out_specs=[pair(2 * rows) if near else turned, pair(there), pair(there)],
            scratch_shapes=[
                pltpu.VMEM((there, 2 * rows), F32),
                pltpu.VMEM((128, 2 * rows), F32),
            ],
        ),
        out_shape=[out(2 * rows) if near else jax.ShapeDtypeStruct((width, 2 * rows), F32), out(there), out(there)],
        compiler_params=pltpu.CompilerParams(vmem_limit_bytes=VMEM_LIMIT),
        cost_estimate=pl.CostEstimate(
            flops=40 * rows * there * width,
            bytes_accessed=8 * (there + rows) * width,
            transcendentals=2 * rows * there * width // HEAD_DIM,
        ),
    )(flags, qrow, kcol, q, k, v, o, g, lse, cosine, sine, *([part] if near else []))


def fold_kernel(
    count, size, rows, first, table_ref, dk_ref, dv_ref, x_ref, mask_ref, embed_ref, gain_ref, own_hbm, other_hbm, *refs,
):
    near = first == 0
    refs = list(refs)
    dq_ref, dh_ref = refs[:2] if near else (None, None)
    outs = refs[2:] if near else refs
    if near:
        da_ref, dgain_ref, clean_ref, noisy_ref, dembed_ref, acc_ref, own_ref, other_ref, sems = outs
    else:
        da_ref, dgain_ref, acc_ref, own_ref, other_ref, sems = outs
    tile = pl.program_id(0)

    @pl.when(tile == 0)
    def _():
        pieces = []
        for hbm, ref in ((own_hbm, own_ref), (other_hbm, other_ref)):
            spots = placed(ref, count, size, table_ref, 0)
            pieces += [(hbm.at[n, pl.ds(0, size), :], spots[n]) for n in range(count)]
        for copy in fetch(pieces, sems):
            copy.wait()
        dgain_ref[...] = jnp.zeros_like(dgain_ref)

    half = own_ref.shape[1] // 3
    cuts = [slice(n * half, (n + 1) * half) for n in range(3)]
    da = None
    for n, w_ref in enumerate((own_ref, other_ref)):
        part = matmul_t(dk_ref[:, cuts[n]], w_ref[:, cuts[1]]) + matmul_t(dv_ref[:, cuts[n]], w_ref[:, cuts[2]])
        da = part if da is None else da + part
    acc_ref[...] = da
    if near:

        @pl.when(tile < 2)
        def _():
            acc_ref[...] += matmul_t(dq_ref[:, cuts[0]], own_ref[:, cuts[0]]) + matmul_t(
                dq_ref[:, cuts[1]], other_ref[:, cuts[0]]
            )

    da = acc_ref[...]
    da_ref[...] = da.astype(BF)
    x = jnp.where(mask_ref[...] > 0, embed_ref[...], x_ref[...].astype(F32))
    centred = x - jnp.mean(x, axis=-1, keepdims=True)
    scale = lax.rsqrt(jnp.mean(centred * centred, axis=-1, keepdims=True) + EPSILON)
    hat = centred * scale
    dgain_ref[...] += jnp.sum(da * hat, axis=0, keepdims=True)
    if near:

        @pl.when(tile == 0)
        def _():
            clean_ref[...] = da

        @pl.when(tile == 1)
        def _():
            noisy = dh_ref[...] + norm_back(hat, scale, gain_ref[...], da)
            noisy_ref[...] = noisy
            dembed_ref[...] = jnp.sum(jnp.where(mask_ref[...] > 0, noisy, 0.0), axis=0, keepdims=True)


def fold(table, first, last, dk, dv, x_all, mask, embed, gain, own, other, rows, dq=None, dh=None):
    width = x_all.shape[1]
    there = (last - first) * rows
    near = first == 0
    count = own.shape[0]
    size = width // count
    columns = own.shape[2]
    whole = lambda shape: spec(shape, lambda t, i: (0, 0))
    moved = lambda n: spec((rows, n), lambda t, i: (t, 0))
    shifted = lambda n: spec((rows, n), lambda t, i: (t + first, 0))
    early = lambda n: spec((rows, n), lambda t, i: (jnp.minimum(t, 1), 0))
    second = lambda n: spec((rows, n), lambda t, i: (1, 0))
    anywhere = pl.BlockSpec(memory_space=pl.ANY)
    line = jax.ShapeDtypeStruct((1, width), F32)
    tile = jax.ShapeDtypeStruct((rows, width), F32)
    return pl.pallas_call(
        functools.partial(fold_kernel, count, size, rows, first),
        grid_spec=pltpu.PrefetchScalarGridSpec(
            num_scalar_prefetch=1,
            grid=(last - first,),
            in_specs=[
                moved(width), moved(width), shifted(width), shifted(1), whole((1, width)), whole((1, width)), anywhere, anywhere,
            ] + ([early(width), second(width)] if near else []),
            out_specs=[moved(width), whole((1, width))]
            + ([whole((rows, width)), whole((rows, width)), whole((1, width))] if near else []),
            scratch_shapes=[
                pltpu.VMEM((rows, width), F32),
                pltpu.VMEM((width, columns), BF),
                pltpu.VMEM((width, columns), BF),
                pltpu.SemaphoreType.DMA((2 * count,)),
            ],
        ),
        out_shape=[jax.ShapeDtypeStruct((there, width), BF), line] + ([tile, tile, line] if near else []),
        compiler_params=pltpu.CompilerParams(vmem_limit_bytes=VMEM_LIMIT),
        cost_estimate=pl.CostEstimate(
            flops=4 * there * width * width,
            bytes_accessed=2 * (4 * there * width + 3 * width * width),
            transcendentals=0,
        ),
    )(table, dk, dv, x_all, mask, embed, gain, own, other, *([dq, dh] if near else []))


def normalise(values):
    centred = values - jnp.mean(values, axis=-1, keepdims=True)
    spread = jnp.mean(centred * centred, axis=-1, keepdims=True)
    scale = lax.rsqrt(spread + EPSILON)
    return centred * scale, scale


def norm_back(hat, scale, gain, grad):
    scaled = grad * gain
    return scale * (
        scaled
        - jnp.mean(scaled, axis=-1, keepdims=True)
        - hat * jnp.mean(scaled * hat, axis=-1, keepdims=True)
    )


ROOT = math.sqrt(2.0 / math.pi)


def gelu_parts(u):
    t = jnp.tanh(ROOT * (u + 0.044715 * (u * u * u)))
    slope = 0.5 * (1.0 + t) + 0.5 * u * (1.0 - t * t) * (ROOT * (1.0 + 3 * 0.044715 * (u * u)))
    return 0.5 * u * (1.0 + t), slope


def mm(a, b):
    return jnp.dot(a, b, preferred_element_type=F32)


def mm_t(a, b):
    return lax.dot_general(a, b, (((1,), (1,)), ((), ())), preferred_element_type=F32)


def t_mm(a, b):
    return lax.dot_general(a, b, (((0,), (0,)), ((), ())), preferred_element_type=F32)


def halves_of_heads(w):
    w = w.reshape(w.shape[0], 3, 2, -1)
    return w[:, :, 0].reshape(w.shape[0], -1), w[:, :, 1].reshape(w.shape[0], -1)


def heads_of_halves(a, b):
    a, b = a.reshape(a.shape[0], 3, -1), b.reshape(b.shape[0], 3, -1)
    return jnp.stack([a, b], 2).reshape(a.shape[0], -1)


def halves_of_units(w, chunk):
    w = w.reshape(w.shape[0], -1, 2, chunk)
    return w[:, :, 0].reshape(w.shape[0], -1), w[:, :, 1].reshape(w.shape[0], -1)


def units_of_halves(a, b, chunk):
    a, b = a.reshape(a.shape[0], -1, chunk), b.reshape(b.shape[0], -1, chunk)
    return jnp.stack([a, b], 2).reshape(a.shape[0], -1)


def lower_in_chain(leaf):
    z, y = lax.shift_right_logical(leaf, 1), leaf & 1
    below = [((2 * (z - s) + at), z >= s) for s in (1, 2, 3) for at in (y, 1 - y)]
    return below[:2] + [(2 * z, y == 1)] + below[2:]


class Chain:
    near = 5

    def __init__(self, rows):
        self.at = Links()
        self.rows = rows
        self.core = self.at.core

    def lower(self, leaf):
        return lower_in_chain(leaf)

    def places(self):
        at = self.at
        n = jnp.arange(4)
        zyx = ((at.z ^ n)[None, None, :] * 2 + (at.y ^ n[:2])[None, :, None]) * 2 + (at.x ^ n[:2])[:, None, None]
        yzx = ((at.z ^ n)[None, :, None] * 2 + (at.y ^ n[:2])[:, None, None]) * 2 + (at.x ^ n[:2])[None, None, :]
        first = zyx.reshape(16)
        columns = jnp.where(jnp.arange(16) % 2 == 0, at.core, 1 - at.core)
        return jnp.stack([first, first ^ (8 * at.core), yzx.reshape(16), columns]).astype(jnp.int32)

    def first_gather(self, hid, w_qkv, w_out, w_up, w_down, vectors):
        at = self.at
        few, chunk, cut = w_qkv.shape[0], w_down.shape[0], w_out.shape[1] // 2
        qkv_a, qkv_b = halves_of_heads(w_qkv)
        row = jnp.pad(vectors[None], ((0, 7), (0, qkv_a.shape[1] - vectors.shape[0])))
        qkv_a, qkv_b = (jnp.concatenate([v, row], axis=0) for v in (qkv_a, qkv_b))
        block = to_column_half(at, qkv_a, qkv_b)
        block = jnp.concatenate(
            [block[:few], block[few + 8 : 2 * few + 8], block[few : few + 8], block[2 * few + 8 :]], axis=0
        )[None]
        beside = at.swap_y(hid, [(i, i + 1) for i in range(0, 8, 2)])
        down_two = at.swap_x(w_down)
        block, hid_up = tie(block, hid)
        line = z_gather(at, block)
        line, hid_up = tie(line, hid_up)
        first_hop = at.up(hid_up, 0, 2)
        plane = jnp.concatenate([line, at.swap_y(line)], axis=0)
        up_a, up_b = halves_of_units(w_up, chunk)
        one_a = jnp.concatenate([w_out[:, :cut], up_a], axis=1)
        one_b = jnp.concatenate([w_out[:, cut:], up_b], axis=1)
        one = to_column_half(at, one_a, one_b)[None]
        down_two = jnp.stack([w_down, down_two])[None]
        first_hop, plane, beside, one, down_two = tie(first_hop, plane, beside, one, down_two)
        other = at.swap_x(plane)
        second_hop = at.up(first_hop, 1, 2)
        first_over = at.swap_y(first_hop, [(i, i ^ 1) for i in range(2, 8)])
        second_hop, first_over, one = tie(second_hop, first_over, one)
        third_hop = at.up(second_hop, 2, 2)
        second_over = at.swap_y(second_hop, [(i, i ^ 1) for i in range(4, 8)])
        qkv = jnp.concatenate([plane, other], axis=0)
        third_hop, second_over, qkv, one = tie(third_hop, second_over, qkv, one)
        third_over = at.swap_y(third_hop, [(i, i ^ 1) for i in range(6, 8)])
        qkv_both = (qkv, at.swap_core(qkv))
        line = z_gather(at, one)
        third_over, qkv_both, line = tie(third_over, qkv_both, line)
        m = 2 * few
        vec = jnp.concatenate([qkv[:, m, : vectors.shape[0]], qkv[:, m + 8, : vectors.shape[0]]], axis=1)
        order = (self.places()[0][None, :] == jnp.arange(16)[:, None]).astype(BF)
        vec = mm(order, vec).reshape(32, -1)
        lower = [first_hop, first_over, beside, second_hop, second_over, third_hop, third_over]
        return lower, qkv_both, vec, (line, down_two)

    def second_start(self, state):
        line, down_two = state
        return jnp.concatenate([line, self.at.swap_y(line)], axis=0), z_gather(self.at, down_two)

    def second_go_on(self, state):
        plane, line = state
        at = self.at
        one = jnp.concatenate([plane, at.swap_x(plane)], axis=0)
        down = jnp.concatenate([line, at.swap_y(line)], axis=0)
        return one, down.reshape((16,) + down.shape[2:])

    def second_end(self, state):
        one, down = state
        return (one, self.at.swap_core(one)), (down, self.at.swap_core(down))

    def unit_bias(self, bias, chunk):
        a, b = halves_of_units(bias[None], chunk)
        return jnp.where(self.core == 0, a, b), jnp.where(self.core == 0, b, a)

    def unit_bias_back(self, own, other, chunk):
        a = jnp.where(self.core == 0, own, other)
        b = jnp.where(self.core == 0, other, own)
        return units_of_halves(a, b, chunk)[0]

    def backward(self, run):
        at = self.at
        rows = self.rows
        cores = lambda g: (8, 2, g.shape[0] // 16, g.shape[1])
        down_other, up_other = run.feed_other()
        down_got, up_got = at.swap_core(down_other), at.swap_core(up_other)
        down_own, up_own, out_own, out_other = run.feed_own(self)
        down = plus(down_own, down_got).astype(BF).reshape(cores(down_own))
        up = plus(up_own, up_got).astype(BF)
        up = up.reshape((4, 2, 2, up.shape[0] // 16, up.shape[1]))
        down_keep, down_send = choose(at.x, down, 1)
        up_keep, up_send = choose(at.y, up, 1)
        (down_keep, down_send, up_keep, up_send, out_own, out_other, run.grad_mixed) = tie(
            down_keep, down_send, up_keep, up_send, out_own, out_other, run.grad_mixed
        )
        down_got, up_got, out_got = at.swap_x(down_send), at.swap_y(up_send), at.swap_core(out_other)
        far = run.far_tiles()
        down_got, up_got, out_got, far = tie(down_got, up_got, out_got, far)
        far_da, far_gain = run.far_fold(far)
        down = plus(down_keep, down_got).astype(BF)
        down = down.reshape((4, 2) + down.shape[1:])
        down_keep, down_send = choose(at.y, down, 1)
        up = plus(up_keep, up_got).astype(BF)
        up_keep, up_send = z_parts(at, up)
        out = plus(out_own, out_got).astype(BF)
        out_keep, out_send = choose(at.x, out, 1)
        tiles = [far_da[n * rows : (n + 1) * rows] for n in range(4)]
        (down_keep, down_send, up_keep, up_send, out_keep, out_send, tiles, far) = tie(
            down_keep, down_send, up_keep, up_send, out_keep, out_send, tiles, far
        )
        down_got, up_got, out_got = at.swap_y(down_send), z_move(at, up_send), at.swap_x(out_send)
        third = at.swap_y(tiles[3], [(i, i ^ 1) for i in range(6, 8)])
        second = at.swap_y(tiles[1], [(i, i ^ 1) for i in range(4, 8)])
        near = run.near_tiles(far)
        down_got, up_got, out_got, third, second, near, tiles = tie(
            down_got, up_got, out_got, third, second, near, tiles
        )
        down = plus(down_keep, down_got).astype(BF)
        down_keep, down_send = z_parts(at, down)
        up = z_total(up_keep, up_got).astype(BF)
        up_keep, up_send = choose(at.x, up, 0)
        out = plus(out_keep, out_got).astype(BF)
        out = out.reshape((4, 2) + out.shape[1:])
        out_keep, out_send = choose(at.y, out, 1)
        cur = plus(tiles[2], third).astype(BF)
        (down_keep, down_send, up_keep, up_send, out_keep, out_send, cur, near) = tie(
            down_keep, down_send, up_keep, up_send, out_keep, out_send, cur, near
        )
        cur = at.down(cur, 3, 3)
        down_got, up_got, out_got = z_move(at, down_send), at.swap_x(up_send), at.swap_y(out_send)
        near_da, clean, vec = run.near_fold(near, far_gain)
        near_da, clean, vec, cur = tie(near_da, clean, vec, cur)
        first = at.swap_y(near_da[3 * rows : 4 * rows], [(i, i ^ 1) for i in range(2, 8)])
        beside = at.swap_y(near_da[4 * rows : 5 * rows], [(i, i - 1) for i in range(1, 8, 2)])
        cur = (plus(tiles[0], second) + cur.astype(F32)).astype(BF)
        other = run.qkv_other(vec, self)
        other, cur = tie(other, cur)
        cur = at.down(cur, 2, 3)
        other_got = [at.swap_core(v) for v in other]
        own = run.qkv_own(vec, self)
        other_got, own, first, cur, beside, down_got, up_got, out_got = tie(
            other_got, own, first, cur, beside, down_got, up_got, out_got
        )
        a, b = (plus(v, got).astype(BF) for v, got in zip(own, other_got))
        b = b.reshape((4, 2) + b.shape[1:])
        a_keep, a_send = choose(at.x, a, 1)
        b_keep, b_send = choose(at.y, b, 1)
        cur = (plus(near_da[2 * rows : 3 * rows], first) + cur.astype(F32)).astype(BF)
        out = plus(out_keep, out_got).astype(BF)
        out_keep, out_send = z_parts(at, out)
        a_keep, a_send, b_keep, b_send, cur, out_send = tie(a_keep, a_send, b_keep, b_send, cur, out_send)
        a_got, b_got, cur, out_got = at.swap_x(a_send), at.swap_y(b_send), at.down(cur, 1, 3), z_move(at, out_send)
        sum_down = z_total(down_keep, down_got)
        sum_up = self.join_units(plus(up_keep, up_got), run.chunk)
        a_got, b_got, cur, out_got = tie(a_got, b_got, cur, out_got)
        a = plus(a_keep, a_got).astype(BF)
        a = a.reshape((4, 2) + a.shape[1:])
        a_keep, a_send = choose(at.y, a, 1)
        b_keep, b_send = z_parts(at, plus(b_keep, b_got).astype(BF))
        a_keep, a_send, b_keep, b_send = tie(a_keep, a_send, b_keep, b_send)
        a_got, b_got = at.swap_y(a_send), z_move(at, b_send)
        grad_hidden = run.last(clean + cur.astype(F32) + beside.astype(F32))
        sum_out = jnp.concatenate(from_column_half(at, z_total(out_keep, out_got)), axis=1)
        a_got, b_got = tie(a_got, b_got)
        a_keep, a_send = z_parts(at, plus(a_keep, a_got).astype(BF))
        b_keep, b_send = choose(at.x, z_total(b_keep, b_got).astype(BF), 0)
        a_keep, a_send, b_keep, b_send = tie(a_keep, a_send, b_keep, b_send)
        a_got, b_got = z_move(at, a_send), at.swap_x(b_send)
        a_got, b_got = tie(a_got, b_got)
        m = run.few * 2
        a, b = z_total(a_keep, a_got), plus(b_keep, b_got)
        rest = jnp.concatenate([a[:m], b], axis=1)
        sum_qkv = heads_of_halves(*from_column_half(at, rest))
        return sum_down, sum_up, sum_out, sum_qkv, a[m, : run.vectors], grad_hidden

    def join_units(self, g, chunk):
        return units_of_halves(*from_column_half(self.at, g), chunk)

    def out_pieces(self, g):
        half = g.shape[0] // 2
        g = jnp.where(self.core == 0, g, jnp.concatenate([g[half:], g[:half]], axis=0))
        g = g.reshape(8, 2, g.shape[0] // 16, 2, g.shape[1] // 2)
        return choose(self.core, g, 3)

    def qkv_pieces(self, q, k, v, vec, other):
        m = q.shape[0] // 16
        a = jnp.concatenate([q, k[:, : k.shape[1] // 3]], axis=1).reshape(8, 2, m, -1)
        b = jnp.concatenate([k[:, k.shape[1] // 3 :], v], axis=1).reshape(8, 2, m, -1)
        n = vec.shape[1]
        rows = pick(vec.astype(BF).reshape(8, 2, 2, n), 1 - self.core if other else self.core, 2)[:, :, None]
        rows = jnp.pad(rows, ((0, 0), (0, 0), (0, 7), (0, a.shape[3] - n)))
        return [jnp.concatenate([a, rows], axis=2), b]


AXES = ("leaf", "fsdp")


class Whole:
    def __init__(self, rows, leaves, devices):
        self.rows, self.leaves, self.devices = rows, leaves, devices
        self.leaf = lax.axis_index("leaf")
        self.near = 2 + (leaves - 1) // 2

    def lower(self, leaf):
        return [(leaf - s, leaf >= s) for s in range(1, self.leaves)]

    def places(self):
        return jnp.array([[0, 0], [0, 0], [0, 0], [0, 1]], jnp.int32)

    def first_gather(self, hid, w_qkv, w_out, w_up, w_down, vectors):
        tree = lax.all_gather(hid, "leaf", axis=0, tiled=False)
        lower = [pick(tree, jnp.maximum(leaf, 0), 0) for leaf, _ in self.lower(self.leaf)]
        every = lambda w: lax.all_gather(w, AXES, axis=0, tiled=True)
        qkv = tuple(v[None] for v in halves_of_heads(every(w_qkv)))
        return lower, qkv, every(vectors[None]), (every(w_out), every(w_up), every(w_down))

    def second_start(self, state):
        return state

    def second_go_on(self, state):
        return state

    def second_end(self, state):
        out_w, up_w, down_w = state
        half, cut = down_w.shape[0] // 2, out_w.shape[1] // 2
        one = tuple(
            jnp.concatenate([out_w[:, n * cut : (n + 1) * cut], up_w[:, n * half : (n + 1) * half]], axis=1)[None]
            for n in range(2)
        )
        return one, tuple(down_w[None, n * half : (n + 1) * half] for n in range(2))

    def unit_bias(self, bias, chunk):
        half = bias.shape[0] // 2
        return bias[None, :half], bias[None, half:]

    def unit_bias_back(self, own, other, chunk):
        return jnp.concatenate([own, other], axis=1)[0]

    def scatter(self, g):
        return lax.psum_scatter(g.astype(F32), AXES, scatter_dimension=0, tiled=True)

    def out_pieces(self, g):
        return g, g

    def qkv_pieces(self, q, k, v, vec, other):
        return [jnp.concatenate([q, k, v], axis=1), vec]

    def backward(self, run):
        rows = self.rows
        down_other, up_other = run.feed_other()
        down_own, up_own, out, _ = run.feed_own(self)
        far = run.far_tiles()
        far_da, far_gain = run.far_fold(far)
        near = run.near_tiles(far)
        near_da, clean, vec = run.near_fold(near, far_gain)
        own, vec = run.qkv_own(vec, self)
        other, _ = run.qkv_other(vec, self)
        tiles = jnp.concatenate([near_da[:rows], near_da[2 * rows :], far_da], axis=0)
        tiles = tiles.reshape((self.leaves, rows) + tiles.shape[1:])
        order = [pick(tiles, (self.leaf - n) % self.leaves, 0) for n in range(self.leaves)]
        total = lax.psum_scatter(jnp.concatenate(order, axis=0), "leaf", scatter_dimension=0, tiled=True)
        return (
            self.scatter(jnp.concatenate([down_own, down_other], axis=0)),
            self.scatter(jnp.concatenate([up_own, up_other], axis=1)),
            self.scatter(out),
            self.scatter(heads_of_halves(own, other)),
            self.scatter(vec)[0],
            run.last(total.astype(F32)),
        )


class Backward:
    pass


def shards(
    leaves,
    groups,
    hidden,
    noise_mask,
    seg_blocks,
    parents,
    ln1_gain,
    w_qkv,
    w_out,
    ln2_gain,
    w_up,
    up_bias,
    w_down,
    down_bias,
    mask_embed,
    cotangent,
):
    rows = hidden.shape[1]
    width = hidden.shape[2]
    half = width // 2
    devices = leaves * groups
    net = Chain(rows) if (leaves, groups) == (8, 4) else Whole(rows, leaves, devices)
    chunk = w_down.shape[0]
    few = ln1_gain.shape[0]
    leaf = lax.axis_index("leaf")

    hid = hidden[0]
    query_cols, query_rows, key_cols, key_rows, flags = tables(net.lower, leaf, seg_blocks, parents, rows)
    tiles = flags.shape[0]
    lanes = jnp.arange(128, dtype=jnp.int32)
    exponent = (lanes % (HEAD_DIM // 2)).astype(F32) * (-math.log(10000.0) / (HEAD_DIM // 2))
    angles = key_cols[:, 2:3] * jnp.exp(exponent)
    cosine = jnp.cos(angles)
    sine = jnp.sin(angles) * jnp.where((lanes % HEAD_DIM) < HEAD_DIM // 2, -1.0, 1.0)
    places = net.places()
    mask = jnp.pad(noise_mask[0].astype(F32)[:, None], ((rows, (tiles - 2) * rows), (0, 0)))

    vectors = jnp.concatenate([ln1_gain, ln2_gain, down_bias, mask_embed, up_bias])
    lower, qkv_w, vec, coming = net.first_gather(hid, w_qkv, w_out, w_up, w_down, vectors)
    gain_one, gain_two, down_b, embed = (
        vec[:, n * few : (n + 1) * few].reshape(1, width).astype(F32) for n in range(4)
    )
    up_b = jnp.concatenate(net.unit_bias(vec[:, 4 * few :].reshape(-1).astype(F32), chunk), axis=0)
    x_all = jnp.concatenate([hid, hid] + lower, axis=0)
    x_all, coming, cosine, sine = tie(x_all, coming, cosine, sine)
    coming = net.second_start(coming)
    a_all, query, key, value = project(
        places, x_all, mask, embed, gain_one, qkv_w[0], qkv_w[1], cosine, sine, rows
    )
    coming, query, a_all = tie(coming, query, a_all)
    coming = net.second_go_on(coming)
    mixed, log_norm = attend(flags, query_cols, key_rows, query, key, value, rows)
    coming, mixed = tie(coming, mixed)
    one_w, down_w = net.second_end(coming)
    norm_rows = log_norm.T
    grad_two = cotangent[0].reshape(2 * rows, width)
    (
        output, normed_two, act, grad_pre, grad_one, grad_mixed, grad_after, grad_gain_two, grad_up_b, grad_down_b,
    ) = middle(places, mixed, x_all, mask, embed, grad_two, gain_two, up_b, down_b, one_w, down_w)
    output = output.reshape(1, 2, rows, width)
    units = act.shape[1] // 2

    run = Backward()
    run.chunk, run.few, run.vectors, run.grad_mixed = chunk, few, vectors.shape[0], grad_mixed
    cut = net.near

    def feed_other():
        return t_mm(act[:, units:], grad_two).astype(BF), t_mm(normed_two, grad_pre[:, units:]).astype(BF)

    def feed_own(net):
        down, up = t_mm(act[:, :units], grad_two).astype(BF), t_mm(normed_two, grad_pre[:, :units]).astype(BF)
        return (down, up) + tuple(net.out_pieces(t_mm(mixed, grad_one).astype(BF)))

    def far_tiles():
        return attend_back(
            cut, tiles, flags, query_rows, key_cols, query, key, value, mixed, run.grad_mixed, norm_rows, cosine, sine, rows
        )

    def far_fold(far):
        run.far = far
        return fold(places, cut, tiles, far[1], far[2], x_all, mask, embed, gain_one, qkv_w[0], qkv_w[1], rows)

    def near_tiles(far):
        run.far = far
        return attend_back(
            0, cut, flags, query_rows, key_cols, query, key, value, mixed, run.grad_mixed, norm_rows, cosine, sine, rows, far[0]
        )

    def near_fold(near, far_gain):
        run.near = near
        da, gain, clean, run.noisy, grad_embed = fold(
            places, 0, cut, near[1], near[2], x_all, mask, embed, gain_one, qkv_w[0], qkv_w[1], rows, near[0], grad_after
        )
        parts = (gain + far_gain, grad_gain_two, grad_down_b, grad_embed, net.unit_bias_back(grad_up_b[:1], grad_up_b[1:], chunk))
        vec = jnp.concatenate([v.reshape(devices, -1) for v in parts], axis=1)
        run.keys, run.values = (jnp.concatenate([run.near[n], run.far[n]], axis=0) for n in (1, 2))
        return da, clean, vec

    def qkv_half(n, vec, net):
        at = slice(n * half, (n + 1) * half)
        q = t_mm(a_all[: 2 * rows], run.near[0][:, at]).astype(BF)
        k, v = (t_mm(a_all, g[:, at]).astype(BF) for g in (run.keys, run.values))
        return net.qkv_pieces(q, k, v, vec, n == 1)

    def last(total):
        hat, scale = normalise(hid.astype(F32))
        masked = (noise_mask[0] == 1)[:, None]
        clean = grad_after[:rows] + norm_back(hat, scale, gain_one, total)
        return (clean + jnp.where(masked, 0.0, run.noisy)).astype(BF)[None]

    run.feed_other, run.feed_own, run.far_tiles, run.far_fold = feed_other, feed_own, far_tiles, far_fold
    run.near_tiles, run.near_fold, run.last = near_tiles, near_fold, last
    run.qkv_own = lambda vec, net: qkv_half(0, vec, net)
    run.qkv_other = lambda vec, net: qkv_half(1, vec, net)
    sum_down, sum_up, sum_out, sum_qkv, sum_vec, grad_hidden = net.backward(run)
    piece = lambda n: sum_vec[n * few : (n + 1) * few]
    return (
        output,
        grad_hidden,
        piece(0),
        sum_qkv,
        sum_out,
        piece(1),
        sum_up,
        sum_vec[4 * few :],
        sum_down,
        piece(2),
        piece(3),
    )


def solution(mesh):
    split = ("leaf", "fsdp")
    in_specs = (
        P("fsdp", "leaf", None),
        P("fsdp", "leaf"),
        P("fsdp", None),
        P("fsdp", None),
        P(split),
        P(split, None),
        P(split, None),
        P(split),
        P(split, None),
        P(split),
        P(split, None),
        P(split),
        P(split),
        P("fsdp", None, "leaf", None),
    )
    out_specs = (
        P("fsdp", None, "leaf", None),
        P("fsdp", "leaf", None),
        P(split),
        P(split, None),
        P(split, None),
        P(split),
        P(split, None),
        P(split),
        P(split, None),
        P(split),
        P(split),
    )
    body = functools.partial(shards, mesh.shape["leaf"], mesh.shape["fsdp"])
    return jax.shard_map(body, mesh=mesh, in_specs=in_specs, out_specs=out_specs, check_vma=False)
```

```python
import functools
import math

import jax
import jax.numpy as jnp
from jax import lax
from jax.experimental import pallas as pl
from jax.experimental.pallas import tpu as pltpu
from jax.sharding import PartitionSpec as P

HEAD_DIM = 64
BLOCK = 16
NEG_FILL = -1000000000.0
EPSILON = 1e-05
VMEM_LIMIT = 56 * 1024 * 1024
BF = jnp.bfloat16
F32 = jnp.float32


class Links:
    def __init__(self):
        leaf = lax.axis_index("leaf")
        fsdp = lax.axis_index("fsdp")
        self.z, self.y = leaf // 2, leaf % 2
        self.x, self.core = fsdp // 2, fsdp % 2

    def swap_core(self, v):
        return lax.ppermute(v, "fsdp", [(i, i ^ 1) for i in range(4)])

    def swap_x(self, v):
        return lax.ppermute(v, "fsdp", [(i, i ^ 2) for i in range(4)])

    def swap_y(self, v, pairs=None):
        return lax.ppermute(v, "leaf", pairs or [(i, i ^ 1) for i in range(8)])

    def swap_z(self, v, n):
        return lax.ppermute(v, "leaf", [(i, i ^ (2 * n)) for i in range(8)])

    def up(self, v, first, last):
        return lax.ppermute(v, "leaf", [(i, i + 2) for i in range(2 * first, 2 * last + 2)])

    def down(self, v, first, last):
        return lax.ppermute(v, "leaf", [(i, i - 2) for i in range(2 * first, 2 * last + 2)])


def both(bit, own, other, axis):
    return jnp.where(
        bit == 0, jnp.stack([own, other], axis), jnp.stack([other, own], axis)
    )


def tie(*values):
    flat, tree = jax.tree.flatten(values)
    return jax.tree.unflatten(tree, lax.optimization_barrier(tuple(flat)))


def z_gather(at, block):
    return jnp.concatenate([block] + [at.swap_z(block, n) for n in (1, 2, 3)], axis=0)


def pick(v, index, axis):
    return lax.dynamic_index_in_dim(v, index, axis, keepdims=False)


def choose(bit, v, axis):
    return pick(v, bit, axis), pick(v, 1 - bit, axis)


def plus(a, b):
    return a.astype(F32) + b.astype(F32)


def joined(mine, got, index, axis):
    return plus(pick(mine, index, axis), pick(got, index, axis)).astype(BF)


def halve(bit, mine, got, axis):
    return joined(mine, got, bit, axis), joined(mine, got, 1 - bit, axis)


def z_parts(at, mine, got):
    return joined(mine, got, at.z, 0), [joined(mine, got, at.z ^ n, 0) for n in (1, 2, 3)]


def z_move(at, parts):
    return [at.swap_z(part, n) for n, part in zip((1, 2, 3), parts)]


def z_total(keep, got):
    return plus(keep, got[0]) + plus(got[1], got[2])


def to_column_half(at, half_a, half_b):
    keep = jnp.where(at.core == 0, half_a, half_b)
    send = jnp.where(at.core == 0, half_b, half_a)
    got = at.swap_core(send)
    return both(at.core, keep, got, 0).reshape(2 * keep.shape[0], keep.shape[1])


def from_column_half(at, g):
    g = g.reshape(2, g.shape[0] // 2, g.shape[1])
    keep, send = choose(at.core, g, 0)
    got = at.swap_core(send)
    return jnp.where(at.core == 0, keep, got), jnp.where(at.core == 0, got, keep)


def spec(shape, index_map):
    return pl.BlockSpec(shape, index_map)


def turn(values, cosine, sine):
    lane = lax.broadcasted_iota(jnp.int32, (values.shape[0], 128), 1)
    low_half = (lane % HEAD_DIM) < HEAD_DIM // 2
    groups = []
    for n in range(values.shape[1] // 128):
        part = values[:, n * 128 : (n + 1) * 128]
        swapped = jnp.where(low_half, pltpu.roll(part, 96, 1), pltpu.roll(part, 32, 1))
        groups.append(part * cosine + swapped * sine)
    return groups


def column(row):
    return jnp.broadcast_to(row, (8, row.shape[1])).T[:, :1]


def tables_kernel(places, rows, leaf_ref, seg_ref, parent_ref, qcol_ref, qrow_ref, kcol_ref, krow_ref, flag_ref, pad_ref):
    leaf = leaf_ref[0]
    blocks = rows // BLOCK
    slots = 16
    seg = column(seg_ref[...].astype(F32))
    lane = lax.broadcasted_iota(jnp.int32, (seg.shape[0], 128), 1).astype(F32)
    length = jnp.sum(jnp.where(seg == lane, 1.0, 0.0), axis=0, keepdims=True)
    start = jnp.sum(jnp.where(seg < lane, 1.0, 0.0), axis=0, keepdims=True)
    pad_ref[...] = jnp.zeros_like(pad_ref)
    pad_ref[0:1, 0 : parent_ref.shape[1]] = parent_ref[...].astype(F32)
    parent_row = pad_ref[0:1, :]
    lane = lax.broadcasted_iota(jnp.int32, (slots, 128), 1).astype(F32)
    slot = lax.broadcasted_iota(jnp.int32, (slots, 1), 0).astype(F32)
    parent = column(parent_row)[:slots]
    look = lambda index, row: jnp.sum(jnp.where(index == lane, row, 0.0), axis=1, keepdims=True)
    grand = look(parent, parent_row)
    start = look(slot, start)
    shift = jnp.where(slot > 0, look(parent, length), 0.0) + jnp.where(parent > 0, look(grand, length), 0.0) - start

    def facts(block):
        own = jnp.sum(jnp.where(block >= start, 1.0, 0.0), axis=0, keepdims=True) - 1.0
        take = lambda col: jnp.sum(jnp.where(slot == own, col, 0.0), axis=0, keepdims=True)
        return own, take(parent), take(grand), take(shift)

    token = lax.broadcasted_iota(jnp.int32, (1, rows), 1)
    zero = jnp.zeros((1, rows), F32)
    tiles = [(leaf, leaf >= 0), (leaf, leaf < 0)] + places(leaf)
    for t, (place, valid) in enumerate(tiles):
        first = jnp.maximum(place, 0) * blocks
        block = (first + lax.shift_right_logical(token, 4)).astype(F32)
        own, one, two, move = facts(block)
        position = (move + block) * BLOCK + (token & (BLOCK - 1)).astype(F32)
        at = slice(t * rows, (t + 1) * rows)
        if t < 2:
            limit = block + (1.0 if t == 0 else 0.0)
            lines = jnp.concatenate([own, one, two, limit, zero, zero, zero, zero], axis=0)
            qrow_ref[:, at] = lines
            qcol_ref[at, :] = lines.T
        lines = jnp.concatenate(
            [jnp.where(valid, own, -1.0), block, position, zero, zero, zero, zero, zero], axis=0
        )
        krow_ref[:, at] = lines
        kcol_ref[at, :] = lines.T
    queries = qcol_ref[pl.ds(0, 2 * blocks, stride=BLOCK), :]
    lane = lax.broadcasted_iota(jnp.int32, (1, 128), 1)
    for t, (place, valid) in enumerate(tiles):
        if t < 2:
            flag_ref[t] = 1
            continue
        block = (jnp.maximum(place, 0) * blocks + lane).astype(F32)
        own = facts(block)[0]
        allowed = (
            ((own == queries[:, 0:1]) | (own == queries[:, 1:2]) | (own == queries[:, 2:3]))
            & (block < queries[:, 3:4])
            & (lane < blocks)
            & valid
        )
        flag_ref[t] = jnp.max(jnp.where(allowed, 1.0, 0.0)).astype(jnp.int32)


def tables(places, leaf, seg, parent, rows):
    tiles = 2 + len(places(leaf))
    total = tiles * rows
    smem = pl.BlockSpec(memory_space=pltpu.SMEM)
    vmem = pl.BlockSpec(memory_space=pltpu.VMEM)
    shapes = [(2 * rows, 8), (8, 2 * rows), (total, 8), (8, total)]
    return pl.pallas_call(
        functools.partial(tables_kernel, places, rows),
        in_specs=[smem, vmem, vmem],
        out_specs=[vmem] * 4 + [smem],
        out_shape=[jax.ShapeDtypeStruct(shape, F32) for shape in shapes] + [jax.ShapeDtypeStruct((tiles,), jnp.int32)],
        name="tables",
        scratch_shapes=[pltpu.VMEM((8, 128), F32)],
    )(leaf.reshape(1), seg, parent)


def fetch(pieces, sems):
    copies = [pltpu.make_async_copy(src, dst, sems.at[n]) for n, (src, dst) in enumerate(pieces)]
    for copy in copies:
        copy.start()
    return copies


def placed(blocks, ref, size, table, row):
    pieces = []
    for hbm in blocks:
        for n in range(hbm.shape[0]):
            place = pl.multiple_of(table[row, len(pieces)] * size, size)
            pieces.append((hbm.at[n, pl.ds(0, size), :], ref.at[pl.ds(place, size), :]))
    return pieces


def tiled(sources, ref, rows):
    return [(src, ref.at[pl.ds(n * rows, rows), :]) for n, src in enumerate(sources)]


def project_kernel(
    blocks, sources, size, rows, table_ref, mask_ref, embed_ref, gain_ref, cos_ref, sin_ref, *refs,
):
    own_hbm, other_hbm, tiles = refs[:blocks], refs[blocks : 2 * blocks], refs[2 * blocks : 2 * blocks + sources]
    q_ref, k_ref, v_ref, x_ref, own_ref, other_ref, sems = refs[2 * blocks + sources :]
    tile = pl.program_id(0)
    step = k_ref.shape[0]

    @pl.when(tile == 0)
    def _():
        pieces = tiled([tiles[0]] + list(tiles), x_ref, rows)
        count = len(pieces)
        pieces += placed(own_hbm, own_ref, size, table_ref, 0) + placed(other_hbm, other_ref, size, table_ref, 0)
        copies = fetch(pieces, sems)
        for copy in copies[:count]:
            copy.wait()
        masked = column(mask_ref[...].astype(F32)) > 0
        x_ref[rows : 2 * rows, :] = jnp.where(masked, embed_ref[...], x_ref[rows : 2 * rows, :].astype(F32)).astype(BF)
        for copy in copies[count:]:
            copy.wait()

    x = x_ref[pl.ds(pl.multiple_of(tile * step, step), step), :].astype(F32)
    centred = x - jnp.mean(x, axis=-1, keepdims=True)
    spread = jnp.mean(centred * centred, axis=-1, keepdims=True)
    a = (centred * lax.rsqrt(spread + EPSILON) * gain_ref[...]).astype(BF)
    cosine, sine = cos_ref[...], sin_ref[...]
    half = own_ref.shape[1] // 3
    for n, w_ref in enumerate((own_ref, other_ref)):
        base = n * half
        keys = jnp.dot(a, w_ref[:, half : 2 * half], preferred_element_type=F32)
        for g, part in enumerate(turn(keys, cosine, sine)):
            k_ref[:, base + g * 128 : base + (g + 1) * 128] = part.astype(BF)
        values = jnp.dot(a, w_ref[:, 2 * half :], preferred_element_type=F32)
        v_ref[:, base : base + half] = values.astype(BF)

    @pl.when(tile * step < 2 * rows)
    def _():
        lines = q_ref.shape[0]
        for n, w_ref in enumerate((own_ref, other_ref)):
            base = n * half
            q = jnp.dot(a[:lines], w_ref[:, :half], preferred_element_type=F32)
            for g, part in enumerate(turn(q, cosine[:lines], sine[:lines])):
                q_ref[:, base + g * 128 : base + (g + 1) * 128] = part.astype(BF)


def project(table, tiles, mask, embed, gain, own, other, cosine, sine):
    rows, width = tiles[0].shape
    total = (len(tiles) + 1) * rows
    step = next(n for n in (3 * rows, 2 * rows, rows) if total % n == 0)
    q_step = min(step, 2 * rows)
    last_q = 2 * rows // q_step - 1
    count = sum(v.shape[0] for v in own)
    columns = own[0].shape[2]
    whole = lambda v: spec(v.shape, lambda t, i: (0, 0))
    moved = lambda n: spec((step, n), lambda t, i: (t, 0))
    out = lambda n: jax.ShapeDtypeStruct((n, width), BF)
    anywhere = pl.BlockSpec(memory_space=pl.ANY)
    far = list(own) + list(other) + list(tiles)
    return pl.pallas_call(
        functools.partial(project_kernel, len(own), len(tiles), width // count, rows),
        grid_spec=pltpu.PrefetchScalarGridSpec(
            num_scalar_prefetch=1,
            grid=(total // step,),
            in_specs=[whole(mask), whole(embed), whole(gain), moved(128), moved(128)] + [anywhere] * len(far),
            out_specs=[
                spec((q_step, width), lambda t, i: (jnp.minimum(t, last_q), 0)),
                moved(width),
                moved(width),
            ],
            scratch_shapes=[
                pltpu.VMEM((total, width), BF),
                pltpu.VMEM((width, columns), BF),
                pltpu.VMEM((width, columns), BF),
                pltpu.SemaphoreType.DMA((2 * count + len(tiles) + 1,)),
            ],
        ),
        out_shape=[out(2 * rows), out(total), out(total)],
        compiler_params=pltpu.CompilerParams(vmem_limit_bytes=VMEM_LIMIT),
        cost_estimate=pl.CostEstimate(
            flops=2 * total * width * 2 * width + 4 * rows * width * width,
            bytes_accessed=2 * (3 * total * width + 3 * width * width),
            transcendentals=0,
        ),
        name="project",
    )(table, mask, embed, gain, cosine, sine, *far)


def middle_kernel(
    blocks_one, blocks_two, size, chunk, table_ref, o_ref, x_ref, mask_ref, embed_ref, dy_ref, gain_ref, up_b_ref,
    down_b_ref, *refs,
):
    refs = list(refs)
    take = lambda n: [refs.pop(0) for _ in range(n)]
    ones, twos = (take(blocks_one), take(blocks_one)), (take(blocks_two), take(blocks_two))
    y_ref, b_ref, g_ref, du_ref, dh_low_ref, do_ref, dh_ref, dgain_ref, dup_b_ref, ddown_b_ref = take(10)
    out_ref, up_ref, down_ref, sems = refs
    cut = out_ref.shape[1] // 2
    units = up_ref.shape[2]
    pieces_out, pieces_up, pieces_down = [], [], []
    for n in range(2):
        columns = pl.ds(pl.multiple_of(table_ref[3, n] * cut, cut), cut)
        spots = [(hbm, j) for hbm in ones[n] for j in range(hbm.shape[0])]
        for place, (hbm, j) in enumerate(spots):
            to = pl.ds(pl.multiple_of(table_ref[1, place] * size, size), size)
            pieces_out.append((hbm.at[j, :, pl.ds(0, cut)], out_ref.at[to, columns]))
            to = pl.ds(pl.multiple_of(table_ref[0, place] * size, size), size)
            pieces_up.append((hbm.at[j, :, pl.ds(cut, units)], up_ref.at[n, to, :]))
        pieces_down += placed(twos[n], down_ref.at[n], chunk, table_ref, 2)
    copies = fetch(pieces_out + pieces_up + pieces_down, sems)
    for copy in copies[: len(pieces_out)]:
        copy.wait()
    x = x_ref[...].astype(F32)
    masked = column(mask_ref[...].astype(F32)) > 0
    x = jnp.concatenate([x, jnp.where(masked, embed_ref[...], x)], axis=0)
    h = x + jnp.dot(o_ref[...], out_ref[...], preferred_element_type=F32)
    centred = h - jnp.mean(h, axis=-1, keepdims=True)
    spread = jnp.mean(centred * centred, axis=-1, keepdims=True)
    scale = lax.rsqrt(spread + EPSILON)
    hat = centred * scale
    b = (hat * gain_ref[...]).astype(BF)
    b_ref[...] = b
    dy = dy_ref[...]
    ddown_b_ref[...] = jnp.sum(dy.astype(F32), axis=0, keepdims=True)
    for copy in copies[len(pieces_out) :]:
        copy.wait()
    y = h + down_b_ref[...]
    db = None
    wide = next(n for n in (768, 512, 384, 256, 128) if units % n == 0)
    for n in range(2):
        for c in range(0, units, wide):
            at = slice(c, c + wide)
            to = slice(n * units + c, n * units + c + wide)
            u = jnp.dot(b, up_ref[n, :, at], preferred_element_type=F32) + up_b_ref[n : n + 1, at]
            g, slope = gelu_parts(u)
            g = g.astype(BF)
            g_ref[:, to] = g
            y = y + jnp.dot(g, down_ref[n, at, :], preferred_element_type=F32)
            du = (matmul_t(dy, down_ref[n, at, :]) * slope).astype(BF)
            du_ref[:, to] = du
            dup_b_ref[n : n + 1, at] = jnp.sum(du.astype(F32), axis=0, keepdims=True)
            part = matmul_t(du, up_ref[n, :, at])
            db = part if db is None else db + part
    y_ref[...] = y.astype(BF)
    dgain_ref[...] = jnp.sum(db * hat, axis=0, keepdims=True)
    dh = dy.astype(F32) + norm_back(hat, scale, gain_ref[...], db)
    dh_ref[...] = dh
    low = dh.astype(BF)
    dh_low_ref[...] = low
    do_ref[...] = matmul_t(low, out_ref[...]).astype(BF)


def middle(table, o, x, mask, embed, dy, gain, up_b, down_b, one, two):
    rows, width = o.shape
    count = sum(v.shape[0] for v in one[0])
    size, columns = one[0][0].shape[1:]
    chunk = two[0][0].shape[1]
    units = columns - width // 2
    full = lambda shape: spec(shape, lambda t, i: (0, 0))
    near = (o, x, mask, embed, dy, gain, up_b, down_b)
    far = list(one[0]) + list(one[1]) + list(two[0]) + list(two[1])
    shapes = [
        ((rows, width), BF), ((rows, width), BF), ((rows, 2 * units), BF), ((rows, 2 * units), BF), ((rows, width), BF),
        ((rows, width), BF), ((rows, width), F32), ((1, width), F32), ((2, units), F32), ((1, width), F32),
    ]
    return pl.pallas_call(
        functools.partial(middle_kernel, len(one[0]), len(two[0]), size, chunk),
        grid_spec=pltpu.PrefetchScalarGridSpec(
            num_scalar_prefetch=1,
            grid=(1,),
            in_specs=[full(v.shape) for v in near] + [pl.BlockSpec(memory_space=pl.ANY)] * len(far),
            out_specs=[full(shape) for shape, _ in shapes],
            scratch_shapes=[
                pltpu.VMEM((width, width), BF),
                pltpu.VMEM((2, width, units), BF),
                pltpu.VMEM((2, units, width), BF),
                pltpu.SemaphoreType.DMA((6 * count,)),
            ],
        ),
        out_shape=[jax.ShapeDtypeStruct(shape, kind) for shape, kind in shapes],
        compiler_params=pltpu.CompilerParams(vmem_limit_bytes=VMEM_LIMIT),
        cost_estimate=pl.CostEstimate(
            flops=2 * rows * width * (2 * width + 8 * units),
            bytes_accessed=4 * (width * width + 4 * units * width),
            transcendentals=2 * rows * units,
        ),
        name="middle",
    )(table, *near, *far)


def matmul_t(a, b):
    return lax.dot_general(a, b, (((1,), (1,)), ((), ())), preferred_element_type=F32)


def attend_kernel(
    rows, tiles, flag_ref, qcol_ref, krow_ref, q_ref, k_ref, v_ref, o_ref, lse_ref,
    bias_ref, s_ref, top_ref, sum_ref, acc_ref,
):
    pair = pl.program_id(0)
    both_rows = 2 * rows

    def span(t):
        return slice(t * rows, (t + 1) * rows)

    def lines(t):
        return slice(rows, both_rows) if t == 1 else slice(0, both_rows)

    @pl.when(pair == 0)
    def _():
        lse_ref[...] = jnp.zeros_like(lse_ref)
        own = qcol_ref[:, 0:1]
        up_one = qcol_ref[:, 1:2]
        up_two = qcol_ref[:, 2:3]
        limit = qcol_ref[:, 3:4]
        for t in range(tiles):
            if t == 1:
                r = lax.broadcasted_iota(jnp.int32, (rows, rows), 0) // BLOCK
                c = lax.broadcasted_iota(jnp.int32, (rows, rows), 1) // BLOCK
                bias_ref[rows:, span(t)] = jnp.where(r == c, 0.0, NEG_FILL)
            else:
                seg = krow_ref[0:1, span(t)]
                index = krow_ref[1:2, span(t)]
                ok = ((seg == own) | (seg == up_one) | (seg == up_two)) & (index < limit)
                bias_ref[:, span(t)] = jnp.where(ok, 0.0, NEG_FILL)

    lane = lax.broadcasted_iota(jnp.int32, (both_rows, 128), 1)
    queries = [jnp.where((lane // HEAD_DIM) == h, q_ref[...] * 0.125, 0).astype(BF) for h in range(2)]
    top_ref[...] = jnp.full_like(top_ref, -3.0e38)
    for t in range(tiles):

        @pl.when(flag_ref[t] > 0)
        def _():
            at = lines(t)
            keys, bias = k_ref[span(t), :], bias_ref[at, span(t)]
            for h in range(2):
                s = matmul_t(queries[h][at], keys) + bias
                s_ref[h, at, span(t)] = s
                best = top_ref[h, at, :]
                for c in range(rows // 128):
                    best = jnp.maximum(best, s[:, c * 128 : (c + 1) * 128])
                top_ref[h, at, :] = best

    tops = [jnp.max(top_ref[h], axis=-1, keepdims=True) for h in range(2)]
    sum_ref[...] = jnp.zeros_like(sum_ref)
    acc_ref[...] = jnp.zeros_like(acc_ref)
    for t in range(tiles):

        @pl.when(flag_ref[t] > 0)
        def _():
            at = lines(t)
            values = v_ref[span(t), :]
            for h in range(2):
                p = jnp.exp(s_ref[h, at, span(t)] - tops[h][at])
                part = sum_ref[h, at, :]
                for c in range(rows // 128):
                    part = part + p[:, c * 128 : (c + 1) * 128]
                sum_ref[h, at, :] = part
                acc_ref[h, at, :] += jnp.dot(p.astype(BF), values, preferred_element_type=F32)

    outs, norms = [], lse_ref[...]
    for h in range(2):
        total = jnp.sum(sum_ref[h], axis=-1, keepdims=True)
        outs.append(acc_ref[h] / total)
        norms = jnp.where(lane == 2 * pair + h, tops[h] + jnp.log(total), norms)
    lse_ref[...] = norms
    o_ref[...] = jnp.where(lane < HEAD_DIM, outs[0], outs[1]).astype(BF)


def attend(flags, qcol, krow, q, k, v, rows):
    width = q.shape[1]
    total = k.shape[0]
    tiles = total // rows
    pair = lambda n: spec((n, 128), lambda p, f: (0, p))
    fixed = lambda shape: spec(shape, lambda p, f: (0, 0))
    return pl.pallas_call(
        functools.partial(attend_kernel, rows, tiles),
        grid_spec=pltpu.PrefetchScalarGridSpec(
            num_scalar_prefetch=1,
            grid=(width // 128,),
            in_specs=[fixed(qcol.shape), fixed(krow.shape), pair(2 * rows), pair(total), pair(total)],
            out_specs=[pair(2 * rows), fixed((2 * rows, 128))],
            scratch_shapes=[
                pltpu.VMEM((2 * rows, total), F32),
                pltpu.VMEM((2, 2 * rows, total), F32),
                pltpu.VMEM((2, 2 * rows, 128), F32),
                pltpu.VMEM((2, 2 * rows, 128), F32),
                pltpu.VMEM((2, 2 * rows, 128), F32),
            ],
        ),
        out_shape=[
            jax.ShapeDtypeStruct((2 * rows, width), BF),
            jax.ShapeDtypeStruct((2 * rows, 128), F32),
        ],
        compiler_params=pltpu.CompilerParams(vmem_limit_bytes=VMEM_LIMIT),
        cost_estimate=pl.CostEstimate(
            flops=16 * rows * total * width,
            bytes_accessed=4 * (total + rows) * width,
            transcendentals=2 * rows * total * width // HEAD_DIM,
        ),
        name="attend",
    )(flags, qcol, krow, q, k, v)


def attend_back_kernel(
    rows, first, last, flag_ref, qrow_ref, kcol_ref, q_ref, k_ref, v_ref, o_ref, g_ref, lse_ref, *refs,
):
    refs = list(refs)
    near = first == 0
    cos_ref, sin_ref = refs[:2]
    part_ref = refs[2] if near else None
    dq_ref, dk_ref, dv_ref, bias_ref, acc_ref = refs[-5:]
    pair = pl.program_id(0)
    both_rows = 2 * rows

    def span(t):
        return slice(t * rows, (t + 1) * rows)

    def lines(t):
        return slice(rows, both_rows) if t == 1 else slice(0, both_rows)

    @pl.when(pair == 0)
    def _():
        own = qrow_ref[0:1, :]
        up_one = qrow_ref[1:2, :]
        up_two = qrow_ref[2:3, :]
        limit = qrow_ref[3:4, :]
        for t in range(first, last):
            if t == 1:
                r = lax.broadcasted_iota(jnp.int32, (rows, rows), 0) // BLOCK
                c = lax.broadcasted_iota(jnp.int32, (rows, rows), 1) // BLOCK
                bias_ref[span(t - first), rows:] = jnp.where(r == c, 0.0, NEG_FILL)
            else:
                seg = kcol_ref[span(t), 0:1]
                index = kcol_ref[span(t), 1:2]
                ok = ((seg == own) | (seg == up_one) | (seg == up_two)) & (index < limit)
                bias_ref[span(t - first), :] = jnp.where(ok, 0.0, NEG_FILL)

    lane = lax.broadcasted_iota(jnp.int32, (both_rows, 128), 1)
    acc_ref[...] = part_ref[...] if near else jnp.zeros_like(acc_ref)
    queries, grads, deltas, norms = [], [], [], []
    product = (o_ref[...].astype(F32) * g_ref[...].astype(F32)).T
    for h in range(2):
        mine = (lane // HEAD_DIM) == h
        queries.append(jnp.where(mine, q_ref[...] * 0.125, 0).astype(BF))
        grads.append(jnp.where(mine, g_ref[...], 0).astype(BF))
        deltas.append(jnp.sum(product[h * HEAD_DIM : (h + 1) * HEAD_DIM], axis=0, keepdims=True))
        norms.append(lse_ref[pl.ds(2 * pair + h, 1), :])
    for t in range(first, last):
        to = span(t - first)

        @pl.when(flag_ref[t] == 0)
        def _():
            dk_ref[to, :] = jnp.zeros((rows, 128), BF)
            dv_ref[to, :] = jnp.zeros((rows, 128), BF)

        @pl.when(flag_ref[t] > 0)
        def _():
            at = lines(t)
            keys, values = k_ref[span(t), :], v_ref[span(t), :]
            keys_t = keys.astype(F32).T.astype(BF)
            dk = dv = None
            for h in range(2):
                q, g = queries[h][at], grads[h][at]
                s = matmul_t(keys, q) + bias_ref[to, at]
                p = jnp.exp(s - norms[h][:, at])
                dp = matmul_t(values, g)
                ds = (p * (dp - deltas[h][:, at])).astype(BF)
                part_v = jnp.dot(p.astype(BF), g, preferred_element_type=F32)
                part_k = jnp.dot(ds, q, preferred_element_type=F32)
                dv = part_v if dv is None else dv + part_v
                dk = part_k if dk is None else dk + part_k
                half = slice(h * HEAD_DIM, (h + 1) * HEAD_DIM)
                acc_ref[half, at] += jnp.dot(keys_t[half], ds, preferred_element_type=F32)
            [dk] = turn(dk, cos_ref[span(t), :], -sin_ref[span(t), :])
            dk_ref[to, :] = dk.astype(BF)
            dv_ref[to, :] = dv.astype(BF)

    if near:
        dq = acc_ref[...].T * 0.125
        [dq] = turn(dq, cos_ref[:both_rows, :], -sin_ref[:both_rows, :])
        dq_ref[...] = dq.astype(BF)
    else:
        dq_ref[...] = acc_ref[...]


def attend_back(first, last, flags, qrow, kcol, q, k, v, o, g, lse, cosine, sine, rows, part=None):
    width = q.shape[1]
    total = k.shape[0]
    there = (last - first) * rows
    near = first == 0
    pair = lambda n: spec((n, 128), lambda p, f: (0, p))
    turned = spec((128, 2 * rows), lambda p, f: (p, 0))
    fixed = lambda shape: spec(shape, lambda p, f: (0, 0))
    out = lambda n: jax.ShapeDtypeStruct((n, width), BF)
    return pl.pallas_call(
        functools.partial(attend_back_kernel, rows, first, last),
        grid_spec=pltpu.PrefetchScalarGridSpec(
            num_scalar_prefetch=1,
            grid=(width // 128,),
            in_specs=[
                fixed(qrow.shape), fixed(kcol.shape), pair(2 * rows), pair(total), pair(total),
                pair(2 * rows), pair(2 * rows), fixed(lse.shape), fixed(cosine.shape), fixed(sine.shape),
            ] + ([turned] if near else []),
            out_specs=[pair(2 * rows) if near else turned, pair(there), pair(there)],
            scratch_shapes=[
                pltpu.VMEM((there, 2 * rows), F32),
                pltpu.VMEM((128, 2 * rows), F32),
            ],
        ),
        out_shape=[out(2 * rows) if near else jax.ShapeDtypeStruct((width, 2 * rows), F32), out(there), out(there)],
        compiler_params=pltpu.CompilerParams(vmem_limit_bytes=VMEM_LIMIT),
        cost_estimate=pl.CostEstimate(
            flops=40 * rows * there * width,
            bytes_accessed=8 * (there + rows) * width,
            transcendentals=2 * rows * there * width // HEAD_DIM,
        ),
        name="attend_back_near" if near else "attend_back_far",
    )(flags, qrow, kcol, q, k, v, o, g, lse, cosine, sine, *([part] if near else []))


def t_matmul(a, b):
    return lax.dot_general(a, b, (((0,), (0,)), ((), ())), preferred_element_type=F32)


def fold_kernel(near, blocks, sources, size, rows, table_ref, mask_ref, embed_ref, gain_ref, dk_ref, dv_ref, *refs):
    refs = list(refs)
    take = lambda n: [refs.pop(0) for _ in range(n)]
    if near:
        dq_ref, dh_ref, part_ref = take(3)
    own_hbm, other_hbm, tiles = take(blocks), take(blocks), take(sources)
    if near:
        da_ref, dgain_ref, clean_ref, noisy_ref, dembed_ref = take(5)
        piece_refs = take(4)
    else:
        da_ref, dgain_ref, part_ref = take(3)
    acc_ref, x_ref, own_ref, other_ref, sems = refs[:5]
    dkv_ref, dwq_ref = refs[5:] if near else (part_ref, None)
    tile = pl.program_id(0)
    width = x_ref.shape[1]
    half = own_ref.shape[1] // 3
    cuts = [slice(n * half, (n + 1) * half) for n in range(3)]

    @pl.when(tile == 0)
    def _():
        pieces = tiled(([tiles[0]] if near else []) + tiles, x_ref, rows)
        count = len(pieces)
        pieces += placed(own_hbm, own_ref, size, table_ref, 0) + placed(other_hbm, other_ref, size, table_ref, 0)
        copies = fetch(pieces, sems)
        dgain_ref[...] = jnp.zeros_like(dgain_ref)
        if near:
            dkv_ref[...] = part_ref[...]
            dwq_ref[...] = jnp.zeros_like(dwq_ref)
        else:
            dkv_ref[...] = jnp.zeros_like(dkv_ref)
        for copy in copies[:count]:
            copy.wait()
        if near:
            masked = column(mask_ref[...].astype(F32)) > 0
            x_ref[rows : 2 * rows, :] = jnp.where(
                masked, embed_ref[...], x_ref[rows : 2 * rows, :].astype(F32)
            ).astype(BF)
        for copy in copies[count:]:
            copy.wait()

    x = x_ref[pl.ds(pl.multiple_of(tile * rows, rows), rows), :].astype(F32)
    centred = x - jnp.mean(x, axis=-1, keepdims=True)
    scale = lax.rsqrt(jnp.mean(centred * centred, axis=-1, keepdims=True) + EPSILON)
    hat = centred * scale
    a = (hat * gain_ref[...]).astype(BF)
    dk, dv = dk_ref[...], dv_ref[...]
    dkv_ref[:, :width] += t_matmul(a, dk)
    dkv_ref[:, width:] += t_matmul(a, dv)
    da = None
    for n, w_ref in enumerate((own_ref, other_ref)):
        part = matmul_t(dk[:, cuts[n]], w_ref[:, cuts[1]]) + matmul_t(dv[:, cuts[n]], w_ref[:, cuts[2]])
        da = part if da is None else da + part
    acc_ref[...] = da
    if near:

        @pl.when(tile < 2)
        def _():
            dq = dq_ref[...]
            acc_ref[...] += matmul_t(dq[:, cuts[0]], own_ref[:, cuts[0]]) + matmul_t(dq[:, cuts[1]], other_ref[:, cuts[0]])
            dwq_ref[...] += t_matmul(a, dq)

    da = acc_ref[...]
    da_ref[...] = da.astype(BF)
    dgain_ref[...] += jnp.sum(da * hat, axis=0, keepdims=True)
    if near:

        @pl.when(tile == 0)
        def _():
            clean_ref[...] = da

        @pl.when(tile == 1)
        def _():
            noisy = dh_ref[...] + norm_back(hat, scale, gain_ref[...], da)
            noisy_ref[...] = noisy
            masked = column(mask_ref[...].astype(F32)) > 0
            dembed_ref[...] = jnp.sum(jnp.where(masked, noisy, 0.0), axis=0, keepdims=True)

        @pl.when(tile == pl.num_programs(0) - 1)
        def _():
            third = half // 3
            for n in range(2):
                base = n * half
                first_ref, second_ref = piece_refs[2 * n], piece_refs[2 * n + 1]
                first_ref[:, :half] = dwq_ref[:, base : base + half].astype(BF)
                first_ref[:, half:] = dkv_ref[:, base : base + third].astype(BF)
                second_ref[:, : half - third] = dkv_ref[:, base + third : base + half].astype(BF)
                second_ref[:, half - third :] = dkv_ref[:, width + base : width + base + half].astype(BF)


def fold(table, tiles, dk, dv, mask, embed, gain, own, other, near=None):
    rows, width = tiles[0].shape
    there = dk.shape[0]
    count = sum(v.shape[0] for v in own)
    columns = own[0].shape[2]
    whole = lambda shape: spec(shape, lambda t, i: (0, 0))
    moved = spec((rows, width), lambda t, i: (t, 0))
    anywhere = pl.BlockSpec(memory_space=pl.ANY)
    line = ((1, width), F32)
    part = ((width, 2 * width), F32)
    pieces = [((width, columns * n // 9), BF) for n in (4, 5)] * 2
    fixed = [line] + ([((rows, width), F32)] * 2 + [line] + pieces if near else [part])
    extra = [spec((rows, width), lambda t, i: (jnp.minimum(t, 1), 0)), spec((rows, width), lambda t, i: (1, 0)), whole(part[0])]
    far = list(own) + list(other) + list(tiles)
    return pl.pallas_call(
        functools.partial(fold_kernel, near is not None, len(own), len(tiles), width // count, rows),
        grid_spec=pltpu.PrefetchScalarGridSpec(
            num_scalar_prefetch=1,
            grid=(there // rows,),
            in_specs=[whole(v.shape) for v in (mask, embed, gain)]
            + [moved, moved]
            + (extra if near else [])
            + [anywhere] * len(far),
            out_specs=[moved] + [whole(shape) for shape, _ in fixed],
            scratch_shapes=[
                pltpu.VMEM((rows, width), F32),
                pltpu.VMEM((there, width), BF),
                pltpu.VMEM((width, columns), BF),
                pltpu.VMEM((width, columns), BF),
                pltpu.SemaphoreType.DMA((2 * count + len(tiles) + 1,)),
            ]
            + ([pltpu.VMEM(part[0], F32), pltpu.VMEM((width, width), F32)] if near else []),
        ),
        out_shape=[jax.ShapeDtypeStruct((there, width), BF)] + [jax.ShapeDtypeStruct(shape, kind) for shape, kind in fixed],
        compiler_params=pltpu.CompilerParams(vmem_limit_bytes=VMEM_LIMIT),
        cost_estimate=pl.CostEstimate(
            flops=8 * there * width * width,
            bytes_accessed=2 * (4 * there * width + 9 * width * width),
            transcendentals=0,
        ),
        name="fold_near" if near else "fold_far",
    )(table, mask, embed, gain, dk, dv, *(near or ()), *far)


def normalise(values):
    centred = values - jnp.mean(values, axis=-1, keepdims=True)
    spread = jnp.mean(centred * centred, axis=-1, keepdims=True)
    scale = lax.rsqrt(spread + EPSILON)
    return centred * scale, scale


def norm_back(hat, scale, gain, grad):
    scaled = grad * gain
    return scale * (
        scaled
        - jnp.mean(scaled, axis=-1, keepdims=True)
        - hat * jnp.mean(scaled * hat, axis=-1, keepdims=True)
    )


ROOT = math.sqrt(2.0 / math.pi)


def gelu_parts(u):
    t = jnp.tanh(ROOT * (u + 0.044715 * (u * u * u)))
    slope = 0.5 * (1.0 + t) + 0.5 * u * (1.0 - t * t) * (ROOT * (1.0 + 3 * 0.044715 * (u * u)))
    return 0.5 * u * (1.0 + t), slope


def mm(a, b):
    return jnp.dot(a, b, preferred_element_type=F32)


def mm_t(a, b):
    return lax.dot_general(a, b, (((1,), (1,)), ((), ())), preferred_element_type=F32)


def t_mm(a, b):
    return lax.dot_general(a, b, (((0,), (0,)), ((), ())), preferred_element_type=F32)


def halves_of_heads(w):
    w = w.reshape(w.shape[0], 3, 2, -1)
    return w[:, :, 0].reshape(w.shape[0], -1), w[:, :, 1].reshape(w.shape[0], -1)


def heads_of_halves(a, b):
    a, b = a.reshape(a.shape[0], 3, -1), b.reshape(b.shape[0], 3, -1)
    return jnp.stack([a, b], 2).reshape(a.shape[0], -1)


def halves_of_units(w, chunk):
    w = w.reshape(w.shape[0], -1, 2, chunk)
    return w[:, :, 0].reshape(w.shape[0], -1), w[:, :, 1].reshape(w.shape[0], -1)


def units_of_halves(a, b, chunk):
    a, b = a.reshape(a.shape[0], -1, chunk), b.reshape(b.shape[0], -1, chunk)
    return jnp.stack([a, b], 2).reshape(a.shape[0], -1)


def lower_in_chain(leaf):
    z, y = lax.shift_right_logical(leaf, 1), leaf & 1
    below = [((2 * (z - s) + at), z >= s) for s in (1, 2, 3) for at in (y, 1 - y)]
    return below[:2] + [(2 * z, y == 1)] + below[2:]


class Chain:
    near = 5

    def __init__(self, rows):
        self.at = Links()
        self.rows = rows
        self.core = self.at.core

    def lower(self, leaf):
        return lower_in_chain(leaf)

    def places(self):
        at = self.at
        n = jnp.arange(4)
        zyx = ((at.z ^ n)[None, None, :] * 2 + (at.y ^ n[:2])[None, :, None]) * 2 + (at.x ^ n[:2])[:, None, None]
        yzx = ((at.z ^ n)[None, :, None] * 2 + (at.y ^ n[:2])[:, None, None]) * 2 + (at.x ^ n[:2])[None, None, :]
        first = zyx.reshape(16)
        columns = jnp.where(jnp.arange(16) % 2 == 0, at.core, 1 - at.core)
        return jnp.stack([first, first ^ (8 * at.core), yzx.reshape(16), columns]).astype(jnp.int32)

    def first_gather(self, hid, w_qkv, w_out, w_up, w_down, vectors, early):
        at = self.at
        few, chunk, cut = w_qkv.shape[0], w_down.shape[0], w_out.shape[1] // 2
        qkv_a, qkv_b = halves_of_heads(w_qkv)
        row = jnp.pad(vectors[None], ((0, 7), (0, qkv_a.shape[1] - vectors.shape[0])))
        qkv_a, qkv_b = (jnp.concatenate([v, row], axis=0) for v in (qkv_a, qkv_b))
        block = to_column_half(at, qkv_a, qkv_b)
        block = jnp.concatenate(
            [block[:few], block[few + 8 : 2 * few + 8], block[few : few + 8], block[2 * few + 8 :]], axis=0
        )[None]
        beside = at.swap_y(hid, [(i, i + 1) for i in range(0, 8, 2)])
        down_two = at.swap_x(w_down)
        up_a, up_b = halves_of_units(w_up, chunk)
        one_a = jnp.concatenate([w_out[:, :cut], up_a], axis=1)
        one_b = jnp.concatenate([w_out[:, cut:], up_b], axis=1)
        block, hid_up, one_a, one_b = tie(block, hid, one_a, one_b)
        line = z_gather(at, block)
        one = to_column_half(at, one_a, one_b)[None]
        line, hid_up, one, beside, down_two, early = tie(line, hid_up, one, beside, down_two, early)
        first_hop = at.up(hid_up, 0, 2)
        plane = jnp.concatenate([line, at.swap_y(line)], axis=0)
        one_line = [one, at.swap_z(one, 1)]
        down_two = jnp.stack([w_down, down_two])[None]
        first_hop, plane, one_line, down_two = tie(first_hop, plane, one_line, down_two)
        far = at.swap_x(plane)
        other = [at.swap_core(plane)]
        second_hop = at.up(first_hop, 1, 2)
        first_over = at.swap_y(first_hop, [(i, i ^ 1) for i in range(2, 8)])
        second_hop, first_over, other, one_line = tie(second_hop, first_over, other, one_line)
        third_hop = at.up(second_hop, 2, 2)
        second_over = at.swap_y(second_hop, [(i, i ^ 1) for i in range(4, 8)])
        one_line.append(at.swap_z(one_line[0], 2))
        third_hop, second_over, far, one_line = tie(third_hop, second_over, far, one_line)
        third_over = at.swap_y(third_hop, [(i, i ^ 1) for i in range(6, 8)])
        other.append(at.swap_core(far))
        one_line.append(at.swap_z(one_line[0], 3))
        m = 2 * few
        n = vectors.shape[0]
        vec = jnp.concatenate([v[:, at_row, :n] for at_row in (m, m + 8) for v in (plane, far)], axis=0)
        vec = jnp.concatenate([vec[:16], vec[16:]], axis=1)
        order = (self.places()[0][None, :] == jnp.arange(16)[:, None]).astype(BF)
        vec = mm(order, vec).reshape(32, -1)
        third_over, other, one_line, vec, down_two = tie(third_over, other, one_line, vec, down_two)
        line = jnp.concatenate(one_line, axis=0)
        lower = [first_hop, first_over, beside, second_hop, second_over, third_hop, third_over]
        return lower, ((plane, far), tuple(other)), vec, (line, down_two), early

    def second_start(self, state):
        line, down_two = state
        return jnp.concatenate([line, self.at.swap_y(line)], axis=0), z_gather(self.at, down_two)

    def second_go_on(self, state):
        plane, line = state
        at = self.at
        near = line.reshape((8,) + line.shape[2:])
        one = (plane, at.swap_x(plane)), [at.swap_core(plane)]
        down = (near, at.swap_y(near)), [at.swap_core(near)]
        return one, down

    def second_end(self, state):
        return [(own, tuple(other + [self.at.swap_core(own[1])])) for own, other in state]

    def unit_bias(self, bias, chunk):
        a, b = halves_of_units(bias[None], chunk)
        return jnp.where(self.core == 0, a, b), jnp.where(self.core == 0, b, a)

    def unit_bias_back(self, own, other, chunk):
        a = jnp.where(self.core == 0, own, other)
        b = jnp.where(self.core == 0, other, own)
        return units_of_halves(a, b, chunk)[0]

    def backward(self, run):
        at = self.at
        rows = self.rows
        lower_z = lambda s: [(i, i ^ 1) for i in range(2 * s, 8)]
        down_other, rest_other = run.feed_other(self)
        down_got, rest_got = at.swap_core(down_other), at.swap_core(rest_other)
        down_own, rest_own = run.feed_own(self)
        by_x = lambda g: g.reshape(8, 2, g.shape[0] // 16, g.shape[1])
        by_y = lambda g: g.reshape(4, 2, 2, g.shape[0] // 16, g.shape[1])
        split_y = lambda g: g.reshape((4, 2) + g.shape[1:])
        down_keep, down_send = halve(at.x, by_x(down_own), by_x(down_got), 1)
        rest_keep, rest_send = halve(at.y, by_y(rest_own), by_y(rest_got), 1)
        down_keep, down_send, rest_keep, rest_send, run.grad_mixed = tie(
            down_keep, down_send, rest_keep, rest_send, run.grad_mixed
        )
        down_got, rest_got = at.swap_x(down_send), at.swap_y(rest_send)
        far = run.far_tiles()
        down_got, rest_got, far = tie(down_got, rest_got, far)
        down_keep, down_send = halve(at.y, split_y(down_keep), split_y(down_got), 1)
        rest_keep, rest_send = z_parts(at, rest_keep, rest_got)
        down_keep, down_send, rest_keep, rest_send, far = tie(down_keep, down_send, rest_keep, rest_send, far)
        down_got = at.swap_y(down_send)
        far_da, far_gain, far_part = run.far_fold(far)
        tiles = [far_da[n * rows : (n + 1) * rows] for n in range(4)]
        over = jnp.concatenate([tiles[1], tiles[3]], axis=0)
        down_got, tiles, over, far = tie(down_got, tiles, over, far)
        over = at.swap_y(over, lower_z(2))
        rest_got = z_move(at, rest_send)
        near = run.near_tiles(far)
        rest_got, over, near, tiles, down_got = tie(rest_got, over, near, tiles, down_got)
        down_keep, down_send = z_parts(at, down_keep, down_got)
        rest = z_total(rest_keep, rest_got).astype(BF)
        rest_keep, rest_send = choose(at.x, rest, 0)
        cur = plus(tiles[2], over[rows:]).astype(BF)
        down_keep, down_send, rest_keep, rest_send, cur, near = tie(
            down_keep, down_send, rest_keep, rest_send, cur, near
        )
        cur = at.down(cur, 3, 3)
        down_got, rest_got = z_move(at, down_send), at.swap_x(rest_send)
        near_da, clean, vec, pieces = run.near_fold(near, far_gain, far_part)
        near_da, pieces, cur, down_got, rest_got = tie(near_da, pieces, cur, down_got, rest_got)
        cur = (plus(tiles[0], over[:rows]) + cur.astype(F32)).astype(BF)
        own, other = self.qkv_pieces(pieces, vec)
        across = near_da[3 * rows :]
        across, cur, own, other = tie(across, cur, own, other)
        first = at.swap_y(across[:rows], lower_z(1))
        beside = at.swap_y(across[rows:], [(i, i - 1) for i in range(1, 8, 2)])
        cur = at.down(cur, 2, 3)
        a_got, b_got = (at.swap_core(v) for v in other)
        sum_down = z_total(down_keep, down_got)
        rest = plus(rest_keep, rest_got)
        first, cur, beside, a_got, b_got = tie(first, cur, beside, a_got, b_got)
        a_keep, a_send = halve(at.x, own[0], a_got, 1)
        b_keep, b_send = halve(at.y, split_y(own[1]), split_y(b_got), 1)
        cur = (plus(near_da[2 * rows : 3 * rows], first) + cur.astype(F32)).astype(BF)
        a_keep, a_send, b_keep, b_send, cur, rest = tie(a_keep, a_send, b_keep, b_send, cur, rest)
        a_got, b_got, cur = at.swap_x(a_send), at.swap_y(b_send), at.down(cur, 1, 3)
        sum_out, sum_up = self.join_rest(rest, run.chunk, run.width)
        a_got, b_got, cur, sum_out, sum_up, sum_down = tie(a_got, b_got, cur, sum_out, sum_up, sum_down)
        a_keep, a_send = halve(at.y, split_y(a_keep), split_y(a_got), 1)
        b_keep, b_send = z_parts(at, b_keep, b_got)
        a_keep, a_send, b_keep, b_send = tie(a_keep, a_send, b_keep, b_send)
        a_got, b_got = at.swap_y(a_send), z_move(at, b_send)
        grad_hidden = run.last(clean + cur.astype(F32) + beside.astype(F32))
        a_got, b_got, grad_hidden = tie(a_got, b_got, grad_hidden)
        a_keep, a_send = z_parts(at, a_keep, a_got)
        b_keep, b_send = choose(at.x, z_total(b_keep, b_got).astype(BF), 0)
        a_keep, a_send, b_keep, b_send = tie(a_keep, a_send, b_keep, b_send)
        a_got, b_got = z_move(at, a_send), at.swap_x(b_send)
        a_got, b_got = tie(a_got, b_got)
        m = run.few * 2
        a, b = z_total(a_keep, a_got), plus(b_keep, b_got)
        sum_qkv = heads_of_halves(*from_column_half(at, jnp.concatenate([a[:m], b], axis=1)))
        return sum_down, sum_up, sum_out, sum_qkv, a[m, : run.vectors], grad_hidden

    def join_rest(self, g, chunk, width):
        a, b = from_column_half(self.at, g)
        cut = width // 2
        out = jnp.concatenate([a[:, :cut], b[:, :cut]], axis=1)
        return out, units_of_halves(a[:, cut:], b[:, cut:], chunk)

    def rest_pieces(self, out, up, other):
        half = out.shape[0] // 2
        core = 1 - self.core if other else self.core
        out = lax.dynamic_slice_in_dim(out, core * half, half, axis=1)
        out = jnp.where(self.core == 0, out, jnp.concatenate([out[half:], out[:half]], axis=0))
        return jnp.concatenate([out.astype(BF), up], axis=1)

    def qkv_pieces(self, pieces, vec):
        cut = [v.reshape(8, 2, v.shape[0] // 16, v.shape[1]) for v in pieces]
        n = vec.shape[1]
        vec = vec.astype(BF).reshape(8, 2, 2, n)
        found = []
        for h, core in enumerate((self.core, 1 - self.core)):
            rows = pick(vec, core, 2)[:, :, None]
            rows = jnp.pad(rows, ((0, 0), (0, 0), (0, 7), (0, cut[0].shape[3] - n)))
            found.append((jnp.concatenate([cut[2 * h], rows], axis=2), cut[2 * h + 1]))
        return found


AXES = ("leaf", "fsdp")


class Whole:
    def __init__(self, rows, leaves, devices):
        self.rows, self.leaves, self.devices = rows, leaves, devices
        self.leaf = lax.axis_index("leaf")
        self.near = 2 + (leaves - 1) // 2

    def lower(self, leaf):
        return [(leaf - s, leaf >= s) for s in range(1, self.leaves)]

    def places(self):
        return jnp.array([[0, 0], [0, 0], [0, 0], [0, 1]], jnp.int32)

    def first_gather(self, hid, w_qkv, w_out, w_up, w_down, vectors, early):
        tree = lax.all_gather(hid, "leaf", axis=0, tiled=False)
        lower = [pick(tree, jnp.maximum(leaf, 0), 0) for leaf, _ in self.lower(self.leaf)]
        every = lambda w: lax.all_gather(w, AXES, axis=0, tiled=True)
        qkv = tuple((v[None],) for v in halves_of_heads(every(w_qkv)))
        return lower, qkv, every(vectors[None]), (every(w_out), every(w_up), every(w_down)), early

    def second_start(self, state):
        return state

    def second_go_on(self, state):
        return state

    def second_end(self, state):
        out_w, up_w, down_w = state
        half, cut = down_w.shape[0] // 2, out_w.shape[1] // 2
        one = tuple(
            (jnp.concatenate([out_w[:, n * cut : (n + 1) * cut], up_w[:, n * half : (n + 1) * half]], axis=1)[None],)
            for n in range(2)
        )
        return one, tuple((down_w[None, n * half : (n + 1) * half],) for n in range(2))

    def unit_bias(self, bias, chunk):
        half = bias.shape[0] // 2
        return bias[None, :half], bias[None, half:]

    def unit_bias_back(self, own, other, chunk):
        return jnp.concatenate([own, other], axis=1)[0]

    def scatter(self, g):
        return lax.psum_scatter(g.astype(F32), AXES, scatter_dimension=0, tiled=True)

    def rest_pieces(self, out, up, other):
        cut = out.shape[1] // 2
        return jnp.concatenate([out[:, cut:] if other else out[:, :cut], up.astype(F32)], axis=1)

    def backward(self, run):
        rows = self.rows
        down_other, rest_other = run.feed_other(self)
        down_own, rest_own = run.feed_own(self)
        far = run.far_tiles()
        far_da, far_gain, far_part = run.far_fold(far)
        near = run.near_tiles(far)
        near_da, clean, vec, pieces = run.near_fold(near, far_gain, far_part)
        tiles = jnp.concatenate([near_da[:rows], near_da[2 * rows :], far_da], axis=0)
        tiles = tiles.reshape((self.leaves, rows) + tiles.shape[1:])
        order = [pick(tiles, (self.leaf - n) % self.leaves, 0) for n in range(self.leaves)]
        total = lax.psum_scatter(jnp.concatenate(order, axis=0), "leaf", scatter_dimension=0, tiled=True)
        cut = run.width // 2
        return (
            self.scatter(jnp.concatenate([down_own, down_other], axis=0)),
            self.scatter(jnp.concatenate([rest_own[:, cut:], rest_other[:, cut:]], axis=1)),
            self.scatter(jnp.concatenate([rest_own[:, :cut], rest_other[:, :cut]], axis=1)),
            self.scatter(heads_of_halves(*(jnp.concatenate(pieces[n : n + 2], axis=1) for n in (0, 2)))),
            self.scatter(vec)[0],
            run.last(total.astype(F32)),
        )


class Backward:
    pass


def shards(
    leaves,
    groups,
    hidden,
    noise_mask,
    seg_blocks,
    parents,
    ln1_gain,
    w_qkv,
    w_out,
    ln2_gain,
    w_up,
    up_bias,
    w_down,
    down_bias,
    mask_embed,
    cotangent,
):
    rows = hidden.shape[1]
    width = hidden.shape[2]
    half = width // 2
    devices = leaves * groups
    net = Chain(rows) if (leaves, groups) == (8, 4) else Whole(rows, leaves, devices)
    chunk = w_down.shape[0]
    few = ln1_gain.shape[0]
    leaf = lax.axis_index("leaf")

    hid = hidden[0]
    query_cols, query_rows, key_cols, key_rows, flags = tables(net.lower, leaf, seg_blocks, parents, rows)
    tiles = flags.shape[0]
    lanes = jnp.arange(128, dtype=jnp.int32)
    exponent = (lanes % (HEAD_DIM // 2)).astype(F32) * (-math.log(10000.0) / (HEAD_DIM // 2))
    angles = key_cols[:, 2:3] * jnp.exp(exponent)
    cosine = jnp.cos(angles)
    sine = jnp.sin(angles) * jnp.where((lanes % HEAD_DIM) < HEAD_DIM // 2, -1.0, 1.0)
    places = net.places()

    vectors = jnp.concatenate([ln1_gain, ln2_gain, down_bias, mask_embed, up_bias])
    lower, qkv_w, vec, coming, (cosine, sine) = net.first_gather(
        hid, w_qkv, w_out, w_up, w_down, vectors, (cosine, sine)
    )
    gain_one, gain_two, down_b, embed = (
        vec[:, n * few : (n + 1) * few].reshape(1, width).astype(F32) for n in range(4)
    )
    up_b = jnp.concatenate(net.unit_bias(vec[:, 4 * few :].reshape(-1).astype(F32), chunk), axis=0)
    coming = net.second_start(coming)
    query, key, value = project(
        places, [hid] + lower, noise_mask, embed, gain_one, qkv_w[0], qkv_w[1], cosine, sine
    )
    coming, query = tie(coming, query)
    coming = net.second_go_on(coming)
    mixed, log_norm = attend(flags, query_cols, key_rows, query, key, value, rows)
    coming, mixed = tie(coming, mixed)
    one_w, down_w = net.second_end(coming)
    norm_rows = log_norm.T
    grad_two = cotangent[0].reshape(2 * rows, width)
    (
        output, normed_two, act, grad_pre, grad_one, grad_mixed, grad_after, grad_gain_two, grad_up_b, grad_down_b,
    ) = middle(places, mixed, hid, noise_mask, embed, grad_two, gain_two, up_b, down_b, one_w, down_w)
    output = output.reshape(1, 2, rows, width)
    units = act.shape[1] // 2

    run = Backward()
    run.chunk, run.few, run.vectors, run.grad_mixed, run.width = chunk, few, vectors.shape[0], grad_mixed, width
    cut = net.near

    def feed(n, net):
        at = slice(n * units, (n + 1) * units)
        down, up = t_mm(act[:, at], grad_two).astype(BF), t_mm(normed_two, grad_pre[:, at]).astype(BF)
        return down, net.rest_pieces(t_mm(mixed, grad_one), up, n == 1)

    def far_tiles():
        return attend_back(
            cut, tiles, flags, query_rows, key_cols, query, key, value, mixed, run.grad_mixed, norm_rows, cosine, sine, rows
        )

    def far_fold(far):
        return fold(places, lower[cut - 2 :], far[1], far[2], noise_mask, embed, gain_one, qkv_w[0], qkv_w[1])

    def near_tiles(far):
        return attend_back(
            0, cut, flags, query_rows, key_cols, query, key, value, mixed, run.grad_mixed, norm_rows, cosine, sine, rows, far[0]
        )

    def near_fold(near, far_gain, far_part):
        da, gain, clean, run.noisy, grad_embed, *pieces = fold(
            places, [hid] + lower[: cut - 2], near[1], near[2], noise_mask, embed, gain_one, qkv_w[0], qkv_w[1],
            (near[0], grad_after, far_part),
        )
        parts = (gain + far_gain, grad_gain_two, grad_down_b, grad_embed, net.unit_bias_back(grad_up_b[:1], grad_up_b[1:], chunk))
        vec = jnp.concatenate([v.reshape(devices, -1) for v in parts], axis=1)
        return da, clean, vec, pieces

    def last(total):
        hat, scale = normalise(hid.astype(F32))
        masked = (noise_mask[0] == 1)[:, None]
        clean = grad_after[:rows] + norm_back(hat, scale, gain_one, total)
        return (clean + jnp.where(masked, 0.0, run.noisy)).astype(BF)[None]

    run.feed_own = lambda net: feed(0, net)
    run.feed_other = lambda net: feed(1, net)
    run.far_tiles, run.far_fold, run.near_tiles, run.near_fold, run.last = far_tiles, far_fold, near_tiles, near_fold, last
    sum_down, sum_up, sum_out, sum_qkv, sum_vec, grad_hidden = net.backward(run)
    piece = lambda n: sum_vec[n * few : (n + 1) * few]
    return (
        output,
        grad_hidden,
        piece(0),
        sum_qkv,
        sum_out,
        piece(1),
        sum_up,
        sum_vec[4 * few :],
        sum_down,
        piece(2),
        piece(3),
    )


def solution(mesh):
    split = ("leaf", "fsdp")
    in_specs = (
        P("fsdp", "leaf", None),
        P("fsdp", "leaf"),
        P("fsdp", None),
        P("fsdp", None),
        P(split),
        P(split, None),
        P(split, None),
        P(split),
        P(split, None),
        P(split),
        P(split, None),
        P(split),
        P(split),
        P("fsdp", None, "leaf", None),
    )
    out_specs = (
        P("fsdp", None, "leaf", None),
        P("fsdp", "leaf", None),
        P(split),
        P(split, None),
        P(split, None),
        P(split),
        P(split, None),
        P(split),
        P(split, None),
        P(split),
        P(split),
    )
    body = functools.partial(shards, mesh.shape["leaf"], mesh.shape["fsdp"])
    return jax.shard_map(body, mesh=mesh, in_specs=in_specs, out_specs=out_specs, check_vma=False)
```

```python
import functools
import math

import jax
import jax.numpy as jnp
from jax import lax
from jax.experimental import pallas as pl
from jax.experimental.pallas import tpu as pltpu
from jax.sharding import PartitionSpec as P

HEAD_DIM = 64
BLOCK = 16
NEG_FILL = -1000000000.0
EPSILON = 1e-05


def vmem(mebibytes):
    return pltpu.CompilerParams(vmem_limit_bytes=mebibytes * 2**20)


BF = jnp.bfloat16
F32 = jnp.float32


class Links:
    def __init__(self):
        leaf = lax.axis_index("leaf")
        fsdp = lax.axis_index("fsdp")
        self.z, self.y = leaf // 2, leaf % 2
        self.x, self.core = fsdp // 2, fsdp % 2

    def swap_core(self, v):
        return lax.ppermute(v, "fsdp", [(i, i ^ 1) for i in range(4)])

    def swap_x(self, v):
        return lax.ppermute(v, "fsdp", [(i, i ^ 2) for i in range(4)])

    def swap_y(self, v, pairs=None):
        return lax.ppermute(v, "leaf", pairs or [(i, i ^ 1) for i in range(8)])

    def swap_z(self, v, n):
        return lax.ppermute(v, "leaf", [(i, i ^ (2 * n)) for i in range(8)])

    def up(self, v, first, last):
        return lax.ppermute(v, "leaf", [(i, i + 2) for i in range(2 * first, 2 * last + 2)])

    def down(self, v, first, last):
        return lax.ppermute(v, "leaf", [(i, i - 2) for i in range(2 * first, 2 * last + 2)])


def both(bit, own, other, axis):
    return jnp.where(
        bit == 0, jnp.stack([own, other], axis), jnp.stack([other, own], axis)
    )


def tie(*values):
    flat, tree = jax.tree.flatten(values)
    return jax.tree.unflatten(tree, lax.optimization_barrier(tuple(flat)))


def z_gather(at, block):
    return jnp.concatenate([block] + [at.swap_z(block, n) for n in (1, 2, 3)], axis=0)


def pick(v, index, axis):
    return lax.dynamic_index_in_dim(v, index, axis, keepdims=False)


def choose(bit, v, axis):
    return pick(v, bit, axis), pick(v, 1 - bit, axis)


def plus(a, b):
    return a.astype(F32) + b.astype(F32)


def joined(mine, got, index, axis):
    return plus(pick(mine, index, axis), pick(got, index, axis)).astype(BF)


def halve(bit, mine, got, axis):
    return joined(mine, got, bit, axis), joined(mine, got, 1 - bit, axis)


def z_parts(at, mine, got):
    return joined(mine, got, at.z, 0), [joined(mine, got, at.z ^ n, 0) for n in (1, 2, 3)]


def z_move(at, parts):
    return [at.swap_z(part, n) for n, part in zip((1, 2, 3), parts)]


def z_total(keep, got):
    return plus(keep, got[0]) + plus(got[1], got[2])


def to_column_half(at, half_a, half_b):
    keep = jnp.where(at.core == 0, half_a, half_b)
    send = jnp.where(at.core == 0, half_b, half_a)
    got = at.swap_core(send)
    return both(at.core, keep, got, 0).reshape(2 * keep.shape[0], keep.shape[1])


def from_column_half(at, g):
    g = g.reshape(2, g.shape[0] // 2, g.shape[1])
    keep, send = choose(at.core, g, 0)
    got = at.swap_core(send)
    return jnp.where(at.core == 0, keep, got), jnp.where(at.core == 0, got, keep)


def spec(shape, index_map):
    return pl.BlockSpec(shape, index_map)


def turn(values, cosine, sine):
    lane = lax.broadcasted_iota(jnp.int32, (values.shape[0], 128), 1)
    low_half = (lane % HEAD_DIM) < HEAD_DIM // 2
    groups = []
    for n in range(values.shape[1] // 128):
        part = values[:, n * 128 : (n + 1) * 128]
        swapped = jnp.where(low_half, pltpu.roll(part, 96, 1), pltpu.roll(part, 32, 1))
        groups.append(part * cosine + swapped * sine)
    return groups


def column(row):
    return jnp.broadcast_to(row, (8, row.shape[1])).T[:, :1]


def tables_kernel(places, rows, leaf_ref, seg_ref, parent_ref, qcol_ref, qrow_ref, kcol_ref, krow_ref, flag_ref, pad_ref):
    leaf = leaf_ref[0]
    blocks = rows // BLOCK
    slots = 16
    seg = column(seg_ref[...].astype(F32))
    lane = lax.broadcasted_iota(jnp.int32, (seg.shape[0], 128), 1).astype(F32)
    length = jnp.sum(jnp.where(seg == lane, 1.0, 0.0), axis=0, keepdims=True)
    start = jnp.sum(jnp.where(seg < lane, 1.0, 0.0), axis=0, keepdims=True)
    pad_ref[...] = jnp.zeros_like(pad_ref)
    pad_ref[0:1, 0 : parent_ref.shape[1]] = parent_ref[...].astype(F32)
    parent_row = pad_ref[0:1, :]
    lane = lax.broadcasted_iota(jnp.int32, (slots, 128), 1).astype(F32)
    slot = lax.broadcasted_iota(jnp.int32, (slots, 1), 0).astype(F32)
    parent = column(parent_row)[:slots]
    look = lambda index, row: jnp.sum(jnp.where(index == lane, row, 0.0), axis=1, keepdims=True)
    grand = look(parent, parent_row)
    start = look(slot, start)
    shift = jnp.where(slot > 0, look(parent, length), 0.0) + jnp.where(parent > 0, look(grand, length), 0.0) - start

    def facts(block):
        own = jnp.sum(jnp.where(block >= start, 1.0, 0.0), axis=0, keepdims=True) - 1.0
        take = lambda col: jnp.sum(jnp.where(slot == own, col, 0.0), axis=0, keepdims=True)
        return own, take(parent), take(grand), take(shift)

    token = lax.broadcasted_iota(jnp.int32, (1, rows), 1)
    zero = jnp.zeros((1, rows), F32)
    tiles = [(leaf, leaf >= 0), (leaf, leaf < 0)] + places(leaf)
    for t, (place, valid) in enumerate(tiles):
        first = jnp.maximum(place, 0) * blocks
        block = (first + lax.shift_right_logical(token, 4)).astype(F32)
        own, one, two, move = facts(block)
        position = (move + block) * BLOCK + (token & (BLOCK - 1)).astype(F32)
        at = slice(t * rows, (t + 1) * rows)
        if t < 2:
            limit = block + (1.0 if t == 0 else 0.0)
            lines = jnp.concatenate([own, one, two, limit, zero, zero, zero, zero], axis=0)
            qrow_ref[:, at] = lines
            qcol_ref[at, :] = lines.T
        lines = jnp.concatenate(
            [jnp.where(valid, own, -1.0), block, position, zero, zero, zero, zero, zero], axis=0
        )
        krow_ref[:, at] = lines
        kcol_ref[at, :] = lines.T
    queries = qcol_ref[pl.ds(0, 2 * blocks, stride=BLOCK), :]
    lane = lax.broadcasted_iota(jnp.int32, (1, 128), 1)
    for t, (place, valid) in enumerate(tiles):
        if t < 2:
            flag_ref[t] = 1
            continue
        block = (jnp.maximum(place, 0) * blocks + lane).astype(F32)
        own = facts(block)[0]
        allowed = (
            ((own == queries[:, 0:1]) | (own == queries[:, 1:2]) | (own == queries[:, 2:3]))
            & (block < queries[:, 3:4])
            & (lane < blocks)
            & valid
        )
        flag_ref[t] = jnp.max(jnp.where(allowed, 1.0, 0.0)).astype(jnp.int32)


def tables(places, leaf, seg, parent, rows):
    tiles = 2 + len(places(leaf))
    total = tiles * rows
    smem = pl.BlockSpec(memory_space=pltpu.SMEM)
    vmem = pl.BlockSpec(memory_space=pltpu.VMEM)
    shapes = [(2 * rows, 8), (8, 2 * rows), (total, 8), (8, total)]
    return pl.pallas_call(
        functools.partial(tables_kernel, places, rows),
        in_specs=[smem, vmem, vmem],
        out_specs=[vmem] * 4 + [smem],
        out_shape=[jax.ShapeDtypeStruct(shape, F32) for shape in shapes] + [jax.ShapeDtypeStruct((tiles,), jnp.int32)],
        name="tables",
        scratch_shapes=[pltpu.VMEM((8, 128), F32)],
    )(leaf.reshape(1), seg, parent)


def fetch(pieces, sems):
    copies = [pltpu.make_async_copy(src, dst, sems.at[n]) for n, (src, dst) in enumerate(pieces)]
    for copy in copies:
        copy.start()
    return copies


def placed(blocks, ref, size, table, row):
    pieces = []
    for hbm in blocks:
        for n in range(hbm.shape[0]):
            place = pl.multiple_of(table[row, len(pieces)] * size, size)
            pieces.append((hbm.at[n, pl.ds(0, size), :], ref.at[pl.ds(place, size), :]))
    return pieces


def tiled(sources, ref, rows):
    return [(src, ref.at[pl.ds(n * rows, rows), :]) for n, src in enumerate(sources)]


def project_kernel(
    blocks, sources, size, rows, table_ref, mask_ref, embed_ref, gain_ref, cos_ref, sin_ref, *refs,
):
    own_hbm, other_hbm, tiles = refs[:blocks], refs[blocks : 2 * blocks], refs[2 * blocks : 2 * blocks + sources]
    q_ref, k_ref, v_ref, x_ref, own_ref, other_ref, sems = refs[2 * blocks + sources :]
    tile = pl.program_id(0)
    step = k_ref.shape[1]

    @pl.when(tile == 0)
    def _():
        pieces = tiled([tiles[0]] + list(tiles), x_ref, rows)
        count = len(pieces)
        pieces += placed(own_hbm, own_ref, size, table_ref, 0) + placed(other_hbm, other_ref, size, table_ref, 0)
        copies = fetch(pieces, sems)
        for copy in copies[:count]:
            copy.wait()
        masked = column(mask_ref[...].astype(F32)) > 0
        x_ref[rows : 2 * rows, :] = jnp.where(masked, embed_ref[...], x_ref[rows : 2 * rows, :].astype(F32)).astype(BF)
        for copy in copies[count:]:
            copy.wait()

    x = x_ref[pl.ds(pl.multiple_of(tile * step, step), step), :].astype(F32)
    centred = x - jnp.mean(x, axis=-1, keepdims=True)
    spread = jnp.mean(centred * centred, axis=-1, keepdims=True)
    a = (centred * lax.rsqrt(spread + EPSILON) * gain_ref[...]).astype(BF)
    cosine, sine = cos_ref[...], sin_ref[...]
    half = own_ref.shape[1] // 3
    for n, w_ref in enumerate((own_ref, other_ref)):
        base = n * half
        keys = jnp.dot(a, w_ref[:, half : 2 * half], preferred_element_type=F32)
        values = jnp.dot(a, w_ref[:, 2 * half :], preferred_element_type=F32)
        for g, part in enumerate(turn(keys, cosine, sine)):
            k_ref[base // 128 + g] = part.astype(BF)
            v_ref[base // 128 + g] = values[:, g * 128 : (g + 1) * 128].astype(BF)

    @pl.when(tile * step < 2 * rows)
    def _():
        lines = q_ref.shape[0]
        for n, w_ref in enumerate((own_ref, other_ref)):
            base = n * half
            q = jnp.dot(a[:lines], w_ref[:, :half], preferred_element_type=F32)
            for g, part in enumerate(turn(q, cosine[:lines], sine[:lines])):
                q_ref[:, base + g * 128 : base + (g + 1) * 128] = part.astype(BF)


def project(table, tiles, mask, embed, gain, own, other, cosine, sine):
    rows, width = tiles[0].shape
    total = (len(tiles) + 1) * rows
    step = next(n for n in (3 * rows, 2 * rows, rows) if total % n == 0)
    q_step = min(step, 2 * rows)
    last_q = 2 * rows // q_step - 1
    count = sum(v.shape[0] for v in own)
    columns = own[0].shape[2]
    whole = lambda v: spec(v.shape, lambda t, i: (0, 0))
    moved = lambda n: spec((step, n), lambda t, i: (t, 0))
    pairs = spec((width // 128, step, 128), lambda t, i: (0, t, 0))
    out = lambda n: jax.ShapeDtypeStruct((n, width), BF)
    anywhere = pl.BlockSpec(memory_space=pl.ANY)
    far = list(own) + list(other) + list(tiles)
    return pl.pallas_call(
        functools.partial(project_kernel, len(own), len(tiles), width // count, rows),
        grid_spec=pltpu.PrefetchScalarGridSpec(
            num_scalar_prefetch=1,
            grid=(total // step,),
            in_specs=[whole(mask), whole(embed), whole(gain), moved(128), moved(128)] + [anywhere] * len(far),
            out_specs=[
                spec((q_step, width), lambda t, i: (jnp.minimum(t, last_q), 0)),
                pairs,
                pairs,
            ],
            scratch_shapes=[
                pltpu.VMEM((total, width), BF),
                pltpu.VMEM((width, columns), BF),
                pltpu.VMEM((width, columns), BF),
                pltpu.SemaphoreType.DMA((2 * count + len(tiles) + 1,)),
            ],
        ),
        out_shape=[out(2 * rows)] + [jax.ShapeDtypeStruct((width // 128, total, 128), BF)] * 2,
        compiler_params=vmem(26 if total <= 10 * rows else 40),
        cost_estimate=pl.CostEstimate(
            flops=2 * total * width * 2 * width + 4 * rows * width * width,
            bytes_accessed=2 * (3 * total * width + 3 * width * width),
            transcendentals=0,
        ),
        name="project",
    )(table, mask, embed, gain, cosine, sine, *far)


def middle_kernel(
    blocks_one, blocks_two, size, chunk, table_ref, o_ref, x_ref, mask_ref, embed_ref, dy_ref, gain_ref, up_b_ref,
    down_b_ref, *refs,
):
    refs = list(refs)
    take = lambda n: [refs.pop(0) for _ in range(n)]
    ones, twos = (take(blocks_one), take(blocks_one)), (take(blocks_two), take(blocks_two))
    y_ref, b_ref, g_ref, du_ref, dh_low_ref, do_ref, dh_ref, dgain_ref, dup_b_ref, ddown_b_ref = take(10)
    out_ref, up_ref, down_ref, sems = refs
    cut = out_ref.shape[1] // 2
    units = up_ref.shape[2]
    pieces_out, pieces = [], []
    for n in range(2):
        columns = pl.ds(pl.multiple_of(table_ref[3, n] * cut, cut), cut)
        spots = [(hbm, j) for hbm in ones[n] for j in range(hbm.shape[0])]
        pieces.append([])
        for place, (hbm, j) in enumerate(spots):
            to = pl.ds(pl.multiple_of(table_ref[1, place] * size, size), size)
            pieces_out.append((hbm.at[j, :, pl.ds(0, cut)], out_ref.at[to, columns]))
            to = pl.ds(pl.multiple_of(table_ref[0, place] * size, size), size)
            pieces[n].append((hbm.at[j, :, pl.ds(cut, units)], up_ref.at[n, to, :]))
        pieces[n] += placed(twos[n], down_ref.at[n], chunk, table_ref, 2)
    copies = fetch(pieces_out + pieces[0] + pieces[1], sems)
    for copy in copies[: len(pieces_out)]:
        copy.wait()
    x = x_ref[...].astype(F32)
    masked = column(mask_ref[...].astype(F32)) > 0
    x = jnp.concatenate([x, jnp.where(masked, embed_ref[...], x)], axis=0)
    h = x + jnp.dot(o_ref[...], out_ref[...], preferred_element_type=F32)
    centred = h - jnp.mean(h, axis=-1, keepdims=True)
    spread = jnp.mean(centred * centred, axis=-1, keepdims=True)
    scale = lax.rsqrt(spread + EPSILON)
    hat = centred * scale
    b = (hat * gain_ref[...]).astype(BF)
    b_ref[...] = b
    dy = dy_ref[...]
    ddown_b_ref[...] = jnp.sum(dy.astype(F32), axis=0, keepdims=True)
    y = h + down_b_ref[...]
    db = None
    wide = next(n for n in (768, 512, 384, 256, 128) if units % n == 0)
    for n in range(2):
        done = len(pieces_out) + n * len(pieces[0])
        for copy in copies[done : done + len(pieces[n])]:
            copy.wait()
        for c in range(0, units, wide):
            at = slice(c, c + wide)
            to = slice(n * units + c, n * units + c + wide)
            u = jnp.dot(b, up_ref[n, :, at], preferred_element_type=F32) + up_b_ref[n : n + 1, at]
            g, slope = gelu_parts(u)
            g = g.astype(BF)
            g_ref[:, to] = g
            y = y + jnp.dot(g, down_ref[n, at, :], preferred_element_type=F32)
            du = (matmul_t(dy, down_ref[n, at, :]) * slope).astype(BF)
            du_ref[:, to] = du
            dup_b_ref[n : n + 1, at] = jnp.sum(du.astype(F32), axis=0, keepdims=True)
            part = matmul_t(du, up_ref[n, :, at])
            db = part if db is None else db + part
    y_ref[...] = y.astype(BF)
    dgain_ref[...] = jnp.sum(db * hat, axis=0, keepdims=True)
    dh = dy.astype(F32) + norm_back(hat, scale, gain_ref[...], db)
    dh_ref[...] = dh
    low = dh.astype(BF)
    dh_low_ref[...] = low
    do_ref[...] = matmul_t(low, out_ref[...]).astype(BF)


def middle(table, o, x, mask, embed, dy, gain, up_b, down_b, one, two):
    rows, width = o.shape
    count = sum(v.shape[0] for v in one[0])
    size, columns = one[0][0].shape[1:]
    chunk = two[0][0].shape[1]
    units = columns - width // 2
    full = lambda shape: spec(shape, lambda t, i: (0, 0))
    near = (o, x, mask, embed, dy, gain, up_b, down_b)
    far = list(one[0]) + list(one[1]) + list(two[0]) + list(two[1])
    shapes = [
        ((rows, width), BF), ((rows, width), BF), ((rows, 2 * units), BF), ((rows, 2 * units), BF), ((rows, width), BF),
        ((rows, width), BF), ((rows, width), F32), ((1, width), F32), ((2, units), F32), ((1, width), F32),
    ]
    return pl.pallas_call(
        functools.partial(middle_kernel, len(one[0]), len(two[0]), size, chunk),
        grid_spec=pltpu.PrefetchScalarGridSpec(
            num_scalar_prefetch=1,
            grid=(1,),
            in_specs=[full(v.shape) for v in near] + [pl.BlockSpec(memory_space=pl.ANY)] * len(far),
            out_specs=[full(shape) for shape, _ in shapes],
            scratch_shapes=[
                pltpu.VMEM((width, width), BF),
                pltpu.VMEM((2, width, units), BF),
                pltpu.VMEM((2, units, width), BF),
                pltpu.SemaphoreType.DMA((6 * count,)),
            ],
        ),
        out_shape=[jax.ShapeDtypeStruct(shape, kind) for shape, kind in shapes],
        compiler_params=vmem(44),
        cost_estimate=pl.CostEstimate(
            flops=2 * rows * width * (2 * width + 8 * units),
            bytes_accessed=4 * (width * width + 4 * units * width),
            transcendentals=2 * rows * units,
        ),
        name="middle",
    )(table, *near, *far)


def matmul_t(a, b):
    return lax.dot_general(a, b, (((1,), (1,)), ((), ())), preferred_element_type=F32)


def groups(tiles, first=2):
    found = [(first, first + 2)] if first == 2 else []
    found = [] if first > 2 else [(2, min(4, tiles))] + ([(4, 5)] if tiles > 4 else [])
    start = max(first, 5)
    return found + [(n, min(n + 2, tiles)) for n in range(start, tiles, 2)]


def attend_kernel(
    rows, tiles, flag_ref, qcol_ref, krow_ref, q_ref, k_ref, v_ref, o_ref, lse_ref,
    bias_ref, s_ref, top_ref, sum_ref, acc_ref,
):
    pair = pl.program_id(0)
    both_rows = 2 * rows

    def span(t):
        return slice(t * rows, (t + 1) * rows)

    def lines(t):
        return slice(rows, both_rows) if t == 1 else slice(0, both_rows)

    @pl.when(pair == 0)
    def _():
        lse_ref[...] = jnp.zeros_like(lse_ref)
        own = qcol_ref[:, 0:1]
        up_one = qcol_ref[:, 1:2]
        up_two = qcol_ref[:, 2:3]
        limit = qcol_ref[:, 3:4]
        for t in range(tiles):
            if t == 1:
                r = lax.broadcasted_iota(jnp.int32, (rows, rows), 0) // BLOCK
                c = lax.broadcasted_iota(jnp.int32, (rows, rows), 1) // BLOCK
                bias_ref[rows:, span(t)] = jnp.where(r == c, 0.0, NEG_FILL)
            else:
                seg = krow_ref[0:1, span(t)]
                index = krow_ref[1:2, span(t)]
                ok = ((seg == own) | (seg == up_one) | (seg == up_two)) & (index < limit)
                bias_ref[:, span(t)] = jnp.where(ok, 0.0, NEG_FILL)

    lane = lax.broadcasted_iota(jnp.int32, (both_rows, 128), 1)
    queries = [jnp.where((lane // HEAD_DIM) == h, q_ref[...] * 0.125, 0).astype(BF) for h in range(2)]
    top_ref[...] = jnp.full_like(top_ref, -3.0e38)

    def scores(first, last, at):
        cut = slice(first * rows, last * rows)
        keys = k_ref[0, cut, :]
        for h in range(2):
            s = matmul_t(queries[h][at], keys) + bias_ref[at, cut]
            s_ref[h, at, cut] = s
            best = top_ref[h, at, :]
            for c in range(s.shape[1] // 128):
                best = jnp.maximum(best, s[:, c * 128 : (c + 1) * 128])
            top_ref[h, at, :] = best

    def weigh(first, last, at):
        cut = slice(first * rows, last * rows)
        values = v_ref[0, cut, :]
        for h in range(2):
            p = jnp.exp(s_ref[h, at, cut] - tops[h][at])
            part = sum_ref[h, at, :]
            for c in range(p.shape[1] // 128):
                part = part + p[:, c * 128 : (c + 1) * 128]
            sum_ref[h, at, :] = part
            acc_ref[h, at, :] += jnp.dot(p.astype(BF), values, preferred_element_type=F32)

    upper, lower, all_rows = slice(0, rows), slice(rows, both_rows), slice(0, both_rows)

    def each(step):
        step(0, 1, upper)
        step(0, 2, lower)
        for first, last in groups(tiles):
            some = flag_ref[first]
            for t in range(first + 1, last):
                some = some + flag_ref[t]
            pl.when(some > 0)(functools.partial(step, first, last, all_rows))

    each(scores)
    tops = [jnp.max(top_ref[h], axis=-1, keepdims=True) for h in range(2)]
    sum_ref[...] = jnp.zeros_like(sum_ref)
    acc_ref[...] = jnp.zeros_like(acc_ref)
    each(weigh)
    outs, norms = [], lse_ref[...]
    for h in range(2):
        total = jnp.sum(sum_ref[h], axis=-1, keepdims=True)
        outs.append(acc_ref[h] / total)
        norms = jnp.where(lane == 2 * pair + h, tops[h] + jnp.log(total), norms)
    lse_ref[...] = norms
    o_ref[...] = jnp.where(lane < HEAD_DIM, outs[0], outs[1]).astype(BF)


def attend(flags, qcol, krow, q, k, v, rows):
    width = q.shape[1]
    total = k.shape[1]
    tiles = total // rows
    whole_pair = spec((1, total, 128), lambda p, f: (p, 0, 0))
    pair = lambda n: spec((n, 128), lambda p, f: (0, p))
    fixed = lambda shape: spec(shape, lambda p, f: (0, 0))
    return pl.pallas_call(
        functools.partial(attend_kernel, rows, tiles),
        grid_spec=pltpu.PrefetchScalarGridSpec(
            num_scalar_prefetch=1,
            grid=(width // 128,),
            in_specs=[fixed(qcol.shape), fixed(krow.shape), pair(2 * rows), whole_pair, whole_pair],
            out_specs=[pair(2 * rows), fixed((2 * rows, 128))],
            scratch_shapes=[
                pltpu.VMEM((2 * rows, total), F32),
                pltpu.VMEM((2, 2 * rows, total), F32),
                pltpu.VMEM((2, 2 * rows, 128), F32),
                pltpu.VMEM((2, 2 * rows, 128), F32),
                pltpu.VMEM((2, 2 * rows, 128), F32),
            ],
        ),
        out_shape=[
            jax.ShapeDtypeStruct((2 * rows, width), BF),
            jax.ShapeDtypeStruct((2 * rows, 128), F32),
        ],
        compiler_params=vmem(28 if tiles <= 10 else 52),
        cost_estimate=pl.CostEstimate(
            flops=16 * rows * total * width,
            bytes_accessed=4 * (total + rows) * width,
            transcendentals=2 * rows * total * width // HEAD_DIM,
        ),
        name="attend",
    )(flags, qcol, krow, q, k, v)


def attend_back_kernel(
    rows, first, last, flag_ref, qrow_ref, krow_ref, q_ref, k_ref, v_ref, o_ref, g_ref, lse_ref, *refs,
):
    refs = list(refs)
    near = first == 0
    cos_ref, sin_ref = refs[:2]
    part_ref = refs[2] if near else None
    dq_ref, dk_ref, dv_ref, bias_ref, acc_ref = refs[-5:]
    pair = pl.program_id(0)
    both_rows = 2 * rows

    def span(t):
        return slice(t * rows, (t + 1) * rows)

    @pl.when(pair == 0)
    def _():
        own = qrow_ref[0:1, :]
        up_one = qrow_ref[1:2, :]
        up_two = qrow_ref[2:3, :]
        limit = qrow_ref[3:4, :]
        for t in range(first, last):
            if t == 1:
                r = lax.broadcasted_iota(jnp.int32, (rows, both_rows), 0) // BLOCK
                c = lax.broadcasted_iota(jnp.int32, (rows, both_rows), 1) // BLOCK
                bias_ref[span(t - first), :] = jnp.where(r + rows // BLOCK == c, 0.0, NEG_FILL)
            else:
                facts = krow_ref[:, span(t - first)].T
                seg = facts[:, 0:1]
                index = facts[:, 1:2]
                ok = ((seg == own) | (seg == up_one) | (seg == up_two)) & (index < limit)
                bias_ref[span(t - first), :] = jnp.where(ok, 0.0, NEG_FILL)

    lane = lax.broadcasted_iota(jnp.int32, (both_rows, 128), 1)
    acc_ref[...] = part_ref[...] if near else jnp.zeros_like(acc_ref)
    queries, grads, deltas, norms, queries_t, grads_t = [], [], [], [], [], []
    product = (o_ref[...].astype(F32) * g_ref[...].astype(F32)).T
    for h in range(2):
        mine = (lane // HEAD_DIM) == h
        queries.append(jnp.where(mine, q_ref[...] * 0.125, 0).astype(BF))
        grads.append(jnp.where(mine, g_ref[...], 0).astype(BF))
        queries_t.append(queries[h].astype(F32).T.astype(BF))
        grads_t.append(grads[h].astype(F32).T.astype(BF))
        deltas.append(jnp.sum(product[h * HEAD_DIM : (h + 1) * HEAD_DIM], axis=0, keepdims=True))
        norms.append(lse_ref[pl.ds(2 * pair + h, 1), :])

    def step(start, end):
        to = slice((start - first) * rows, (end - first) * rows)
        keys, values = k_ref[0, to, :], v_ref[0, to, :]
        keys_t = keys.astype(F32).T.astype(BF)
        dk = dv = None
        for h in range(2):
            q, g = queries[h], grads[h]
            s = jnp.dot(keys, queries_t[h], preferred_element_type=F32) + bias_ref[to, :]
            p = jnp.exp(s - norms[h])
            dp = jnp.dot(values, grads_t[h], preferred_element_type=F32)
            ds = (p * (dp - deltas[h])).astype(BF)
            part_v = jnp.dot(p.astype(BF), g, preferred_element_type=F32)
            part_k = jnp.dot(ds, q, preferred_element_type=F32)
            dv = part_v if dv is None else dv + part_v
            dk = part_k if dk is None else dk + part_k
            half = slice(h * HEAD_DIM, (h + 1) * HEAD_DIM)
            acc_ref[half, :] += jnp.dot(keys_t[half], ds, preferred_element_type=F32)
        [dk] = turn(dk, cos_ref[to, :], -sin_ref[to, :])
        dk_ref[0, to, :] = dk.astype(BF)
        dv_ref[0, to, :] = dv.astype(BF)

    if near:
        step(0, 2)
    for start, end in groups(last, max(first, 2)):
        some = flag_ref[start]
        for t in range(start + 1, end):
            some = some + flag_ref[t]
        to = slice((start - first) * rows, (end - first) * rows)

        @pl.when(some == 0)
        def _():
            dk_ref[0, to, :] = jnp.zeros(((end - start) * rows, 128), BF)
            dv_ref[0, to, :] = jnp.zeros(((end - start) * rows, 128), BF)

        pl.when(some > 0)(functools.partial(step, start, end))

    if near:
        dq = acc_ref[...].T * 0.125
        [dq] = turn(dq, cos_ref[:both_rows, :], -sin_ref[:both_rows, :])
        dq_ref[...] = dq.astype(BF)
    else:
        dq_ref[...] = acc_ref[...]


def attend_back(first, last, flags, qrow, krow, q, k, v, o, g, lse, cosine, sine, rows, part=None):
    width = q.shape[1]
    there = (last - first) * rows
    near = first == 0
    some_pair = lambda n: spec((1, n, 128), lambda p, f: (p, 0, 0))
    taken_pair = spec((pl.Element(1), pl.Element(there), pl.Element(128)), lambda p, f: (p, first * rows, 0))
    taken = spec((pl.Element(there), pl.Element(128)), lambda p, f: (first * rows, 0))
    pair = lambda n: spec((n, 128), lambda p, f: (0, p))
    turned = spec((128, 2 * rows), lambda p, f: (p, 0))
    fixed = lambda shape: spec(shape, lambda p, f: (0, 0))
    out = lambda n: jax.ShapeDtypeStruct((n, width), BF)
    return pl.pallas_call(
        functools.partial(attend_back_kernel, rows, first, last),
        grid_spec=pltpu.PrefetchScalarGridSpec(
            num_scalar_prefetch=1,
            grid=(width // 128,),
            in_specs=[
                fixed(qrow.shape), spec((pl.Element(8), pl.Element(there)), lambda p, f: (0, first * rows)), pair(2 * rows),
                taken_pair, taken_pair, pair(2 * rows), pair(2 * rows), fixed(lse.shape), taken, taken,
            ] + ([turned] if near else []),
            out_specs=[pair(2 * rows) if near else turned, some_pair(there), some_pair(there)],
            scratch_shapes=[
                pltpu.VMEM((there, 2 * rows), F32),
                pltpu.VMEM((128, 2 * rows), F32),
            ],
        ),
        out_shape=[out(2 * rows) if near else jax.ShapeDtypeStruct((width, 2 * rows), F32)]
        + [jax.ShapeDtypeStruct((width // 128, there, 128), BF)] * 2,
        compiler_params=vmem(30 if there <= 5 * rows else 44),
        cost_estimate=pl.CostEstimate(
            flops=40 * rows * there * width,
            bytes_accessed=8 * (there + rows) * width,
            transcendentals=2 * rows * there * width // HEAD_DIM,
        ),
        name="attend_back_near" if near else "attend_back_far",
    )(flags, qrow, krow, q, k, v, o, g, lse, cosine, sine, *([part] if near else []))


def t_matmul(a, b):
    return lax.dot_general(a, b, (((0,), (0,)), ((), ())), preferred_element_type=F32)


def normed(x):
    centred = x - jnp.mean(x, axis=-1, keepdims=True)
    scale = lax.rsqrt(jnp.mean(centred * centred, axis=-1, keepdims=True) + EPSILON)
    return centred * scale, scale


def fold_kernel(near, blocks, sources, size, rows, table_ref, mask_ref, embed_ref, gain_ref, *refs):
    refs = list(refs)
    take = lambda n: [refs.pop(0) for _ in range(n)]
    if near:
        dq_ref, dh_ref = take(2)
    own_hbm, other_hbm, tiles = take(blocks), take(blocks), take(sources)
    hbm = take(4 if near else 2)
    if near:
        da_ref, dgain_ref, clean_ref, noisy_ref, dembed_ref = take(5)
        piece_refs = take(4)
    else:
        da_ref, dgain_ref = take(2)
    x_ref, own_ref, other_ref = take(3)
    grads = take(len(hbm))
    a_ref = refs.pop(0) if near else None
    [sems] = refs
    there, width = da_ref.shape
    half = own_ref.shape[1] // 3
    pairs = half // 128
    cuts = [slice(n * half, (n + 1) * half) for n in range(3)]
    first = tiled(([tiles[0]] if near else []) + tiles, x_ref, rows)
    second = list(zip(hbm, grads))
    third = placed(own_hbm, own_ref, size, table_ref, 0) + placed(other_hbm, other_ref, size, table_ref, 0)
    copies = fetch(first + second + third, sems)
    for copy in copies[: len(first)]:
        copy.wait()
    if near:
        masked = column(mask_ref[...].astype(F32)) > 0
        noisy_rows = slice(rows, 2 * rows)
        x_ref[noisy_rows, :] = jnp.where(masked, embed_ref[...], x_ref[noisy_rows, :].astype(F32)).astype(BF)
        for t in range(x_ref.shape[0] // rows):
            at = slice(t * rows, (t + 1) * rows)
            a_ref[at, :] = (normed(x_ref[at, :].astype(F32))[0] * gain_ref[...]).astype(BF)
    for copy in copies[len(first) :]:
        copy.wait()

    def side(ref, n, at):
        return jnp.concatenate([ref[n * pairs + p, at, :] for p in range(pairs)], axis=1)

    dgain = jnp.zeros((1, width), F32)
    for t in range(there // rows):
        at = slice(t * rows, (t + 1) * rows)
        da = None
        for n, w_ref in enumerate((own_ref, other_ref)):
            part = matmul_t(side(grads[0], n, at), w_ref[:, cuts[1]]) + matmul_t(side(grads[1], n, at), w_ref[:, cuts[2]])
            if near and t < 2:
                part = part + matmul_t(dq_ref[at, cuts[n]], w_ref[:, cuts[0]])
            da = part if da is None else da + part
        da_ref[at, :] = da.astype(BF)
        hat, scale = normed(x_ref[at, :].astype(F32))
        dgain = dgain + jnp.sum(da * hat, axis=0, keepdims=True)
        if near and t == 0:
            clean_ref[...] = da
        if near and t == 1:
            noisy = dh_ref[...] + norm_back(hat, scale, gain_ref[...], da)
            noisy_ref[...] = noisy
            dembed_ref[...] = jnp.sum(jnp.where(masked, noisy, 0.0), axis=0, keepdims=True)
    dgain_ref[...] = dgain
    if near:
        both_rows = slice(0, 2 * rows)
        near_rows, far_rows = slice(0, there), slice(there, x_ref.shape[0])
        lines = slice(0, there)
        far_lines = slice(0, x_ref.shape[0] - there)
        third = half // 3
        for n in range(2):
            first_ref, second_ref = piece_refs[2 * n], piece_refs[2 * n + 1]
            first_ref[:, :half] = t_matmul(a_ref[both_rows, :], dq_ref[:, cuts[n]]).astype(BF)
            keys, values = (
                (
                    t_matmul(a_ref[near_rows, :], side(grads[m], n, lines))
                    + t_matmul(a_ref[far_rows, :], side(grads[m + 2], n, far_lines))
                ).astype(BF)
                for m in range(2)
            )
            first_ref[:, half:] = keys[:, :third]
            second_ref[:, : half - third] = keys[:, third:]
            second_ref[:, half - third :] = values


def fold(table, tiles, dk, dv, mask, embed, gain, own, other, near=None):
    rows, width = tiles[0].shape
    there = dk.shape[1]
    total = (len(tiles) + 1) * rows if near else there
    count = sum(v.shape[0] for v in own)
    columns = own[0].shape[2]
    whole = lambda shape: spec(shape, lambda t, i: (0,) * len(shape))
    anywhere = pl.BlockSpec(memory_space=pl.ANY)
    line = ((1, width), F32)
    pieces = [((width, columns * n // 9), BF) for n in (4, 5)] * 2
    outs = [((there, width), BF), line] + ([((rows, width), F32)] * 2 + [line] + pieces if near else [])
    grads = [dk, dv] + list(near[2:] if near else ())
    far = list(own) + list(other) + list(tiles) + grads
    extra = [whole(near[0].shape), spec((rows, width), lambda t, i: (1, 0))] if near else []
    return pl.pallas_call(
        functools.partial(fold_kernel, near is not None, len(own), len(tiles), width // count, rows),
        grid_spec=pltpu.PrefetchScalarGridSpec(
            num_scalar_prefetch=1,
            grid=(1,),
            in_specs=[whole(v.shape) for v in (mask, embed, gain)] + extra + [anywhere] * len(far),
            out_specs=[whole(shape) for shape, _ in outs],
            scratch_shapes=[
                pltpu.VMEM((total, width), BF),
                pltpu.VMEM((width, columns), BF),
                pltpu.VMEM((width, columns), BF),
            ]
            + [pltpu.VMEM(v.shape, BF) for v in grads]
            + ([pltpu.VMEM((total, width), BF)] if near else [])
            + [pltpu.SemaphoreType.DMA((2 * count + len(tiles) + len(grads) + 1,))],
        ),
        out_shape=[jax.ShapeDtypeStruct(shape, kind) for shape, kind in outs],
        compiler_params=vmem(44 if total <= 10 * rows else 58),
        cost_estimate=pl.CostEstimate(
            flops=8 * there * width * width,
            bytes_accessed=2 * (4 * there * width + 9 * width * width),
            transcendentals=0,
        ),
        name="fold_near" if near else "fold_far",
    )(table, mask, embed, gain, *(near[:2] if near else ()), *far)


def normalise(values):
    centred = values - jnp.mean(values, axis=-1, keepdims=True)
    spread = jnp.mean(centred * centred, axis=-1, keepdims=True)
    scale = lax.rsqrt(spread + EPSILON)
    return centred * scale, scale


def norm_back(hat, scale, gain, grad):
    scaled = grad * gain
    return scale * (
        scaled
        - jnp.mean(scaled, axis=-1, keepdims=True)
        - hat * jnp.mean(scaled * hat, axis=-1, keepdims=True)
    )


ROOT = math.sqrt(2.0 / math.pi)


def gelu_parts(u):
    t = jnp.tanh(ROOT * (u + 0.044715 * (u * u * u)))
    slope = 0.5 * (1.0 + t) + 0.5 * u * (1.0 - t * t) * (ROOT * (1.0 + 3 * 0.044715 * (u * u)))
    return 0.5 * u * (1.0 + t), slope


def mm(a, b):
    return jnp.dot(a, b, preferred_element_type=F32)


def mm_t(a, b):
    return lax.dot_general(a, b, (((1,), (1,)), ((), ())), preferred_element_type=F32)


def t_mm(a, b):
    return lax.dot_general(a, b, (((0,), (0,)), ((), ())), preferred_element_type=F32)


def halves_of_heads(w):
    w = w.reshape(w.shape[0], 3, 2, -1)
    return w[:, :, 0].reshape(w.shape[0], -1), w[:, :, 1].reshape(w.shape[0], -1)


def heads_of_halves(a, b):
    a, b = a.reshape(a.shape[0], 3, -1), b.reshape(b.shape[0], 3, -1)
    return jnp.stack([a, b], 2).reshape(a.shape[0], -1)


def halves_of_units(w, chunk):
    w = w.reshape(w.shape[0], -1, 2, chunk)
    return w[:, :, 0].reshape(w.shape[0], -1), w[:, :, 1].reshape(w.shape[0], -1)


def units_of_halves(a, b, chunk):
    a, b = a.reshape(a.shape[0], -1, chunk), b.reshape(b.shape[0], -1, chunk)
    return jnp.stack([a, b], 2).reshape(a.shape[0], -1)


def lower_in_chain(leaf):
    z, y = lax.shift_right_logical(leaf, 1), leaf & 1
    below = [((2 * (z - s) + at), z >= s) for s in (1, 2, 3) for at in (y, 1 - y)]
    return below[:2] + [(2 * z, y == 1)] + below[2:]


class Chain:
    near = 5

    def __init__(self, rows):
        self.at = Links()
        self.rows = rows
        self.core = self.at.core

    def lower(self, leaf):
        return lower_in_chain(leaf)

    def places(self):
        at = self.at
        n = jnp.arange(4)
        zyx = ((at.z ^ n)[None, None, :] * 2 + (at.y ^ n[:2])[None, :, None]) * 2 + (at.x ^ n[:2])[:, None, None]
        yzx = ((at.z ^ n)[None, :, None] * 2 + (at.y ^ n[:2])[:, None, None]) * 2 + (at.x ^ n[:2])[None, None, :]
        first = zyx.reshape(16)
        columns = jnp.where(jnp.arange(16) % 2 == 0, at.core, 1 - at.core)
        return jnp.stack([first, first ^ (8 * at.core), yzx.reshape(16), columns]).astype(jnp.int32)

    def first_gather(self, hid, w_qkv, w_out, w_up, w_down, vectors, facts, early):
        at = self.at
        few, chunk, cut = w_qkv.shape[0], w_down.shape[0], w_out.shape[1] // 2
        qkv_a, qkv_b = halves_of_heads(w_qkv)
        row = jnp.pad(vectors, ((0, 7), (0, qkv_a.shape[1] - vectors.shape[1])))
        qkv_a, qkv_b = (jnp.concatenate([v, row], axis=0) for v in (qkv_a, qkv_b))
        block = to_column_half(at, qkv_a, qkv_b)
        spare = jnp.zeros((6, block.shape[1]), BF)
        block = jnp.concatenate(
            [block[:few], block[few + 8 : 2 * few + 8], block[few : few + 1], block[2 * few + 8 : 2 * few + 9], spare],
            axis=0,
        )[None]
        up_a, up_b = halves_of_units(w_up, chunk)
        one_a = jnp.concatenate([w_out[:, :cut], up_a], axis=1)
        one_b = jnp.concatenate([w_out[:, cut:], up_b], axis=1)
        block, hid_up, one_a, one_b = tie(block, hid, one_a, one_b)
        line = z_gather(at, block)
        beside = at.swap_y(hid_up, [(i, i + 1) for i in range(0, 8, 2)])
        one = to_column_half(at, one_a, one_b)[None]
        line, hid_up, one, beside, down_two, facts = tie(line, hid_up, one, beside, w_down, facts)
        first_hop = at.up(hid_up, 0, 2)
        plane = jnp.concatenate([line, at.swap_y(line)], axis=0)
        one_line = [one, at.swap_z(one, 1)]
        down_two = at.swap_x(down_two)
        turns = early(facts)
        first_hop, plane, one_line, down_two, turns = tie(first_hop, plane, one_line, down_two, turns)
        down_two = jnp.stack([w_down, down_two])[None]
        far = at.swap_x(plane)
        other = [at.swap_core(plane)]
        second_hop = at.up(first_hop, 1, 2)
        first_over = at.swap_y(first_hop, [(i, i ^ 1) for i in range(2, 8)])
        second_hop, first_over, other, one_line = tie(second_hop, first_over, other, one_line)
        third_hop = at.up(second_hop, 2, 2)
        second_over = at.swap_y(second_hop, [(i, i ^ 1) for i in range(4, 8)])
        one_line.append(at.swap_z(one_line[0], 2))
        third_hop, second_over, far, one_line = tie(third_hop, second_over, far, one_line)
        third_over = at.swap_y(third_hop, [(i, i ^ 1) for i in range(6, 8)])
        other.append(at.swap_core(far))
        one_line.append(at.swap_z(one_line[0], 3))
        m = 2 * few
        n = vectors.shape[1]
        vec = jnp.concatenate([plane[:, m : m + 2, :n], far[:, m : m + 2, :n]], axis=0).reshape(16, 2 * n)
        order = (self.places()[0][None, :] == jnp.arange(16)[:, None]).astype(BF)
        vec = mm(order, vec).reshape(32, -1)
        third_over, other, one_line, vec, down_two = tie(third_over, other, one_line, vec, down_two)
        line = jnp.concatenate(one_line, axis=0)
        lower = [first_hop, first_over, beside, second_hop, second_over, third_hop, third_over]
        return lower, ((plane, far), tuple(other)), vec, (line, down_two), turns

    def second_start(self, state):
        line, down_two = state
        return jnp.concatenate([line, self.at.swap_y(line)], axis=0), z_gather(self.at, down_two)

    def second_go_on(self, state):
        plane, line = state
        at = self.at
        near = line.reshape((8,) + line.shape[2:])
        one = (plane, at.swap_x(plane)), [at.swap_core(plane)]
        down = (near, at.swap_y(near)), [at.swap_core(near)]
        return one, down

    def second_end(self, state):
        return [(own, tuple(other + [self.at.swap_core(own[1])])) for own, other in state]

    def unit_bias(self, bias, chunk):
        a, b = halves_of_units(bias[None], chunk)
        return jnp.where(self.core == 0, a, b), jnp.where(self.core == 0, b, a)

    def unit_bias_back(self, own, other, chunk):
        a = jnp.where(self.core == 0, own, other)
        b = jnp.where(self.core == 0, other, own)
        return units_of_halves(a, b, chunk)[0]

    def backward(self, run):
        at = self.at
        rows = self.rows
        lower_z = lambda s: [(i, i ^ 1) for i in range(2 * s, 8)]
        down_other, rest_other = run.feed_other(self)
        down_got, rest_got = at.swap_core(down_other), at.swap_core(rest_other)
        down_own, rest_own = run.feed_own(self)
        by_x = lambda g: g.reshape(8, 2, g.shape[0] // 16, g.shape[1])
        by_y = lambda g: g.reshape(4, 2, 2, g.shape[0] // 16, g.shape[1])
        split_y = lambda g: g.reshape((4, 2) + g.shape[1:])
        down_keep, down_send = halve(at.x, by_x(down_own), by_x(down_got), 1)
        rest_keep, rest_send = halve(at.y, by_y(rest_own), by_y(rest_got), 1)
        down_keep, down_send, rest_keep, rest_send, run.grad_mixed = tie(
            down_keep, down_send, rest_keep, rest_send, run.grad_mixed
        )
        down_got, rest_got = at.swap_x(down_send), at.swap_y(rest_send)
        far = run.far_tiles()
        down_got, rest_got, far = tie(down_got, rest_got, far)
        down_keep, down_send = halve(at.y, split_y(down_keep), split_y(down_got), 1)
        rest_keep, rest_send = z_parts(at, rest_keep, rest_got)
        down_keep, down_send, rest_keep, rest_send, far = tie(down_keep, down_send, rest_keep, rest_send, far)
        down_got = at.swap_y(down_send)
        far_da, far_gain = run.far_fold(far)
        tiles = [far_da[n * rows : (n + 1) * rows] for n in range(4)]
        over = jnp.concatenate([tiles[1], tiles[3]], axis=0)
        down_got, tiles, over, far = tie(down_got, tiles, over, far)
        over = at.swap_y(over, lower_z(2))
        rest_got = z_move(at, rest_send)
        near = run.near_tiles(far)
        rest_got, over, near, tiles, down_got = tie(rest_got, over, near, tiles, down_got)
        down_keep, down_send = z_parts(at, down_keep, down_got)
        rest = z_total(rest_keep, rest_got).astype(BF)
        rest_keep, rest_send = choose(at.x, rest, 0)
        cur = plus(tiles[2], over[rows:]).astype(BF)
        down_keep, down_send, rest_keep, rest_send, cur, near = tie(
            down_keep, down_send, rest_keep, rest_send, cur, near
        )
        cur = at.down(cur, 3, 3)
        down_got, rest_got = z_move(at, down_send), at.swap_x(rest_send)
        near_da, clean, vec, pieces = run.near_fold(near, far_gain, far)
        near_da, pieces, cur, down_got, rest_got = tie(near_da, pieces, cur, down_got, rest_got)
        cur = (plus(tiles[0], over[:rows]) + cur.astype(F32)).astype(BF)
        own, other = self.qkv_pieces(pieces, vec)
        across = near_da[3 * rows :]
        across, cur, own, other = tie(across, cur, own, other)
        first = at.swap_y(across[:rows], lower_z(1))
        cur = at.down(cur, 2, 3)
        a_got, b_got = (at.swap_core(v) for v in other)
        sum_down = z_total(down_keep, down_got)
        rest = plus(rest_keep, rest_got)
        first, cur, a_got, b_got = tie(first, cur, a_got, b_got)
        a_keep, a_send = halve(at.x, own[0], a_got, 1)
        b_keep, b_send = halve(at.y, split_y(own[1]), split_y(b_got), 1)
        cur = (plus(near_da[2 * rows : 3 * rows], first) + cur.astype(F32)).astype(BF)
        a_keep, a_send, b_keep, b_send, cur, rest = tie(a_keep, a_send, b_keep, b_send, cur, rest)
        a_got, b_got, cur = at.swap_x(a_send), at.swap_y(b_send), at.down(cur, 1, 3)
        sum_out, sum_up = self.join_rest(rest, run.chunk, run.width)
        a_got, b_got, cur, sum_out, sum_up, sum_down = tie(a_got, b_got, cur, sum_out, sum_up, sum_down)
        a_keep, a_send = halve(at.y, split_y(a_keep), split_y(a_got), 1)
        b_keep, b_send = z_parts(at, b_keep, b_got)
        a_keep, a_send, b_keep, b_send, across = tie(a_keep, a_send, b_keep, b_send, across)
        a_got, b_got = at.swap_y(a_send), z_move(at, b_send)
        beside = at.swap_y(across[rows:], [(i, i - 1) for i in range(1, 8, 2)])
        a_got, b_got, beside = tie(a_got, b_got, beside)
        a_keep, a_send = z_parts(at, a_keep, a_got)
        b_keep, b_send = choose(at.x, z_total(b_keep, b_got).astype(BF), 0)
        a_keep, a_send, b_keep, b_send = tie(a_keep, a_send, b_keep, b_send)
        a_got, b_got = z_move(at, a_send), at.swap_x(b_send)
        grad_hidden = run.last(clean + cur.astype(F32) + beside.astype(F32))
        a_got, b_got, grad_hidden = tie(a_got, b_got, grad_hidden)
        m = run.few * 2
        a, b = z_total(a_keep, a_got), plus(b_keep, b_got)
        sum_qkv = heads_of_halves(*from_column_half(at, jnp.concatenate([a[:m], b], axis=1)))
        return sum_down, sum_up, sum_out, sum_qkv, a[m, : run.vectors], grad_hidden

    def join_rest(self, g, chunk, width):
        a, b = from_column_half(self.at, g)
        cut = width // 2
        out = jnp.concatenate([a[:, :cut], b[:, :cut]], axis=1)
        return out, units_of_halves(a[:, cut:], b[:, cut:], chunk)

    def rest_pieces(self, out, up, other):
        half = out.shape[0] // 2
        core = 1 - self.core if other else self.core
        out = lax.dynamic_slice_in_dim(out, core * half, half, axis=1)
        out = jnp.where(self.core == 0, out, jnp.concatenate([out[half:], out[:half]], axis=0))
        return jnp.concatenate([out.astype(BF), up], axis=1)

    def qkv_pieces(self, pieces, vec):
        cut = [v.reshape(8, 2, v.shape[0] // 16, v.shape[1]) for v in pieces]
        n = vec.shape[1]
        vec = vec.astype(BF).reshape(8, 2, 2, n)
        found = []
        for h, core in enumerate((self.core, 1 - self.core)):
            rows = pick(vec, core, 2)[:, :, None]
            rows = jnp.pad(rows, ((0, 0), (0, 0), (0, 7), (0, cut[0].shape[3] - n)))
            found.append((jnp.concatenate([cut[2 * h], rows], axis=2), cut[2 * h + 1]))
        return found


AXES = ("leaf", "fsdp")


class Whole:
    def __init__(self, rows, leaves, devices):
        self.rows, self.leaves, self.devices = rows, leaves, devices
        self.leaf = lax.axis_index("leaf")
        self.near = 2 + (leaves - 1) // 2

    def lower(self, leaf):
        return [(leaf - s, leaf >= s) for s in range(1, self.leaves)]

    def places(self):
        return jnp.array([[0, 0], [0, 0], [0, 0], [0, 1]], jnp.int32)

    def first_gather(self, hid, w_qkv, w_out, w_up, w_down, vectors, facts, early):
        tree = lax.all_gather(hid, "leaf", axis=0, tiled=False)
        lower = [pick(tree, jnp.maximum(leaf, 0), 0) for leaf, _ in self.lower(self.leaf)]
        every = lambda w: lax.all_gather(w, AXES, axis=0, tiled=True)
        qkv = tuple((v[None],) for v in halves_of_heads(every(w_qkv)))
        return lower, qkv, every(vectors), (every(w_out), every(w_up), every(w_down)), early(facts)

    def second_start(self, state):
        return state

    def second_go_on(self, state):
        return state

    def second_end(self, state):
        out_w, up_w, down_w = state
        half, cut = down_w.shape[0] // 2, out_w.shape[1] // 2
        one = tuple(
            (jnp.concatenate([out_w[:, n * cut : (n + 1) * cut], up_w[:, n * half : (n + 1) * half]], axis=1)[None],)
            for n in range(2)
        )
        return one, tuple((down_w[None, n * half : (n + 1) * half],) for n in range(2))

    def unit_bias(self, bias, chunk):
        half = bias.shape[0] // 2
        return bias[None, :half], bias[None, half:]

    def unit_bias_back(self, own, other, chunk):
        return jnp.concatenate([own, other], axis=1)[0]

    def scatter(self, g):
        return lax.psum_scatter(g.astype(F32), AXES, scatter_dimension=0, tiled=True)

    def rest_pieces(self, out, up, other):
        cut = out.shape[1] // 2
        return jnp.concatenate([out[:, cut:] if other else out[:, :cut], up.astype(F32)], axis=1)

    def backward(self, run):
        rows = self.rows
        down_other, rest_other = run.feed_other(self)
        down_own, rest_own = run.feed_own(self)
        far = run.far_tiles()
        far_da, far_gain = run.far_fold(far)
        near = run.near_tiles(far)
        near_da, clean, vec, pieces = run.near_fold(near, far_gain, far)
        tiles = jnp.concatenate([near_da[:rows], near_da[2 * rows :], far_da], axis=0)
        tiles = tiles.reshape((self.leaves, rows) + tiles.shape[1:])
        order = [pick(tiles, (self.leaf - n) % self.leaves, 0) for n in range(self.leaves)]
        total = lax.psum_scatter(jnp.concatenate(order, axis=0), "leaf", scatter_dimension=0, tiled=True)
        cut = run.width // 2
        return (
            self.scatter(jnp.concatenate([down_own, down_other], axis=0)),
            self.scatter(jnp.concatenate([rest_own[:, cut:], rest_other[:, cut:]], axis=1)),
            self.scatter(jnp.concatenate([rest_own[:, :cut], rest_other[:, :cut]], axis=1)),
            self.scatter(heads_of_halves(*(jnp.concatenate(pieces[n : n + 2], axis=1) for n in (0, 2)))),
            self.scatter(vec)[0],
            run.last(total.astype(F32)),
        )


class Backward:
    pass


def shards(
    leaves,
    groups,
    hidden,
    noise_mask,
    seg_blocks,
    parents,
    ln1_gain,
    w_qkv,
    w_out,
    ln2_gain,
    w_up,
    up_bias,
    w_down,
    down_bias,
    mask_embed,
    cotangent,
):
    rows = hidden.shape[1]
    width = hidden.shape[2]
    half = width // 2
    devices = leaves * groups
    net = Chain(rows) if (leaves, groups) == (8, 4) else Whole(rows, leaves, devices)
    chunk = w_down.shape[0]
    few = ln1_gain.shape[0]
    leaf = lax.axis_index("leaf")

    hid = hidden[0]
    query_cols, query_rows, key_cols, key_rows, flags = tables(net.lower, leaf, seg_blocks, parents, rows)
    tiles = flags.shape[0]
    lanes = jnp.arange(128, dtype=jnp.int32)
    exponent = (lanes % (HEAD_DIM // 2)).astype(F32) * (-math.log(10000.0) / (HEAD_DIM // 2))

    def turns(facts):
        angles = facts[:, 2:3] * jnp.exp(exponent)
        sign = jnp.where((lanes % HEAD_DIM) < HEAD_DIM // 2, -1.0, 1.0)
        return jnp.cos(angles), jnp.sin(angles) * sign

    places = net.places()

    length = 4 * few + up_bias.shape[0]
    vectors = sum(
        jnp.pad(v[None], ((0, 0), (n * few, length - n * few - v.shape[0])))
        for n, v in enumerate((ln1_gain, ln2_gain, down_bias, mask_embed, up_bias))
    )
    lower, qkv_w, vec, coming, (cosine, sine) = net.first_gather(
        hid, w_qkv, w_out, w_up, w_down, vectors, key_cols, turns
    )
    gain_one, gain_two, down_b, embed = (
        vec[:, n * few : (n + 1) * few].reshape(1, width).astype(F32) for n in range(4)
    )
    up_b = jnp.concatenate(net.unit_bias(vec[:, 4 * few :].reshape(-1).astype(F32), chunk), axis=0)
    coming = net.second_start(coming)
    query, key, value = project(
        places, [hid] + lower, noise_mask, embed, gain_one, qkv_w[0], qkv_w[1], cosine, sine
    )
    coming, query = tie(coming, query)
    coming = net.second_go_on(coming)
    mixed, log_norm = attend(flags, query_cols, key_rows, query, key, value, rows)
    coming, mixed = tie(coming, mixed)
    one_w, down_w = net.second_end(coming)
    norm_rows = log_norm.T
    grad_two = cotangent[0].reshape(2 * rows, width)
    (
        output, normed_two, act, grad_pre, grad_one, grad_mixed, grad_after, grad_gain_two, grad_up_b, grad_down_b,
    ) = middle(places, mixed, hid, noise_mask, embed, grad_two, gain_two, up_b, down_b, one_w, down_w)
    output = output.reshape(1, 2, rows, width)
    units = act.shape[1] // 2

    run = Backward()
    run.chunk, run.few, run.vectors, run.grad_mixed, run.width = chunk, few, length, grad_mixed, width
    cut = net.near

    def feed(n, net):
        at = slice(n * units, (n + 1) * units)
        down, up = t_mm(act[:, at], grad_two).astype(BF), t_mm(normed_two, grad_pre[:, at]).astype(BF)
        return down, net.rest_pieces(t_mm(mixed, grad_one), up, n == 1)

    def far_tiles():
        return attend_back(
            cut, tiles, flags, query_rows, key_rows, query, key, value, mixed, run.grad_mixed, norm_rows, cosine, sine, rows
        )

    def far_fold(far):
        return fold(places, lower[cut - 2 :], far[1], far[2], noise_mask, embed, gain_one, qkv_w[0], qkv_w[1])

    def near_tiles(far):
        return attend_back(
            0, cut, flags, query_rows, key_rows, query, key, value, mixed, run.grad_mixed, norm_rows, cosine, sine, rows, far[0]
        )

    def near_fold(near, far_gain, far):
        da, gain, clean, run.noisy, grad_embed, *pieces = fold(
            places, [hid] + lower, near[1], near[2], noise_mask, embed, gain_one, qkv_w[0], qkv_w[1],
            (near[0], grad_after, far[1], far[2]),
        )
        parts = (gain + far_gain, grad_gain_two, grad_down_b, grad_embed, net.unit_bias_back(grad_up_b[:1], grad_up_b[1:], chunk))
        vec = jnp.concatenate([v.reshape(devices, -1) for v in parts], axis=1)
        return da, clean, vec, pieces

    def last(total):
        hat, scale = normalise(hid.astype(F32))
        masked = (noise_mask[0] == 1)[:, None]
        clean = grad_after[:rows] + norm_back(hat, scale, gain_one, total)
        return (clean + jnp.where(masked, 0.0, run.noisy)).astype(BF)[None]

    run.feed_own = lambda net: feed(0, net)
    run.feed_other = lambda net: feed(1, net)
    run.far_tiles, run.far_fold, run.near_tiles, run.near_fold, run.last = far_tiles, far_fold, near_tiles, near_fold, last
    sum_down, sum_up, sum_out, sum_qkv, sum_vec, grad_hidden = net.backward(run)
    piece = lambda n: sum_vec[n * few : (n + 1) * few]
    return (
        output,
        grad_hidden,
        piece(0),
        sum_qkv,
        sum_out,
        piece(1),
        sum_up,
        sum_vec[4 * few :],
        sum_down,
        piece(2),
        piece(3),
    )


def solution(mesh):
    split = ("leaf", "fsdp")
    in_specs = (
        P("fsdp", "leaf", None),
        P("fsdp", "leaf"),
        P("fsdp", None),
        P("fsdp", None),
        P(split),
        P(split, None),
        P(split, None),
        P(split),
        P(split, None),
        P(split),
        P(split, None),
        P(split),
        P(split),
        P("fsdp", None, "leaf", None),
    )
    out_specs = (
        P("fsdp", None, "leaf", None),
        P("fsdp", "leaf", None),
        P(split),
        P(split, None),
        P(split, None),
        P(split),
        P(split, None),
        P(split),
        P(split, None),
        P(split),
        P(split),
    )
    body = functools.partial(shards, mesh.shape["leaf"], mesh.shape["fsdp"])
    return jax.shard_map(body, mesh=mesh, in_specs=in_specs, out_specs=out_specs, check_vma=False)
```

```python
import functools
import math

import jax
import jax.numpy as jnp
from jax import lax
from jax.experimental import pallas as pl
from jax.experimental.pallas import tpu as pltpu
from jax.sharding import PartitionSpec as P

HEAD_DIM = 64
BLOCK = 16
NEG_FILL = -1000000000.0
EPSILON = 1e-05


def vmem(mebibytes):
    return pltpu.CompilerParams(vmem_limit_bytes=mebibytes * 2**20)


BF = jnp.bfloat16
F32 = jnp.float32


class Links:
    def __init__(self):
        leaf = lax.axis_index("leaf")
        fsdp = lax.axis_index("fsdp")
        self.z, self.y = leaf // 2, leaf % 2
        self.x, self.core = fsdp // 2, fsdp % 2

    def swap_core(self, v):
        return lax.ppermute(v, "fsdp", [(i, i ^ 1) for i in range(4)])

    def swap_x(self, v):
        return lax.ppermute(v, "fsdp", [(i, i ^ 2) for i in range(4)])

    def swap_y(self, v, pairs=None):
        return lax.ppermute(v, "leaf", pairs or [(i, i ^ 1) for i in range(8)])

    def swap_z(self, v, n):
        return lax.ppermute(v, "leaf", [(i, i ^ (2 * n)) for i in range(8)])

    def up(self, v, first, last):
        return lax.ppermute(v, "leaf", [(i, i + 2) for i in range(2 * first, 2 * last + 2)])

    def down(self, v, first, last):
        return lax.ppermute(v, "leaf", [(i, i - 2) for i in range(2 * first, 2 * last + 2)])


def both(bit, own, other, axis):
    return jnp.where(
        bit == 0, jnp.stack([own, other], axis), jnp.stack([other, own], axis)
    )


def tie(*values):
    flat, tree = jax.tree.flatten(values)
    return jax.tree.unflatten(tree, lax.optimization_barrier(tuple(flat)))


def z_gather(at, block):
    return jnp.concatenate([block] + [at.swap_z(block, n) for n in (1, 2, 3)], axis=0)


def pick(v, index, axis):
    return lax.dynamic_index_in_dim(v, index, axis, keepdims=False)


def choose(bit, v, axis):
    return pick(v, bit, axis), pick(v, 1 - bit, axis)


def plus(a, b):
    return a.astype(F32) + b.astype(F32)


def joined(mine, got, index, axis):
    return plus(pick(mine, index, axis), pick(got, index, axis)).astype(BF)


def halve(bit, mine, got, axis):
    return joined(mine, got, bit, axis), joined(mine, got, 1 - bit, axis)


def z_parts(at, mine, got):
    return joined(mine, got, at.z, 0), [joined(mine, got, at.z ^ n, 0) for n in (1, 2, 3)]


def z_move(at, parts):
    return [at.swap_z(part, n) for n, part in zip((1, 2, 3), parts)]


def z_total(keep, got):
    return plus(keep, got[0]) + plus(got[1], got[2])


def to_column_half(at, half_a, half_b):
    keep = jnp.where(at.core == 0, half_a, half_b)
    send = jnp.where(at.core == 0, half_b, half_a)
    got = at.swap_core(send)
    return both(at.core, keep, got, 0).reshape(2 * keep.shape[0], keep.shape[1])


def from_column_half(at, g):
    g = g.reshape(2, g.shape[0] // 2, g.shape[1])
    keep, send = choose(at.core, g, 0)
    got = at.swap_core(send)
    return jnp.where(at.core == 0, keep, got), jnp.where(at.core == 0, got, keep)


def spec(shape, index_map):
    return pl.BlockSpec(shape, index_map)


def turn(values, cosine, sine):
    lane = lax.broadcasted_iota(jnp.int32, (values.shape[0], 128), 1)
    low_half = (lane % HEAD_DIM) < HEAD_DIM // 2
    groups = []
    for n in range(values.shape[1] // 128):
        part = values[:, n * 128 : (n + 1) * 128]
        swapped = jnp.where(low_half, pltpu.roll(part, 96, 1), pltpu.roll(part, 32, 1))
        groups.append(part * cosine + swapped * sine)
    return groups


def column(row):
    return jnp.broadcast_to(row, (8, row.shape[1])).T[:, :1]


def tables_kernel(places, rows, leaf_ref, seg_ref, parent_ref, qcol_ref, qrow_ref, kcol_ref, krow_ref, flag_ref, pad_ref):
    leaf = leaf_ref[0]
    blocks = rows // BLOCK
    slots = 16
    seg = column(seg_ref[...].astype(F32))
    lane = lax.broadcasted_iota(jnp.int32, (seg.shape[0], 128), 1).astype(F32)
    length = jnp.sum(jnp.where(seg == lane, 1.0, 0.0), axis=0, keepdims=True)
    start = jnp.sum(jnp.where(seg < lane, 1.0, 0.0), axis=0, keepdims=True)
    pad_ref[...] = jnp.zeros_like(pad_ref)
    pad_ref[0:1, 0 : parent_ref.shape[1]] = parent_ref[...].astype(F32)
    parent_row = pad_ref[0:1, :]
    lane = lax.broadcasted_iota(jnp.int32, (slots, 128), 1).astype(F32)
    slot = lax.broadcasted_iota(jnp.int32, (slots, 1), 0).astype(F32)
    parent = column(parent_row)[:slots]
    look = lambda index, row: jnp.sum(jnp.where(index == lane, row, 0.0), axis=1, keepdims=True)
    grand = look(parent, parent_row)
    start = look(slot, start)
    shift = jnp.where(slot > 0, look(parent, length), 0.0) + jnp.where(parent > 0, look(grand, length), 0.0) - start

    def facts(block):
        own = jnp.sum(jnp.where(block >= start, 1.0, 0.0), axis=0, keepdims=True) - 1.0
        take = lambda col: jnp.sum(jnp.where(slot == own, col, 0.0), axis=0, keepdims=True)
        return own, take(parent), take(grand), take(shift)

    token = lax.broadcasted_iota(jnp.int32, (1, rows), 1)
    zero = jnp.zeros((1, rows), F32)
    tiles = [(leaf, leaf >= 0), (leaf, leaf < 0)] + places(leaf)
    for t, (place, valid) in enumerate(tiles):
        first = jnp.maximum(place, 0) * blocks
        block = (first + lax.shift_right_logical(token, 4)).astype(F32)
        own, one, two, move = facts(block)
        position = (move + block) * BLOCK + (token & (BLOCK - 1)).astype(F32)
        at = slice(t * rows, (t + 1) * rows)
        if t < 2:
            limit = block + (1.0 if t == 0 else 0.0)
            lines = jnp.concatenate([own, one, two, limit, zero, zero, zero, zero], axis=0)
            qrow_ref[:, at] = lines
            qcol_ref[at, :] = lines.T
        lines = jnp.concatenate(
            [jnp.where(valid, own, -1.0), block, position, zero, zero, zero, zero, zero], axis=0
        )
        krow_ref[:, at] = lines
        kcol_ref[at, :] = lines.T
    queries = qcol_ref[pl.ds(0, 2 * blocks, stride=BLOCK), :]
    lane = lax.broadcasted_iota(jnp.int32, (1, 128), 1)
    for t, (place, valid) in enumerate(tiles):
        if t < 2:
            flag_ref[t] = 1
            continue
        block = (jnp.maximum(place, 0) * blocks + lane).astype(F32)
        own = facts(block)[0]
        allowed = (
            ((own == queries[:, 0:1]) | (own == queries[:, 1:2]) | (own == queries[:, 2:3]))
            & (block < queries[:, 3:4])
            & (lane < blocks)
            & valid
        )
        flag_ref[t] = jnp.max(jnp.where(allowed, 1.0, 0.0)).astype(jnp.int32)


def tables(places, leaf, seg, parent, rows):
    tiles = 2 + len(places(leaf))
    total = tiles * rows
    smem = pl.BlockSpec(memory_space=pltpu.SMEM)
    vmem = pl.BlockSpec(memory_space=pltpu.VMEM)
    shapes = [(2 * rows, 8), (8, 2 * rows), (total, 8), (8, total)]
    return pl.pallas_call(
        functools.partial(tables_kernel, places, rows),
        in_specs=[smem, vmem, vmem],
        out_specs=[vmem] * 4 + [smem],
        out_shape=[jax.ShapeDtypeStruct(shape, F32) for shape in shapes] + [jax.ShapeDtypeStruct((tiles,), jnp.int32)],
        name="tables",
        scratch_shapes=[pltpu.VMEM((8, 128), F32)],
    )(leaf.reshape(1), seg, parent)


def fetch(pieces, sems):
    copies = [pltpu.make_async_copy(src, dst, sems.at[n]) for n, (src, dst) in enumerate(pieces)]
    for copy in copies:
        copy.start()
    return copies


def placed(blocks, ref, size, table, row):
    pieces = []
    for hbm in blocks:
        for n in range(hbm.shape[0]):
            place = pl.multiple_of(table[row, len(pieces)] * size, size)
            pieces.append((hbm.at[n, pl.ds(0, size), :], ref.at[pl.ds(place, size), :]))
    return pieces


def tiled(sources, ref, rows):
    return [(src, ref.at[pl.ds(n * rows, rows), :]) for n, src in enumerate(sources)]


def project_kernel(
    blocks, sources, size, rows, table_ref, mask_ref, embed_ref, gain_ref, cos_ref, sin_ref, *refs,
):
    own_hbm, other_hbm, tiles = refs[:blocks], refs[blocks : 2 * blocks], refs[2 * blocks : 2 * blocks + sources]
    q_ref, k_ref, v_ref, x_ref, own_ref, other_ref, sems = refs[2 * blocks + sources :]
    tile = pl.program_id(0)
    step = k_ref.shape[1]

    @pl.when(tile == 0)
    def _():
        pieces = tiled([tiles[0]] + list(tiles), x_ref, rows)
        count = len(pieces)
        pieces += placed(own_hbm, own_ref, size, table_ref, 0) + placed(other_hbm, other_ref, size, table_ref, 0)
        copies = fetch(pieces, sems)
        for copy in copies[:count]:
            copy.wait()
        masked = column(mask_ref[...].astype(F32)) > 0
        x_ref[rows : 2 * rows, :] = jnp.where(masked, embed_ref[...], x_ref[rows : 2 * rows, :].astype(F32)).astype(BF)
        for copy in copies[count:]:
            copy.wait()

    x = x_ref[pl.ds(pl.multiple_of(tile * step, step), step), :].astype(F32)
    centred = x - jnp.mean(x, axis=-1, keepdims=True)
    spread = jnp.mean(centred * centred, axis=-1, keepdims=True)
    a = (centred * lax.rsqrt(spread + EPSILON) * gain_ref[...]).astype(BF)
    cosine, sine = cos_ref[...], sin_ref[...]
    half = own_ref.shape[1] // 3
    for n, w_ref in enumerate((own_ref, other_ref)):
        base = n * half
        keys = jnp.dot(a, w_ref[:, half : 2 * half], preferred_element_type=F32)
        values = jnp.dot(a, w_ref[:, 2 * half :], preferred_element_type=F32)
        for g, part in enumerate(turn(keys, cosine, sine)):
            k_ref[base // 128 + g] = part.astype(BF)
            v_ref[base // 128 + g] = values[:, g * 128 : (g + 1) * 128].astype(BF)

    @pl.when(tile * step < 2 * rows)
    def _():
        lines = q_ref.shape[0]
        for n, w_ref in enumerate((own_ref, other_ref)):
            base = n * half
            q = jnp.dot(a[:lines], w_ref[:, :half], preferred_element_type=F32)
            for g, part in enumerate(turn(q, cosine[:lines], sine[:lines])):
                q_ref[:, base + g * 128 : base + (g + 1) * 128] = part.astype(BF)


def project(table, tiles, mask, embed, gain, own, other, cosine, sine):
    rows, width = tiles[0].shape
    total = (len(tiles) + 1) * rows
    step = next(n for n in (3 * rows, 2 * rows, rows) if total % n == 0)
    q_step = min(step, 2 * rows)
    last_q = 2 * rows // q_step - 1
    count = sum(v.shape[0] for v in own)
    columns = own[0].shape[2]
    whole = lambda v: spec(v.shape, lambda t, i: (0, 0))
    moved = lambda n: spec((step, n), lambda t, i: (t, 0))
    pairs = spec((width // 128, step, 128), lambda t, i: (0, t, 0))
    out = lambda n: jax.ShapeDtypeStruct((n, width), BF)
    anywhere = pl.BlockSpec(memory_space=pl.ANY)
    far = list(own) + list(other) + list(tiles)
    return pl.pallas_call(
        functools.partial(project_kernel, len(own), len(tiles), width // count, rows),
        grid_spec=pltpu.PrefetchScalarGridSpec(
            num_scalar_prefetch=1,
            grid=(total // step,),
            in_specs=[whole(mask), whole(embed), whole(gain), moved(128), moved(128)] + [anywhere] * len(far),
            out_specs=[
                spec((q_step, width), lambda t, i: (jnp.minimum(t, last_q), 0)),
                pairs,
                pairs,
            ],
            scratch_shapes=[
                pltpu.VMEM((total, width), BF),
                pltpu.VMEM((width, columns), BF),
                pltpu.VMEM((width, columns), BF),
                pltpu.SemaphoreType.DMA((2 * count + len(tiles) + 1,)),
            ],
        ),
        out_shape=[out(2 * rows)] + [jax.ShapeDtypeStruct((width // 128, total, 128), BF)] * 2,
        compiler_params=vmem(26 if total <= 10 * rows else 40),
        cost_estimate=pl.CostEstimate(
            flops=2 * total * width * 2 * width + 4 * rows * width * width,
            bytes_accessed=2 * (3 * total * width + 3 * width * width),
            transcendentals=0,
        ),
        name="project",
    )(table, mask, embed, gain, cosine, sine, *far)


def middle_kernel(
    blocks_one, blocks_two, size, chunk, table_ref, o_ref, x_ref, mask_ref, embed_ref, dy_ref, gain_ref, up_b_ref,
    down_b_ref, *refs,
):
    refs = list(refs)
    take = lambda n: [refs.pop(0) for _ in range(n)]
    ones, twos = (take(blocks_one), take(blocks_one)), (take(blocks_two), take(blocks_two))
    y_ref, b_ref, g_ref, du_ref, dh_low_ref, do_ref, dh_ref, dup_b_ref, ddown_b_ref = take(9)
    out_ref, up_ref, down_ref, sems = refs
    cut = out_ref.shape[1] // 2
    units = up_ref.shape[2]
    pieces_out, pieces = [], []
    for n in range(2):
        columns = pl.ds(pl.multiple_of(table_ref[3, n] * cut, cut), cut)
        spots = [(hbm, j) for hbm in ones[n] for j in range(hbm.shape[0])]
        pieces.append([])
        for place, (hbm, j) in enumerate(spots):
            to = pl.ds(pl.multiple_of(table_ref[1, place] * size, size), size)
            pieces_out.append((hbm.at[j, :, pl.ds(0, cut)], out_ref.at[to, columns]))
            to = pl.ds(pl.multiple_of(table_ref[0, place] * size, size), size)
            pieces[n].append((hbm.at[j, :, pl.ds(cut, units)], up_ref.at[n, to, :]))
        pieces[n] += placed(twos[n], down_ref.at[n], chunk, table_ref, 2)
    copies = fetch(pieces_out + pieces[0] + pieces[1], sems)
    for copy in copies[: len(pieces_out)]:
        copy.wait()
    x = x_ref[...].astype(F32)
    masked = column(mask_ref[...].astype(F32)) > 0
    x = jnp.concatenate([x, jnp.where(masked, embed_ref[...], x)], axis=0)
    h = x + jnp.dot(o_ref[...], out_ref[...], preferred_element_type=F32)
    centred = h - jnp.mean(h, axis=-1, keepdims=True)
    spread = jnp.mean(centred * centred, axis=-1, keepdims=True)
    scale = lax.rsqrt(spread + EPSILON)
    hat = centred * scale
    b = (hat * gain_ref[...]).astype(BF)
    b_ref[...] = b
    dy = dy_ref[...]
    ddown_b_ref[...] = jnp.sum(dy.astype(F32), axis=0, keepdims=True)
    y = h + down_b_ref[...]
    db = None
    wide = next(n for n in (768, 512, 384, 256, 128) if units % n == 0)
    for n in range(2):
        done = len(pieces_out) + n * len(pieces[0])
        for copy in copies[done : done + len(pieces[n])]:
            copy.wait()
        for c in range(0, units, wide):
            at = slice(c, c + wide)
            to = slice(n * units + c, n * units + c + wide)
            u = jnp.dot(b, up_ref[n, :, at], preferred_element_type=F32) + up_b_ref[n : n + 1, at]
            g, slope = gelu_parts(u)
            g = g.astype(BF)
            g_ref[:, to] = g
            y = y + jnp.dot(g, down_ref[n, at, :], preferred_element_type=F32)
            du = (matmul_t(dy, down_ref[n, at, :]) * slope).astype(BF)
            du_ref[:, to] = du
            dup_b_ref[n : n + 1, at] = jnp.sum(du.astype(F32), axis=0, keepdims=True)
            part = matmul_t(du, up_ref[n, :, at])
            db = part if db is None else db + part
    y_ref[...] = y.astype(BF)
    dh = dy.astype(F32) + norm_back(hat, scale, gain_ref[...], db)
    dh_ref[...] = dh
    low = dh.astype(BF)
    dh_low_ref[...] = low
    do_ref[...] = matmul_t(low, out_ref[...]).astype(BF)


def middle(table, o, x, mask, embed, dy, gain, up_b, down_b, one, two):
    rows, width = o.shape
    count = sum(v.shape[0] for v in one[0])
    size, columns = one[0][0].shape[1:]
    chunk = two[0][0].shape[1]
    units = columns - width // 2
    full = lambda shape: spec(shape, lambda t, i: (0, 0))
    near = (o, x, mask, embed, dy, gain, up_b, down_b)
    far = list(one[0]) + list(one[1]) + list(two[0]) + list(two[1])
    shapes = [
        ((rows, width), BF), ((rows, width), BF), ((rows, 2 * units), BF), ((rows, 2 * units), BF), ((rows, width), BF),
        ((rows, width), BF), ((rows, width), F32), ((2, units), F32), ((1, width), F32),
    ]
    return pl.pallas_call(
        functools.partial(middle_kernel, len(one[0]), len(two[0]), size, chunk),
        grid_spec=pltpu.PrefetchScalarGridSpec(
            num_scalar_prefetch=1,
            grid=(1,),
            in_specs=[full(v.shape) for v in near] + [pl.BlockSpec(memory_space=pl.ANY)] * len(far),
            out_specs=[full(shape) for shape, _ in shapes],
            scratch_shapes=[
                pltpu.VMEM((width, width), BF),
                pltpu.VMEM((2, width, units), BF),
                pltpu.VMEM((2, units, width), BF),
                pltpu.SemaphoreType.DMA((6 * count,)),
            ],
        ),
        out_shape=[jax.ShapeDtypeStruct(shape, kind) for shape, kind in shapes],
        compiler_params=vmem(44),
        cost_estimate=pl.CostEstimate(
            flops=2 * rows * width * (2 * width + 8 * units),
            bytes_accessed=4 * (width * width + 4 * units * width),
            transcendentals=2 * rows * units,
        ),
        name="middle",
    )(table, *near, *far)


def matmul_t(a, b):
    return lax.dot_general(a, b, (((1,), (1,)), ((), ())), preferred_element_type=F32)


def groups(tiles, first=2):
    found = [(first, first + 2)] if first == 2 else []
    found = [] if first > 2 else [(2, min(4, tiles))] + ([(4, 5)] if tiles > 4 else [])
    start = max(first, 5)
    return found + [(n, min(n + 2, tiles)) for n in range(start, tiles, 2)]


def attend_kernel(
    rows, tiles, flag_ref, qcol_ref, krow_ref, q_ref, k_ref, v_ref, o_ref, lse_ref,
    bias_ref, s_ref, top_ref, sum_ref, acc_ref,
):
    pair = pl.program_id(0)
    both_rows = 2 * rows

    def span(t):
        return slice(t * rows, (t + 1) * rows)

    def lines(t):
        return slice(rows, both_rows) if t == 1 else slice(0, both_rows)

    @pl.when(pair == 0)
    def _():
        lse_ref[...] = jnp.zeros_like(lse_ref)
        own = qcol_ref[:, 0:1]
        up_one = qcol_ref[:, 1:2]
        up_two = qcol_ref[:, 2:3]
        limit = qcol_ref[:, 3:4]
        for t in range(tiles):
            if t == 1:
                r = lax.broadcasted_iota(jnp.int32, (rows, rows), 0) // BLOCK
                c = lax.broadcasted_iota(jnp.int32, (rows, rows), 1) // BLOCK
                bias_ref[rows:, span(t)] = jnp.where(r == c, 0.0, NEG_FILL)
            else:
                seg = krow_ref[0:1, span(t)]
                index = krow_ref[1:2, span(t)]
                ok = ((seg == own) | (seg == up_one) | (seg == up_two)) & (index < limit)
                bias_ref[:, span(t)] = jnp.where(ok, 0.0, NEG_FILL)

    lane = lax.broadcasted_iota(jnp.int32, (both_rows, 128), 1)
    queries = [jnp.where((lane // HEAD_DIM) == h, q_ref[...] * 0.125, 0).astype(BF) for h in range(2)]
    top_ref[...] = jnp.full_like(top_ref, -3.0e38)

    def scores(first, last, at):
        cut = slice(first * rows, last * rows)
        keys = k_ref[0, cut, :]
        for h in range(2):
            s = matmul_t(queries[h][at], keys) + bias_ref[at, cut]
            s_ref[h, at, cut] = s
            best = top_ref[h, at, :]
            for c in range(s.shape[1] // 128):
                best = jnp.maximum(best, s[:, c * 128 : (c + 1) * 128])
            top_ref[h, at, :] = best

    def weigh(first, last, at):
        cut = slice(first * rows, last * rows)
        values = v_ref[0, cut, :]
        for h in range(2):
            p = jnp.exp(s_ref[h, at, cut] - tops[h][at])
            part = sum_ref[h, at, :]
            for c in range(p.shape[1] // 128):
                part = part + p[:, c * 128 : (c + 1) * 128]
            sum_ref[h, at, :] = part
            acc_ref[h, at, :] += jnp.dot(p.astype(BF), values, preferred_element_type=F32)

    upper, lower, all_rows = slice(0, rows), slice(rows, both_rows), slice(0, both_rows)

    def each(step):
        step(0, 1, upper)
        step(0, 2, lower)
        for first, last in groups(tiles):
            some = flag_ref[first]
            for t in range(first + 1, last):
                some = some + flag_ref[t]
            pl.when(some > 0)(functools.partial(step, first, last, all_rows))

    each(scores)
    tops = [jnp.max(top_ref[h], axis=-1, keepdims=True) for h in range(2)]
    sum_ref[...] = jnp.zeros_like(sum_ref)
    acc_ref[...] = jnp.zeros_like(acc_ref)
    each(weigh)
    outs, norms = [], lse_ref[...]
    for h in range(2):
        total = jnp.sum(sum_ref[h], axis=-1, keepdims=True)
        outs.append(acc_ref[h] / total)
        norms = jnp.where(lane == 2 * pair + h, tops[h] + jnp.log(total), norms)
    lse_ref[...] = norms
    o_ref[...] = jnp.where(lane < HEAD_DIM, outs[0], outs[1]).astype(BF)


def attend(flags, qcol, krow, q, k, v, rows):
    width = q.shape[1]
    total = k.shape[1]
    tiles = total // rows
    whole_pair = spec((1, total, 128), lambda p, f: (p, 0, 0))
    pair = lambda n: spec((n, 128), lambda p, f: (0, p))
    fixed = lambda shape: spec(shape, lambda p, f: (0, 0))
    return pl.pallas_call(
        functools.partial(attend_kernel, rows, tiles),
        grid_spec=pltpu.PrefetchScalarGridSpec(
            num_scalar_prefetch=1,
            grid=(width // 128,),
            in_specs=[fixed(qcol.shape), fixed(krow.shape), pair(2 * rows), whole_pair, whole_pair],
            out_specs=[pair(2 * rows), fixed((2 * rows, 128))],
            scratch_shapes=[
                pltpu.VMEM((2 * rows, total), F32),
                pltpu.VMEM((2, 2 * rows, total), F32),
                pltpu.VMEM((2, 2 * rows, 128), F32),
                pltpu.VMEM((2, 2 * rows, 128), F32),
                pltpu.VMEM((2, 2 * rows, 128), F32),
            ],
        ),
        out_shape=[
            jax.ShapeDtypeStruct((2 * rows, width), BF),
            jax.ShapeDtypeStruct((2 * rows, 128), F32),
        ],
        compiler_params=vmem(28 if tiles <= 10 else 52),
        cost_estimate=pl.CostEstimate(
            flops=16 * rows * total * width,
            bytes_accessed=4 * (total + rows) * width,
            transcendentals=2 * rows * total * width // HEAD_DIM,
        ),
        name="attend",
    )(flags, qcol, krow, q, k, v)


def attend_back_kernel(
    rows, first, last, flag_ref, qrow_ref, krow_ref, q_ref, k_ref, v_ref, o_ref, g_ref, lse_ref, *refs,
):
    refs = list(refs)
    near = first == 0
    cos_ref, sin_ref = refs[:2]
    part_ref = refs[2] if near else None
    dq_ref, dk_ref, dv_ref, bias_ref, acc_ref = refs[-5:]
    pair = pl.program_id(0)
    both_rows = 2 * rows

    def span(t):
        return slice(t * rows, (t + 1) * rows)

    @pl.when(pair == 0)
    def _():
        own = qrow_ref[0:1, :]
        up_one = qrow_ref[1:2, :]
        up_two = qrow_ref[2:3, :]
        limit = qrow_ref[3:4, :]
        for t in range(first, last):
            if t == 1:
                r = lax.broadcasted_iota(jnp.int32, (rows, both_rows), 0) // BLOCK
                c = lax.broadcasted_iota(jnp.int32, (rows, both_rows), 1) // BLOCK
                bias_ref[span(t - first), :] = jnp.where(r + rows // BLOCK == c, 0.0, NEG_FILL)
            else:
                facts = krow_ref[:, span(t - first)].T
                seg = facts[:, 0:1]
                index = facts[:, 1:2]
                ok = ((seg == own) | (seg == up_one) | (seg == up_two)) & (index < limit)
                bias_ref[span(t - first), :] = jnp.where(ok, 0.0, NEG_FILL)

    lane = lax.broadcasted_iota(jnp.int32, (both_rows, 128), 1)
    acc_ref[...] = part_ref[...] if near else jnp.zeros_like(acc_ref)
    queries, grads, deltas, norms, queries_t, grads_t = [], [], [], [], [], []
    product = (o_ref[...].astype(F32) * g_ref[...].astype(F32)).T
    for h in range(2):
        mine = (lane // HEAD_DIM) == h
        queries.append(jnp.where(mine, q_ref[...] * 0.125, 0).astype(BF))
        grads.append(jnp.where(mine, g_ref[...], 0).astype(BF))
        queries_t.append(queries[h].astype(F32).T.astype(BF))
        grads_t.append(grads[h].astype(F32).T.astype(BF))
        deltas.append(jnp.sum(product[h * HEAD_DIM : (h + 1) * HEAD_DIM], axis=0, keepdims=True))
        norms.append(lse_ref[pl.ds(2 * pair + h, 1), :])

    def step(start, end):
        to = slice((start - first) * rows, (end - first) * rows)
        keys, values = k_ref[0, to, :], v_ref[0, to, :]
        keys_t = keys.astype(F32).T.astype(BF)
        dk = dv = None
        for h in range(2):
            q, g = queries[h], grads[h]
            s = jnp.dot(keys, queries_t[h], preferred_element_type=F32) + bias_ref[to, :]
            p = jnp.exp(s - norms[h])
            dp = jnp.dot(values, grads_t[h], preferred_element_type=F32)
            ds = (p * (dp - deltas[h])).astype(BF)
            part_v = jnp.dot(p.astype(BF), g, preferred_element_type=F32)
            part_k = jnp.dot(ds, q, preferred_element_type=F32)
            dv = part_v if dv is None else dv + part_v
            dk = part_k if dk is None else dk + part_k
            half = slice(h * HEAD_DIM, (h + 1) * HEAD_DIM)
            acc_ref[half, :] += jnp.dot(keys_t[half], ds, preferred_element_type=F32)
        [dk] = turn(dk, cos_ref[to, :], -sin_ref[to, :])
        dk_ref[0, to, :] = dk.astype(BF)
        dv_ref[0, to, :] = dv.astype(BF)

    if near:
        step(0, 2)
    for start, end in groups(last, max(first, 2)):
        some = flag_ref[start]
        for t in range(start + 1, end):
            some = some + flag_ref[t]
        to = slice((start - first) * rows, (end - first) * rows)

        @pl.when(some == 0)
        def _():
            dk_ref[0, to, :] = jnp.zeros(((end - start) * rows, 128), BF)
            dv_ref[0, to, :] = jnp.zeros(((end - start) * rows, 128), BF)

        pl.when(some > 0)(functools.partial(step, start, end))

    if near:
        dq = acc_ref[...].T * 0.125
        [dq] = turn(dq, cos_ref[:both_rows, :], -sin_ref[:both_rows, :])
        dq_ref[...] = dq.astype(BF)
    else:
        dq_ref[...] = acc_ref[...]


def attend_back(first, last, flags, qrow, krow, q, k, v, o, g, lse, cosine, sine, rows, part=None):
    width = q.shape[1]
    there = (last - first) * rows
    near = first == 0
    some_pair = lambda n: spec((1, n, 128), lambda p, f: (p, 0, 0))
    taken_pair = spec((pl.Element(1), pl.Element(there), pl.Element(128)), lambda p, f: (p, first * rows, 0))
    taken = spec((pl.Element(there), pl.Element(128)), lambda p, f: (first * rows, 0))
    pair = lambda n: spec((n, 128), lambda p, f: (0, p))
    turned = spec((128, 2 * rows), lambda p, f: (p, 0))
    fixed = lambda shape: spec(shape, lambda p, f: (0, 0))
    out = lambda n: jax.ShapeDtypeStruct((n, width), BF)
    return pl.pallas_call(
        functools.partial(attend_back_kernel, rows, first, last),
        grid_spec=pltpu.PrefetchScalarGridSpec(
            num_scalar_prefetch=1,
            grid=(width // 128,),
            in_specs=[
                fixed(qrow.shape), spec((pl.Element(8), pl.Element(there)), lambda p, f: (0, first * rows)), pair(2 * rows),
                taken_pair, taken_pair, pair(2 * rows), pair(2 * rows), fixed(lse.shape), taken, taken,
            ] + ([turned] if near else []),
            out_specs=[pair(2 * rows) if near else turned, some_pair(there), some_pair(there)],
            scratch_shapes=[
                pltpu.VMEM((there, 2 * rows), F32),
                pltpu.VMEM((128, 2 * rows), F32),
            ],
        ),
        out_shape=[out(2 * rows) if near else jax.ShapeDtypeStruct((width, 2 * rows), F32)]
        + [jax.ShapeDtypeStruct((width // 128, there, 128), BF)] * 2,
        compiler_params=vmem(30 if there <= 5 * rows else 44),
        cost_estimate=pl.CostEstimate(
            flops=40 * rows * there * width,
            bytes_accessed=8 * (there + rows) * width,
            transcendentals=2 * rows * there * width // HEAD_DIM,
        ),
        name="attend_back_near" if near else "attend_back_far",
    )(flags, qrow, krow, q, k, v, o, g, lse, cosine, sine, *([part] if near else []))


def t_matmul(a, b):
    return lax.dot_general(a, b, (((0,), (0,)), ((), ())), preferred_element_type=F32)


def normed(x):
    centred = x - jnp.mean(x, axis=-1, keepdims=True)
    scale = lax.rsqrt(jnp.mean(centred * centred, axis=-1, keepdims=True) + EPSILON)
    return centred * scale, scale


def side(ref, n, at):
    pairs = ref.shape[0] // 2
    return jnp.concatenate([ref[n * pairs + p, at, :] for p in range(pairs)], axis=1)


def fold_rows_kernel(near, blocks, size, rows, table_ref, *refs):
    refs = list(refs)
    take = lambda n: [refs.pop(0) for _ in range(n)]
    if near:
        [dq_ref] = take(1)
    own_hbm, other_hbm, hbm = take(blocks), take(blocks), take(2)
    if near:
        [clean_ref] = take(1)
    da_ref, own_ref, other_ref = take(3)
    grads, sems = refs[:2], refs[2]
    half = own_ref.shape[1] // 3
    cuts = [slice(n * half, (n + 1) * half) for n in range(3)]
    pieces = list(zip(hbm, grads))
    pieces += placed(own_hbm, own_ref, size, table_ref, 0) + placed(other_hbm, other_ref, size, table_ref, 0)
    for copy in fetch(pieces, sems):
        copy.wait()
    first = 2 if near else 0
    for t in range(grads[0].shape[1] // rows):
        if near and t == 1:
            continue
        at = slice(t * rows, (t + 1) * rows)
        da = None
        for n, w_ref in enumerate((own_ref, other_ref)):
            part = matmul_t(side(grads[0], n, at), w_ref[:, cuts[1]]) + matmul_t(side(grads[1], n, at), w_ref[:, cuts[2]])
            if near and t == 0:
                part = part + matmul_t(dq_ref[at, cuts[n]], w_ref[:, cuts[0]])
            da = part if da is None else da + part
        if near and t == 0:
            clean_ref[...] = da
        else:
            da_ref[(t - first) * rows : (t - first + 1) * rows, :] = da.astype(BF)


def fold_rows(table, dk, dv, own, other, rows, dq=None):
    width = own[0].shape[2] * 2 // 3
    there = dk.shape[1]
    near = dq is not None
    count = sum(v.shape[0] for v in own)
    columns = own[0].shape[2]
    whole = lambda shape: spec(shape, lambda t, i: (0,) * len(shape))
    outs = ([((rows, width), F32)] if near else []) + [((there - (2 * rows if near else 0), width), BF)]
    far = list(own) + list(other) + [dk, dv]
    return pl.pallas_call(
        functools.partial(fold_rows_kernel, near, len(own), width // count, rows),
        grid_spec=pltpu.PrefetchScalarGridSpec(
            num_scalar_prefetch=1,
            grid=(1,),
            in_specs=([whole(dq.shape)] if near else []) + [pl.BlockSpec(memory_space=pl.ANY)] * len(far),
            out_specs=[whole(shape) for shape, _ in outs],
            scratch_shapes=[
                pltpu.VMEM((width, columns), BF),
                pltpu.VMEM((width, columns), BF),
                pltpu.VMEM(dk.shape, BF),
                pltpu.VMEM(dv.shape, BF),
                pltpu.SemaphoreType.DMA((2 * count + 2,)),
            ],
        ),
        out_shape=[jax.ShapeDtypeStruct(shape, kind) for shape, kind in outs],
        compiler_params=vmem(28 if there <= 5 * rows else 40),
        cost_estimate=pl.CostEstimate(
            flops=4 * there * width * width, bytes_accessed=2 * (3 * there * width + 3 * width * width), transcendentals=0
        ),
        name="fold_rows_near" if near else "fold_rows_far",
    )(table, *([dq] if near else []), *far)


def fold_weights_kernel(blocks, sources, size, rows, table_ref, mask_ref, embed_ref, gain_ref, dq_ref, dh_ref, *refs):
    refs = list(refs)
    take = lambda n: [refs.pop(0) for _ in range(n)]
    own_hbm, other_hbm, tiles, hbm = take(blocks), take(blocks), take(sources), take(4)
    piece_refs, noisy_ref, dembed_ref = take(2), *take(2)
    x_ref, a_ref, own_ref, other_ref = take(4)
    grads, sems = take(4), refs[0]
    half = own_ref.shape[1] // 3
    cuts = [slice(n * half, (n + 1) * half) for n in range(3)]
    first = tiled([tiles[0]] + tiles, x_ref, rows)
    second = list(zip(hbm, grads))
    third = placed(own_hbm, own_ref, size, table_ref, 0) + placed(other_hbm, other_ref, size, table_ref, 0)
    copies = fetch(first + second + third, sems)
    for copy in copies[: len(first)]:
        copy.wait()
    masked = column(mask_ref[...].astype(F32)) > 0
    noisy_rows = slice(rows, 2 * rows)
    x_ref[noisy_rows, :] = jnp.where(masked, embed_ref[...], x_ref[noisy_rows, :].astype(F32)).astype(BF)
    for t in range(x_ref.shape[0] // rows):
        at = slice(t * rows, (t + 1) * rows)
        a_ref[at, :] = (normed(x_ref[at, :].astype(F32))[0] * gain_ref[...]).astype(BF)
    for copy in copies[len(first) :]:
        copy.wait()
    there, total = grads[0].shape[1], x_ref.shape[0]
    da = None
    for n, w_ref in enumerate((own_ref, other_ref)):
        part = matmul_t(side(grads[0], n, noisy_rows), w_ref[:, cuts[1]]) + matmul_t(
            side(grads[1], n, noisy_rows), w_ref[:, cuts[2]]
        )
        part = part + matmul_t(dq_ref[noisy_rows, cuts[n]], w_ref[:, cuts[0]])
        da = part if da is None else da + part
    hat, scale = normed(x_ref[noisy_rows, :].astype(F32))
    noisy = dh_ref[...] + norm_back(hat, scale, gain_ref[...], da)
    noisy_ref[...] = noisy
    dembed_ref[...] = jnp.sum(jnp.where(masked, noisy, 0.0), axis=0, keepdims=True)
    for n in range(2):
        piece_refs[n][:, cuts[0]] = t_matmul(a_ref[0 : 2 * rows, :], dq_ref[:, cuts[n]]).astype(BF)
        for m in range(2):
            piece_refs[n][:, cuts[m + 1]] = (
                t_matmul(a_ref[0:there, :], side(grads[m], n, slice(0, there)))
                + t_matmul(a_ref[there:total, :], side(grads[m + 2], n, slice(0, total - there)))
            ).astype(BF)


def fold_weights(table, tiles, near, far, dh, mask, embed, gain, own, other):
    rows, width = tiles[0].shape
    total = (len(tiles) + 1) * rows
    count = sum(v.shape[0] for v in own)
    columns = own[0].shape[2]
    whole = lambda shape: spec(shape, lambda t, i: (0,) * len(shape))
    outs = [((width, columns), BF)] * 2 + [((rows, width), F32), ((1, width), F32)]
    grads = [near[1], near[2], far[1], far[2]]
    distant = list(own) + list(other) + list(tiles) + grads
    return pl.pallas_call(
        functools.partial(fold_weights_kernel, len(own), len(tiles), width // count, rows),
        grid_spec=pltpu.PrefetchScalarGridSpec(
            num_scalar_prefetch=1,
            grid=(1,),
            in_specs=[whole(v.shape) for v in (mask, embed, gain, near[0])]
            + [spec((rows, width), lambda t, i: (1, 0))]
            + [pl.BlockSpec(memory_space=pl.ANY)] * len(distant),
            out_specs=[whole(shape) for shape, _ in outs],
            scratch_shapes=[
                pltpu.VMEM((total, width), BF),
                pltpu.VMEM((total, width), BF),
                pltpu.VMEM((width, columns), BF),
                pltpu.VMEM((width, columns), BF),
            ]
            + [pltpu.VMEM(v.shape, BF) for v in grads]
            + [pltpu.SemaphoreType.DMA((2 * count + len(tiles) + 5,))],
        ),
        out_shape=[jax.ShapeDtypeStruct(shape, kind) for shape, kind in outs],
        compiler_params=vmem(44 if total <= 10 * rows else 58),
        cost_estimate=pl.CostEstimate(
            flops=4 * total * width * width, bytes_accessed=2 * (4 * total * width + 6 * width * width), transcendentals=0
        ),
        name="fold_weights",
    )(table, mask, embed, gain, near[0], dh, *distant)


def normalise(values):
    centred = values - jnp.mean(values, axis=-1, keepdims=True)
    spread = jnp.mean(centred * centred, axis=-1, keepdims=True)
    scale = lax.rsqrt(spread + EPSILON)
    return centred * scale, scale


def norm_back(hat, scale, gain, grad):
    scaled = grad * gain
    return scale * (
        scaled
        - jnp.mean(scaled, axis=-1, keepdims=True)
        - hat * jnp.mean(scaled * hat, axis=-1, keepdims=True)
    )


ROOT = math.sqrt(2.0 / math.pi)


def gelu_parts(u):
    t = jnp.tanh(ROOT * (u + 0.044715 * (u * u * u)))
    slope = 0.5 * (1.0 + t) + 0.5 * u * (1.0 - t * t) * (ROOT * (1.0 + 3 * 0.044715 * (u * u)))
    return 0.5 * u * (1.0 + t), slope


def mm(a, b):
    return jnp.dot(a, b, preferred_element_type=F32)


def mm_t(a, b):
    return lax.dot_general(a, b, (((1,), (1,)), ((), ())), preferred_element_type=F32)


def t_mm(a, b):
    return lax.dot_general(a, b, (((0,), (0,)), ((), ())), preferred_element_type=F32)


def halves_of_heads(w):
    w = w.reshape(w.shape[0], 3, 2, -1)
    return w[:, :, 0].reshape(w.shape[0], -1), w[:, :, 1].reshape(w.shape[0], -1)


def heads_of_halves(a, b):
    a, b = a.reshape(a.shape[0], 3, -1), b.reshape(b.shape[0], 3, -1)
    return jnp.stack([a, b], 2).reshape(a.shape[0], -1)


def halves_of_units(w, chunk):
    w = w.reshape(w.shape[0], -1, 2, chunk)
    return w[:, :, 0].reshape(w.shape[0], -1), w[:, :, 1].reshape(w.shape[0], -1)


def units_of_halves(a, b, chunk):
    a, b = a.reshape(a.shape[0], -1, chunk), b.reshape(b.shape[0], -1, chunk)
    return jnp.stack([a, b], 2).reshape(a.shape[0], -1)


def lower_in_chain(leaf):
    z, y = lax.shift_right_logical(leaf, 1), leaf & 1
    below = [((2 * (z - s) + at), z >= s) for s in (1, 2, 3) for at in (y, 1 - y)]
    return below[:2] + [(2 * z, y == 1)] + below[2:]


class Chain:
    near = 5

    def __init__(self, rows):
        self.at = Links()
        self.rows = rows
        self.core = self.at.core

    def lower(self, leaf):
        return lower_in_chain(leaf)

    def places(self):
        at = self.at
        n = jnp.arange(4)
        zyx = ((at.z ^ n)[None, None, :] * 2 + (at.y ^ n[:2])[None, :, None]) * 2 + (at.x ^ n[:2])[:, None, None]
        yzx = ((at.z ^ n)[None, :, None] * 2 + (at.y ^ n[:2])[:, None, None]) * 2 + (at.x ^ n[:2])[None, None, :]
        first = zyx.reshape(16)
        columns = jnp.where(jnp.arange(16) % 2 == 0, at.core, 1 - at.core)
        return jnp.stack([first, first ^ (8 * at.core), yzx.reshape(16), columns]).astype(jnp.int32)

    def first_gather(self, hid, w_qkv, w_out, w_up, w_down, vectors, facts, early):
        at = self.at
        few, chunk, cut = w_qkv.shape[0], w_down.shape[0], w_out.shape[1] // 2
        qkv_a, qkv_b = halves_of_heads(w_qkv)
        row = jnp.pad(vectors, ((0, 7), (0, qkv_a.shape[1] - vectors.shape[1])))
        qkv_a, qkv_b = (jnp.concatenate([v, row], axis=0) for v in (qkv_a, qkv_b))
        block = to_column_half(at, qkv_a, qkv_b)
        spare = jnp.zeros((6, block.shape[1]), BF)
        block = jnp.concatenate(
            [block[:few], block[few + 8 : 2 * few + 8], block[few : few + 1], block[2 * few + 8 : 2 * few + 9], spare],
            axis=0,
        )[None]
        up_a, up_b = halves_of_units(w_up, chunk)
        one_a = jnp.concatenate([w_out[:, :cut], up_a], axis=1)
        one_b = jnp.concatenate([w_out[:, cut:], up_b], axis=1)
        block, hid_up, one_a, one_b = tie(block, hid, one_a, one_b)
        line = z_gather(at, block)
        beside = at.swap_y(hid_up, [(i, i + 1) for i in range(0, 8, 2)])
        one = to_column_half(at, one_a, one_b)[None]
        line, hid_up, one, beside, down_two, facts = tie(line, hid_up, one, beside, w_down, facts)
        first_hop = at.up(hid_up, 0, 2)
        plane = jnp.concatenate([line, at.swap_y(line)], axis=0)
        one_line = [one, at.swap_z(one, 1)]
        down_two = at.swap_x(down_two)
        turns = early(facts)
        first_hop, plane, one_line, down_two, turns = tie(first_hop, plane, one_line, down_two, turns)
        down_two = jnp.stack([w_down, down_two])[None]
        far = at.swap_x(plane)
        other = [at.swap_core(plane)]
        second_hop = at.up(first_hop, 1, 2)
        first_over = at.swap_y(first_hop, [(i, i ^ 1) for i in range(2, 8)])
        second_hop, first_over, other, one_line = tie(second_hop, first_over, other, one_line)
        third_hop = at.up(second_hop, 2, 2)
        second_over = at.swap_y(second_hop, [(i, i ^ 1) for i in range(4, 8)])
        one_line.append(at.swap_z(one_line[0], 2))
        third_hop, second_over, far, one_line = tie(third_hop, second_over, far, one_line)
        third_over = at.swap_y(third_hop, [(i, i ^ 1) for i in range(6, 8)])
        other.append(at.swap_core(far))
        one_line.append(at.swap_z(one_line[0], 3))
        m = 2 * few
        n = vectors.shape[1]
        vec = jnp.concatenate([plane[:, m : m + 2, :n], far[:, m : m + 2, :n]], axis=0).reshape(16, 2 * n)
        order = (self.places()[0][None, :] == jnp.arange(16)[:, None]).astype(BF)
        vec = mm(order, vec).reshape(32, -1)
        third_over, other, one_line, vec, down_two = tie(third_over, other, one_line, vec, down_two)
        line = jnp.concatenate(one_line, axis=0)
        lower = [first_hop, first_over, beside, second_hop, second_over, third_hop, third_over]
        return lower, ((plane, far), tuple(other)), vec, (line, down_two), turns

    def second_start(self, state):
        line, down_two = state
        return jnp.concatenate([line, self.at.swap_y(line)], axis=0), z_gather(self.at, down_two)

    def second_go_on(self, state):
        plane, line = state
        at = self.at
        near = line.reshape((8,) + line.shape[2:])
        one = (plane, at.swap_x(plane)), [at.swap_core(plane)]
        down = (near, at.swap_y(near)), [at.swap_core(near)]
        return one, down

    def second_end(self, state):
        return [(own, tuple(other + [self.at.swap_core(own[1])])) for own, other in state]

    def unit_bias(self, bias, chunk):
        a, b = halves_of_units(bias[None], chunk)
        return jnp.where(self.core == 0, a, b), jnp.where(self.core == 0, b, a)

    def unit_bias_back(self, own, other, chunk):
        a = jnp.where(self.core == 0, own, other)
        b = jnp.where(self.core == 0, other, own)
        return units_of_halves(a, b, chunk)[0]

    def backward(self, run):
        at = self.at
        rows = self.rows
        lower_z = lambda s: [(i, i ^ 1) for i in range(2 * s, 8)]
        down_other, rest_other = run.feed_other(self)
        down_got, rest_got = at.swap_core(down_other), at.swap_core(rest_other)
        down_own, rest_own = run.feed_own(self)
        by_x = lambda g: g.reshape(8, 2, g.shape[0] // 16, g.shape[1])
        by_y = lambda g: g.reshape(4, 2, 2, g.shape[0] // 16, g.shape[1])
        split_y = lambda g: g.reshape((4, 2) + g.shape[1:])
        down_keep, down_send = halve(at.x, by_x(down_own), by_x(down_got), 1)
        rest_keep, rest_send = halve(at.y, by_y(rest_own), by_y(rest_got), 1)
        down_keep, down_send, rest_keep, rest_send, run.grad_mixed = tie(
            down_keep, down_send, rest_keep, rest_send, run.grad_mixed
        )
        down_got, rest_got = at.swap_x(down_send), at.swap_y(rest_send)
        far = run.far_tiles()
        down_got, rest_got, far = tie(down_got, rest_got, far)
        down_keep, down_send = halve(at.y, split_y(down_keep), split_y(down_got), 1)
        rest_keep, rest_send = z_parts(at, rest_keep, rest_got)
        down_keep, down_send, rest_keep, rest_send, far = tie(down_keep, down_send, rest_keep, rest_send, far)
        down_got = at.swap_y(down_send)
        far_da = run.far_rows(far)
        tiles = [far_da[n * rows : (n + 1) * rows] for n in range(4)]
        over = jnp.concatenate([tiles[1], tiles[3]], axis=0)
        down_got, tiles, over, far = tie(down_got, tiles, over, far)
        over = at.swap_y(over, lower_z(2))
        rest_got = z_move(at, rest_send)
        near = run.near_tiles(far)
        rest_got, over, near, tiles, down_got = tie(rest_got, over, near, tiles, down_got)
        down_keep, down_send = z_parts(at, down_keep, down_got)
        rest = z_total(rest_keep, rest_got).astype(BF)
        rest_keep, rest_send = choose(at.x, rest, 0)
        cur = plus(tiles[2], over[rows:]).astype(BF)
        down_keep, down_send, rest_keep, rest_send, cur, near = tie(
            down_keep, down_send, rest_keep, rest_send, cur, near
        )
        cur = at.down(cur, 3, 3)
        down_got, rest_got = z_move(at, down_send), at.swap_x(rest_send)
        own, other, vec = run.weights(near, far)
        own, other, vec, cur, down_got, rest_got = tie(own, other, vec, cur, down_got, rest_got)
        own, other = self.qkv_pieces(own, other, vec)
        cur = (plus(tiles[0], over[:rows]) + cur.astype(F32)).astype(BF)
        own, other, cur, near = tie(own, other, cur, near)
        got = at.swap_core(other)
        cur = at.down(cur, 2, 3)
        clean, near_da = run.near_rows(near)
        got, cur, clean, near_da = tie(got, cur, clean, near_da)
        keep, send = halve(at.x, own, got, 1)
        keep, send, cur, near_da = tie(keep, send, cur, near_da)
        got = at.swap_x(send)
        first = at.swap_y(near_da[rows : 2 * rows], lower_z(1))
        beside = at.swap_y(near_da[2 * rows :], [(i, i - 1) for i in range(1, 8, 2)])
        sum_down = z_total(down_keep, down_got)
        sum_out, sum_up = self.join_rest(plus(rest_keep, rest_got), run.chunk, run.width)
        got, first, beside, sum_down, sum_out, sum_up = tie(got, first, beside, sum_down, sum_out, sum_up)
        keep, send = halve(at.y, split_y(keep), split_y(got), 1)
        cur = (plus(near_da[:rows], first) + cur.astype(F32)).astype(BF)
        keep, send, cur = tie(keep, send, cur)
        got, cur = at.swap_y(send), at.down(cur, 1, 3)
        got, cur = tie(got, cur)
        keep, send = z_parts(at, keep, got)
        keep, send = tie(keep, send)
        got = z_move(at, send)
        grad_hidden = run.last(clean + cur.astype(F32) + beside.astype(F32))
        got, grad_hidden = tie(got, grad_hidden)
        m = run.few * 2
        g = z_total(keep, got)
        sum_qkv = heads_of_halves(*from_column_half(at, g[:m]))
        return sum_down, sum_up, sum_out, sum_qkv, g[m, : run.vectors], grad_hidden

    def join_rest(self, g, chunk, width):
        a, b = from_column_half(self.at, g)
        cut = width // 2
        out = jnp.concatenate([a[:, :cut], b[:, :cut]], axis=1)
        return out, units_of_halves(a[:, cut:], b[:, cut:], chunk)

    def rest_pieces(self, out, up, other):
        half = out.shape[0] // 2
        core = 1 - self.core if other else self.core
        out = lax.dynamic_slice_in_dim(out, core * half, half, axis=1)
        out = jnp.where(self.core == 0, out, jnp.concatenate([out[half:], out[:half]], axis=0))
        return jnp.concatenate([out.astype(BF), up], axis=1)

    def qkv_pieces(self, own, other, vec):
        n = vec.shape[1]
        vec = vec.astype(BF).reshape(8, 2, 2, n)
        found = []
        for g, core in ((own, self.core), (other, 1 - self.core)):
            g = g.reshape(8, 2, g.shape[0] // 16, g.shape[1])
            rows = pick(vec, core, 2)[:, :, None]
            rows = jnp.pad(rows, ((0, 0), (0, 0), (0, 7), (0, g.shape[3] - n)))
            found.append(jnp.concatenate([g, rows], axis=2))
        return found


AXES = ("leaf", "fsdp")


class Whole:
    def __init__(self, rows, leaves, devices):
        self.rows, self.leaves, self.devices = rows, leaves, devices
        self.leaf = lax.axis_index("leaf")
        self.near = 2 + (leaves - 1) // 2

    def lower(self, leaf):
        return [(leaf - s, leaf >= s) for s in range(1, self.leaves)]

    def places(self):
        return jnp.array([[0, 0], [0, 0], [0, 0], [0, 1]], jnp.int32)

    def first_gather(self, hid, w_qkv, w_out, w_up, w_down, vectors, facts, early):
        tree = lax.all_gather(hid, "leaf", axis=0, tiled=False)
        lower = [pick(tree, jnp.maximum(leaf, 0), 0) for leaf, _ in self.lower(self.leaf)]
        every = lambda w: lax.all_gather(w, AXES, axis=0, tiled=True)
        qkv = tuple((v[None],) for v in halves_of_heads(every(w_qkv)))
        return lower, qkv, every(vectors), (every(w_out), every(w_up), every(w_down)), early(facts)

    def second_start(self, state):
        return state

    def second_go_on(self, state):
        return state

    def second_end(self, state):
        out_w, up_w, down_w = state
        half, cut = down_w.shape[0] // 2, out_w.shape[1] // 2
        one = tuple(
            (jnp.concatenate([out_w[:, n * cut : (n + 1) * cut], up_w[:, n * half : (n + 1) * half]], axis=1)[None],)
            for n in range(2)
        )
        return one, tuple((down_w[None, n * half : (n + 1) * half],) for n in range(2))

    def unit_bias(self, bias, chunk):
        half = bias.shape[0] // 2
        return bias[None, :half], bias[None, half:]

    def unit_bias_back(self, own, other, chunk):
        return jnp.concatenate([own, other], axis=1)[0]

    def scatter(self, g):
        return lax.psum_scatter(g.astype(F32), AXES, scatter_dimension=0, tiled=True)

    def rest_pieces(self, out, up, other):
        cut = out.shape[1] // 2
        return jnp.concatenate([out[:, cut:] if other else out[:, :cut], up.astype(F32)], axis=1)

    def backward(self, run):
        rows = self.rows
        down_other, rest_other = run.feed_other(self)
        down_own, rest_own = run.feed_own(self)
        far = run.far_tiles()
        far_da = run.far_rows(far)
        near = run.near_tiles(far)
        own, other, vec = run.weights(near, far)
        clean, near_da = run.near_rows(near)
        tiles = jnp.concatenate([clean.astype(BF), near_da, far_da], axis=0)
        tiles = tiles.reshape((self.leaves, rows) + tiles.shape[1:])
        order = [pick(tiles, (self.leaf - n) % self.leaves, 0) for n in range(self.leaves)]
        total = lax.psum_scatter(jnp.concatenate(order, axis=0), "leaf", scatter_dimension=0, tiled=True)
        cut = run.width // 2
        return (
            self.scatter(jnp.concatenate([down_own, down_other], axis=0)),
            self.scatter(jnp.concatenate([rest_own[:, cut:], rest_other[:, cut:]], axis=1)),
            self.scatter(jnp.concatenate([rest_own[:, :cut], rest_other[:, :cut]], axis=1)),
            self.scatter(heads_of_halves(own, other)),
            self.scatter(vec)[0],
            run.last(total.astype(F32)),
        )


class Backward:
    pass


def shards(
    leaves,
    groups,
    hidden,
    noise_mask,
    seg_blocks,
    parents,
    ln1_gain,
    w_qkv,
    w_out,
    ln2_gain,
    w_up,
    up_bias,
    w_down,
    down_bias,
    mask_embed,
    cotangent,
):
    rows = hidden.shape[1]
    width = hidden.shape[2]
    half = width // 2
    devices = leaves * groups
    net = Chain(rows) if (leaves, groups) == (8, 4) else Whole(rows, leaves, devices)
    chunk = w_down.shape[0]
    few = ln1_gain.shape[0]
    leaf = lax.axis_index("leaf")

    hid = hidden[0]
    query_cols, query_rows, key_cols, key_rows, flags = tables(net.lower, leaf, seg_blocks, parents, rows)
    tiles = flags.shape[0]
    lanes = jnp.arange(128, dtype=jnp.int32)
    exponent = (lanes % (HEAD_DIM // 2)).astype(F32) * (-math.log(10000.0) / (HEAD_DIM // 2))

    def turns(facts):
        angles = facts[:, 2:3] * jnp.exp(exponent)
        sign = jnp.where((lanes % HEAD_DIM) < HEAD_DIM // 2, -1.0, 1.0)
        return jnp.cos(angles), jnp.sin(angles) * sign

    places = net.places()

    length = 4 * few + up_bias.shape[0]
    vectors = sum(
        jnp.pad(v[None], ((0, 0), (n * few, length - n * few - v.shape[0])))
        for n, v in enumerate((ln1_gain, ln2_gain, down_bias, mask_embed, up_bias))
    )
    lower, qkv_w, vec, coming, (cosine, sine) = net.first_gather(
        hid, w_qkv, w_out, w_up, w_down, vectors, key_cols, turns
    )
    gain_one, gain_two, down_b, embed = (
        vec[:, n * few : (n + 1) * few].reshape(1, width).astype(F32) for n in range(4)
    )
    up_b = jnp.concatenate(net.unit_bias(vec[:, 4 * few :].reshape(-1).astype(F32), chunk), axis=0)
    coming = net.second_start(coming)
    query, key, value = project(
        places, [hid] + lower, noise_mask, embed, gain_one, qkv_w[0], qkv_w[1], cosine, sine
    )
    coming, query = tie(coming, query)
    coming = net.second_go_on(coming)
    mixed, log_norm = attend(flags, query_cols, key_rows, query, key, value, rows)
    coming, mixed = tie(coming, mixed)
    one_w, down_w = net.second_end(coming)
    norm_rows = log_norm.T
    grad_two = cotangent[0].reshape(2 * rows, width)
    (
        output, normed_two, act, grad_pre, grad_one, grad_mixed, grad_after, grad_up_b, grad_down_b,
    ) = middle(places, mixed, hid, noise_mask, embed, grad_two, gain_two, up_b, down_b, one_w, down_w)
    output = output.reshape(1, 2, rows, width)
    units = act.shape[1] // 2

    run = Backward()
    run.chunk, run.few, run.vectors, run.grad_mixed, run.width = chunk, few, length - 2 * few, grad_mixed, width
    cut = net.near

    def feed(n, net):
        at = slice(n * units, (n + 1) * units)
        down, up = t_mm(act[:, at], grad_two).astype(BF), t_mm(normed_two, grad_pre[:, at]).astype(BF)
        return down, net.rest_pieces(t_mm(mixed, grad_one), up, n == 1)

    def far_tiles():
        return attend_back(
            cut, tiles, flags, query_rows, key_rows, query, key, value, mixed, run.grad_mixed, norm_rows, cosine, sine, rows
        )

    def far_rows(far):
        return fold_rows(places, far[1], far[2], qkv_w[0], qkv_w[1], rows)[0]

    def near_tiles(far):
        return attend_back(
            0, cut, flags, query_rows, key_rows, query, key, value, mixed, run.grad_mixed, norm_rows, cosine, sine, rows, far[0]
        )

    def weights(near, far):
        own, other, run.noisy, grad_embed = fold_weights(
            places, [hid] + lower, near, far, grad_after, noise_mask, embed, gain_one, qkv_w[0], qkv_w[1]
        )
        parts = (grad_down_b, grad_embed, net.unit_bias_back(grad_up_b[:1], grad_up_b[1:], chunk))
        return own, other, jnp.concatenate([v.reshape(devices, -1) for v in parts], axis=1)

    def near_rows(near):
        return fold_rows(places, near[1], near[2], qkv_w[0], qkv_w[1], rows, near[0])

    def last(total):
        hat, scale = normalise(hid.astype(F32))
        masked = (noise_mask[0] == 1)[:, None]
        clean = grad_after[:rows] + norm_back(hat, scale, gain_one, total)
        return (clean + jnp.where(masked, 0.0, run.noisy)).astype(BF)[None]

    run.feed_own = lambda net: feed(0, net)
    run.feed_other = lambda net: feed(1, net)
    run.far_tiles, run.far_rows, run.near_tiles, run.near_rows = far_tiles, far_rows, near_tiles, near_rows
    run.weights, run.last = weights, last
    sum_down, sum_up, sum_out, sum_qkv, sum_vec, grad_hidden = net.backward(run)
    from_weight = lambda w, g, gain: jnp.sum(w.astype(F32) * g, axis=1) / gain.astype(F32)
    return (
        output,
        grad_hidden,
        from_weight(w_qkv, sum_qkv, ln1_gain),
        sum_qkv,
        sum_out,
        from_weight(w_up, sum_up, ln2_gain),
        sum_up,
        sum_vec[2 * few :],
        sum_down,
        sum_vec[:few],
        sum_vec[few : 2 * few],
    )


def solution(mesh):
    split = ("leaf", "fsdp")
    in_specs = (
        P("fsdp", "leaf", None),
        P("fsdp", "leaf"),
        P("fsdp", None),
        P("fsdp", None),
        P(split),
        P(split, None),
        P(split, None),
        P(split),
        P(split, None),
        P(split),
        P(split, None),
        P(split),
        P(split),
        P("fsdp", None, "leaf", None),
    )
    out_specs = (
        P("fsdp", None, "leaf", None),
        P("fsdp", "leaf", None),
        P(split),
        P(split, None),
        P(split, None),
        P(split),
        P(split, None),
        P(split),
        P(split, None),
        P(split),
        P(split),
    )
    body = functools.partial(shards, mesh.shape["leaf"], mesh.shape["fsdp"])
    return jax.shard_map(body, mesh=mesh, in_specs=in_specs, out_specs=out_specs, check_vma=False)
```

```python
import functools
import math

import jax
import jax.numpy as jnp
from jax import lax
from jax.experimental import pallas as pl
from jax.experimental.pallas import tpu as pltpu
from jax.sharding import PartitionSpec as P

HEAD_DIM = 64
BLOCK = 16
NEG_FILL = -1000000000.0
EPSILON = 1e-05


def vmem(mebibytes):
    return pltpu.CompilerParams(vmem_limit_bytes=mebibytes * 2**20)


BF = jnp.bfloat16
F32 = jnp.float32


class Links:
    def __init__(self):
        leaf = lax.axis_index("leaf")
        fsdp = lax.axis_index("fsdp")
        self.z, self.y = leaf // 2, leaf % 2
        self.x, self.core = fsdp // 2, fsdp % 2

    def swap_core(self, v):
        return lax.ppermute(v, "fsdp", [(i, i ^ 1) for i in range(4)])

    def swap_x(self, v):
        return lax.ppermute(v, "fsdp", [(i, i ^ 2) for i in range(4)])

    def swap_y(self, v, pairs=None):
        return lax.ppermute(v, "leaf", pairs or [(i, i ^ 1) for i in range(8)])

    def swap_z(self, v, n):
        return lax.ppermute(v, "leaf", [(i, i ^ (2 * n)) for i in range(8)])

    def up(self, v, first, last):
        return lax.ppermute(v, "leaf", [(i, i + 2) for i in range(2 * first, 2 * last + 2)])

    def down(self, v, first, last):
        return lax.ppermute(v, "leaf", [(i, i - 2) for i in range(2 * first, 2 * last + 2)])


def both(bit, own, other, axis):
    return jnp.where(
        bit == 0, jnp.stack([own, other], axis), jnp.stack([other, own], axis)
    )


def tie(*values):
    flat, tree = jax.tree.flatten(values)
    return jax.tree.unflatten(tree, lax.optimization_barrier(tuple(flat)))


def z_gather(at, block):
    return jnp.concatenate([block] + [at.swap_z(block, n) for n in (1, 2, 3)], axis=0)


def pick(v, index, axis):
    return lax.dynamic_index_in_dim(v, index, axis, keepdims=False)


def choose(bit, v, axis):
    return pick(v, bit, axis), pick(v, 1 - bit, axis)


def plus(a, b):
    return a.astype(F32) + b.astype(F32)


def joined(mine, got, index, axis):
    return plus(pick(mine, index, axis), pick(got, index, axis)).astype(BF)


def halve(bit, mine, got, axis):
    return joined(mine, got, bit, axis), joined(mine, got, 1 - bit, axis)


def z_parts(at, mine, got):
    return joined(mine, got, at.z, 0), [joined(mine, got, at.z ^ n, 0) for n in (1, 2, 3)]


def z_move(at, parts):
    return [at.swap_z(part, n) for n, part in zip((1, 2, 3), parts)]


def z_total(keep, got):
    return plus(keep, got[0]) + plus(got[1], got[2])


def to_column_half(at, half_a, half_b):
    keep = jnp.where(at.core == 0, half_a, half_b)
    send = jnp.where(at.core == 0, half_b, half_a)
    got = at.swap_core(send)
    return both(at.core, keep, got, 0).reshape(2 * keep.shape[0], keep.shape[1])


def from_column_half(at, g):
    g = g.reshape(2, g.shape[0] // 2, g.shape[1])
    keep, send = choose(at.core, g, 0)
    got = at.swap_core(send)
    return jnp.where(at.core == 0, keep, got), jnp.where(at.core == 0, got, keep)


def spec(shape, index_map):
    return pl.BlockSpec(shape, index_map)


def turn(values, cosine, sine):
    lane = lax.broadcasted_iota(jnp.int32, (values.shape[0], 128), 1)
    low_half = (lane % HEAD_DIM) < HEAD_DIM // 2
    groups = []
    for n in range(values.shape[1] // 128):
        part = values[:, n * 128 : (n + 1) * 128]
        swapped = jnp.where(low_half, pltpu.roll(part, 96, 1), pltpu.roll(part, 32, 1))
        groups.append(part * cosine + swapped * sine)
    return groups


def column(row):
    return jnp.broadcast_to(row, (8, row.shape[1])).T[:, :1]


def tables_kernel(places, rows, leaf_ref, seg_ref, parent_ref, qcol_ref, qrow_ref, kcol_ref, krow_ref, flag_ref, pad_ref):
    leaf = leaf_ref[0]
    blocks = rows // BLOCK
    slots = 16
    seg = column(seg_ref[...].astype(F32))
    lane = lax.broadcasted_iota(jnp.int32, (seg.shape[0], 128), 1).astype(F32)
    length = jnp.sum(jnp.where(seg == lane, 1.0, 0.0), axis=0, keepdims=True)
    start = jnp.sum(jnp.where(seg < lane, 1.0, 0.0), axis=0, keepdims=True)
    pad_ref[...] = jnp.zeros_like(pad_ref)
    pad_ref[0:1, 0 : parent_ref.shape[1]] = parent_ref[...].astype(F32)
    parent_row = pad_ref[0:1, :]
    lane = lax.broadcasted_iota(jnp.int32, (slots, 128), 1).astype(F32)
    slot = lax.broadcasted_iota(jnp.int32, (slots, 1), 0).astype(F32)
    parent = column(parent_row)[:slots]
    look = lambda index, row: jnp.sum(jnp.where(index == lane, row, 0.0), axis=1, keepdims=True)
    grand = look(parent, parent_row)
    start = look(slot, start)
    shift = jnp.where(slot > 0, look(parent, length), 0.0) + jnp.where(parent > 0, look(grand, length), 0.0) - start

    def facts(block):
        own = jnp.sum(jnp.where(block >= start, 1.0, 0.0), axis=0, keepdims=True) - 1.0
        take = lambda col: jnp.sum(jnp.where(slot == own, col, 0.0), axis=0, keepdims=True)
        return own, take(parent), take(grand), take(shift)

    token = lax.broadcasted_iota(jnp.int32, (1, rows), 1)
    zero = jnp.zeros((1, rows), F32)
    tiles = [(leaf, leaf >= 0), (leaf, leaf < 0)] + places(leaf)
    for t, (place, valid) in enumerate(tiles):
        first = jnp.maximum(place, 0) * blocks
        block = (first + lax.shift_right_logical(token, 4)).astype(F32)
        own, one, two, move = facts(block)
        position = (move + block) * BLOCK + (token & (BLOCK - 1)).astype(F32)
        at = slice(t * rows, (t + 1) * rows)
        if t < 2:
            limit = block + (1.0 if t == 0 else 0.0)
            lines = jnp.concatenate([own, one, two, limit, zero, zero, zero, zero], axis=0)
            qrow_ref[:, at] = lines
            qcol_ref[at, :] = lines.T
        lines = jnp.concatenate(
            [jnp.where(valid, own, -1.0), block, position, zero, zero, zero, zero, zero], axis=0
        )
        krow_ref[:, at] = lines
        kcol_ref[at, :] = lines.T
    queries = qcol_ref[pl.ds(0, 2 * blocks, stride=BLOCK), :]
    lane = lax.broadcasted_iota(jnp.int32, (1, 128), 1)
    for t, (place, valid) in enumerate(tiles):
        if t < 2:
            flag_ref[t] = 1
            continue
        block = (jnp.maximum(place, 0) * blocks + lane).astype(F32)
        own = facts(block)[0]
        allowed = (
            ((own == queries[:, 0:1]) | (own == queries[:, 1:2]) | (own == queries[:, 2:3]))
            & (block < queries[:, 3:4])
            & (lane < blocks)
            & valid
        )
        flag_ref[t] = jnp.max(jnp.where(allowed, 1.0, 0.0)).astype(jnp.int32)


def tables(places, leaf, seg, parent, rows):
    tiles = 2 + len(places(leaf))
    total = tiles * rows
    smem = pl.BlockSpec(memory_space=pltpu.SMEM)
    vmem = pl.BlockSpec(memory_space=pltpu.VMEM)
    shapes = [(2 * rows, 8), (8, 2 * rows), (total, 8), (8, total)]
    return pl.pallas_call(
        functools.partial(tables_kernel, places, rows),
        in_specs=[smem, vmem, vmem],
        out_specs=[vmem] * 4 + [smem],
        out_shape=[jax.ShapeDtypeStruct(shape, F32) for shape in shapes] + [jax.ShapeDtypeStruct((tiles,), jnp.int32)],
        name="tables",
        scratch_shapes=[pltpu.VMEM((8, 128), F32)],
    )(leaf.reshape(1), seg, parent)


def fetch(pieces, sems):
    copies = [pltpu.make_async_copy(src, dst, sems.at[n]) for n, (src, dst) in enumerate(pieces)]
    for copy in copies:
        copy.start()
    return copies


def placed(blocks, ref, size, table, row):
    pieces = []
    for hbm in blocks:
        for n in range(hbm.shape[0]):
            place = pl.multiple_of(table[row, len(pieces)] * size, size)
            pieces.append((hbm.at[n, pl.ds(0, size), :], ref.at[pl.ds(place, size), :]))
    return pieces


def tiled(sources, ref, rows):
    return [(src, ref.at[pl.ds(n * rows, rows), :]) for n, src in enumerate(sources)]


def project_kernel(
    blocks, sources, size, rows, table_ref, mask_ref, embed_ref, gain_ref, cos_ref, sin_ref, *refs,
):
    own_hbm, other_hbm, tiles = refs[:blocks], refs[blocks : 2 * blocks], refs[2 * blocks : 2 * blocks + sources]
    q_ref, k_ref, v_ref, x_ref, own_ref, other_ref, sems = refs[2 * blocks + sources :]
    tile = pl.program_id(0)
    step = k_ref.shape[1]

    @pl.when(tile == 0)
    def _():
        pieces = tiled([tiles[0]] + list(tiles), x_ref, rows)
        count = len(pieces)
        pieces += placed(own_hbm, own_ref, size, table_ref, 0) + placed(other_hbm, other_ref, size, table_ref, 0)
        copies = fetch(pieces, sems)
        for copy in copies[:count]:
            copy.wait()
        masked = column(mask_ref[...].astype(F32)) > 0
        x_ref[rows : 2 * rows, :] = jnp.where(masked, embed_ref[...], x_ref[rows : 2 * rows, :].astype(F32)).astype(BF)
        for copy in copies[count:]:
            copy.wait()

    x = x_ref[pl.ds(pl.multiple_of(tile * step, step), step), :].astype(F32)
    centred = x - jnp.mean(x, axis=-1, keepdims=True)
    spread = jnp.mean(centred * centred, axis=-1, keepdims=True)
    a = (centred * lax.rsqrt(spread + EPSILON) * gain_ref[...]).astype(BF)
    cosine, sine = cos_ref[...], sin_ref[...]
    half = own_ref.shape[1] // 3
    for n, w_ref in enumerate((own_ref, other_ref)):
        base = n * half
        keys = jnp.dot(a, w_ref[:, half : 2 * half], preferred_element_type=F32)
        values = jnp.dot(a, w_ref[:, 2 * half :], preferred_element_type=F32)
        for g, part in enumerate(turn(keys, cosine, sine)):
            k_ref[base // 128 + g] = part.astype(BF)
            v_ref[base // 128 + g] = values[:, g * 128 : (g + 1) * 128].astype(BF)

    @pl.when(tile * step < 2 * rows)
    def _():
        lines = q_ref.shape[0]
        for n, w_ref in enumerate((own_ref, other_ref)):
            base = n * half
            q = jnp.dot(a[:lines], w_ref[:, :half], preferred_element_type=F32)
            for g, part in enumerate(turn(q, cosine[:lines], sine[:lines])):
                q_ref[:, base + g * 128 : base + (g + 1) * 128] = part.astype(BF)


def project(table, tiles, mask, embed, gain, own, other, cosine, sine):
    rows, width = tiles[0].shape
    total = (len(tiles) + 1) * rows
    step = next(n for n in (3 * rows, 2 * rows, rows) if total % n == 0)
    q_step = min(step, 2 * rows)
    last_q = 2 * rows // q_step - 1
    count = sum(v.shape[0] for v in own)
    columns = own[0].shape[2]
    whole = lambda v: spec(v.shape, lambda t, i: (0, 0))
    moved = lambda n: spec((step, n), lambda t, i: (t, 0))
    pairs = spec((width // 128, step, 128), lambda t, i: (0, t, 0))
    out = lambda n: jax.ShapeDtypeStruct((n, width), BF)
    anywhere = pl.BlockSpec(memory_space=pl.ANY)
    far = list(own) + list(other) + list(tiles)
    return pl.pallas_call(
        functools.partial(project_kernel, len(own), len(tiles), width // count, rows),
        grid_spec=pltpu.PrefetchScalarGridSpec(
            num_scalar_prefetch=1,
            grid=(total // step,),
            in_specs=[whole(mask), whole(embed), whole(gain), moved(128), moved(128)] + [anywhere] * len(far),
            out_specs=[
                spec((q_step, width), lambda t, i: (jnp.minimum(t, last_q), 0)),
                pairs,
                pairs,
            ],
            scratch_shapes=[
                pltpu.VMEM((total, width), BF),
                pltpu.VMEM((width, columns), BF),
                pltpu.VMEM((width, columns), BF),
                pltpu.SemaphoreType.DMA((2 * count + len(tiles) + 1,)),
            ],
        ),
        out_shape=[out(2 * rows)] + [jax.ShapeDtypeStruct((width // 128, total, 128), BF)] * 2,
        compiler_params=vmem(26 if total <= 10 * rows else 40),
        cost_estimate=pl.CostEstimate(
            flops=2 * total * width * 2 * width + 4 * rows * width * width,
            bytes_accessed=2 * (3 * total * width + 3 * width * width),
            transcendentals=0,
        ),
        name="project",
    )(table, mask, embed, gain, cosine, sine, *far)


def middle_kernel(
    blocks_one, blocks_two, size, chunk, table_ref, o_ref, x_ref, mask_ref, embed_ref, dy_ref, gain_ref, up_b_ref,
    down_b_ref, *refs,
):
    refs = list(refs)
    take = lambda n: [refs.pop(0) for _ in range(n)]
    ones, twos = (take(blocks_one), take(blocks_one)), (take(blocks_two), take(blocks_two))
    y_ref, b_ref, g_ref, du_ref, dh_low_ref, do_ref, dh_ref, dup_b_ref, ddown_b_ref = take(9)
    out_ref, up_ref, down_ref, sems = refs
    cut = out_ref.shape[1] // 2
    units = up_ref.shape[2]
    pieces_out, pieces = [], []
    for n in range(2):
        columns = pl.ds(pl.multiple_of(table_ref[3, n] * cut, cut), cut)
        spots = [(hbm, j) for hbm in ones[n] for j in range(hbm.shape[0])]
        pieces.append([])
        for place, (hbm, j) in enumerate(spots):
            to = pl.ds(pl.multiple_of(table_ref[1, place] * size, size), size)
            pieces_out.append((hbm.at[j, :, pl.ds(0, cut)], out_ref.at[to, columns]))
            to = pl.ds(pl.multiple_of(table_ref[0, place] * size, size), size)
            pieces[n].append((hbm.at[j, :, pl.ds(cut, units)], up_ref.at[n, to, :]))
        pieces[n] += placed(twos[n], down_ref.at[n], chunk, table_ref, 2)
    copies = fetch(pieces_out + pieces[0] + pieces[1], sems)
    for copy in copies[: len(pieces_out)]:
        copy.wait()
    x = x_ref[...].astype(F32)
    masked = column(mask_ref[...].astype(F32)) > 0
    x = jnp.concatenate([x, jnp.where(masked, embed_ref[...], x)], axis=0)
    h = x + jnp.dot(o_ref[...], out_ref[...], preferred_element_type=F32)
    centred = h - jnp.mean(h, axis=-1, keepdims=True)
    spread = jnp.mean(centred * centred, axis=-1, keepdims=True)
    scale = lax.rsqrt(spread + EPSILON)
    hat = centred * scale
    b = (hat * gain_ref[...]).astype(BF)
    b_ref[...] = b
    dy = dy_ref[...]
    ddown_b_ref[...] = jnp.sum(dy.astype(F32), axis=0, keepdims=True)
    y = h + down_b_ref[...]
    db = None
    wide = next(n for n in (768, 512, 384, 256, 128) if units % n == 0)
    for n in range(2):
        done = len(pieces_out) + n * len(pieces[0])
        for copy in copies[done : done + len(pieces[n])]:
            copy.wait()
        for c in range(0, units, wide):
            at = slice(c, c + wide)
            to = slice(n * units + c, n * units + c + wide)
            u = jnp.dot(b, up_ref[n, :, at], preferred_element_type=F32) + up_b_ref[n : n + 1, at]
            g, slope = gelu_parts(u)
            g = g.astype(BF)
            g_ref[:, to] = g
            y = y + jnp.dot(g, down_ref[n, at, :], preferred_element_type=F32)
            du = (matmul_t(dy, down_ref[n, at, :]) * slope).astype(BF)
            du_ref[:, to] = du
            dup_b_ref[n : n + 1, at] = jnp.sum(du.astype(F32), axis=0, keepdims=True)
            part = matmul_t(du, up_ref[n, :, at])
            db = part if db is None else db + part
    y_ref[...] = y.astype(BF)
    dh = dy.astype(F32) + norm_back(hat, scale, gain_ref[...], db)
    dh_ref[...] = dh
    low = dh.astype(BF)
    dh_low_ref[...] = low
    do_ref[...] = matmul_t(low, out_ref[...]).astype(BF)


def middle(table, o, x, mask, embed, dy, gain, up_b, down_b, one, two):
    rows, width = o.shape
    count = sum(v.shape[0] for v in one[0])
    size, columns = one[0][0].shape[1:]
    chunk = two[0][0].shape[1]
    units = columns - width // 2
    full = lambda shape: spec(shape, lambda t, i: (0, 0))
    near = (o, x, mask, embed, dy, gain, up_b, down_b)
    far = list(one[0]) + list(one[1]) + list(two[0]) + list(two[1])
    shapes = [
        ((rows, width), BF), ((rows, width), BF), ((rows, 2 * units), BF), ((rows, 2 * units), BF), ((rows, width), BF),
        ((rows, width), BF), ((rows, width), F32), ((2, units), F32), ((1, width), F32),
    ]
    return pl.pallas_call(
        functools.partial(middle_kernel, len(one[0]), len(two[0]), size, chunk),
        grid_spec=pltpu.PrefetchScalarGridSpec(
            num_scalar_prefetch=1,
            grid=(1,),
            in_specs=[full(v.shape) for v in near] + [pl.BlockSpec(memory_space=pl.ANY)] * len(far),
            out_specs=[full(shape) for shape, _ in shapes],
            scratch_shapes=[
                pltpu.VMEM((width, width), BF),
                pltpu.VMEM((2, width, units), BF),
                pltpu.VMEM((2, units, width), BF),
                pltpu.SemaphoreType.DMA((6 * count,)),
            ],
        ),
        out_shape=[jax.ShapeDtypeStruct(shape, kind) for shape, kind in shapes],
        compiler_params=vmem(44),
        cost_estimate=pl.CostEstimate(
            flops=2 * rows * width * (2 * width + 8 * units),
            bytes_accessed=4 * (width * width + 4 * units * width),
            transcendentals=2 * rows * units,
        ),
        name="middle",
    )(table, *near, *far)


def matmul_t(a, b):
    return lax.dot_general(a, b, (((1,), (1,)), ((), ())), preferred_element_type=F32)


def groups(tiles, first=2):
    found = [(first, first + 2)] if first == 2 else []
    found = [] if first > 2 else [(2, min(4, tiles))] + ([(4, 5)] if tiles > 4 else [])
    start = max(first, 5)
    return found + [(n, min(n + 2, tiles)) for n in range(start, tiles, 2)]


def attend_kernel(
    rows, tiles, flag_ref, qcol_ref, krow_ref, q_ref, k_ref, v_ref, o_ref, lse_ref,
    bias_ref, s_ref, top_ref, sum_ref, acc_ref,
):
    pair = pl.program_id(0)
    both_rows = 2 * rows

    def span(t):
        return slice(t * rows, (t + 1) * rows)

    def lines(t):
        return slice(rows, both_rows) if t == 1 else slice(0, both_rows)

    @pl.when(pair == 0)
    def _():
        lse_ref[...] = jnp.zeros_like(lse_ref)
        own = qcol_ref[:, 0:1]
        up_one = qcol_ref[:, 1:2]
        up_two = qcol_ref[:, 2:3]
        limit = qcol_ref[:, 3:4]
        for t in range(tiles):
            if t == 1:
                r = lax.broadcasted_iota(jnp.int32, (rows, rows), 0) // BLOCK
                c = lax.broadcasted_iota(jnp.int32, (rows, rows), 1) // BLOCK
                bias_ref[rows:, span(t)] = jnp.where(r == c, 0.0, NEG_FILL)
            else:
                seg = krow_ref[0:1, span(t)]
                index = krow_ref[1:2, span(t)]
                ok = ((seg == own) | (seg == up_one) | (seg == up_two)) & (index < limit)
                bias_ref[:, span(t)] = jnp.where(ok, 0.0, NEG_FILL)

    lane = lax.broadcasted_iota(jnp.int32, (both_rows, 128), 1)
    queries = [jnp.where((lane // HEAD_DIM) == h, q_ref[...] * 0.125, 0).astype(BF) for h in range(2)]
    top_ref[...] = jnp.full_like(top_ref, -3.0e38)

    def scores(first, last, at):
        cut = slice(first * rows, last * rows)
        keys = k_ref[0, cut, :]
        for h in range(2):
            s = matmul_t(queries[h][at], keys) + bias_ref[at, cut]
            s_ref[h, at, cut] = s
            best = top_ref[h, at, :]
            for c in range(s.shape[1] // 128):
                best = jnp.maximum(best, s[:, c * 128 : (c + 1) * 128])
            top_ref[h, at, :] = best

    def weigh(first, last, at):
        cut = slice(first * rows, last * rows)
        values = v_ref[0, cut, :]
        for h in range(2):
            p = jnp.exp(s_ref[h, at, cut] - tops[h][at])
            part = sum_ref[h, at, :]
            for c in range(p.shape[1] // 128):
                part = part + p[:, c * 128 : (c + 1) * 128]
            sum_ref[h, at, :] = part
            acc_ref[h, at, :] += jnp.dot(p.astype(BF), values, preferred_element_type=F32)

    upper, lower, all_rows = slice(0, rows), slice(rows, both_rows), slice(0, both_rows)

    def each(step):
        step(0, 1, upper)
        step(0, 2, lower)
        for first, last in groups(tiles):
            some = flag_ref[first]
            for t in range(first + 1, last):
                some = some + flag_ref[t]
            pl.when(some > 0)(functools.partial(step, first, last, all_rows))

    each(scores)
    tops = [jnp.max(top_ref[h], axis=-1, keepdims=True) for h in range(2)]
    sum_ref[...] = jnp.zeros_like(sum_ref)
    acc_ref[...] = jnp.zeros_like(acc_ref)
    each(weigh)
    outs, norms = [], lse_ref[...]
    for h in range(2):
        total = jnp.sum(sum_ref[h], axis=-1, keepdims=True)
        outs.append(acc_ref[h] / total)
        norms = jnp.where(lane == 2 * pair + h, tops[h] + jnp.log(total), norms)
    lse_ref[...] = norms
    o_ref[...] = jnp.where(lane < HEAD_DIM, outs[0], outs[1]).astype(BF)


def attend(flags, qcol, krow, q, k, v, rows):
    width = q.shape[1]
    total = k.shape[1]
    tiles = total // rows
    whole_pair = spec((1, total, 128), lambda p, f: (p, 0, 0))
    pair = lambda n: spec((n, 128), lambda p, f: (0, p))
    fixed = lambda shape: spec(shape, lambda p, f: (0, 0))
    return pl.pallas_call(
        functools.partial(attend_kernel, rows, tiles),
        grid_spec=pltpu.PrefetchScalarGridSpec(
            num_scalar_prefetch=1,
            grid=(width // 128,),
            in_specs=[fixed(qcol.shape), fixed(krow.shape), pair(2 * rows), whole_pair, whole_pair],
            out_specs=[pair(2 * rows), fixed((2 * rows, 128))],
            scratch_shapes=[
                pltpu.VMEM((2 * rows, total), F32),
                pltpu.VMEM((2, 2 * rows, total), F32),
                pltpu.VMEM((2, 2 * rows, 128), F32),
                pltpu.VMEM((2, 2 * rows, 128), F32),
                pltpu.VMEM((2, 2 * rows, 128), F32),
            ],
        ),
        out_shape=[
            jax.ShapeDtypeStruct((2 * rows, width), BF),
            jax.ShapeDtypeStruct((2 * rows, 128), F32),
        ],
        compiler_params=vmem(28 if tiles <= 10 else 52),
        cost_estimate=pl.CostEstimate(
            flops=16 * rows * total * width,
            bytes_accessed=4 * (total + rows) * width,
            transcendentals=2 * rows * total * width // HEAD_DIM,
        ),
        name="attend",
    )(flags, qcol, krow, q, k, v)


def attend_back_kernel(
    rows, first, last, flag_ref, qrow_ref, krow_ref, q_ref, k_ref, v_ref, o_ref, g_ref, lse_ref, *refs,
):
    refs = list(refs)
    near = first == 0
    cos_ref, sin_ref = refs[:2]
    part_ref = refs[2] if near else None
    dq_ref, dk_ref, dv_ref, bias_ref, acc_ref = refs[-5:]
    pair = pl.program_id(0)
    both_rows = 2 * rows

    def span(t):
        return slice(t * rows, (t + 1) * rows)

    @pl.when(pair == 0)
    def _():
        own = qrow_ref[0:1, :]
        up_one = qrow_ref[1:2, :]
        up_two = qrow_ref[2:3, :]
        limit = qrow_ref[3:4, :]
        for t in range(first, last):
            if t == 1:
                r = lax.broadcasted_iota(jnp.int32, (rows, both_rows), 0) // BLOCK
                c = lax.broadcasted_iota(jnp.int32, (rows, both_rows), 1) // BLOCK
                bias_ref[span(t - first), :] = jnp.where(r + rows // BLOCK == c, 0.0, NEG_FILL)
            else:
                facts = krow_ref[:, span(t - first)].T
                seg = facts[:, 0:1]
                index = facts[:, 1:2]
                ok = ((seg == own) | (seg == up_one) | (seg == up_two)) & (index < limit)
                bias_ref[span(t - first), :] = jnp.where(ok, 0.0, NEG_FILL)

    lane = lax.broadcasted_iota(jnp.int32, (both_rows, 128), 1)
    acc_ref[...] = part_ref[...] if near else jnp.zeros_like(acc_ref)
    queries, grads, deltas, norms, queries_t, grads_t = [], [], [], [], [], []
    product = (o_ref[...].astype(F32) * g_ref[...].astype(F32)).T
    for h in range(2):
        mine = (lane // HEAD_DIM) == h
        queries.append(jnp.where(mine, q_ref[...] * 0.125, 0).astype(BF))
        grads.append(jnp.where(mine, g_ref[...], 0).astype(BF))
        queries_t.append(queries[h].astype(F32).T.astype(BF))
        grads_t.append(grads[h].astype(F32).T.astype(BF))
        deltas.append(jnp.sum(product[h * HEAD_DIM : (h + 1) * HEAD_DIM], axis=0, keepdims=True))
        norms.append(lse_ref[pl.ds(2 * pair + h, 1), :])

    def step(start, end):
        to = slice((start - first) * rows, (end - first) * rows)
        keys, values = k_ref[0, to, :], v_ref[0, to, :]
        keys_t = keys.astype(F32).T.astype(BF)
        dk = dv = None
        for h in range(2):
            q, g = queries[h], grads[h]
            s = jnp.dot(keys, queries_t[h], preferred_element_type=F32) + bias_ref[to, :]
            p = jnp.exp(s - norms[h])
            dp = jnp.dot(values, grads_t[h], preferred_element_type=F32)
            ds = (p * (dp - deltas[h])).astype(BF)
            part_v = jnp.dot(p.astype(BF), g, preferred_element_type=F32)
            part_k = jnp.dot(ds, q, preferred_element_type=F32)
            dv = part_v if dv is None else dv + part_v
            dk = part_k if dk is None else dk + part_k
            half = slice(h * HEAD_DIM, (h + 1) * HEAD_DIM)
            acc_ref[half, :] += jnp.dot(keys_t[half], ds, preferred_element_type=F32)
        [dk] = turn(dk, cos_ref[to, :], -sin_ref[to, :])
        dk_ref[0, to, :] = dk.astype(BF)
        dv_ref[0, to, :] = dv.astype(BF)

    if near:
        step(0, 2)
    for start, end in groups(last, max(first, 2)):
        some = flag_ref[start]
        for t in range(start + 1, end):
            some = some + flag_ref[t]
        to = slice((start - first) * rows, (end - first) * rows)

        @pl.when(some == 0)
        def _():
            dk_ref[0, to, :] = jnp.zeros(((end - start) * rows, 128), BF)
            dv_ref[0, to, :] = jnp.zeros(((end - start) * rows, 128), BF)

        pl.when(some > 0)(functools.partial(step, start, end))

    if near:
        dq = acc_ref[...].T * 0.125
        [dq] = turn(dq, cos_ref[:both_rows, :], -sin_ref[:both_rows, :])
        dq_ref[...] = dq.astype(BF)
    else:
        dq_ref[...] = acc_ref[...]


def attend_back(first, last, flags, qrow, krow, q, k, v, o, g, lse, cosine, sine, rows, part=None):
    width = q.shape[1]
    there = (last - first) * rows
    near = first == 0
    some_pair = lambda n: spec((1, n, 128), lambda p, f: (p, 0, 0))
    taken_pair = spec((pl.Element(1), pl.Element(there), pl.Element(128)), lambda p, f: (p, first * rows, 0))
    taken = spec((pl.Element(there), pl.Element(128)), lambda p, f: (first * rows, 0))
    pair = lambda n: spec((n, 128), lambda p, f: (0, p))
    turned = spec((128, 2 * rows), lambda p, f: (p, 0))
    fixed = lambda shape: spec(shape, lambda p, f: (0, 0))
    out = lambda n: jax.ShapeDtypeStruct((n, width), BF)
    return pl.pallas_call(
        functools.partial(attend_back_kernel, rows, first, last),
        grid_spec=pltpu.PrefetchScalarGridSpec(
            num_scalar_prefetch=1,
            grid=(width // 128,),
            in_specs=[
                fixed(qrow.shape), spec((pl.Element(8), pl.Element(there)), lambda p, f: (0, first * rows)), pair(2 * rows),
                taken_pair, taken_pair, pair(2 * rows), pair(2 * rows), fixed(lse.shape), taken, taken,
            ] + ([turned] if near else []),
            out_specs=[pair(2 * rows) if near else turned, some_pair(there), some_pair(there)],
            scratch_shapes=[
                pltpu.VMEM((there, 2 * rows), F32),
                pltpu.VMEM((128, 2 * rows), F32),
            ],
        ),
        out_shape=[out(2 * rows) if near else jax.ShapeDtypeStruct((width, 2 * rows), F32)]
        + [jax.ShapeDtypeStruct((width // 128, there, 128), BF)] * 2,
        compiler_params=vmem(30 if there <= 5 * rows else 44),
        cost_estimate=pl.CostEstimate(
            flops=40 * rows * there * width,
            bytes_accessed=8 * (there + rows) * width,
            transcendentals=2 * rows * there * width // HEAD_DIM,
        ),
        name="attend_back_near" if near else "attend_back_far",
    )(flags, qrow, krow, q, k, v, o, g, lse, cosine, sine, *([part] if near else []))


def t_matmul(a, b):
    return lax.dot_general(a, b, (((0,), (0,)), ((), ())), preferred_element_type=F32)


def normed(x):
    centred = x - jnp.mean(x, axis=-1, keepdims=True)
    scale = lax.rsqrt(jnp.mean(centred * centred, axis=-1, keepdims=True) + EPSILON)
    return centred * scale, scale


def side(ref, n, at):
    pairs = ref.shape[0] // 2
    return jnp.concatenate([ref[n * pairs + p, at, :] for p in range(pairs)], axis=1)


def fold_rows_kernel(near, blocks, size, rows, table_ref, *refs):
    refs = list(refs)
    take = lambda n: [refs.pop(0) for _ in range(n)]
    if near:
        [dq_ref] = take(1)
    own_hbm, other_hbm, hbm = take(blocks), take(blocks), take(2)
    if near:
        [clean_ref] = take(1)
    da_ref, own_ref, other_ref = take(3)
    grads, sems = refs[:2], refs[2]
    half = own_ref.shape[1] // 3
    cuts = [slice(n * half, (n + 1) * half) for n in range(3)]
    pieces = list(zip(hbm, grads))
    pieces += placed(own_hbm, own_ref, size, table_ref, 0) + placed(other_hbm, other_ref, size, table_ref, 0)
    for copy in fetch(pieces, sems):
        copy.wait()
    first = 2 if near else 0
    for t in range(grads[0].shape[1] // rows):
        if near and t == 1:
            continue
        at = slice(t * rows, (t + 1) * rows)
        da = None
        for n, w_ref in enumerate((own_ref, other_ref)):
            part = matmul_t(side(grads[0], n, at), w_ref[:, cuts[1]]) + matmul_t(side(grads[1], n, at), w_ref[:, cuts[2]])
            if near and t == 0:
                part = part + matmul_t(dq_ref[at, cuts[n]], w_ref[:, cuts[0]])
            da = part if da is None else da + part
        if near and t == 0:
            clean_ref[...] = da
        else:
            da_ref[(t - first) * rows : (t - first + 1) * rows, :] = da.astype(BF)


def fold_rows(table, dk, dv, own, other, rows, dq=None):
    width = own[0].shape[2] * 2 // 3
    there = dk.shape[1]
    near = dq is not None
    count = sum(v.shape[0] for v in own)
    columns = own[0].shape[2]
    whole = lambda shape: spec(shape, lambda t, i: (0,) * len(shape))
    outs = ([((rows, width), F32)] if near else []) + [((there - (2 * rows if near else 0), width), BF)]
    far = list(own) + list(other) + [dk, dv]
    return pl.pallas_call(
        functools.partial(fold_rows_kernel, near, len(own), width // count, rows),
        grid_spec=pltpu.PrefetchScalarGridSpec(
            num_scalar_prefetch=1,
            grid=(1,),
            in_specs=([whole(dq.shape)] if near else []) + [pl.BlockSpec(memory_space=pl.ANY)] * len(far),
            out_specs=[whole(shape) for shape, _ in outs],
            scratch_shapes=[
                pltpu.VMEM((width, columns), BF),
                pltpu.VMEM((width, columns), BF),
                pltpu.VMEM(dk.shape, BF),
                pltpu.VMEM(dv.shape, BF),
                pltpu.SemaphoreType.DMA((2 * count + 2,)),
            ],
        ),
        out_shape=[jax.ShapeDtypeStruct(shape, kind) for shape, kind in outs],
        compiler_params=vmem(28 if there <= 5 * rows else 40),
        cost_estimate=pl.CostEstimate(
            flops=4 * there * width * width, bytes_accessed=2 * (3 * there * width + 3 * width * width), transcendentals=0
        ),
        name="fold_rows_near" if near else "fold_rows_far",
    )(table, *([dq] if near else []), *far)


def fold_weights_kernel(blocks, sources, size, rows, table_ref, mask_ref, embed_ref, gain_ref, dq_ref, dh_ref, *refs):
    refs = list(refs)
    take = lambda n: [refs.pop(0) for _ in range(n)]
    own_hbm, other_hbm, tiles, hbm = take(blocks), take(blocks), take(sources), take(4)
    piece_refs, noisy_ref, dembed_ref = take(2), *take(2)
    x_ref, a_ref, own_ref, other_ref = take(4)
    grads, sems = take(4), refs[0]
    half = own_ref.shape[1] // 3
    cuts = [slice(n * half, (n + 1) * half) for n in range(3)]
    first = tiled([tiles[0]] + tiles, x_ref, rows)
    second = list(zip(hbm, grads))
    third = placed(own_hbm, own_ref, size, table_ref, 0) + placed(other_hbm, other_ref, size, table_ref, 0)
    copies = fetch(first + second + third, sems)
    for copy in copies[: len(first)]:
        copy.wait()
    masked = column(mask_ref[...].astype(F32)) > 0
    noisy_rows = slice(rows, 2 * rows)
    x_ref[noisy_rows, :] = jnp.where(masked, embed_ref[...], x_ref[noisy_rows, :].astype(F32)).astype(BF)
    for t in range(x_ref.shape[0] // rows):
        at = slice(t * rows, (t + 1) * rows)
        a_ref[at, :] = (normed(x_ref[at, :].astype(F32))[0] * gain_ref[...]).astype(BF)
    for copy in copies[len(first) :]:
        copy.wait()
    there, total = grads[0].shape[1], x_ref.shape[0]
    da = None
    for n, w_ref in enumerate((own_ref, other_ref)):
        part = matmul_t(side(grads[0], n, noisy_rows), w_ref[:, cuts[1]]) + matmul_t(
            side(grads[1], n, noisy_rows), w_ref[:, cuts[2]]
        )
        part = part + matmul_t(dq_ref[noisy_rows, cuts[n]], w_ref[:, cuts[0]])
        da = part if da is None else da + part
    hat, scale = normed(x_ref[noisy_rows, :].astype(F32))
    noisy = dh_ref[...] + norm_back(hat, scale, gain_ref[...], da)
    noisy_ref[...] = noisy
    dembed_ref[...] = jnp.sum(jnp.where(masked, noisy, 0.0), axis=0, keepdims=True)
    for n in range(2):
        piece_refs[n][:, cuts[0]] = t_matmul(a_ref[0 : 2 * rows, :], dq_ref[:, cuts[n]]).astype(BF)
        for m in range(2):
            piece_refs[n][:, cuts[m + 1]] = (
                t_matmul(a_ref[0:there, :], side(grads[m], n, slice(0, there)))
                + t_matmul(a_ref[there:total, :], side(grads[m + 2], n, slice(0, total - there)))
            ).astype(BF)


def fold_weights(table, tiles, near, far, dh, mask, embed, gain, own, other):
    rows, width = tiles[0].shape
    total = (len(tiles) + 1) * rows
    count = sum(v.shape[0] for v in own)
    columns = own[0].shape[2]
    whole = lambda shape: spec(shape, lambda t, i: (0,) * len(shape))
    outs = [((width, columns), BF)] * 2 + [((rows, width), F32), ((1, width), F32)]
    grads = [near[1], near[2], far[1], far[2]]
    distant = list(own) + list(other) + list(tiles) + grads
    return pl.pallas_call(
        functools.partial(fold_weights_kernel, len(own), len(tiles), width // count, rows),
        grid_spec=pltpu.PrefetchScalarGridSpec(
            num_scalar_prefetch=1,
            grid=(1,),
            in_specs=[whole(v.shape) for v in (mask, embed, gain, near[0])]
            + [spec((rows, width), lambda t, i: (1, 0))]
            + [pl.BlockSpec(memory_space=pl.ANY)] * len(distant),
            out_specs=[whole(shape) for shape, _ in outs],
            scratch_shapes=[
                pltpu.VMEM((total, width), BF),
                pltpu.VMEM((total, width), BF),
                pltpu.VMEM((width, columns), BF),
                pltpu.VMEM((width, columns), BF),
            ]
            + [pltpu.VMEM(v.shape, BF) for v in grads]
            + [pltpu.SemaphoreType.DMA((2 * count + len(tiles) + 5,))],
        ),
        out_shape=[jax.ShapeDtypeStruct(shape, kind) for shape, kind in outs],
        compiler_params=vmem(44 if total <= 10 * rows else 58),
        cost_estimate=pl.CostEstimate(
            flops=4 * total * width * width, bytes_accessed=2 * (4 * total * width + 6 * width * width), transcendentals=0
        ),
        name="fold_weights",
    )(table, mask, embed, gain, near[0], dh, *distant)


def normalise(values):
    centred = values - jnp.mean(values, axis=-1, keepdims=True)
    spread = jnp.mean(centred * centred, axis=-1, keepdims=True)
    scale = lax.rsqrt(spread + EPSILON)
    return centred * scale, scale


def norm_back(hat, scale, gain, grad):
    scaled = grad * gain
    return scale * (
        scaled
        - jnp.mean(scaled, axis=-1, keepdims=True)
        - hat * jnp.mean(scaled * hat, axis=-1, keepdims=True)
    )


ROOT = math.sqrt(2.0 / math.pi)


def gelu_parts(u):
    t = jnp.tanh(ROOT * (u + 0.044715 * (u * u * u)))
    slope = 0.5 * (1.0 + t) + 0.5 * u * (1.0 - t * t) * (ROOT * (1.0 + 3 * 0.044715 * (u * u)))
    return 0.5 * u * (1.0 + t), slope


def mm(a, b):
    return jnp.dot(a, b, preferred_element_type=F32)


def mm_t(a, b):
    return lax.dot_general(a, b, (((1,), (1,)), ((), ())), preferred_element_type=F32)


def t_mm(a, b):
    return lax.dot_general(a, b, (((0,), (0,)), ((), ())), preferred_element_type=F32)


def halves_of_heads(w):
    w = w.reshape(w.shape[0], 3, 2, -1)
    return w[:, :, 0].reshape(w.shape[0], -1), w[:, :, 1].reshape(w.shape[0], -1)


def heads_of_halves(a, b):
    a, b = a.reshape(a.shape[0], 3, -1), b.reshape(b.shape[0], 3, -1)
    return jnp.stack([a, b], 2).reshape(a.shape[0], -1)


def halves_of_units(w, chunk):
    w = w.reshape(w.shape[0], -1, 2, chunk)
    return w[:, :, 0].reshape(w.shape[0], -1), w[:, :, 1].reshape(w.shape[0], -1)


def units_of_halves(a, b, chunk):
    a, b = a.reshape(a.shape[0], -1, chunk), b.reshape(b.shape[0], -1, chunk)
    return jnp.stack([a, b], 2).reshape(a.shape[0], -1)


def lower_in_chain(leaf):
    z, y = lax.shift_right_logical(leaf, 1), leaf & 1
    below = [((2 * (z - s) + at), z >= s) for s in (1, 2, 3) for at in (y, 1 - y)]
    return below[:2] + [(2 * z, y == 1)] + below[2:]


class Chain:
    near = 5

    def __init__(self, rows):
        self.at = Links()
        self.rows = rows
        self.core = self.at.core

    def lower(self, leaf):
        return lower_in_chain(leaf)

    def places(self):
        at = self.at
        n = jnp.arange(4)
        zyx = ((at.z ^ n)[None, None, :] * 2 + (at.y ^ n[:2])[None, :, None]) * 2 + (at.x ^ n[:2])[:, None, None]
        yzx = ((at.z ^ n)[None, :, None] * 2 + (at.y ^ n[:2])[:, None, None]) * 2 + (at.x ^ n[:2])[None, None, :]
        first = zyx.reshape(16)
        columns = jnp.where(jnp.arange(16) % 2 == 0, at.core, 1 - at.core)
        return jnp.stack([first, first ^ (8 * at.core), yzx.reshape(16), columns]).astype(jnp.int32)

    def first_gather(self, hid, w_qkv, w_out, w_up, w_down, vectors, facts, early):
        at = self.at
        few, chunk, cut = w_qkv.shape[0], w_down.shape[0], w_out.shape[1] // 2
        qkv_a, qkv_b = halves_of_heads(w_qkv)
        row = jnp.pad(vectors, ((0, 7), (0, qkv_a.shape[1] - vectors.shape[1])))
        qkv_a, qkv_b = (jnp.concatenate([v, row], axis=0) for v in (qkv_a, qkv_b))
        block = to_column_half(at, qkv_a, qkv_b)
        spare = jnp.zeros((6, block.shape[1]), BF)
        block = jnp.concatenate(
            [block[:few], block[few + 8 : 2 * few + 8], block[few : few + 1], block[2 * few + 8 : 2 * few + 9], spare],
            axis=0,
        )[None]
        up_a, up_b = halves_of_units(w_up, chunk)
        one_a = jnp.concatenate([w_out[:, :cut], up_a], axis=1)
        one_b = jnp.concatenate([w_out[:, cut:], up_b], axis=1)
        block, hid_up, one_a, one_b = tie(block, hid, one_a, one_b)
        line = z_gather(at, block)
        beside = at.swap_y(hid_up, [(i, i + 1) for i in range(0, 8, 2)])
        one = to_column_half(at, one_a, one_b)[None]
        line, hid_up, one, beside, down_two, facts = tie(line, hid_up, one, beside, w_down, facts)
        first_hop = at.up(hid_up, 0, 2)
        plane = jnp.concatenate([line, at.swap_y(line)], axis=0)
        one_line = [one, at.swap_z(one, 1)]
        down_two = at.swap_x(down_two)
        turns = early(facts)
        first_hop, plane, one_line, down_two, turns = tie(first_hop, plane, one_line, down_two, turns)
        down_two = jnp.stack([w_down, down_two])[None]
        far = at.swap_x(plane)
        other = [at.swap_core(plane)]
        second_hop = at.up(first_hop, 1, 2)
        first_over = at.swap_y(first_hop, [(i, i ^ 1) for i in range(2, 8)])
        second_hop, first_over, other, one_line = tie(second_hop, first_over, other, one_line)
        third_hop = at.up(second_hop, 2, 2)
        second_over = at.swap_y(second_hop, [(i, i ^ 1) for i in range(4, 8)])
        one_line.append(at.swap_z(one_line[0], 2))
        third_hop, second_over, far, one_line = tie(third_hop, second_over, far, one_line)
        third_over = at.swap_y(third_hop, [(i, i ^ 1) for i in range(6, 8)])
        other.append(at.swap_core(far))
        one_line.append(at.swap_z(one_line[0], 3))
        m = 2 * few
        n = vectors.shape[1]
        vec = jnp.concatenate([plane[:, m : m + 2, :n], far[:, m : m + 2, :n]], axis=0).reshape(16, 2 * n)
        order = (self.places()[0][None, :] == jnp.arange(16)[:, None]).astype(BF)
        vec = mm(order, vec).reshape(32, -1)
        third_over, other, one_line, vec, down_two = tie(third_over, other, one_line, vec, down_two)
        line = jnp.concatenate(one_line, axis=0)
        lower = [first_hop, first_over, beside, second_hop, second_over, third_hop, third_over]
        return lower, ((plane, far), tuple(other)), vec, (line, down_two), turns

    def second_start(self, state):
        line, down_two = state
        return jnp.concatenate([line, self.at.swap_y(line)], axis=0), z_gather(self.at, down_two)

    def second_go_on(self, state):
        plane, line = state
        at = self.at
        near = line.reshape((8,) + line.shape[2:])
        one = (plane, at.swap_x(plane)), [at.swap_core(plane)]
        down = (near, at.swap_y(near)), [at.swap_core(near)]
        return one, down

    def second_end(self, state):
        return [(own, tuple(other + [self.at.swap_core(own[1])])) for own, other in state]

    def unit_bias(self, bias, chunk):
        a, b = halves_of_units(bias[None], chunk)
        return jnp.where(self.core == 0, a, b), jnp.where(self.core == 0, b, a)

    def unit_bias_back(self, own, other, chunk):
        a = jnp.where(self.core == 0, own, other)
        b = jnp.where(self.core == 0, other, own)
        return units_of_halves(a, b, chunk)[0]

    def backward(self, run):
        at = self.at
        rows = self.rows
        lower_z = lambda s: [(i, i ^ 1) for i in range(2 * s, 8)]
        down_other, rest_other = run.feed_other(self)
        down_got, rest_got = at.swap_core(down_other), at.swap_core(rest_other)
        down_own, rest_own = run.feed_own(self)
        by_x = lambda g: g.reshape(8, 2, g.shape[0] // 16, g.shape[1])
        by_y = lambda g: g.reshape(4, 2, 2, g.shape[0] // 16, g.shape[1])
        split_y = lambda g: g.reshape((4, 2) + g.shape[1:])
        down_keep, down_send = halve(at.x, by_x(down_own), by_x(down_got), 1)
        rest_keep, rest_send = halve(at.y, by_y(rest_own), by_y(rest_got), 1)
        down_keep, down_send, rest_keep, rest_send, run.grad_mixed = tie(
            down_keep, down_send, rest_keep, rest_send, run.grad_mixed
        )
        down_got, rest_got = at.swap_x(down_send), at.swap_y(rest_send)
        far = run.far_tiles()
        down_got, rest_got, far = tie(down_got, rest_got, far)
        down_keep, down_send = halve(at.y, split_y(down_keep), split_y(down_got), 1)
        rest_keep, rest_send = z_parts(at, rest_keep, rest_got)
        down_keep, down_send, rest_keep, rest_send, far = tie(down_keep, down_send, rest_keep, rest_send, far)
        far_da = run.far_rows(far)
        tiles = [far_da[n * rows : (n + 1) * rows] for n in range(4)]
        over = jnp.concatenate([tiles[1], tiles[3]], axis=0)
        down_send, tiles, over, far = tie(down_send, tiles, over, far)
        over = at.swap_y(over, lower_z(2))
        down_got = at.swap_y(down_send)
        rest_got = z_move(at, rest_send)
        near = run.near_tiles(far)
        rest_got, over, near, tiles, down_got = tie(rest_got, over, near, tiles, down_got)
        down_keep, down_send = z_parts(at, down_keep, down_got)
        rest = z_total(rest_keep, rest_got).astype(BF)
        rest_keep, rest_send = choose(at.x, rest, 0)
        cur = plus(tiles[2], over[rows:]).astype(BF)
        down_keep, down_send, rest_keep, rest_send, cur, near = tie(
            down_keep, down_send, rest_keep, rest_send, cur, near
        )
        cur = at.down(cur, 3, 3)
        down_got, rest_got = z_move(at, down_send), at.swap_x(rest_send)
        own, other, vec = run.weights(near, far)
        own, other, vec, cur, down_got, rest_got = tie(own, other, vec, cur, down_got, rest_got)
        own, other = self.qkv_pieces(own, other, vec)
        cur = (plus(tiles[0], over[:rows]) + cur.astype(F32)).astype(BF)
        own, other, cur, near = tie(own, other, cur, near)
        got = at.swap_core(other)
        cur = at.down(cur, 2, 3)
        clean, near_da = run.near_rows(near)
        got, cur, clean, near_da = tie(got, cur, clean, near_da)
        keep, send = halve(at.x, own, got, 1)
        keep, send, cur, near_da = tie(keep, send, cur, near_da)
        got = at.swap_x(send)
        first = at.swap_y(near_da[rows : 2 * rows], lower_z(1))
        beside = at.swap_y(near_da[2 * rows :], [(i, i - 1) for i in range(1, 8, 2)])
        sum_down = z_total(down_keep, down_got)
        sum_out, sum_up = self.join_rest(plus(rest_keep, rest_got), run.chunk, run.width)
        got, first, beside, sum_down, sum_out, sum_up = tie(got, first, beside, sum_down, sum_out, sum_up)
        keep, send = halve(at.y, split_y(keep), split_y(got), 1)
        cur = (plus(near_da[:rows], first) + cur.astype(F32)).astype(BF)
        keep, send, cur = tie(keep, send, cur)
        got, cur = at.swap_y(send), at.down(cur, 1, 3)
        got, cur = tie(got, cur)
        keep, send = z_parts(at, keep, got)
        keep, send = tie(keep, send)
        got = z_move(at, send)
        grad_hidden = run.last(clean + cur.astype(F32) + beside.astype(F32))
        got, grad_hidden = tie(got, grad_hidden)
        m = run.few * 2
        g = z_total(keep, got)
        sum_qkv = heads_of_halves(*from_column_half(at, g[:m]))
        return sum_down, sum_up, sum_out, sum_qkv, g[m, : run.vectors], grad_hidden

    def join_rest(self, g, chunk, width):
        a, b = from_column_half(self.at, g)
        cut = width // 2
        out = jnp.concatenate([a[:, :cut], b[:, :cut]], axis=1)
        return out, units_of_halves(a[:, cut:], b[:, cut:], chunk)

    def rest_pieces(self, out, up, other):
        half = out.shape[0] // 2
        core = 1 - self.core if other else self.core
        out = lax.dynamic_slice_in_dim(out, core * half, half, axis=1)
        out = jnp.where(self.core == 0, out, jnp.concatenate([out[half:], out[:half]], axis=0))
        return jnp.concatenate([out.astype(BF), up], axis=1)

    def qkv_pieces(self, own, other, vec):
        n = vec.shape[1]
        vec = vec.astype(BF).reshape(8, 2, 2, n)
        found = []
        for g, core in ((own, self.core), (other, 1 - self.core)):
            g = g.reshape(8, 2, g.shape[0] // 16, g.shape[1])
            rows = pick(vec, core, 2)[:, :, None]
            rows = jnp.pad(rows, ((0, 0), (0, 0), (0, 7), (0, g.shape[3] - n)))
            found.append(jnp.concatenate([g, rows], axis=2))
        return found


AXES = ("leaf", "fsdp")


class Whole:
    def __init__(self, rows, leaves, devices):
        self.rows, self.leaves, self.devices = rows, leaves, devices
        self.leaf = lax.axis_index("leaf")
        self.near = 2 + (leaves - 1) // 2

    def lower(self, leaf):
        return [(leaf - s, leaf >= s) for s in range(1, self.leaves)]

    def places(self):
        return jnp.array([[0, 0], [0, 0], [0, 0], [0, 1]], jnp.int32)

    def first_gather(self, hid, w_qkv, w_out, w_up, w_down, vectors, facts, early):
        tree = lax.all_gather(hid, "leaf", axis=0, tiled=False)
        lower = [pick(tree, jnp.maximum(leaf, 0), 0) for leaf, _ in self.lower(self.leaf)]
        every = lambda w: lax.all_gather(w, AXES, axis=0, tiled=True)
        qkv = tuple((v[None],) for v in halves_of_heads(every(w_qkv)))
        return lower, qkv, every(vectors), (every(w_out), every(w_up), every(w_down)), early(facts)

    def second_start(self, state):
        return state

    def second_go_on(self, state):
        return state

    def second_end(self, state):
        out_w, up_w, down_w = state
        half, cut = down_w.shape[0] // 2, out_w.shape[1] // 2
        one = tuple(
            (jnp.concatenate([out_w[:, n * cut : (n + 1) * cut], up_w[:, n * half : (n + 1) * half]], axis=1)[None],)
            for n in range(2)
        )
        return one, tuple((down_w[None, n * half : (n + 1) * half],) for n in range(2))

    def unit_bias(self, bias, chunk):
        half = bias.shape[0] // 2
        return bias[None, :half], bias[None, half:]

    def unit_bias_back(self, own, other, chunk):
        return jnp.concatenate([own, other], axis=1)[0]

    def scatter(self, g):
        return lax.psum_scatter(g.astype(F32), AXES, scatter_dimension=0, tiled=True)

    def rest_pieces(self, out, up, other):
        cut = out.shape[1] // 2
        return jnp.concatenate([out[:, cut:] if other else out[:, :cut], up.astype(F32)], axis=1)

    def backward(self, run):
        rows = self.rows
        down_other, rest_other = run.feed_other(self)
        down_own, rest_own = run.feed_own(self)
        far = run.far_tiles()
        far_da = run.far_rows(far)
        near = run.near_tiles(far)
        own, other, vec = run.weights(near, far)
        clean, near_da = run.near_rows(near)
        tiles = jnp.concatenate([clean.astype(BF), near_da, far_da], axis=0)
        tiles = tiles.reshape((self.leaves, rows) + tiles.shape[1:])
        order = [pick(tiles, (self.leaf - n) % self.leaves, 0) for n in range(self.leaves)]
        total = lax.psum_scatter(jnp.concatenate(order, axis=0), "leaf", scatter_dimension=0, tiled=True)
        cut = run.width // 2
        return (
            self.scatter(jnp.concatenate([down_own, down_other], axis=0)),
            self.scatter(jnp.concatenate([rest_own[:, cut:], rest_other[:, cut:]], axis=1)),
            self.scatter(jnp.concatenate([rest_own[:, :cut], rest_other[:, :cut]], axis=1)),
            self.scatter(heads_of_halves(own, other)),
            self.scatter(vec)[0],
            run.last(total.astype(F32)),
        )


class Backward:
    pass


def shards(
    leaves,
    groups,
    hidden,
    noise_mask,
    seg_blocks,
    parents,
    ln1_gain,
    w_qkv,
    w_out,
    ln2_gain,
    w_up,
    up_bias,
    w_down,
    down_bias,
    mask_embed,
    cotangent,
):
    rows = hidden.shape[1]
    width = hidden.shape[2]
    half = width // 2
    devices = leaves * groups
    net = Chain(rows) if (leaves, groups) == (8, 4) else Whole(rows, leaves, devices)
    chunk = w_down.shape[0]
    few = ln1_gain.shape[0]
    leaf = lax.axis_index("leaf")

    hid = hidden[0]
    tiles = 2 + len(net.lower(leaf))
    lanes = jnp.arange(128, dtype=jnp.int32)
    exponent = (lanes % (HEAD_DIM // 2)).astype(F32) * (-math.log(10000.0) / (HEAD_DIM // 2))

    def turns(facts):
        found = tables(net.lower, leaf, facts, parents, rows)
        angles = found[2][:, 2:3] * jnp.exp(exponent)
        sign = jnp.where((lanes % HEAD_DIM) < HEAD_DIM // 2, -1.0, 1.0)
        return jnp.cos(angles), jnp.sin(angles) * sign, found

    places = net.places()

    length = 4 * few + up_bias.shape[0]
    vectors = sum(
        jnp.pad(v[None], ((0, 0), (n * few, length - n * few - v.shape[0])))
        for n, v in enumerate((ln1_gain, ln2_gain, down_bias, mask_embed, up_bias))
    )
    lower, qkv_w, vec, coming, (cosine, sine, found) = net.first_gather(
        hid, w_qkv, w_out, w_up, w_down, vectors, seg_blocks, turns
    )
    query_cols, query_rows, key_cols, key_rows, flags = found
    gain_one, gain_two, down_b, embed = (
        vec[:, n * few : (n + 1) * few].reshape(1, width).astype(F32) for n in range(4)
    )
    up_b = jnp.concatenate(net.unit_bias(vec[:, 4 * few :].reshape(-1).astype(F32), chunk), axis=0)
    coming = net.second_start(coming)
    query, key, value = project(
        places, [hid] + lower, noise_mask, embed, gain_one, qkv_w[0], qkv_w[1], cosine, sine
    )
    coming, query = tie(coming, query)
    coming = net.second_go_on(coming)
    mixed, log_norm = attend(flags, query_cols, key_rows, query, key, value, rows)
    coming, mixed = tie(coming, mixed)
    one_w, down_w = net.second_end(coming)
    norm_rows = log_norm.T
    grad_two = cotangent[0].reshape(2 * rows, width)
    (
        output, normed_two, act, grad_pre, grad_one, grad_mixed, grad_after, grad_up_b, grad_down_b,
    ) = middle(places, mixed, hid, noise_mask, embed, grad_two, gain_two, up_b, down_b, one_w, down_w)
    output = output.reshape(1, 2, rows, width)
    units = act.shape[1] // 2

    run = Backward()
    run.chunk, run.few, run.vectors, run.grad_mixed, run.width = chunk, few, length - 2 * few, grad_mixed, width
    cut = net.near

    def feed(n, net):
        at = slice(n * units, (n + 1) * units)
        down, up = t_mm(act[:, at], grad_two).astype(BF), t_mm(normed_two, grad_pre[:, at]).astype(BF)
        return down, net.rest_pieces(t_mm(mixed, grad_one), up, n == 1)

    def far_tiles():
        return attend_back(
            cut, tiles, flags, query_rows, key_rows, query, key, value, mixed, run.grad_mixed, norm_rows, cosine, sine, rows
        )

    def far_rows(far):
        return fold_rows(places, far[1], far[2], qkv_w[0], qkv_w[1], rows)[0]

    def near_tiles(far):
        return attend_back(
            0, cut, flags, query_rows, key_rows, query, key, value, mixed, run.grad_mixed, norm_rows, cosine, sine, rows, far[0]
        )

    def weights(near, far):
        own, other, run.noisy, grad_embed = fold_weights(
            places, [hid] + lower, near, far, grad_after, noise_mask, embed, gain_one, qkv_w[0], qkv_w[1]
        )
        parts = (grad_down_b, grad_embed, net.unit_bias_back(grad_up_b[:1], grad_up_b[1:], chunk))
        return own, other, jnp.concatenate([v.reshape(devices, -1) for v in parts], axis=1)

    def near_rows(near):
        return fold_rows(places, near[1], near[2], qkv_w[0], qkv_w[1], rows, near[0])

    def last(total):
        hat, scale = normalise(hid.astype(F32))
        masked = (noise_mask[0] == 1)[:, None]
        clean = grad_after[:rows] + norm_back(hat, scale, gain_one, total)
        return (clean + jnp.where(masked, 0.0, run.noisy)).astype(BF)[None]

    run.feed_own = lambda net: feed(0, net)
    run.feed_other = lambda net: feed(1, net)
    run.far_tiles, run.far_rows, run.near_tiles, run.near_rows = far_tiles, far_rows, near_tiles, near_rows
    run.weights, run.last = weights, last
    sum_down, sum_up, sum_out, sum_qkv, sum_vec, grad_hidden = net.backward(run)
    from_weight = lambda w, g, gain: jnp.sum(w.astype(F32) * g, axis=1) / gain.astype(F32)
    return (
        output,
        grad_hidden,
        from_weight(w_qkv, sum_qkv, ln1_gain),
        sum_qkv,
        sum_out,
        from_weight(w_up, sum_up, ln2_gain),
        sum_up,
        sum_vec[2 * few :],
        sum_down,
        sum_vec[:few],
        sum_vec[few : 2 * few],
    )


def solution(mesh):
    split = ("leaf", "fsdp")
    in_specs = (
        P("fsdp", "leaf", None),
        P("fsdp", "leaf"),
        P("fsdp", None),
        P("fsdp", None),
        P(split),
        P(split, None),
        P(split, None),
        P(split),
        P(split, None),
        P(split),
        P(split, None),
        P(split),
        P(split),
        P("fsdp", None, "leaf", None),
    )
    out_specs = (
        P("fsdp", None, "leaf", None),
        P("fsdp", "leaf", None),
        P(split),
        P(split, None),
        P(split, None),
        P(split),
        P(split, None),
        P(split),
        P(split, None),
        P(split),
        P(split),
    )
    body = functools.partial(shards, mesh.shape["leaf"], mesh.shape["fsdp"])
    return jax.shard_map(body, mesh=mesh, in_specs=in_specs, out_specs=out_specs, check_vma=False)
```

```python
import functools
import math

import jax
import jax.numpy as jnp
from jax import lax
from jax.experimental import pallas as pl
from jax.experimental.pallas import tpu as pltpu
from jax.sharding import PartitionSpec as P

HEAD_DIM = 64
BLOCK = 16
NEG_FILL = -1000000000.0
EPSILON = 1e-05


def vmem(mebibytes):
    return pltpu.CompilerParams(vmem_limit_bytes=mebibytes * 2**20)


BF = jnp.bfloat16
F32 = jnp.float32


class Links:
    def __init__(self):
        leaf = lax.axis_index("leaf")
        fsdp = lax.axis_index("fsdp")
        self.z, self.y = leaf // 2, leaf % 2
        self.x, self.core = fsdp // 2, fsdp % 2

    def swap_core(self, v):
        return lax.ppermute(v, "fsdp", [(i, i ^ 1) for i in range(4)])

    def swap_x(self, v):
        return lax.ppermute(v, "fsdp", [(i, i ^ 2) for i in range(4)])

    def swap_y(self, v, pairs=None):
        return lax.ppermute(v, "leaf", pairs or [(i, i ^ 1) for i in range(8)])

    def swap_z(self, v, n):
        return lax.ppermute(v, "leaf", [(i, i ^ (2 * n)) for i in range(8)])

    def up(self, v, first, last):
        return lax.ppermute(v, "leaf", [(i, i + 2) for i in range(2 * first, 2 * last + 2)])

    def down(self, v, first, last):
        return lax.ppermute(v, "leaf", [(i, i - 2) for i in range(2 * first, 2 * last + 2)])


def both(bit, own, other, axis):
    return jnp.where(
        bit == 0, jnp.stack([own, other], axis), jnp.stack([other, own], axis)
    )


def tie(*values):
    flat, tree = jax.tree.flatten(values)
    return jax.tree.unflatten(tree, lax.optimization_barrier(tuple(flat)))


def z_gather(at, block):
    return jnp.concatenate([block] + [at.swap_z(block, n) for n in (1, 2, 3)], axis=0)


def pick(v, index, axis):
    return lax.dynamic_index_in_dim(v, index, axis, keepdims=False)


def choose(bit, v, axis):
    return pick(v, bit, axis), pick(v, 1 - bit, axis)


def plus(a, b):
    return a.astype(F32) + b.astype(F32)


def joined(mine, got, index, axis):
    return plus(pick(mine, index, axis), pick(got, index, axis)).astype(BF)


def halve(bit, mine, got, axis):
    return joined(mine, got, bit, axis), joined(mine, got, 1 - bit, axis)


def z_parts(at, mine, got):
    return joined(mine, got, at.z, 0), [joined(mine, got, at.z ^ n, 0) for n in (1, 2, 3)]


def z_move(at, parts):
    return [at.swap_z(part, n) for n, part in zip((1, 2, 3), parts)]


def z_total(keep, got):
    return plus(keep, got[0]) + plus(got[1], got[2])


def to_column_half(at, half_a, half_b):
    keep = jnp.where(at.core == 0, half_a, half_b)
    send = jnp.where(at.core == 0, half_b, half_a)
    got = at.swap_core(send)
    return both(at.core, keep, got, 0).reshape(2 * keep.shape[0], keep.shape[1])


def from_column_half(at, g):
    g = g.reshape(2, g.shape[0] // 2, g.shape[1])
    keep, send = choose(at.core, g, 0)
    got = at.swap_core(send)
    return jnp.where(at.core == 0, keep, got), jnp.where(at.core == 0, got, keep)


def spec(shape, index_map):
    return pl.BlockSpec(shape, index_map)


def turn(values, cosine, sine):
    lane = lax.broadcasted_iota(jnp.int32, (values.shape[0], 128), 1)
    low_half = (lane % HEAD_DIM) < HEAD_DIM // 2
    groups = []
    for n in range(values.shape[1] // 128):
        part = values[:, n * 128 : (n + 1) * 128]
        swapped = jnp.where(low_half, pltpu.roll(part, 96, 1), pltpu.roll(part, 32, 1))
        groups.append(part * cosine + swapped * sine)
    return groups


def column(row):
    return jnp.broadcast_to(row, (8, row.shape[1])).T[:, :1]


def tables_kernel(places, rows, leaf_ref, seg_ref, parent_ref, qcol_ref, qrow_ref, kcol_ref, krow_ref, flag_ref, pad_ref):
    leaf = leaf_ref[0]
    blocks = rows // BLOCK
    slots = 16
    seg = column(seg_ref[...].astype(F32))
    lane = lax.broadcasted_iota(jnp.int32, (seg.shape[0], 128), 1).astype(F32)
    length = jnp.sum(jnp.where(seg == lane, 1.0, 0.0), axis=0, keepdims=True)
    start = jnp.sum(jnp.where(seg < lane, 1.0, 0.0), axis=0, keepdims=True)
    pad_ref[...] = jnp.zeros_like(pad_ref)
    pad_ref[0:1, 0 : parent_ref.shape[1]] = parent_ref[...].astype(F32)
    parent_row = pad_ref[0:1, :]
    lane = lax.broadcasted_iota(jnp.int32, (slots, 128), 1).astype(F32)
    slot = lax.broadcasted_iota(jnp.int32, (slots, 1), 0).astype(F32)
    parent = column(parent_row)[:slots]
    look = lambda index, row: jnp.sum(jnp.where(index == lane, row, 0.0), axis=1, keepdims=True)
    grand = look(parent, parent_row)
    start = look(slot, start)
    shift = jnp.where(slot > 0, look(parent, length), 0.0) + jnp.where(parent > 0, look(grand, length), 0.0) - start

    def facts(block):
        own = jnp.sum(jnp.where(block >= start, 1.0, 0.0), axis=0, keepdims=True) - 1.0
        take = lambda col: jnp.sum(jnp.where(slot == own, col, 0.0), axis=0, keepdims=True)
        return own, take(parent), take(grand), take(shift)

    token = lax.broadcasted_iota(jnp.int32, (1, rows), 1)
    zero = jnp.zeros((1, rows), F32)
    tiles = [(leaf, leaf >= 0), (leaf, leaf < 0)] + places(leaf)
    for t, (place, valid) in enumerate(tiles):
        first = jnp.maximum(place, 0) * blocks
        block = (first + lax.shift_right_logical(token, 4)).astype(F32)
        own, one, two, move = facts(block)
        position = (move + block) * BLOCK + (token & (BLOCK - 1)).astype(F32)
        at = slice(t * rows, (t + 1) * rows)
        if t < 2:
            limit = block + (1.0 if t == 0 else 0.0)
            lines = jnp.concatenate([own, one, two, limit, zero, zero, zero, zero], axis=0)
            qrow_ref[:, at] = lines
            qcol_ref[at, :] = lines.T
        lines = jnp.concatenate(
            [jnp.where(valid, own, -1.0), block, position, zero, zero, zero, zero, zero], axis=0
        )
        krow_ref[:, at] = lines
        kcol_ref[at, :] = lines.T
    queries = qcol_ref[pl.ds(0, 2 * blocks, stride=BLOCK), :]
    lane = lax.broadcasted_iota(jnp.int32, (1, 128), 1)
    for t, (place, valid) in enumerate(tiles):
        if t < 2:
            flag_ref[t] = 1
            continue
        block = (jnp.maximum(place, 0) * blocks + lane).astype(F32)
        own = facts(block)[0]
        allowed = (
            ((own == queries[:, 0:1]) | (own == queries[:, 1:2]) | (own == queries[:, 2:3]))
            & (block < queries[:, 3:4])
            & (lane < blocks)
            & valid
        )
        flag_ref[t] = jnp.max(jnp.where(allowed, 1.0, 0.0)).astype(jnp.int32)


def tables(places, leaf, seg, parent, rows):
    tiles = 2 + len(places(leaf))
    total = tiles * rows
    smem = pl.BlockSpec(memory_space=pltpu.SMEM)
    vmem = pl.BlockSpec(memory_space=pltpu.VMEM)
    shapes = [(2 * rows, 8), (8, 2 * rows), (total, 8), (8, total)]
    return pl.pallas_call(
        functools.partial(tables_kernel, places, rows),
        in_specs=[smem, vmem, vmem],
        out_specs=[vmem] * 4 + [smem],
        out_shape=[jax.ShapeDtypeStruct(shape, F32) for shape in shapes] + [jax.ShapeDtypeStruct((tiles,), jnp.int32)],
        name="tables",
        scratch_shapes=[pltpu.VMEM((8, 128), F32)],
    )(leaf.reshape(1), seg, parent)


def fetch(pieces, sems):
    copies = [pltpu.make_async_copy(src, dst, sems.at[n]) for n, (src, dst) in enumerate(pieces)]
    for copy in copies:
        copy.start()
    return copies


def placed(blocks, ref, size, table, row):
    pieces = []
    for hbm in blocks:
        for n in range(hbm.shape[0]):
            place = pl.multiple_of(table[row, len(pieces)] * size, size)
            pieces.append((hbm.at[n, pl.ds(0, size), :], ref.at[pl.ds(place, size), :]))
    return pieces


def tiled(sources, ref, rows):
    return [(src, ref.at[pl.ds(n * rows, rows), :]) for n, src in enumerate(sources)]


def project_kernel(
    blocks, sources, size, rows, table_ref, mask_ref, embed_ref, gain_ref, cos_ref, sin_ref, *refs,
):
    own_hbm, other_hbm, tiles = refs[:blocks], refs[blocks : 2 * blocks], refs[2 * blocks : 2 * blocks + sources]
    q_ref, k_ref, v_ref, x_ref, own_ref, other_ref, sems = refs[2 * blocks + sources :]
    tile = pl.program_id(0)
    step = k_ref.shape[1]

    @pl.when(tile == 0)
    def _():
        pieces = tiled([tiles[0]] + list(tiles), x_ref, rows)
        count = len(pieces)
        pieces += placed(own_hbm, own_ref, size, table_ref, 0) + placed(other_hbm, other_ref, size, table_ref, 0)
        copies = fetch(pieces, sems)
        for copy in copies[:count]:
            copy.wait()
        masked = column(mask_ref[...].astype(F32)) > 0
        x_ref[rows : 2 * rows, :] = jnp.where(masked, embed_ref[...], x_ref[rows : 2 * rows, :].astype(F32)).astype(BF)
        for copy in copies[count:]:
            copy.wait()

    x = x_ref[pl.ds(pl.multiple_of(tile * step, step), step), :].astype(F32)
    centred = x - jnp.mean(x, axis=-1, keepdims=True)
    spread = jnp.mean(centred * centred, axis=-1, keepdims=True)
    a = (centred * lax.rsqrt(spread + EPSILON) * gain_ref[...]).astype(BF)
    cosine, sine = cos_ref[...], sin_ref[...]
    half = own_ref.shape[1] // 3
    for n, w_ref in enumerate((own_ref, other_ref)):
        base = n * half
        keys = jnp.dot(a, w_ref[:, half : 2 * half], preferred_element_type=F32)
        values = jnp.dot(a, w_ref[:, 2 * half :], preferred_element_type=F32)
        for g, part in enumerate(turn(keys, cosine, sine)):
            k_ref[base // 128 + g] = part.astype(BF)
            v_ref[base // 128 + g] = values[:, g * 128 : (g + 1) * 128].astype(BF)

    @pl.when(tile * step < 2 * rows)
    def _():
        lines = q_ref.shape[0]
        for n, w_ref in enumerate((own_ref, other_ref)):
            base = n * half
            q = jnp.dot(a[:lines], w_ref[:, :half], preferred_element_type=F32)
            for g, part in enumerate(turn(q, cosine[:lines], sine[:lines])):
                q_ref[:, base + g * 128 : base + (g + 1) * 128] = part.astype(BF)


def project(table, tiles, mask, embed, gain, own, other, cosine, sine):
    rows, width = tiles[0].shape
    total = (len(tiles) + 1) * rows
    step = next(n for n in (3 * rows, 2 * rows, rows) if total % n == 0)
    q_step = min(step, 2 * rows)
    last_q = 2 * rows // q_step - 1
    count = sum(v.shape[0] for v in own)
    columns = own[0].shape[2]
    whole = lambda v: spec(v.shape, lambda t, i: (0, 0))
    moved = lambda n: spec((step, n), lambda t, i: (t, 0))
    pairs = spec((width // 128, step, 128), lambda t, i: (0, t, 0))
    out = lambda n: jax.ShapeDtypeStruct((n, width), BF)
    anywhere = pl.BlockSpec(memory_space=pl.ANY)
    far = list(own) + list(other) + list(tiles)
    return pl.pallas_call(
        functools.partial(project_kernel, len(own), len(tiles), width // count, rows),
        grid_spec=pltpu.PrefetchScalarGridSpec(
            num_scalar_prefetch=1,
            grid=(total // step,),
            in_specs=[whole(mask), whole(embed), whole(gain), moved(128), moved(128)] + [anywhere] * len(far),
            out_specs=[
                spec((q_step, width), lambda t, i: (jnp.minimum(t, last_q), 0)),
                pairs,
                pairs,
            ],
            scratch_shapes=[
                pltpu.VMEM((total, width), BF),
                pltpu.VMEM((width, columns), BF),
                pltpu.VMEM((width, columns), BF),
                pltpu.SemaphoreType.DMA((2 * count + len(tiles) + 1,)),
            ],
        ),
        out_shape=[out(2 * rows)] + [jax.ShapeDtypeStruct((width // 128, total, 128), BF)] * 2,
        compiler_params=vmem(26 if total <= 10 * rows else 40),
        cost_estimate=pl.CostEstimate(
            flops=2 * total * width * 2 * width + 4 * rows * width * width,
            bytes_accessed=2 * (3 * total * width + 3 * width * width),
            transcendentals=0,
        ),
        name="project",
    )(table, mask, embed, gain, cosine, sine, *far)


def middle_kernel(
    blocks_one, blocks_two, size, chunk, table_ref, o_ref, x_ref, mask_ref, embed_ref, dy_ref, gain_ref, up_b_ref,
    down_b_ref, *refs,
):
    refs = list(refs)
    take = lambda n: [refs.pop(0) for _ in range(n)]
    ones, twos = (take(blocks_one), take(blocks_one)), (take(blocks_two), take(blocks_two))
    y_ref, b_ref, g_ref, du_ref, dh_low_ref, do_ref, dh_ref, dup_b_ref, ddown_b_ref = take(9)
    out_ref, up_ref, down_ref, sems = refs
    cut = out_ref.shape[1] // 2
    units = up_ref.shape[2]
    pieces_out, pieces = [], []
    for n in range(2):
        columns = pl.ds(pl.multiple_of(table_ref[3, n] * cut, cut), cut)
        spots = [(hbm, j) for hbm in ones[n] for j in range(hbm.shape[0])]
        pieces.append([])
        for place, (hbm, j) in enumerate(spots):
            to = pl.ds(pl.multiple_of(table_ref[1, place] * size, size), size)
            pieces_out.append((hbm.at[j, :, pl.ds(0, cut)], out_ref.at[to, columns]))
            to = pl.ds(pl.multiple_of(table_ref[0, place] * size, size), size)
            pieces[n].append((hbm.at[j, :, pl.ds(cut, units)], up_ref.at[n, to, :]))
        pieces[n] += placed(twos[n], down_ref.at[n], chunk, table_ref, 2)
    copies = fetch(pieces_out + pieces[0] + pieces[1], sems)
    for copy in copies[: len(pieces_out)]:
        copy.wait()
    x = x_ref[...].astype(F32)
    masked = column(mask_ref[...].astype(F32)) > 0
    x = jnp.concatenate([x, jnp.where(masked, embed_ref[...], x)], axis=0)
    h = x + jnp.dot(o_ref[...], out_ref[...], preferred_element_type=F32)
    centred = h - jnp.mean(h, axis=-1, keepdims=True)
    spread = jnp.mean(centred * centred, axis=-1, keepdims=True)
    scale = lax.rsqrt(spread + EPSILON)
    hat = centred * scale
    b = (hat * gain_ref[...]).astype(BF)
    b_ref[...] = b
    dy = dy_ref[...]
    ddown_b_ref[...] = jnp.sum(dy.astype(F32), axis=0, keepdims=True)
    y = h + down_b_ref[...]
    db = None
    wide = next(n for n in (768, 512, 384, 256, 128) if units % n == 0)
    for n in range(2):
        done = len(pieces_out) + n * len(pieces[0])
        for copy in copies[done : done + len(pieces[n])]:
            copy.wait()
        for c in range(0, units, wide):
            at = slice(c, c + wide)
            to = slice(n * units + c, n * units + c + wide)
            u = jnp.dot(b, up_ref[n, :, at], preferred_element_type=F32) + up_b_ref[n : n + 1, at]
            g, slope = gelu_parts(u)
            g = g.astype(BF)
            g_ref[:, to] = g
            y = y + jnp.dot(g, down_ref[n, at, :], preferred_element_type=F32)
            du = (matmul_t(dy, down_ref[n, at, :]) * slope).astype(BF)
            du_ref[:, to] = du
            dup_b_ref[n : n + 1, at] = jnp.sum(du.astype(F32), axis=0, keepdims=True)
            part = matmul_t(du, up_ref[n, :, at])
            db = part if db is None else db + part
    y_ref[...] = y.astype(BF)
    dh = dy.astype(F32) + norm_back(hat, scale, gain_ref[...], db)
    dh_ref[...] = dh
    low = dh.astype(BF)
    dh_low_ref[...] = low
    do_ref[...] = matmul_t(low, out_ref[...]).astype(BF)


def middle(table, o, x, mask, embed, dy, gain, up_b, down_b, one, two):
    rows, width = o.shape
    count = sum(v.shape[0] for v in one[0])
    size, columns = one[0][0].shape[1:]
    chunk = two[0][0].shape[1]
    units = columns - width // 2
    full = lambda shape: spec(shape, lambda t, i: (0, 0))
    near = (o, x, mask, embed, dy, gain, up_b, down_b)
    far = list(one[0]) + list(one[1]) + list(two[0]) + list(two[1])
    shapes = [
        ((rows, width), BF), ((rows, width), BF), ((rows, 2 * units), BF), ((rows, 2 * units), BF), ((rows, width), BF),
        ((rows, width), BF), ((rows, width), F32), ((2, units), F32), ((1, width), F32),
    ]
    return pl.pallas_call(
        functools.partial(middle_kernel, len(one[0]), len(two[0]), size, chunk),
        grid_spec=pltpu.PrefetchScalarGridSpec(
            num_scalar_prefetch=1,
            grid=(1,),
            in_specs=[full(v.shape) for v in near] + [pl.BlockSpec(memory_space=pl.ANY)] * len(far),
            out_specs=[full(shape) for shape, _ in shapes],
            scratch_shapes=[
                pltpu.VMEM((width, width), BF),
                pltpu.VMEM((2, width, units), BF),
                pltpu.VMEM((2, units, width), BF),
                pltpu.SemaphoreType.DMA((6 * count,)),
            ],
        ),
        out_shape=[jax.ShapeDtypeStruct(shape, kind) for shape, kind in shapes],
        compiler_params=vmem(44),
        cost_estimate=pl.CostEstimate(
            flops=2 * rows * width * (2 * width + 8 * units),
            bytes_accessed=4 * (width * width + 4 * units * width),
            transcendentals=2 * rows * units,
        ),
        name="middle",
    )(table, *near, *far)


def matmul_t(a, b):
    return lax.dot_general(a, b, (((1,), (1,)), ((), ())), preferred_element_type=F32)


def groups(tiles, first=2, size=2):
    found = []
    for start, end in ((2, min(5, tiles)), (5, tiles)):
        start = max(start, first)
        while start < end:
            found.append((start, min(start + size, end)))
            start += size
    return found


def attend_kernel(
    rows, tiles, flag_ref, qcol_ref, krow_ref, q_ref, k_ref, v_ref, o_ref, lse_ref,
    bias_ref, s_ref, top_ref, sum_ref, acc_ref,
):
    pair = pl.program_id(0)
    both_rows = 2 * rows

    def span(t):
        return slice(t * rows, (t + 1) * rows)

    def lines(t):
        return slice(rows, both_rows) if t == 1 else slice(0, both_rows)

    @pl.when(pair == 0)
    def _():
        lse_ref[...] = jnp.zeros_like(lse_ref)
        own = qcol_ref[:, 0:1]
        up_one = qcol_ref[:, 1:2]
        up_two = qcol_ref[:, 2:3]
        limit = qcol_ref[:, 3:4]
        for t in range(tiles):
            if t == 1:
                r = lax.broadcasted_iota(jnp.int32, (rows, rows), 0) // BLOCK
                c = lax.broadcasted_iota(jnp.int32, (rows, rows), 1) // BLOCK
                bias_ref[rows:, span(t)] = jnp.where(r == c, 0.0, NEG_FILL)
            else:
                seg = krow_ref[0:1, span(t)]
                index = krow_ref[1:2, span(t)]
                ok = ((seg == own) | (seg == up_one) | (seg == up_two)) & (index < limit)
                bias_ref[:, span(t)] = jnp.where(ok, 0.0, NEG_FILL)

    lane = lax.broadcasted_iota(jnp.int32, (both_rows, 128), 1)
    queries = [jnp.where((lane // HEAD_DIM) == h, q_ref[...] * 0.125, 0).astype(BF) for h in range(2)]
    top_ref[...] = jnp.full_like(top_ref, -3.0e38)

    def scores(first, last, at):
        cut = slice(first * rows, last * rows)
        keys = k_ref[0, cut, :]
        for h in range(2):
            s = matmul_t(queries[h][at], keys) + bias_ref[at, cut]
            s_ref[h, at, cut] = s
            best = top_ref[h, at, :]
            for c in range(s.shape[1] // 128):
                best = jnp.maximum(best, s[:, c * 128 : (c + 1) * 128])
            top_ref[h, at, :] = best

    def weigh(first, last, at):
        cut = slice(first * rows, last * rows)
        values = v_ref[0, cut, :]
        for h in range(2):
            p = jnp.exp(s_ref[h, at, cut] - tops[h][at])
            part = sum_ref[h, at, :]
            for c in range(p.shape[1] // 128):
                part = part + p[:, c * 128 : (c + 1) * 128]
            sum_ref[h, at, :] = part
            acc_ref[h, at, :] += jnp.dot(p.astype(BF), values, preferred_element_type=F32)

    upper, lower, all_rows = slice(0, rows), slice(rows, both_rows), slice(0, both_rows)

    def each(step):
        step(0, 1, upper)
        step(0, 2, lower)
        for first, last in groups(tiles, 2, 4):
            some = flag_ref[first]
            for t in range(first + 1, last):
                some = some + flag_ref[t]
            pl.when(some > 0)(functools.partial(step, first, last, all_rows))

    each(scores)
    tops = [jnp.max(top_ref[h], axis=-1, keepdims=True) for h in range(2)]
    sum_ref[...] = jnp.zeros_like(sum_ref)
    acc_ref[...] = jnp.zeros_like(acc_ref)
    each(weigh)
    outs, norms = [], lse_ref[...]
    for h in range(2):
        total = jnp.sum(sum_ref[h], axis=-1, keepdims=True)
        outs.append(acc_ref[h] / total)
        norms = jnp.where(lane == 2 * pair + h, tops[h] + jnp.log(total), norms)
    lse_ref[...] = norms
    o_ref[...] = jnp.where(lane < HEAD_DIM, outs[0], outs[1]).astype(BF)


def attend(flags, qcol, krow, q, k, v, rows):
    width = q.shape[1]
    total = k.shape[1]
    tiles = total // rows
    whole_pair = spec((1, total, 128), lambda p, f: (p, 0, 0))
    pair = lambda n: spec((n, 128), lambda p, f: (0, p))
    fixed = lambda shape: spec(shape, lambda p, f: (0, 0))
    return pl.pallas_call(
        functools.partial(attend_kernel, rows, tiles),
        grid_spec=pltpu.PrefetchScalarGridSpec(
            num_scalar_prefetch=1,
            grid=(width // 128,),
            in_specs=[fixed(qcol.shape), fixed(krow.shape), pair(2 * rows), whole_pair, whole_pair],
            out_specs=[pair(2 * rows), fixed((2 * rows, 128))],
            scratch_shapes=[
                pltpu.VMEM((2 * rows, total), F32),
                pltpu.VMEM((2, 2 * rows, total), F32),
                pltpu.VMEM((2, 2 * rows, 128), F32),
                pltpu.VMEM((2, 2 * rows, 128), F32),
                pltpu.VMEM((2, 2 * rows, 128), F32),
            ],
        ),
        out_shape=[
            jax.ShapeDtypeStruct((2 * rows, width), BF),
            jax.ShapeDtypeStruct((2 * rows, 128), F32),
        ],
        compiler_params=vmem(28 if tiles <= 10 else 52),
        cost_estimate=pl.CostEstimate(
            flops=16 * rows * total * width,
            bytes_accessed=4 * (total + rows) * width,
            transcendentals=2 * rows * total * width // HEAD_DIM,
        ),
        name="attend",
    )(flags, qcol, krow, q, k, v)


def attend_back_kernel(
    rows, first, last, flag_ref, qrow_ref, krow_ref, q_ref, k_ref, v_ref, o_ref, g_ref, lse_ref, *refs,
):
    refs = list(refs)
    near = first == 0
    cos_ref, sin_ref = refs[:2]
    part_ref = refs[2] if near else None
    dq_ref, dk_ref, dv_ref, bias_ref, acc_ref = refs[-5:]
    pair = pl.program_id(0)
    both_rows = 2 * rows

    def span(t):
        return slice(t * rows, (t + 1) * rows)

    @pl.when(pair == 0)
    def _():
        own = qrow_ref[0:1, :]
        up_one = qrow_ref[1:2, :]
        up_two = qrow_ref[2:3, :]
        limit = qrow_ref[3:4, :]
        for t in range(first, last):
            if t == 1:
                r = lax.broadcasted_iota(jnp.int32, (rows, both_rows), 0) // BLOCK
                c = lax.broadcasted_iota(jnp.int32, (rows, both_rows), 1) // BLOCK
                bias_ref[span(t - first), :] = jnp.where(r + rows // BLOCK == c, 0.0, NEG_FILL)
            else:
                facts = krow_ref[:, span(t - first)].T
                seg = facts[:, 0:1]
                index = facts[:, 1:2]
                ok = ((seg == own) | (seg == up_one) | (seg == up_two)) & (index < limit)
                bias_ref[span(t - first), :] = jnp.where(ok, 0.0, NEG_FILL)

    lane = lax.broadcasted_iota(jnp.int32, (both_rows, 128), 1)
    acc_ref[...] = part_ref[...] if near else jnp.zeros_like(acc_ref)
    queries, grads, deltas, norms, queries_t, grads_t = [], [], [], [], [], []
    product = (o_ref[...].astype(F32) * g_ref[...].astype(F32)).T
    for h in range(2):
        mine = (lane // HEAD_DIM) == h
        queries.append(jnp.where(mine, q_ref[...] * 0.125, 0).astype(BF))
        grads.append(jnp.where(mine, g_ref[...], 0).astype(BF))
        queries_t.append(queries[h].astype(F32).T.astype(BF))
        grads_t.append(grads[h].astype(F32).T.astype(BF))
        deltas.append(jnp.sum(product[h * HEAD_DIM : (h + 1) * HEAD_DIM], axis=0, keepdims=True))
        norms.append(lse_ref[pl.ds(2 * pair + h, 1), :])

    def step(start, end):
        to = slice((start - first) * rows, (end - first) * rows)
        keys, values = k_ref[0, to, :], v_ref[0, to, :]
        keys_t = keys.astype(F32).T.astype(BF)
        dk = dv = None
        for h in range(2):
            q, g = queries[h], grads[h]
            s = jnp.dot(keys, queries_t[h], preferred_element_type=F32) + bias_ref[to, :]
            p = jnp.exp(s - norms[h])
            dp = jnp.dot(values, grads_t[h], preferred_element_type=F32)
            ds = (p * (dp - deltas[h])).astype(BF)
            part_v = jnp.dot(p.astype(BF), g, preferred_element_type=F32)
            part_k = jnp.dot(ds, q, preferred_element_type=F32)
            dv = part_v if dv is None else dv + part_v
            dk = part_k if dk is None else dk + part_k
            half = slice(h * HEAD_DIM, (h + 1) * HEAD_DIM)
            acc_ref[half, :] += jnp.dot(keys_t[half], ds, preferred_element_type=F32)
        [dk] = turn(dk, cos_ref[to, :], -sin_ref[to, :])
        dk_ref[0, to, :] = dk.astype(BF)
        dv_ref[0, to, :] = dv.astype(BF)

    if near:
        step(0, 2)
    for start, end in groups(last, max(first, 2), 4):
        some = flag_ref[start]
        for t in range(start + 1, end):
            some = some + flag_ref[t]
        to = slice((start - first) * rows, (end - first) * rows)

        @pl.when(some == 0)
        def _():
            dk_ref[0, to, :] = jnp.zeros(((end - start) * rows, 128), BF)
            dv_ref[0, to, :] = jnp.zeros(((end - start) * rows, 128), BF)

        pl.when(some > 0)(functools.partial(step, start, end))

    if near:
        dq = acc_ref[...].T * 0.125
        [dq] = turn(dq, cos_ref[:both_rows, :], -sin_ref[:both_rows, :])
        dq_ref[...] = dq.astype(BF)
    else:
        dq_ref[...] = acc_ref[...]


def attend_back(first, last, flags, qrow, krow, q, k, v, o, g, lse, cosine, sine, rows, part=None):
    width = q.shape[1]
    there = (last - first) * rows
    near = first == 0
    some_pair = lambda n: spec((1, n, 128), lambda p, f: (p, 0, 0))
    taken_pair = spec((pl.Element(1), pl.Element(there), pl.Element(128)), lambda p, f: (p, first * rows, 0))
    taken = spec((pl.Element(there), pl.Element(128)), lambda p, f: (first * rows, 0))
    pair = lambda n: spec((n, 128), lambda p, f: (0, p))
    turned = spec((128, 2 * rows), lambda p, f: (p, 0))
    fixed = lambda shape: spec(shape, lambda p, f: (0, 0))
    out = lambda n: jax.ShapeDtypeStruct((n, width), BF)
    return pl.pallas_call(
        functools.partial(attend_back_kernel, rows, first, last),
        grid_spec=pltpu.PrefetchScalarGridSpec(
            num_scalar_prefetch=1,
            grid=(width // 128,),
            in_specs=[
                fixed(qrow.shape), spec((pl.Element(8), pl.Element(there)), lambda p, f: (0, first * rows)), pair(2 * rows),
                taken_pair, taken_pair, pair(2 * rows), pair(2 * rows), fixed(lse.shape), taken, taken,
            ] + ([turned] if near else []),
            out_specs=[pair(2 * rows) if near else turned, some_pair(there), some_pair(there)],
            scratch_shapes=[
                pltpu.VMEM((there, 2 * rows), F32),
                pltpu.VMEM((128, 2 * rows), F32),
            ],
        ),
        out_shape=[out(2 * rows) if near else jax.ShapeDtypeStruct((width, 2 * rows), F32)]
        + [jax.ShapeDtypeStruct((width // 128, there, 128), BF)] * 2,
        compiler_params=vmem(30 if there <= 5 * rows else 44),
        cost_estimate=pl.CostEstimate(
            flops=40 * rows * there * width,
            bytes_accessed=8 * (there + rows) * width,
            transcendentals=2 * rows * there * width // HEAD_DIM,
        ),
        name="attend_back_near" if near else "attend_back_far",
    )(flags, qrow, krow, q, k, v, o, g, lse, cosine, sine, *([part] if near else []))


def t_matmul(a, b):
    return lax.dot_general(a, b, (((0,), (0,)), ((), ())), preferred_element_type=F32)


def normed(x):
    centred = x - jnp.mean(x, axis=-1, keepdims=True)
    scale = lax.rsqrt(jnp.mean(centred * centred, axis=-1, keepdims=True) + EPSILON)
    return centred * scale, scale


def side(ref, n, at):
    pairs = ref.shape[0] // 2
    return jnp.concatenate([ref[n * pairs + p, at, :] for p in range(pairs)], axis=1)


def fold_rows_kernel(near, blocks, size, rows, table_ref, *refs):
    refs = list(refs)
    take = lambda n: [refs.pop(0) for _ in range(n)]
    if near:
        [dq_ref] = take(1)
    own_hbm, other_hbm, hbm = take(blocks), take(blocks), take(2)
    if near:
        [clean_ref] = take(1)
    da_ref, own_ref, other_ref = take(3)
    grads, sems = refs[:2], refs[2]
    half = own_ref.shape[1] // 3
    cuts = [slice(n * half, (n + 1) * half) for n in range(3)]
    pieces = list(zip(hbm, grads))
    pieces += placed(own_hbm, own_ref, size, table_ref, 0) + placed(other_hbm, other_ref, size, table_ref, 0)
    for copy in fetch(pieces, sems):
        copy.wait()
    first = 2 if near else 0
    for t in range(grads[0].shape[1] // rows):
        if near and t == 1:
            continue
        at = slice(t * rows, (t + 1) * rows)
        da = None
        for n, w_ref in enumerate((own_ref, other_ref)):
            part = matmul_t(side(grads[0], n, at), w_ref[:, cuts[1]]) + matmul_t(side(grads[1], n, at), w_ref[:, cuts[2]])
            if near and t == 0:
                part = part + matmul_t(dq_ref[at, cuts[n]], w_ref[:, cuts[0]])
            da = part if da is None else da + part
        if near and t == 0:
            clean_ref[...] = da
        else:
            da_ref[(t - first) * rows : (t - first + 1) * rows, :] = da.astype(BF)


def fold_rows(table, dk, dv, own, other, rows, dq=None):
    width = own[0].shape[2] * 2 // 3
    there = dk.shape[1]
    near = dq is not None
    count = sum(v.shape[0] for v in own)
    columns = own[0].shape[2]
    whole = lambda shape: spec(shape, lambda t, i: (0,) * len(shape))
    outs = ([((rows, width), F32)] if near else []) + [((there - (2 * rows if near else 0), width), BF)]
    far = list(own) + list(other) + [dk, dv]
    return pl.pallas_call(
        functools.partial(fold_rows_kernel, near, len(own), width // count, rows),
        grid_spec=pltpu.PrefetchScalarGridSpec(
            num_scalar_prefetch=1,
            grid=(1,),
            in_specs=([whole(dq.shape)] if near else []) + [pl.BlockSpec(memory_space=pl.ANY)] * len(far),
            out_specs=[whole(shape) for shape, _ in outs],
            scratch_shapes=[
                pltpu.VMEM((width, columns), BF),
                pltpu.VMEM((width, columns), BF),
                pltpu.VMEM(dk.shape, BF),
                pltpu.VMEM(dv.shape, BF),
                pltpu.SemaphoreType.DMA((2 * count + 2,)),
            ],
        ),
        out_shape=[jax.ShapeDtypeStruct(shape, kind) for shape, kind in outs],
        compiler_params=vmem(28 if there <= 5 * rows else 40),
        cost_estimate=pl.CostEstimate(
            flops=4 * there * width * width, bytes_accessed=2 * (3 * there * width + 3 * width * width), transcendentals=0
        ),
        name="fold_rows_near" if near else "fold_rows_far",
    )(table, *([dq] if near else []), *far)


def fold_weights_kernel(blocks, sources, size, rows, table_ref, mask_ref, embed_ref, gain_ref, dq_ref, dh_ref, *refs):
    refs = list(refs)
    take = lambda n: [refs.pop(0) for _ in range(n)]
    own_hbm, other_hbm, tiles, hbm = take(blocks), take(blocks), take(sources), take(4)
    piece_refs, noisy_ref, dembed_ref = take(2), *take(2)
    x_ref, a_ref, own_ref, other_ref = take(4)
    grads, sems = take(4), refs[0]
    half = own_ref.shape[1] // 3
    cuts = [slice(n * half, (n + 1) * half) for n in range(3)]
    first = tiled([tiles[0]] + tiles, x_ref, rows)
    second = list(zip(hbm, grads))
    third = placed(own_hbm, own_ref, size, table_ref, 0) + placed(other_hbm, other_ref, size, table_ref, 0)
    copies = fetch(first + second + third, sems)
    for copy in copies[: len(first)]:
        copy.wait()
    masked = column(mask_ref[...].astype(F32)) > 0
    noisy_rows = slice(rows, 2 * rows)
    x_ref[noisy_rows, :] = jnp.where(masked, embed_ref[...], x_ref[noisy_rows, :].astype(F32)).astype(BF)
    for t in range(x_ref.shape[0] // rows):
        at = slice(t * rows, (t + 1) * rows)
        a_ref[at, :] = (normed(x_ref[at, :].astype(F32))[0] * gain_ref[...]).astype(BF)
    for copy in copies[len(first) :]:
        copy.wait()
    there, total = grads[0].shape[1], x_ref.shape[0]
    da = None
    for n, w_ref in enumerate((own_ref, other_ref)):
        part = matmul_t(side(grads[0], n, noisy_rows), w_ref[:, cuts[1]]) + matmul_t(
            side(grads[1], n, noisy_rows), w_ref[:, cuts[2]]
        )
        part = part + matmul_t(dq_ref[noisy_rows, cuts[n]], w_ref[:, cuts[0]])
        da = part if da is None else da + part
    hat, scale = normed(x_ref[noisy_rows, :].astype(F32))
    noisy = dh_ref[...] + norm_back(hat, scale, gain_ref[...], da)
    noisy_ref[...] = noisy
    dembed_ref[...] = jnp.sum(jnp.where(masked, noisy, 0.0), axis=0, keepdims=True)
    for n in range(2):
        piece_refs[n][:, cuts[0]] = t_matmul(a_ref[0 : 2 * rows, :], dq_ref[:, cuts[n]]).astype(BF)
        for m in range(2):
            piece_refs[n][:, cuts[m + 1]] = (
                t_matmul(a_ref[0:there, :], side(grads[m], n, slice(0, there)))
                + t_matmul(a_ref[there:total, :], side(grads[m + 2], n, slice(0, total - there)))
            ).astype(BF)


def fold_weights(table, tiles, near, far, dh, mask, embed, gain, own, other):
    rows, width = tiles[0].shape
    total = (len(tiles) + 1) * rows
    count = sum(v.shape[0] for v in own)
    columns = own[0].shape[2]
    whole = lambda shape: spec(shape, lambda t, i: (0,) * len(shape))
    outs = [((width, columns), BF)] * 2 + [((rows, width), F32), ((1, width), F32)]
    grads = [near[1], near[2], far[1], far[2]]
    distant = list(own) + list(other) + list(tiles) + grads
    return pl.pallas_call(
        functools.partial(fold_weights_kernel, len(own), len(tiles), width // count, rows),
        grid_spec=pltpu.PrefetchScalarGridSpec(
            num_scalar_prefetch=1,
            grid=(1,),
            in_specs=[whole(v.shape) for v in (mask, embed, gain, near[0])]
            + [spec((rows, width), lambda t, i: (1, 0))]
            + [pl.BlockSpec(memory_space=pl.ANY)] * len(distant),
            out_specs=[whole(shape) for shape, _ in outs],
            scratch_shapes=[
                pltpu.VMEM((total, width), BF),
                pltpu.VMEM((total, width), BF),
                pltpu.VMEM((width, columns), BF),
                pltpu.VMEM((width, columns), BF),
            ]
            + [pltpu.VMEM(v.shape, BF) for v in grads]
            + [pltpu.SemaphoreType.DMA((2 * count + len(tiles) + 5,))],
        ),
        out_shape=[jax.ShapeDtypeStruct(shape, kind) for shape, kind in outs],
        compiler_params=vmem(44 if total <= 10 * rows else 58),
        cost_estimate=pl.CostEstimate(
            flops=4 * total * width * width, bytes_accessed=2 * (4 * total * width + 6 * width * width), transcendentals=0
        ),
        name="fold_weights",
    )(table, mask, embed, gain, near[0], dh, *distant)


def normalise(values):
    centred = values - jnp.mean(values, axis=-1, keepdims=True)
    spread = jnp.mean(centred * centred, axis=-1, keepdims=True)
    scale = lax.rsqrt(spread + EPSILON)
    return centred * scale, scale


def norm_back(hat, scale, gain, grad):
    scaled = grad * gain
    return scale * (
        scaled
        - jnp.mean(scaled, axis=-1, keepdims=True)
        - hat * jnp.mean(scaled * hat, axis=-1, keepdims=True)
    )


ROOT = math.sqrt(2.0 / math.pi)


def gelu_parts(u):
    t = jnp.tanh(ROOT * (u + 0.044715 * (u * u * u)))
    slope = 0.5 * (1.0 + t) + 0.5 * u * (1.0 - t * t) * (ROOT * (1.0 + 3 * 0.044715 * (u * u)))
    return 0.5 * u * (1.0 + t), slope


def mm(a, b):
    return jnp.dot(a, b, preferred_element_type=F32)


def mm_t(a, b):
    return lax.dot_general(a, b, (((1,), (1,)), ((), ())), preferred_element_type=F32)


def t_mm(a, b):
    return lax.dot_general(a, b, (((0,), (0,)), ((), ())), preferred_element_type=F32)


def halves_of_heads(w):
    w = w.reshape(w.shape[0], 3, 2, -1)
    return w[:, :, 0].reshape(w.shape[0], -1), w[:, :, 1].reshape(w.shape[0], -1)


def heads_of_halves(a, b):
    a, b = a.reshape(a.shape[0], 3, -1), b.reshape(b.shape[0], 3, -1)
    return jnp.stack([a, b], 2).reshape(a.shape[0], -1)


def halves_of_units(w, chunk):
    w = w.reshape(w.shape[0], -1, 2, chunk)
    return w[:, :, 0].reshape(w.shape[0], -1), w[:, :, 1].reshape(w.shape[0], -1)


def units_of_halves(a, b, chunk):
    a, b = a.reshape(a.shape[0], -1, chunk), b.reshape(b.shape[0], -1, chunk)
    return jnp.stack([a, b], 2).reshape(a.shape[0], -1)


def lower_in_chain(leaf):
    z, y = lax.shift_right_logical(leaf, 1), leaf & 1
    below = [((2 * (z - s) + at), z >= s) for s in (1, 2, 3) for at in (y, 1 - y)]
    return below[:2] + [(2 * z, y == 1)] + below[2:]


class Chain:
    near = 5

    def __init__(self, rows):
        self.at = Links()
        self.rows = rows
        self.core = self.at.core

    def lower(self, leaf):
        return lower_in_chain(leaf)

    def places(self):
        at = self.at
        n = jnp.arange(4)
        zyx = ((at.z ^ n)[None, None, :] * 2 + (at.y ^ n[:2])[None, :, None]) * 2 + (at.x ^ n[:2])[:, None, None]
        yzx = ((at.z ^ n)[None, :, None] * 2 + (at.y ^ n[:2])[:, None, None]) * 2 + (at.x ^ n[:2])[None, None, :]
        first = zyx.reshape(16)
        columns = jnp.where(jnp.arange(16) % 2 == 0, at.core, 1 - at.core)
        return jnp.stack([first, first ^ (8 * at.core), yzx.reshape(16), columns]).astype(jnp.int32)

    def first_gather(self, hid, w_qkv, w_out, w_up, w_down, vectors, facts, early):
        at = self.at
        few, chunk, cut = w_qkv.shape[0], w_down.shape[0], w_out.shape[1] // 2
        qkv_a, qkv_b = halves_of_heads(w_qkv)
        row = jnp.pad(vectors, ((0, 7), (0, qkv_a.shape[1] - vectors.shape[1])))
        qkv_a, qkv_b = (jnp.concatenate([v, row], axis=0) for v in (qkv_a, qkv_b))
        block = to_column_half(at, qkv_a, qkv_b)
        spare = jnp.zeros((6, block.shape[1]), BF)
        block = jnp.concatenate(
            [block[:few], block[few + 8 : 2 * few + 8], block[few : few + 1], block[2 * few + 8 : 2 * few + 9], spare],
            axis=0,
        )[None]
        up_a, up_b = halves_of_units(w_up, chunk)
        one_a = jnp.concatenate([w_out[:, :cut], up_a], axis=1)
        one_b = jnp.concatenate([w_out[:, cut:], up_b], axis=1)
        block, hid_up, one_a, one_b = tie(block, hid, one_a, one_b)
        line = z_gather(at, block)
        beside = at.swap_y(hid_up, [(i, i + 1) for i in range(0, 8, 2)])
        one = to_column_half(at, one_a, one_b)[None]
        line, hid_up, one, beside, down_two, facts = tie(line, hid_up, one, beside, w_down, facts)
        first_hop = at.up(hid_up, 0, 2)
        plane = jnp.concatenate([line, at.swap_y(line)], axis=0)
        one_line = [one, at.swap_z(one, 1)]
        down_two = at.swap_x(down_two)
        turns = early(facts)
        first_hop, plane, one_line, down_two, turns = tie(first_hop, plane, one_line, down_two, turns)
        down_two = jnp.stack([w_down, down_two])[None]
        far = at.swap_x(plane)
        second_hop = at.up(first_hop, 1, 2)
        first_over = at.swap_y(first_hop, [(i, i ^ 1) for i in range(2, 8)])
        second_hop, first_over, one_line, near = tie(second_hop, first_over, one_line, plane)
        third_hop = at.up(second_hop, 2, 2)
        other = [at.swap_core(near)]
        second_over = at.swap_y(second_hop, [(i, i ^ 1) for i in range(4, 8)])
        one_line.append(at.swap_z(one_line[0], 2))
        third_hop, second_over, far, one_line = tie(third_hop, second_over, far, one_line)
        third_over = at.swap_y(third_hop, [(i, i ^ 1) for i in range(6, 8)])
        other.append(at.swap_core(far))
        one_line.append(at.swap_z(one_line[0], 3))
        m = 2 * few
        n = vectors.shape[1]
        vec = jnp.concatenate([plane[:, m : m + 2, :n], far[:, m : m + 2, :n]], axis=0).reshape(16, 2 * n)
        order = (self.places()[0][None, :] == jnp.arange(16)[:, None]).astype(BF)
        vec = mm(order, vec).reshape(32, -1)
        third_over, other, one_line, vec, down_two = tie(third_over, other, one_line, vec, down_two)
        line = jnp.concatenate(one_line, axis=0)
        lower = [first_hop, first_over, beside, second_hop, second_over, third_hop, third_over]
        return lower, ((plane, far), tuple(other)), vec, (line, down_two), turns

    def second_start(self, state):
        line, down_two = state
        return jnp.concatenate([line, self.at.swap_y(line)], axis=0), z_gather(self.at, down_two)

    def second_go_on(self, state):
        plane, line = state
        at = self.at
        near = line.reshape((8,) + line.shape[2:])
        one = (plane, at.swap_x(plane)), [at.swap_core(plane)]
        down = (near, at.swap_y(near)), [at.swap_core(near)]
        return one, down

    def second_end(self, state):
        return [(own, tuple(other + [self.at.swap_core(own[1])])) for own, other in state]

    def unit_bias(self, bias, chunk):
        a, b = halves_of_units(bias[None], chunk)
        return jnp.where(self.core == 0, a, b), jnp.where(self.core == 0, b, a)

    def unit_bias_back(self, own, other, chunk):
        a = jnp.where(self.core == 0, own, other)
        b = jnp.where(self.core == 0, other, own)
        return units_of_halves(a, b, chunk)[0]

    def backward(self, run):
        at = self.at
        rows = self.rows
        lower_z = lambda s: [(i, i ^ 1) for i in range(2 * s, 8)]
        down_other, rest_other = run.feed_other(self)
        down_got, rest_got = at.swap_core(down_other), at.swap_core(rest_other)
        down_own, rest_own = run.feed_own(self)
        by_x = lambda g: g.reshape(8, 2, g.shape[0] // 16, g.shape[1])
        by_y = lambda g: g.reshape(4, 2, 2, g.shape[0] // 16, g.shape[1])
        split_y = lambda g: g.reshape((4, 2) + g.shape[1:])
        down_keep, down_send = halve(at.x, by_x(down_own), by_x(down_got), 1)
        rest_keep, rest_send = halve(at.y, by_y(rest_own), by_y(rest_got), 1)
        down_keep, down_send, rest_keep, rest_send, run.grad_mixed = tie(
            down_keep, down_send, rest_keep, rest_send, run.grad_mixed
        )
        down_got, rest_got = at.swap_x(down_send), at.swap_y(rest_send)
        far = run.far_tiles()
        down_got, rest_got, far = tie(down_got, rest_got, far)
        down_keep, down_send = halve(at.y, split_y(down_keep), split_y(down_got), 1)
        rest_keep, rest_send = z_parts(at, rest_keep, rest_got)
        down_keep, down_send, rest_keep, rest_send, far = tie(down_keep, down_send, rest_keep, rest_send, far)
        far_da = run.far_rows(far)
        tiles = [far_da[n * rows : (n + 1) * rows] for n in range(4)]
        over = jnp.concatenate([tiles[1], tiles[3]], axis=0)
        down_send, tiles, over, far = tie(down_send, tiles, over, far)
        over = at.swap_y(over, lower_z(2))
        down_got = at.swap_y(down_send)
        rest_got = z_move(at, rest_send)
        near = run.near_tiles(far)
        rest_got, over, near, tiles, down_got = tie(rest_got, over, near, tiles, down_got)
        down_keep, down_send = z_parts(at, down_keep, down_got)
        rest = z_total(rest_keep, rest_got).astype(BF)
        rest_keep, rest_send = choose(at.x, rest, 0)
        cur = plus(tiles[2], over[rows:]).astype(BF)
        down_keep, down_send, rest_keep, rest_send, cur, near = tie(
            down_keep, down_send, rest_keep, rest_send, cur, near
        )
        cur = at.down(cur, 3, 3)
        down_got, rest_got = z_move(at, down_send), at.swap_x(rest_send)
        own, other, vec = run.weights(near, far)
        own, other, vec, cur, down_got, rest_got = tie(own, other, vec, cur, down_got, rest_got)
        own, other = self.qkv_pieces(own, other, vec)
        cur = (plus(tiles[0], over[:rows]) + cur.astype(F32)).astype(BF)
        own, other, cur, near = tie(own, other, cur, near)
        got = at.swap_core(other)
        cur = at.down(cur, 2, 3)
        clean, near_da = run.near_rows(near)
        got, cur, clean, near_da = tie(got, cur, clean, near_da)
        keep, send = halve(at.x, own, got, 1)
        keep, send, cur, near_da = tie(keep, send, cur, near_da)
        got = at.swap_x(send)
        first = at.swap_y(near_da[rows : 2 * rows], lower_z(1))
        beside = at.swap_y(near_da[2 * rows :], [(i, i - 1) for i in range(1, 8, 2)])
        sum_down = z_total(down_keep, down_got)
        sum_out, sum_up = self.join_rest(plus(rest_keep, rest_got), run.chunk, run.width)
        got, first, beside, sum_down, sum_out, sum_up = tie(got, first, beside, sum_down, sum_out, sum_up)
        keep, send = halve(at.y, split_y(keep), split_y(got), 1)
        cur = (plus(near_da[:rows], first) + cur.astype(F32)).astype(BF)
        keep, send, cur = tie(keep, send, cur)
        got, cur = at.swap_y(send), at.down(cur, 1, 3)
        got, cur = tie(got, cur)
        keep, send = z_parts(at, keep, got)
        keep, send = tie(keep, send)
        got = z_move(at, send)
        grad_hidden = run.last(clean + cur.astype(F32) + beside.astype(F32))
        got, grad_hidden = tie(got, grad_hidden)
        m = run.few * 2
        g = z_total(keep, got)
        sum_qkv = heads_of_halves(*from_column_half(at, g[:m]))
        return sum_down, sum_up, sum_out, sum_qkv, g[m, : run.vectors], grad_hidden

    def join_rest(self, g, chunk, width):
        a, b = from_column_half(self.at, g)
        cut = width // 2
        out = jnp.concatenate([a[:, :cut], b[:, :cut]], axis=1)
        return out, units_of_halves(a[:, cut:], b[:, cut:], chunk)

    def rest_pieces(self, out, up, other):
        half = out.shape[0] // 2
        core = 1 - self.core if other else self.core
        out = lax.dynamic_slice_in_dim(out, core * half, half, axis=1)
        out = jnp.where(self.core == 0, out, jnp.concatenate([out[half:], out[:half]], axis=0))
        return jnp.concatenate([out.astype(BF), up], axis=1)

    def qkv_pieces(self, own, other, vec):
        n = vec.shape[1]
        vec = vec.astype(BF).reshape(8, 2, 2, n)
        found = []
        for g, core in ((own, self.core), (other, 1 - self.core)):
            g = g.reshape(8, 2, g.shape[0] // 16, g.shape[1])
            rows = pick(vec, core, 2)[:, :, None]
            rows = jnp.pad(rows, ((0, 0), (0, 0), (0, 7), (0, g.shape[3] - n)))
            found.append(jnp.concatenate([g, rows], axis=2))
        return found


AXES = ("leaf", "fsdp")


class Whole:
    def __init__(self, rows, leaves, devices):
        self.rows, self.leaves, self.devices = rows, leaves, devices
        self.leaf = lax.axis_index("leaf")
        self.near = 2 + (leaves - 1) // 2

    def lower(self, leaf):
        return [(leaf - s, leaf >= s) for s in range(1, self.leaves)]

    def places(self):
        return jnp.array([[0, 0], [0, 0], [0, 0], [0, 1]], jnp.int32)

    def first_gather(self, hid, w_qkv, w_out, w_up, w_down, vectors, facts, early):
        tree = lax.all_gather(hid, "leaf", axis=0, tiled=False)
        lower = [pick(tree, jnp.maximum(leaf, 0), 0) for leaf, _ in self.lower(self.leaf)]
        every = lambda w: lax.all_gather(w, AXES, axis=0, tiled=True)
        qkv = tuple((v[None],) for v in halves_of_heads(every(w_qkv)))
        return lower, qkv, every(vectors), (every(w_out), every(w_up), every(w_down)), early(facts)

    def second_start(self, state):
        return state

    def second_go_on(self, state):
        return state

    def second_end(self, state):
        out_w, up_w, down_w = state
        half, cut = down_w.shape[0] // 2, out_w.shape[1] // 2
        one = tuple(
            (jnp.concatenate([out_w[:, n * cut : (n + 1) * cut], up_w[:, n * half : (n + 1) * half]], axis=1)[None],)
            for n in range(2)
        )
        return one, tuple((down_w[None, n * half : (n + 1) * half],) for n in range(2))

    def unit_bias(self, bias, chunk):
        half = bias.shape[0] // 2
        return bias[None, :half], bias[None, half:]

    def unit_bias_back(self, own, other, chunk):
        return jnp.concatenate([own, other], axis=1)[0]

    def scatter(self, g):
        return lax.psum_scatter(g.astype(F32), AXES, scatter_dimension=0, tiled=True)

    def rest_pieces(self, out, up, other):
        cut = out.shape[1] // 2
        return jnp.concatenate([out[:, cut:] if other else out[:, :cut], up.astype(F32)], axis=1)

    def backward(self, run):
        rows = self.rows
        down_other, rest_other = run.feed_other(self)
        down_own, rest_own = run.feed_own(self)
        far = run.far_tiles()
        far_da = run.far_rows(far)
        near = run.near_tiles(far)
        own, other, vec = run.weights(near, far)
        clean, near_da = run.near_rows(near)
        tiles = jnp.concatenate([clean.astype(BF), near_da, far_da], axis=0)
        tiles = tiles.reshape((self.leaves, rows) + tiles.shape[1:])
        order = [pick(tiles, (self.leaf - n) % self.leaves, 0) for n in range(self.leaves)]
        total = lax.psum_scatter(jnp.concatenate(order, axis=0), "leaf", scatter_dimension=0, tiled=True)
        cut = run.width // 2
        return (
            self.scatter(jnp.concatenate([down_own, down_other], axis=0)),
            self.scatter(jnp.concatenate([rest_own[:, cut:], rest_other[:, cut:]], axis=1)),
            self.scatter(jnp.concatenate([rest_own[:, :cut], rest_other[:, :cut]], axis=1)),
            self.scatter(heads_of_halves(own, other)),
            self.scatter(vec)[0],
            run.last(total.astype(F32)),
        )


class Backward:
    pass


def shards(
    leaves,
    groups,
    hidden,
    noise_mask,
    seg_blocks,
    parents,
    ln1_gain,
    w_qkv,
    w_out,
    ln2_gain,
    w_up,
    up_bias,
    w_down,
    down_bias,
    mask_embed,
    cotangent,
):
    rows = hidden.shape[1]
    width = hidden.shape[2]
    half = width // 2
    devices = leaves * groups
    net = Chain(rows) if (leaves, groups) == (8, 4) else Whole(rows, leaves, devices)
    chunk = w_down.shape[0]
    few = ln1_gain.shape[0]
    leaf = lax.axis_index("leaf")

    hid = hidden[0]
    tiles = 2 + len(net.lower(leaf))
    lanes = jnp.arange(128, dtype=jnp.int32)
    exponent = (lanes % (HEAD_DIM // 2)).astype(F32) * (-math.log(10000.0) / (HEAD_DIM // 2))

    def turns(facts):
        found = tables(net.lower, leaf, facts, parents, rows)
        angles = found[2][:, 2:3] * jnp.exp(exponent)
        sign = jnp.where((lanes % HEAD_DIM) < HEAD_DIM // 2, -1.0, 1.0)
        return jnp.cos(angles), jnp.sin(angles) * sign, found

    places = net.places()

    length = 4 * few + up_bias.shape[0]
    vectors = sum(
        jnp.pad(v[None], ((0, 0), (n * few, length - n * few - v.shape[0])))
        for n, v in enumerate((ln1_gain, ln2_gain, down_bias, mask_embed, up_bias))
    )
    lower, qkv_w, vec, coming, (cosine, sine, found) = net.first_gather(
        hid, w_qkv, w_out, w_up, w_down, vectors, seg_blocks, turns
    )
    query_cols, query_rows, key_cols, key_rows, flags = found
    gain_one, gain_two, down_b, embed = (
        vec[:, n * few : (n + 1) * few].reshape(1, width).astype(F32) for n in range(4)
    )
    up_b = jnp.concatenate(net.unit_bias(vec[:, 4 * few :].reshape(-1).astype(F32), chunk), axis=0)
    coming = net.second_start(coming)
    query, key, value = project(
        places, [hid] + lower, noise_mask, embed, gain_one, qkv_w[0], qkv_w[1], cosine, sine
    )
    coming, query = tie(coming, query)
    coming = net.second_go_on(coming)
    mixed, log_norm = attend(flags, query_cols, key_rows, query, key, value, rows)
    coming, mixed = tie(coming, mixed)
    one_w, down_w = net.second_end(coming)
    norm_rows = log_norm.T
    grad_two = cotangent[0].reshape(2 * rows, width)
    (
        output, normed_two, act, grad_pre, grad_one, grad_mixed, grad_after, grad_up_b, grad_down_b,
    ) = middle(places, mixed, hid, noise_mask, embed, grad_two, gain_two, up_b, down_b, one_w, down_w)
    output = output.reshape(1, 2, rows, width)
    units = act.shape[1] // 2

    run = Backward()
    run.chunk, run.few, run.vectors, run.grad_mixed, run.width = chunk, few, length - 2 * few, grad_mixed, width
    cut = net.near

    def feed(n, net):
        at = slice(n * units, (n + 1) * units)
        down, up = t_mm(act[:, at], grad_two).astype(BF), t_mm(normed_two, grad_pre[:, at]).astype(BF)
        return down, net.rest_pieces(t_mm(mixed, grad_one), up, n == 1)

    def far_tiles():
        return attend_back(
            cut, tiles, flags, query_rows, key_rows, query, key, value, mixed, run.grad_mixed, norm_rows, cosine, sine, rows
        )

    def far_rows(far):
        return fold_rows(places, far[1], far[2], qkv_w[0], qkv_w[1], rows)[0]

    def near_tiles(far):
        return attend_back(
            0, cut, flags, query_rows, key_rows, query, key, value, mixed, run.grad_mixed, norm_rows, cosine, sine, rows, far[0]
        )

    def weights(near, far):
        own, other, run.noisy, grad_embed = fold_weights(
            places, [hid] + lower, near, far, grad_after, noise_mask, embed, gain_one, qkv_w[0], qkv_w[1]
        )
        parts = (grad_down_b, grad_embed, net.unit_bias_back(grad_up_b[:1], grad_up_b[1:], chunk))
        return own, other, jnp.concatenate([v.reshape(devices, -1) for v in parts], axis=1)

    def near_rows(near):
        return fold_rows(places, near[1], near[2], qkv_w[0], qkv_w[1], rows, near[0])

    def last(total):
        hat, scale = normalise(hid.astype(F32))
        masked = (noise_mask[0] == 1)[:, None]
        clean = grad_after[:rows] + norm_back(hat, scale, gain_one, total)
        return (clean + jnp.where(masked, 0.0, run.noisy)).astype(BF)[None]

    run.feed_own = lambda net: feed(0, net)
    run.feed_other = lambda net: feed(1, net)
    run.far_tiles, run.far_rows, run.near_tiles, run.near_rows = far_tiles, far_rows, near_tiles, near_rows
    run.weights, run.last = weights, last
    sum_down, sum_up, sum_out, sum_qkv, sum_vec, grad_hidden = net.backward(run)
    from_weight = lambda w, g, gain: jnp.sum(w.astype(F32) * g, axis=1) / gain.astype(F32)
    return (
        output,
        grad_hidden,
        from_weight(w_qkv, sum_qkv, ln1_gain),
        sum_qkv,
        sum_out,
        from_weight(w_up, sum_up, ln2_gain),
        sum_up,
        sum_vec[2 * few :],
        sum_down,
        sum_vec[:few],
        sum_vec[few : 2 * few],
    )


def solution(mesh):
    split = ("leaf", "fsdp")
    in_specs = (
        P("fsdp", "leaf", None),
        P("fsdp", "leaf"),
        P("fsdp", None),
        P("fsdp", None),
        P(split),
        P(split, None),
        P(split, None),
        P(split),
        P(split, None),
        P(split),
        P(split, None),
        P(split),
        P(split),
        P("fsdp", None, "leaf", None),
    )
    out_specs = (
        P("fsdp", None, "leaf", None),
        P("fsdp", "leaf", None),
        P(split),
        P(split, None),
        P(split, None),
        P(split),
        P(split, None),
        P(split),
        P(split, None),
        P(split),
        P(split),
    )
    body = functools.partial(shards, mesh.shape["leaf"], mesh.shape["fsdp"])
    return jax.shard_map(body, mesh=mesh, in_specs=in_specs, out_specs=out_specs, check_vma=False)
```

```python
import functools
import math

import jax
import jax.numpy as jnp
from jax import lax
from jax.experimental import pallas as pl
from jax.experimental.pallas import tpu as pltpu
from jax.sharding import PartitionSpec as P

HEAD_DIM = 64
BLOCK = 16
NEG_FILL = -1000000000.0
EPSILON = 1e-05


def vmem(mebibytes):
    return pltpu.CompilerParams(vmem_limit_bytes=mebibytes * 2**20)


BF = jnp.bfloat16
F32 = jnp.float32


class Links:
    def __init__(self):
        leaf = lax.axis_index("leaf")
        fsdp = lax.axis_index("fsdp")
        self.z, self.y = leaf // 2, leaf % 2
        self.x, self.core = fsdp // 2, fsdp % 2

    def swap_core(self, v):
        return lax.ppermute(v, "fsdp", [(i, i ^ 1) for i in range(4)])

    def swap_x(self, v):
        return lax.ppermute(v, "fsdp", [(i, i ^ 2) for i in range(4)])

    def swap_y(self, v, pairs=None):
        return lax.ppermute(v, "leaf", pairs or [(i, i ^ 1) for i in range(8)])

    def swap_z(self, v, n):
        return lax.ppermute(v, "leaf", [(i, i ^ (2 * n)) for i in range(8)])

    def up(self, v, first, last):
        return lax.ppermute(v, "leaf", [(i, i + 2) for i in range(2 * first, 2 * last + 2)])

    def down(self, v, first, last):
        return lax.ppermute(v, "leaf", [(i, i - 2) for i in range(2 * first, 2 * last + 2)])


def both(bit, own, other, axis):
    return jnp.where(
        bit == 0, jnp.stack([own, other], axis), jnp.stack([other, own], axis)
    )


def tie(*values):
    flat, tree = jax.tree.flatten(values)
    return jax.tree.unflatten(tree, lax.optimization_barrier(tuple(flat)))


def z_gather(at, block):
    return jnp.concatenate([block] + [at.swap_z(block, n) for n in (1, 2, 3)], axis=0)


def pick(v, index, axis):
    return lax.dynamic_index_in_dim(v, index, axis, keepdims=False)


def choose(bit, v, axis):
    return pick(v, bit, axis), pick(v, 1 - bit, axis)


def plus(a, b):
    return a.astype(F32) + b.astype(F32)


def joined(mine, got, index, axis):
    return plus(pick(mine, index, axis), pick(got, index, axis)).astype(BF)


def halve(bit, mine, got, axis):
    return joined(mine, got, bit, axis), joined(mine, got, 1 - bit, axis)


def z_parts(at, mine, got):
    return joined(mine, got, at.z, 0), [joined(mine, got, at.z ^ n, 0) for n in (1, 2, 3)]


def z_move(at, parts):
    return [at.swap_z(part, n) for n, part in zip((1, 2, 3), parts)]


def z_total(keep, got):
    return plus(keep, got[0]) + plus(got[1], got[2])


def to_column_half(at, half_a, half_b):
    keep = jnp.where(at.core == 0, half_a, half_b)
    send = jnp.where(at.core == 0, half_b, half_a)
    got = at.swap_core(send)
    return both(at.core, keep, got, 0).reshape(2 * keep.shape[0], keep.shape[1])


def from_column_half(at, g):
    g = g.reshape(2, g.shape[0] // 2, g.shape[1])
    keep, send = choose(at.core, g, 0)
    got = at.swap_core(send)
    return jnp.where(at.core == 0, keep, got), jnp.where(at.core == 0, got, keep)


def spec(shape, index_map):
    return pl.BlockSpec(shape, index_map)


def turn(values, cosine, sine):
    lane = lax.broadcasted_iota(jnp.int32, (values.shape[0], 128), 1)
    low_half = (lane % HEAD_DIM) < HEAD_DIM // 2
    groups = []
    for n in range(values.shape[1] // 128):
        part = values[:, n * 128 : (n + 1) * 128]
        swapped = jnp.where(low_half, pltpu.roll(part, 96, 1), pltpu.roll(part, 32, 1))
        groups.append(part * cosine + swapped * sine)
    return groups


def column(row):
    return jnp.broadcast_to(row, (8, row.shape[1])).T[:, :1]


def tables_kernel(places, rows, leaf_ref, seg_ref, parent_ref, qcol_ref, qrow_ref, kcol_ref, krow_ref, flag_ref, pad_ref):
    leaf = leaf_ref[0]
    blocks = rows // BLOCK
    slots = 16
    seg = column(seg_ref[...].astype(F32))
    lane = lax.broadcasted_iota(jnp.int32, (seg.shape[0], 128), 1).astype(F32)
    length = jnp.sum(jnp.where(seg == lane, 1.0, 0.0), axis=0, keepdims=True)
    start = jnp.sum(jnp.where(seg < lane, 1.0, 0.0), axis=0, keepdims=True)
    pad_ref[...] = jnp.zeros_like(pad_ref)
    pad_ref[0:1, 0 : parent_ref.shape[1]] = parent_ref[...].astype(F32)
    parent_row = pad_ref[0:1, :]
    lane = lax.broadcasted_iota(jnp.int32, (slots, 128), 1).astype(F32)
    slot = lax.broadcasted_iota(jnp.int32, (slots, 1), 0).astype(F32)
    parent = column(parent_row)[:slots]
    look = lambda index, row: jnp.sum(jnp.where(index == lane, row, 0.0), axis=1, keepdims=True)
    grand = look(parent, parent_row)
    start = look(slot, start)
    shift = jnp.where(slot > 0, look(parent, length), 0.0) + jnp.where(parent > 0, look(grand, length), 0.0) - start

    def facts(block):
        own = jnp.sum(jnp.where(block >= start, 1.0, 0.0), axis=0, keepdims=True) - 1.0
        take = lambda col: jnp.sum(jnp.where(slot == own, col, 0.0), axis=0, keepdims=True)
        return own, take(parent), take(grand), take(shift)

    token = lax.broadcasted_iota(jnp.int32, (1, rows), 1)
    zero = jnp.zeros((1, rows), F32)
    tiles = [(leaf, leaf >= 0), (leaf, leaf < 0)] + places(leaf)
    for t, (place, valid) in enumerate(tiles):
        first = jnp.maximum(place, 0) * blocks
        block = (first + lax.shift_right_logical(token, 4)).astype(F32)
        own, one, two, move = facts(block)
        position = (move + block) * BLOCK + (token & (BLOCK - 1)).astype(F32)
        at = slice(t * rows, (t + 1) * rows)
        if t < 2:
            limit = block + (1.0 if t == 0 else 0.0)
            lines = jnp.concatenate([own, one, two, limit, zero, zero, zero, zero], axis=0)
            qrow_ref[:, at] = lines
            qcol_ref[at, :] = lines.T
        lines = jnp.concatenate(
            [jnp.where(valid, own, -1.0), block, position, zero, zero, zero, zero, zero], axis=0
        )
        krow_ref[:, at] = lines
        kcol_ref[at, :] = lines.T
    queries = qcol_ref[pl.ds(0, 2 * blocks, stride=BLOCK), :]
    lane = lax.broadcasted_iota(jnp.int32, (1, 128), 1)
    for t, (place, valid) in enumerate(tiles):
        if t < 2:
            flag_ref[t] = 1
            continue
        block = (jnp.maximum(place, 0) * blocks + lane).astype(F32)
        own = facts(block)[0]
        allowed = (
            ((own == queries[:, 0:1]) | (own == queries[:, 1:2]) | (own == queries[:, 2:3]))
            & (block < queries[:, 3:4])
            & (lane < blocks)
            & valid
        )
        flag_ref[t] = jnp.max(jnp.where(allowed, 1.0, 0.0)).astype(jnp.int32)


def tables(places, leaf, seg, parent, rows):
    tiles = 2 + len(places(leaf))
    total = tiles * rows
    smem = pl.BlockSpec(memory_space=pltpu.SMEM)
    vmem = pl.BlockSpec(memory_space=pltpu.VMEM)
    shapes = [(2 * rows, 8), (8, 2 * rows), (total, 8), (8, total)]
    return pl.pallas_call(
        functools.partial(tables_kernel, places, rows),
        in_specs=[smem, vmem, vmem],
        out_specs=[vmem] * 4 + [smem],
        out_shape=[jax.ShapeDtypeStruct(shape, F32) for shape in shapes] + [jax.ShapeDtypeStruct((tiles,), jnp.int32)],
        name="tables",
        scratch_shapes=[pltpu.VMEM((8, 128), F32)],
    )(leaf.reshape(1), seg, parent)


def fetch(pieces, sems):
    copies = [pltpu.make_async_copy(src, dst, sems.at[n]) for n, (src, dst) in enumerate(pieces)]
    for copy in copies:
        copy.start()
    return copies


def placed(blocks, ref, size, table, row):
    pieces = []
    for hbm in blocks:
        for n in range(hbm.shape[0]):
            place = pl.multiple_of(table[row, len(pieces)] * size, size)
            pieces.append((hbm.at[n, pl.ds(0, size), :], ref.at[pl.ds(place, size), :]))
    return pieces


def tiled(sources, ref, rows):
    return [(src, ref.at[pl.ds(n * rows, rows), :]) for n, src in enumerate(sources)]


def project_kernel(
    blocks, sources, size, rows, table_ref, mask_ref, embed_ref, gain_ref, cos_ref, sin_ref, *refs,
):
    own_hbm, other_hbm, tiles = refs[:blocks], refs[blocks : 2 * blocks], refs[2 * blocks : 2 * blocks + sources]
    q_ref, k_ref, v_ref, x_ref, own_ref, other_ref, sems = refs[2 * blocks + sources :]
    tile = pl.program_id(0)
    step = k_ref.shape[1]

    @pl.when(tile == 0)
    def _():
        pieces = tiled([tiles[0]] + list(tiles), x_ref, rows)
        count = len(pieces)
        pieces += placed(own_hbm, own_ref, size, table_ref, 0) + placed(other_hbm, other_ref, size, table_ref, 0)
        copies = fetch(pieces, sems)
        for copy in copies[:count]:
            copy.wait()
        masked = column(mask_ref[...].astype(F32)) > 0
        x_ref[rows : 2 * rows, :] = jnp.where(masked, embed_ref[...], x_ref[rows : 2 * rows, :].astype(F32)).astype(BF)
        for copy in copies[count:]:
            copy.wait()

    x = x_ref[pl.ds(pl.multiple_of(tile * step, step), step), :].astype(F32)
    centred = x - jnp.mean(x, axis=-1, keepdims=True)
    spread = jnp.mean(centred * centred, axis=-1, keepdims=True)
    a = (centred * lax.rsqrt(spread + EPSILON) * gain_ref[...]).astype(BF)
    cosine, sine = cos_ref[...], sin_ref[...]
    half = own_ref.shape[1] // 3
    for n, w_ref in enumerate((own_ref, other_ref)):
        base = n * half
        keys = jnp.dot(a, w_ref[:, half : 2 * half], preferred_element_type=F32)
        values = jnp.dot(a, w_ref[:, 2 * half :], preferred_element_type=F32)
        for g, part in enumerate(turn(keys, cosine, sine)):
            k_ref[base // 128 + g] = part.astype(BF)
            v_ref[base // 128 + g] = values[:, g * 128 : (g + 1) * 128].astype(BF)

    @pl.when(tile * step < 2 * rows)
    def _():
        lines = q_ref.shape[0]
        for n, w_ref in enumerate((own_ref, other_ref)):
            base = n * half
            q = jnp.dot(a[:lines], w_ref[:, :half], preferred_element_type=F32)
            for g, part in enumerate(turn(q, cosine[:lines], sine[:lines])):
                q_ref[:, base + g * 128 : base + (g + 1) * 128] = part.astype(BF)


def project(table, tiles, mask, embed, gain, own, other, cosine, sine):
    rows, width = tiles[0].shape
    total = (len(tiles) + 1) * rows
    step = next(n for n in (3 * rows, 2 * rows, rows) if total % n == 0)
    q_step = min(step, 2 * rows)
    last_q = 2 * rows // q_step - 1
    count = sum(v.shape[0] for v in own)
    columns = own[0].shape[2]
    whole = lambda v: spec(v.shape, lambda t, i: (0, 0))
    moved = lambda n: spec((step, n), lambda t, i: (t, 0))
    pairs = spec((width // 128, step, 128), lambda t, i: (0, t, 0))
    out = lambda n: jax.ShapeDtypeStruct((n, width), BF)
    anywhere = pl.BlockSpec(memory_space=pl.ANY)
    far = list(own) + list(other) + list(tiles)
    return pl.pallas_call(
        functools.partial(project_kernel, len(own), len(tiles), width // count, rows),
        grid_spec=pltpu.PrefetchScalarGridSpec(
            num_scalar_prefetch=1,
            grid=(total // step,),
            in_specs=[whole(mask), whole(embed), whole(gain), moved(128), moved(128)] + [anywhere] * len(far),
            out_specs=[
                spec((q_step, width), lambda t, i: (jnp.minimum(t, last_q), 0)),
                pairs,
                pairs,
            ],
            scratch_shapes=[
                pltpu.VMEM((total, width), BF),
                pltpu.VMEM((width, columns), BF),
                pltpu.VMEM((width, columns), BF),
                pltpu.SemaphoreType.DMA((2 * count + len(tiles) + 1,)),
            ],
        ),
        out_shape=[out(2 * rows)] + [jax.ShapeDtypeStruct((width // 128, total, 128), BF)] * 2,
        compiler_params=vmem(26 if total <= 10 * rows else 40),
        cost_estimate=pl.CostEstimate(
            flops=2 * total * width * 2 * width + 4 * rows * width * width,
            bytes_accessed=2 * (3 * total * width + 3 * width * width),
            transcendentals=0,
        ),
        name="project",
    )(table, mask, embed, gain, cosine, sine, *far)


def middle_kernel(
    blocks_one, blocks_two, size, chunk, table_ref, o_ref, x_ref, mask_ref, embed_ref, dy_ref, gain_ref, up_b_ref,
    down_b_ref, *refs,
):
    refs = list(refs)
    take = lambda n: [refs.pop(0) for _ in range(n)]
    ones, twos = (take(blocks_one), take(blocks_one)), (take(blocks_two), take(blocks_two))
    y_ref, b_ref, g_ref, du_ref, dh_low_ref, do_ref, dh_ref, dup_b_ref, ddown_b_ref = take(9)
    out_ref, up_ref, down_ref, sems = refs
    cut = out_ref.shape[1] // 2
    units = up_ref.shape[2]
    pieces_out, pieces = [], []
    for n in range(2):
        columns = pl.ds(pl.multiple_of(table_ref[3, n] * cut, cut), cut)
        spots = [(hbm, j) for hbm in ones[n] for j in range(hbm.shape[0])]
        pieces.append([])
        for place, (hbm, j) in enumerate(spots):
            to = pl.ds(pl.multiple_of(table_ref[1, place] * size, size), size)
            pieces_out.append((hbm.at[j, :, pl.ds(0, cut)], out_ref.at[to, columns]))
            to = pl.ds(pl.multiple_of(table_ref[0, place] * size, size), size)
            pieces[n].append((hbm.at[j, :, pl.ds(cut, units)], up_ref.at[n, to, :]))
        pieces[n] += placed(twos[n], down_ref.at[n], chunk, table_ref, 2)
    copies = fetch(pieces_out + pieces[0] + pieces[1], sems)
    for copy in copies[: len(pieces_out)]:
        copy.wait()
    x = x_ref[...].astype(F32)
    masked = column(mask_ref[...].astype(F32)) > 0
    x = jnp.concatenate([x, jnp.where(masked, embed_ref[...], x)], axis=0)
    h = x + jnp.dot(o_ref[...], out_ref[...], preferred_element_type=F32)
    centred = h - jnp.mean(h, axis=-1, keepdims=True)
    spread = jnp.mean(centred * centred, axis=-1, keepdims=True)
    scale = lax.rsqrt(spread + EPSILON)
    hat = centred * scale
    b = (hat * gain_ref[...]).astype(BF)
    b_ref[...] = b
    dy = dy_ref[...]
    ddown_b_ref[...] = jnp.sum(dy.astype(F32), axis=0, keepdims=True)
    y = h + down_b_ref[...]
    db = None
    wide = next(n for n in (768, 512, 384, 256, 128) if units % n == 0)
    for n in range(2):
        done = len(pieces_out) + n * len(pieces[0])
        for copy in copies[done : done + len(pieces[n])]:
            copy.wait()
        for c in range(0, units, wide):
            at = slice(c, c + wide)
            to = slice(n * units + c, n * units + c + wide)
            u = jnp.dot(b, up_ref[n, :, at], preferred_element_type=F32) + up_b_ref[n : n + 1, at]
            g, slope = gelu_parts(u)
            g = g.astype(BF)
            g_ref[:, to] = g
            y = y + jnp.dot(g, down_ref[n, at, :], preferred_element_type=F32)
            du = (matmul_t(dy, down_ref[n, at, :]) * slope).astype(BF)
            du_ref[:, to] = du
            dup_b_ref[n : n + 1, at] = jnp.sum(du.astype(F32), axis=0, keepdims=True)
            part = matmul_t(du, up_ref[n, :, at])
            db = part if db is None else db + part
    y_ref[...] = y.astype(BF)
    dh = dy.astype(F32) + norm_back(hat, scale, gain_ref[...], db)
    dh_ref[...] = dh
    low = dh.astype(BF)
    dh_low_ref[...] = low
    do_ref[...] = matmul_t(low, out_ref[...]).astype(BF)


def middle(table, o, x, mask, embed, dy, gain, up_b, down_b, one, two):
    rows, width = o.shape
    count = sum(v.shape[0] for v in one[0])
    size, columns = one[0][0].shape[1:]
    chunk = two[0][0].shape[1]
    units = columns - width // 2
    full = lambda shape: spec(shape, lambda t, i: (0, 0))
    near = (o, x, mask, embed, dy, gain, up_b, down_b)
    far = list(one[0]) + list(one[1]) + list(two[0]) + list(two[1])
    shapes = [
        ((rows, width), BF), ((rows, width), BF), ((rows, 2 * units), BF), ((rows, 2 * units), BF), ((rows, width), BF),
        ((rows, width), BF), ((rows, width), F32), ((2, units), F32), ((1, width), F32),
    ]
    return pl.pallas_call(
        functools.partial(middle_kernel, len(one[0]), len(two[0]), size, chunk),
        grid_spec=pltpu.PrefetchScalarGridSpec(
            num_scalar_prefetch=1,
            grid=(1,),
            in_specs=[full(v.shape) for v in near] + [pl.BlockSpec(memory_space=pl.ANY)] * len(far),
            out_specs=[full(shape) for shape, _ in shapes],
            scratch_shapes=[
                pltpu.VMEM((width, width), BF),
                pltpu.VMEM((2, width, units), BF),
                pltpu.VMEM((2, units, width), BF),
                pltpu.SemaphoreType.DMA((6 * count,)),
            ],
        ),
        out_shape=[jax.ShapeDtypeStruct(shape, kind) for shape, kind in shapes],
        compiler_params=vmem(44),
        cost_estimate=pl.CostEstimate(
            flops=2 * rows * width * (2 * width + 8 * units),
            bytes_accessed=4 * (width * width + 4 * units * width),
            transcendentals=2 * rows * units,
        ),
        name="middle",
    )(table, *near, *far)


def matmul_t(a, b):
    return lax.dot_general(a, b, (((1,), (1,)), ((), ())), preferred_element_type=F32)


def groups(tiles, first=2, size=2):
    found = []
    for start, end in ((2, min(5, tiles)), (5, tiles)):
        start = max(start, first)
        while start < end:
            found.append((start, min(start + size, end)))
            start += size
    return found


def attend_kernel(
    rows, tiles, flag_ref, qcol_ref, krow_ref, q_ref, k_ref, v_ref, o_ref, lse_ref,
    bias_ref, s_ref, top_ref, sum_ref, acc_ref,
):
    pair = pl.program_id(0)
    both_rows = 2 * rows

    def span(t):
        return slice(t * rows, (t + 1) * rows)

    def lines(t):
        return slice(rows, both_rows) if t == 1 else slice(0, both_rows)

    @pl.when(pair == 0)
    def _():
        lse_ref[...] = jnp.zeros_like(lse_ref)
        own = qcol_ref[:, 0:1]
        up_one = qcol_ref[:, 1:2]
        up_two = qcol_ref[:, 2:3]
        limit = qcol_ref[:, 3:4]
        for t in range(tiles):
            if t == 1:
                r = lax.broadcasted_iota(jnp.int32, (rows, rows), 0) // BLOCK
                c = lax.broadcasted_iota(jnp.int32, (rows, rows), 1) // BLOCK
                bias_ref[rows:, span(t)] = jnp.where(r == c, 0.0, NEG_FILL)
            else:
                seg = krow_ref[0:1, span(t)]
                index = krow_ref[1:2, span(t)]
                ok = ((seg == own) | (seg == up_one) | (seg == up_two)) & (index < limit)
                bias_ref[:, span(t)] = jnp.where(ok, 0.0, NEG_FILL)

    lane = lax.broadcasted_iota(jnp.int32, (both_rows, 128), 1)
    queries = [jnp.where((lane // HEAD_DIM) == h, q_ref[...] * 0.125, 0).astype(BF) for h in range(2)]
    top_ref[...] = jnp.full_like(top_ref, -3.0e38)

    def scores(first, last, at):
        cut = slice(first * rows, last * rows)
        keys = k_ref[0, cut, :]
        for h in range(2):
            s = matmul_t(queries[h][at], keys) + bias_ref[at, cut]
            s_ref[h, at, cut] = s
            best = top_ref[h, at, :]
            for c in range(s.shape[1] // 128):
                best = jnp.maximum(best, s[:, c * 128 : (c + 1) * 128])
            top_ref[h, at, :] = best

    def weigh(first, last, at):
        cut = slice(first * rows, last * rows)
        values = v_ref[0, cut, :]
        for h in range(2):
            p = jnp.exp(s_ref[h, at, cut] - tops[h][at])
            part = sum_ref[h, at, :]
            for c in range(p.shape[1] // 128):
                part = part + p[:, c * 128 : (c + 1) * 128]
            sum_ref[h, at, :] = part
            acc_ref[h, at, :] += jnp.dot(p.astype(BF), values, preferred_element_type=F32)

    upper, lower, all_rows = slice(0, rows), slice(rows, both_rows), slice(0, both_rows)

    def each(step):
        step(0, 1, upper)
        step(0, 2, lower)
        for first, last in groups(tiles, 2, 4):
            some = flag_ref[first]
            for t in range(first + 1, last):
                some = some + flag_ref[t]
            pl.when(some > 0)(functools.partial(step, first, last, all_rows))

    each(scores)
    tops = [jnp.max(top_ref[h], axis=-1, keepdims=True) for h in range(2)]
    sum_ref[...] = jnp.zeros_like(sum_ref)
    acc_ref[...] = jnp.zeros_like(acc_ref)
    each(weigh)
    outs, norms = [], lse_ref[...]
    for h in range(2):
        total = jnp.sum(sum_ref[h], axis=-1, keepdims=True)
        outs.append(acc_ref[h] / total)
        norms = jnp.where(lane == 2 * pair + h, tops[h] + jnp.log(total), norms)
    lse_ref[...] = norms
    o_ref[...] = jnp.where(lane < HEAD_DIM, outs[0], outs[1]).astype(BF)


def attend(flags, qcol, krow, q, k, v, rows):
    width = q.shape[1]
    total = k.shape[1]
    tiles = total // rows
    whole_pair = spec((1, total, 128), lambda p, f: (p, 0, 0))
    pair = lambda n: spec((n, 128), lambda p, f: (0, p))
    fixed = lambda shape: spec(shape, lambda p, f: (0, 0))
    return pl.pallas_call(
        functools.partial(attend_kernel, rows, tiles),
        grid_spec=pltpu.PrefetchScalarGridSpec(
            num_scalar_prefetch=1,
            grid=(width // 128,),
            in_specs=[fixed(qcol.shape), fixed(krow.shape), pair(2 * rows), whole_pair, whole_pair],
            out_specs=[pair(2 * rows), fixed((2 * rows, 128))],
            scratch_shapes=[
                pltpu.VMEM((2 * rows, total), F32),
                pltpu.VMEM((2, 2 * rows, total), F32),
                pltpu.VMEM((2, 2 * rows, 128), F32),
                pltpu.VMEM((2, 2 * rows, 128), F32),
                pltpu.VMEM((2, 2 * rows, 128), F32),
            ],
        ),
        out_shape=[
            jax.ShapeDtypeStruct((2 * rows, width), BF),
            jax.ShapeDtypeStruct((2 * rows, 128), F32),
        ],
        compiler_params=vmem(28 if tiles <= 10 else 52),
        cost_estimate=pl.CostEstimate(
            flops=16 * rows * total * width,
            bytes_accessed=4 * (total + rows) * width,
            transcendentals=2 * rows * total * width // HEAD_DIM,
        ),
        name="attend",
    )(flags, qcol, krow, q, k, v)


def attend_back_kernel(
    rows, first, last, flag_ref, qrow_ref, krow_ref, q_ref, k_ref, v_ref, o_ref, g_ref, lse_ref, *refs,
):
    refs = list(refs)
    near = first == 0
    cos_ref, sin_ref = refs[:2]
    part_ref = refs[2] if near else None
    dq_ref, dk_ref, dv_ref, bias_ref, acc_ref = refs[-5:]
    pair = pl.program_id(0)
    both_rows = 2 * rows

    def span(t):
        return slice(t * rows, (t + 1) * rows)

    @pl.when(pair == 0)
    def _():
        own = qrow_ref[0:1, :]
        up_one = qrow_ref[1:2, :]
        up_two = qrow_ref[2:3, :]
        limit = qrow_ref[3:4, :]
        for t in range(first, last):
            if t == 1:
                r = lax.broadcasted_iota(jnp.int32, (rows, both_rows), 0) // BLOCK
                c = lax.broadcasted_iota(jnp.int32, (rows, both_rows), 1) // BLOCK
                bias_ref[span(t - first), :] = jnp.where(r + rows // BLOCK == c, 0.0, NEG_FILL)
            else:
                facts = krow_ref[:, span(t - first)].T
                seg = facts[:, 0:1]
                index = facts[:, 1:2]
                ok = ((seg == own) | (seg == up_one) | (seg == up_two)) & (index < limit)
                bias_ref[span(t - first), :] = jnp.where(ok, 0.0, NEG_FILL)

    lane = lax.broadcasted_iota(jnp.int32, (both_rows, 128), 1)
    acc_ref[...] = part_ref[...] if near else jnp.zeros_like(acc_ref)
    queries, grads, deltas, norms, queries_t, grads_t = [], [], [], [], [], []
    product = (o_ref[...].astype(F32) * g_ref[...].astype(F32)).T
    for h in range(2):
        mine = (lane // HEAD_DIM) == h
        queries.append(jnp.where(mine, q_ref[...] * 0.125, 0).astype(BF))
        grads.append(jnp.where(mine, g_ref[...], 0).astype(BF))
        queries_t.append(queries[h].astype(F32).T.astype(BF))
        grads_t.append(grads[h].astype(F32).T.astype(BF))
        deltas.append(jnp.sum(product[h * HEAD_DIM : (h + 1) * HEAD_DIM], axis=0, keepdims=True))
        norms.append(lse_ref[pl.ds(2 * pair + h, 1), :])

    def step(start, end):
        to = slice((start - first) * rows, (end - first) * rows)
        keys, values = k_ref[0, to, :], v_ref[0, to, :]
        keys_t = keys.astype(F32).T.astype(BF)
        dk = dv = None
        for h in range(2):
            q, g = queries[h], grads[h]
            s = jnp.dot(keys, queries_t[h], preferred_element_type=F32) + bias_ref[to, :]
            p = jnp.exp(s - norms[h])
            dp = jnp.dot(values, grads_t[h], preferred_element_type=F32)
            ds = (p * (dp - deltas[h])).astype(BF)
            part_v = jnp.dot(p.astype(BF), g, preferred_element_type=F32)
            part_k = jnp.dot(ds, q, preferred_element_type=F32)
            dv = part_v if dv is None else dv + part_v
            dk = part_k if dk is None else dk + part_k
            half = slice(h * HEAD_DIM, (h + 1) * HEAD_DIM)
            acc_ref[half, :] += jnp.dot(keys_t[half], ds, preferred_element_type=F32)
        [dk] = turn(dk, cos_ref[to, :], -sin_ref[to, :])
        dk_ref[0, to, :] = dk.astype(BF)
        dv_ref[0, to, :] = dv.astype(BF)

    if near:
        step(0, 2)
    for start, end in groups(last, max(first, 2), 4):
        some = flag_ref[start]
        for t in range(start + 1, end):
            some = some + flag_ref[t]
        to = slice((start - first) * rows, (end - first) * rows)

        @pl.when(some == 0)
        def _():
            dk_ref[0, to, :] = jnp.zeros(((end - start) * rows, 128), BF)
            dv_ref[0, to, :] = jnp.zeros(((end - start) * rows, 128), BF)

        pl.when(some > 0)(functools.partial(step, start, end))

    if near:
        dq = acc_ref[...].T * 0.125
        [dq] = turn(dq, cos_ref[:both_rows, :], -sin_ref[:both_rows, :])
        dq_ref[...] = dq.astype(BF)
    else:
        dq_ref[...] = acc_ref[...]


def attend_back(first, last, flags, qrow, krow, q, k, v, o, g, lse, cosine, sine, rows, part=None):
    width = q.shape[1]
    there = (last - first) * rows
    near = first == 0
    some_pair = lambda n: spec((1, n, 128), lambda p, f: (p, 0, 0))
    taken_pair = spec((pl.Element(1), pl.Element(there), pl.Element(128)), lambda p, f: (p, first * rows, 0))
    taken = spec((pl.Element(there), pl.Element(128)), lambda p, f: (first * rows, 0))
    pair = lambda n: spec((n, 128), lambda p, f: (0, p))
    turned = spec((128, 2 * rows), lambda p, f: (p, 0))
    fixed = lambda shape: spec(shape, lambda p, f: (0, 0))
    out = lambda n: jax.ShapeDtypeStruct((n, width), BF)
    return pl.pallas_call(
        functools.partial(attend_back_kernel, rows, first, last),
        grid_spec=pltpu.PrefetchScalarGridSpec(
            num_scalar_prefetch=1,
            grid=(width // 128,),
            in_specs=[
                fixed(qrow.shape), spec((pl.Element(8), pl.Element(there)), lambda p, f: (0, first * rows)), pair(2 * rows),
                taken_pair, taken_pair, pair(2 * rows), pair(2 * rows), fixed(lse.shape), taken, taken,
            ] + ([turned] if near else []),
            out_specs=[pair(2 * rows) if near else turned, some_pair(there), some_pair(there)],
            scratch_shapes=[
                pltpu.VMEM((there, 2 * rows), F32),
                pltpu.VMEM((128, 2 * rows), F32),
            ],
        ),
        out_shape=[out(2 * rows) if near else jax.ShapeDtypeStruct((width, 2 * rows), F32)]
        + [jax.ShapeDtypeStruct((width // 128, there, 128), BF)] * 2,
        compiler_params=vmem(30 if there <= 5 * rows else 44),
        cost_estimate=pl.CostEstimate(
            flops=40 * rows * there * width,
            bytes_accessed=8 * (there + rows) * width,
            transcendentals=2 * rows * there * width // HEAD_DIM,
        ),
        name="attend_back_near" if near else "attend_back_far",
    )(flags, qrow, krow, q, k, v, o, g, lse, cosine, sine, *([part] if near else []))


def t_matmul(a, b):
    return lax.dot_general(a, b, (((0,), (0,)), ((), ())), preferred_element_type=F32)


def normed(x):
    centred = x - jnp.mean(x, axis=-1, keepdims=True)
    scale = lax.rsqrt(jnp.mean(centred * centred, axis=-1, keepdims=True) + EPSILON)
    return centred * scale, scale


def side(ref, n, at):
    pairs = ref.shape[0] // 2
    return jnp.concatenate([ref[n * pairs + p, at, :] for p in range(pairs)], axis=1)


def fold_rows_kernel(near, blocks, size, rows, table_ref, *refs):
    refs = list(refs)
    take = lambda n: [refs.pop(0) for _ in range(n)]
    if near:
        [dq_ref] = take(1)
    own_hbm, other_hbm, hbm = take(blocks), take(blocks), take(2)
    if near:
        [clean_ref] = take(1)
    da_ref, own_ref, other_ref = take(3)
    grads, sems = refs[:2], refs[2]
    half = own_ref.shape[1] // 3
    cuts = [slice(n * half, (n + 1) * half) for n in range(3)]
    pieces = list(zip(hbm, grads))
    pieces += placed(own_hbm, own_ref, size, table_ref, 0) + placed(other_hbm, other_ref, size, table_ref, 0)
    for copy in fetch(pieces, sems):
        copy.wait()
    first = 2 if near else 0
    for t in range(grads[0].shape[1] // rows):
        if near and t == 1:
            continue
        at = slice(t * rows, (t + 1) * rows)
        da = None
        for n, w_ref in enumerate((own_ref, other_ref)):
            part = matmul_t(side(grads[0], n, at), w_ref[:, cuts[1]]) + matmul_t(side(grads[1], n, at), w_ref[:, cuts[2]])
            if near and t == 0:
                part = part + matmul_t(dq_ref[at, cuts[n]], w_ref[:, cuts[0]])
            da = part if da is None else da + part
        if near and t == 0:
            clean_ref[...] = da
        else:
            da_ref[(t - first) * rows : (t - first + 1) * rows, :] = da.astype(BF)


def fold_rows(table, dk, dv, own, other, rows, dq=None):
    width = own[0].shape[2] * 2 // 3
    there = dk.shape[1]
    near = dq is not None
    count = sum(v.shape[0] for v in own)
    columns = own[0].shape[2]
    whole = lambda shape: spec(shape, lambda t, i: (0,) * len(shape))
    outs = ([((rows, width), F32)] if near else []) + [((there - (2 * rows if near else 0), width), BF)]
    far = list(own) + list(other) + [dk, dv]
    return pl.pallas_call(
        functools.partial(fold_rows_kernel, near, len(own), width // count, rows),
        grid_spec=pltpu.PrefetchScalarGridSpec(
            num_scalar_prefetch=1,
            grid=(1,),
            in_specs=([whole(dq.shape)] if near else []) + [pl.BlockSpec(memory_space=pl.ANY)] * len(far),
            out_specs=[whole(shape) for shape, _ in outs],
            scratch_shapes=[
                pltpu.VMEM((width, columns), BF),
                pltpu.VMEM((width, columns), BF),
                pltpu.VMEM(dk.shape, BF),
                pltpu.VMEM(dv.shape, BF),
                pltpu.SemaphoreType.DMA((2 * count + 2,)),
            ],
        ),
        out_shape=[jax.ShapeDtypeStruct(shape, kind) for shape, kind in outs],
        compiler_params=vmem(28 if there <= 5 * rows else 40),
        cost_estimate=pl.CostEstimate(
            flops=4 * there * width * width, bytes_accessed=2 * (3 * there * width + 3 * width * width), transcendentals=0
        ),
        name="fold_rows_near" if near else "fold_rows_far",
    )(table, *([dq] if near else []), *far)


def fold_weights_kernel(blocks, sources, size, rows, table_ref, mask_ref, embed_ref, gain_ref, dq_ref, dh_ref, *refs):
    refs = list(refs)
    take = lambda n: [refs.pop(0) for _ in range(n)]
    own_hbm, other_hbm, tiles, hbm = take(blocks), take(blocks), take(sources), take(4)
    piece_refs, noisy_ref, dembed_ref = take(2), *take(2)
    x_ref, a_ref, own_ref, other_ref = take(4)
    grads, sems = take(4), refs[0]
    half = own_ref.shape[1] // 3
    cuts = [slice(n * half, (n + 1) * half) for n in range(3)]
    first = tiled([tiles[0]] + tiles, x_ref, rows)
    second = list(zip(hbm, grads))
    third = placed(own_hbm, own_ref, size, table_ref, 0) + placed(other_hbm, other_ref, size, table_ref, 0)
    copies = fetch(first + second + third, sems)
    for copy in copies[: len(first)]:
        copy.wait()
    masked = column(mask_ref[...].astype(F32)) > 0
    noisy_rows = slice(rows, 2 * rows)
    x_ref[noisy_rows, :] = jnp.where(masked, embed_ref[...], x_ref[noisy_rows, :].astype(F32)).astype(BF)
    for t in range(x_ref.shape[0] // rows):
        at = slice(t * rows, (t + 1) * rows)
        a_ref[at, :] = (normed(x_ref[at, :].astype(F32))[0] * gain_ref[...]).astype(BF)
    for copy in copies[len(first) :]:
        copy.wait()
    there, total = grads[0].shape[1], x_ref.shape[0]
    da = None
    for n, w_ref in enumerate((own_ref, other_ref)):
        part = matmul_t(side(grads[0], n, noisy_rows), w_ref[:, cuts[1]]) + matmul_t(
            side(grads[1], n, noisy_rows), w_ref[:, cuts[2]]
        )
        part = part + matmul_t(dq_ref[noisy_rows, cuts[n]], w_ref[:, cuts[0]])
        da = part if da is None else da + part
    hat, scale = normed(x_ref[noisy_rows, :].astype(F32))
    noisy = dh_ref[...] + norm_back(hat, scale, gain_ref[...], da)
    noisy_ref[...] = noisy
    dembed_ref[...] = jnp.sum(jnp.where(masked, noisy, 0.0), axis=0, keepdims=True)
    for n in range(2):
        piece_refs[n][:, cuts[0]] = t_matmul(a_ref[0 : 2 * rows, :], dq_ref[:, cuts[n]]).astype(BF)
        for m in range(2):
            piece_refs[n][:, cuts[m + 1]] = (
                t_matmul(a_ref[0:there, :], side(grads[m], n, slice(0, there)))
                + t_matmul(a_ref[there:total, :], side(grads[m + 2], n, slice(0, total - there)))
            ).astype(BF)


def fold_weights(table, tiles, near, far, dh, mask, embed, gain, own, other):
    rows, width = tiles[0].shape
    total = (len(tiles) + 1) * rows
    count = sum(v.shape[0] for v in own)
    columns = own[0].shape[2]
    whole = lambda shape: spec(shape, lambda t, i: (0,) * len(shape))
    outs = [((width, columns), BF)] * 2 + [((rows, width), F32), ((1, width), F32)]
    grads = [near[1], near[2], far[1], far[2]]
    distant = list(own) + list(other) + list(tiles) + grads
    return pl.pallas_call(
        functools.partial(fold_weights_kernel, len(own), len(tiles), width // count, rows),
        grid_spec=pltpu.PrefetchScalarGridSpec(
            num_scalar_prefetch=1,
            grid=(1,),
            in_specs=[whole(v.shape) for v in (mask, embed, gain, near[0])]
            + [spec((rows, width), lambda t, i: (1, 0))]
            + [pl.BlockSpec(memory_space=pl.ANY)] * len(distant),
            out_specs=[whole(shape) for shape, _ in outs],
            scratch_shapes=[
                pltpu.VMEM((total, width), BF),
                pltpu.VMEM((total, width), BF),
                pltpu.VMEM((width, columns), BF),
                pltpu.VMEM((width, columns), BF),
            ]
            + [pltpu.VMEM(v.shape, BF) for v in grads]
            + [pltpu.SemaphoreType.DMA((2 * count + len(tiles) + 5,))],
        ),
        out_shape=[jax.ShapeDtypeStruct(shape, kind) for shape, kind in outs],
        compiler_params=vmem(44 if total <= 10 * rows else 58),
        cost_estimate=pl.CostEstimate(
            flops=4 * total * width * width, bytes_accessed=2 * (4 * total * width + 6 * width * width), transcendentals=0
        ),
        name="fold_weights",
    )(table, mask, embed, gain, near[0], dh, *distant)


def normalise(values):
    centred = values - jnp.mean(values, axis=-1, keepdims=True)
    spread = jnp.mean(centred * centred, axis=-1, keepdims=True)
    scale = lax.rsqrt(spread + EPSILON)
    return centred * scale, scale


def norm_back(hat, scale, gain, grad):
    scaled = grad * gain
    return scale * (
        scaled
        - jnp.mean(scaled, axis=-1, keepdims=True)
        - hat * jnp.mean(scaled * hat, axis=-1, keepdims=True)
    )


ROOT = math.sqrt(2.0 / math.pi)


def gelu_parts(u):
    t = jnp.tanh(ROOT * (u + 0.044715 * (u * u * u)))
    slope = 0.5 * (1.0 + t) + 0.5 * u * (1.0 - t * t) * (ROOT * (1.0 + 3 * 0.044715 * (u * u)))
    return 0.5 * u * (1.0 + t), slope


def mm(a, b):
    return jnp.dot(a, b, preferred_element_type=F32)


def mm_t(a, b):
    return lax.dot_general(a, b, (((1,), (1,)), ((), ())), preferred_element_type=F32)


def t_mm(a, b):
    return lax.dot_general(a, b, (((0,), (0,)), ((), ())), preferred_element_type=F32)


def halves_of_heads(w):
    w = w.reshape(w.shape[0], 3, 2, -1)
    return w[:, :, 0].reshape(w.shape[0], -1), w[:, :, 1].reshape(w.shape[0], -1)


def heads_of_halves(a, b):
    a, b = a.reshape(a.shape[0], 3, -1), b.reshape(b.shape[0], 3, -1)
    return jnp.stack([a, b], 2).reshape(a.shape[0], -1)


def halves_of_units(w, chunk):
    w = w.reshape(w.shape[0], -1, 2, chunk)
    return w[:, :, 0].reshape(w.shape[0], -1), w[:, :, 1].reshape(w.shape[0], -1)


def units_of_halves(a, b, chunk):
    a, b = a.reshape(a.shape[0], -1, chunk), b.reshape(b.shape[0], -1, chunk)
    return jnp.stack([a, b], 2).reshape(a.shape[0], -1)


def lower_in_chain(leaf):
    z, y = lax.shift_right_logical(leaf, 1), leaf & 1
    below = [((2 * (z - s) + at), z >= s) for s in (1, 2, 3) for at in (y, 1 - y)]
    return below[:2] + [(2 * z, y == 1)] + below[2:]


class Chain:
    near = 5

    def __init__(self, rows):
        self.at = Links()
        self.rows = rows
        self.core = self.at.core

    def lower(self, leaf):
        return lower_in_chain(leaf)

    def places(self):
        at = self.at
        n = jnp.arange(4)
        zyx = ((at.z ^ n)[None, None, :] * 2 + (at.y ^ n[:2])[None, :, None]) * 2 + (at.x ^ n[:2])[:, None, None]
        yzx = ((at.z ^ n)[None, :, None] * 2 + (at.y ^ n[:2])[:, None, None]) * 2 + (at.x ^ n[:2])[None, None, :]
        first = zyx.reshape(16)
        columns = jnp.where(jnp.arange(16) % 2 == 0, at.core, 1 - at.core)
        return jnp.stack([first, first ^ (8 * at.core), yzx.reshape(16), columns]).astype(jnp.int32)

    def first_gather(self, hid, w_qkv, w_out, w_up, w_down, vectors, facts, early):
        at = self.at
        few, chunk, cut = w_qkv.shape[0], w_down.shape[0], w_out.shape[1] // 2
        qkv_a, qkv_b = halves_of_heads(w_qkv)
        row = jnp.pad(vectors, ((0, 7), (0, qkv_a.shape[1] - vectors.shape[1])))
        qkv_a, qkv_b = (jnp.concatenate([v, row], axis=0) for v in (qkv_a, qkv_b))
        block = to_column_half(at, qkv_a, qkv_b)
        spare = jnp.zeros((6, block.shape[1]), BF)
        block = jnp.concatenate(
            [block[:few], block[few + 8 : 2 * few + 8], block[few : few + 1], block[2 * few + 8 : 2 * few + 9], spare],
            axis=0,
        )[None]
        up_a, up_b = halves_of_units(w_up, chunk)
        one_a = jnp.concatenate([w_out[:, :cut], up_a], axis=1)
        one_b = jnp.concatenate([w_out[:, cut:], up_b], axis=1)
        block, hid_up, one_a, one_b = tie(block, hid, one_a, one_b)
        line = z_gather(at, block)
        beside = at.swap_y(hid_up, [(i, i + 1) for i in range(0, 8, 2)])
        one = to_column_half(at, one_a, one_b)[None]
        line, hid_up, one, beside, down_two, facts = tie(line, hid_up, one, beside, w_down, facts)
        first_hop = at.up(hid_up, 0, 2)
        plane = jnp.concatenate([line, at.swap_y(line)], axis=0)
        one_line = [one, at.swap_z(one, 1)]
        turns = early(facts)
        first_hop, plane, one_line, down_two, turns = tie(first_hop, plane, one_line, down_two, turns)
        far = at.swap_x(plane)
        second_hop = at.up(first_hop, 1, 2)
        first_over = at.swap_y(first_hop, [(i, i ^ 1) for i in range(2, 8)])
        down_two = at.swap_x(down_two)
        second_hop, first_over, one_line, near, down_two = tie(second_hop, first_over, one_line, plane, down_two)
        down_two = jnp.stack([w_down, down_two])[None]
        third_hop = at.up(second_hop, 2, 2)
        other = [at.swap_core(near)]
        second_over = at.swap_y(second_hop, [(i, i ^ 1) for i in range(4, 8)])
        one_line.append(at.swap_z(one_line[0], 2))
        third_hop, second_over, far, one_line = tie(third_hop, second_over, far, one_line)
        third_over = at.swap_y(third_hop, [(i, i ^ 1) for i in range(6, 8)])
        other.append(at.swap_core(far))
        one_line.append(at.swap_z(one_line[0], 3))
        m = 2 * few
        n = vectors.shape[1]
        vec = jnp.concatenate([plane[:, m : m + 2, :n], far[:, m : m + 2, :n]], axis=0).reshape(16, 2 * n)
        order = (self.places()[0][None, :] == jnp.arange(16)[:, None]).astype(BF)
        vec = mm(order, vec).reshape(32, -1)
        third_over, other, one_line, vec, down_two = tie(third_over, other, one_line, vec, down_two)
        line = jnp.concatenate(one_line, axis=0)
        lower = [first_hop, first_over, beside, second_hop, second_over, third_hop, third_over]
        return lower, ((plane, far), tuple(other)), vec, (line, down_two), turns

    def second_start(self, state):
        line, down_two = state
        return jnp.concatenate([line, self.at.swap_y(line)], axis=0), z_gather(self.at, down_two)

    def second_go_on(self, state):
        plane, line = state
        at = self.at
        near = line.reshape((8,) + line.shape[2:])
        one = (plane, at.swap_x(plane)), [at.swap_core(plane)]
        down = (near, at.swap_y(near)), [at.swap_core(near)]
        return one, down

    def second_end(self, state):
        return [(own, tuple(other + [self.at.swap_core(own[1])])) for own, other in state]

    def unit_bias(self, bias, chunk):
        a, b = halves_of_units(bias[None], chunk)
        return jnp.where(self.core == 0, a, b), jnp.where(self.core == 0, b, a)

    def unit_bias_back(self, own, other, chunk):
        a = jnp.where(self.core == 0, own, other)
        b = jnp.where(self.core == 0, other, own)
        return units_of_halves(a, b, chunk)[0]

    def backward(self, run):
        at = self.at
        rows = self.rows
        lower_z = lambda s: [(i, i ^ 1) for i in range(2 * s, 8)]
        down_other, rest_other = run.feed_other(self)
        down_got, rest_got = at.swap_core(down_other), at.swap_core(rest_other)
        down_own, rest_own = run.feed_own(self)
        by_x = lambda g: g.reshape(8, 2, g.shape[0] // 16, g.shape[1])
        by_y = lambda g: g.reshape(4, 2, 2, g.shape[0] // 16, g.shape[1])
        split_y = lambda g: g.reshape((4, 2) + g.shape[1:])
        down_keep, down_send = halve(at.x, by_x(down_own), by_x(down_got), 1)
        rest_keep, rest_send = halve(at.y, by_y(rest_own), by_y(rest_got), 1)
        down_keep, down_send, rest_keep, rest_send, run.grad_mixed = tie(
            down_keep, down_send, rest_keep, rest_send, run.grad_mixed
        )
        down_got, rest_got = at.swap_x(down_send), at.swap_y(rest_send)
        far = run.far_tiles()
        down_got, rest_got, far = tie(down_got, rest_got, far)
        down_keep, down_send = halve(at.y, split_y(down_keep), split_y(down_got), 1)
        rest_keep, rest_send = z_parts(at, rest_keep, rest_got)
        down_keep, down_send, rest_keep, rest_send, far = tie(down_keep, down_send, rest_keep, rest_send, far)
        far_da = run.far_rows(far)
        tiles = [far_da[n * rows : (n + 1) * rows] for n in range(4)]
        over = jnp.concatenate([tiles[1], tiles[3]], axis=0)
        down_send, tiles, over, far = tie(down_send, tiles, over, far)
        over = at.swap_y(over, lower_z(2))
        down_got = at.swap_y(down_send)
        rest_got = z_move(at, rest_send)
        near = run.near_tiles(far)
        rest_got, over, near, tiles, down_got = tie(rest_got, over, near, tiles, down_got)
        down_keep, down_send = z_parts(at, down_keep, down_got)
        rest = z_total(rest_keep, rest_got).astype(BF)
        rest_keep, rest_send = choose(at.x, rest, 0)
        cur = plus(tiles[2], over[rows:]).astype(BF)
        down_keep, down_send, rest_keep, rest_send, cur, near = tie(
            down_keep, down_send, rest_keep, rest_send, cur, near
        )
        cur = at.down(cur, 3, 3)
        down_got, rest_got = z_move(at, down_send), at.swap_x(rest_send)
        own, other, vec = run.weights(near, far)
        own, other, vec, cur, down_got, rest_got = tie(own, other, vec, cur, down_got, rest_got)
        own, other = self.qkv_pieces(own, other, vec)
        cur = (plus(tiles[0], over[:rows]) + cur.astype(F32)).astype(BF)
        own, other, cur, near = tie(own, other, cur, near)
        got = at.swap_core(other)
        cur = at.down(cur, 2, 3)
        clean, near_da = run.near_rows(near)
        got, cur, clean, near_da = tie(got, cur, clean, near_da)
        keep, send = halve(at.x, own, got, 1)
        keep, send, cur, near_da = tie(keep, send, cur, near_da)
        got = at.swap_x(send)
        first = at.swap_y(near_da[rows : 2 * rows], lower_z(1))
        beside = at.swap_y(near_da[2 * rows :], [(i, i - 1) for i in range(1, 8, 2)])
        sum_down = z_total(down_keep, down_got)
        sum_out, sum_up = self.join_rest(plus(rest_keep, rest_got), run.chunk, run.width)
        got, first, beside, sum_down, sum_out, sum_up = tie(got, first, beside, sum_down, sum_out, sum_up)
        keep, send = halve(at.y, split_y(keep), split_y(got), 1)
        cur = (plus(near_da[:rows], first) + cur.astype(F32)).astype(BF)
        keep, send, cur = tie(keep, send, cur)
        got, cur = at.swap_y(send), at.down(cur, 1, 3)
        got, cur = tie(got, cur)
        keep, send = z_parts(at, keep, got)
        keep, send = tie(keep, send)
        got = z_move(at, send)
        grad_hidden = run.last(clean + cur.astype(F32) + beside.astype(F32))
        got, grad_hidden = tie(got, grad_hidden)
        m = run.few * 2
        g = z_total(keep, got)
        sum_qkv = heads_of_halves(*from_column_half(at, g[:m]))
        return sum_down, sum_up, sum_out, sum_qkv, g[m, : run.vectors], grad_hidden

    def join_rest(self, g, chunk, width):
        a, b = from_column_half(self.at, g)
        cut = width // 2
        out = jnp.concatenate([a[:, :cut], b[:, :cut]], axis=1)
        return out, units_of_halves(a[:, cut:], b[:, cut:], chunk)

    def rest_pieces(self, out, up, other):
        half = out.shape[0] // 2
        core = 1 - self.core if other else self.core
        out = lax.dynamic_slice_in_dim(out, core * half, half, axis=1)
        out = jnp.where(self.core == 0, out, jnp.concatenate([out[half:], out[:half]], axis=0))
        return jnp.concatenate([out.astype(BF), up], axis=1)

    def qkv_pieces(self, own, other, vec):
        n = vec.shape[1]
        vec = vec.astype(BF).reshape(8, 2, 2, n)
        found = []
        for g, core in ((own, self.core), (other, 1 - self.core)):
            g = g.reshape(8, 2, g.shape[0] // 16, g.shape[1])
            rows = pick(vec, core, 2)[:, :, None]
            rows = jnp.pad(rows, ((0, 0), (0, 0), (0, 7), (0, g.shape[3] - n)))
            found.append(jnp.concatenate([g, rows], axis=2))
        return found


AXES = ("leaf", "fsdp")


class Whole:
    def __init__(self, rows, leaves, devices):
        self.rows, self.leaves, self.devices = rows, leaves, devices
        self.leaf = lax.axis_index("leaf")
        self.near = 2 + (leaves - 1) // 2

    def lower(self, leaf):
        return [(leaf - s, leaf >= s) for s in range(1, self.leaves)]

    def places(self):
        return jnp.array([[0, 0], [0, 0], [0, 0], [0, 1]], jnp.int32)

    def first_gather(self, hid, w_qkv, w_out, w_up, w_down, vectors, facts, early):
        tree = lax.all_gather(hid, "leaf", axis=0, tiled=False)
        lower = [pick(tree, jnp.maximum(leaf, 0), 0) for leaf, _ in self.lower(self.leaf)]
        every = lambda w: lax.all_gather(w, AXES, axis=0, tiled=True)
        qkv = tuple((v[None],) for v in halves_of_heads(every(w_qkv)))
        return lower, qkv, every(vectors), (every(w_out), every(w_up), every(w_down)), early(facts)

    def second_start(self, state):
        return state

    def second_go_on(self, state):
        return state

    def second_end(self, state):
        out_w, up_w, down_w = state
        half, cut = down_w.shape[0] // 2, out_w.shape[1] // 2
        one = tuple(
            (jnp.concatenate([out_w[:, n * cut : (n + 1) * cut], up_w[:, n * half : (n + 1) * half]], axis=1)[None],)
            for n in range(2)
        )
        return one, tuple((down_w[None, n * half : (n + 1) * half],) for n in range(2))

    def unit_bias(self, bias, chunk):
        half = bias.shape[0] // 2
        return bias[None, :half], bias[None, half:]

    def unit_bias_back(self, own, other, chunk):
        return jnp.concatenate([own, other], axis=1)[0]

    def scatter(self, g):
        return lax.psum_scatter(g.astype(F32), AXES, scatter_dimension=0, tiled=True)

    def rest_pieces(self, out, up, other):
        cut = out.shape[1] // 2
        return jnp.concatenate([out[:, cut:] if other else out[:, :cut], up.astype(F32)], axis=1)

    def backward(self, run):
        rows = self.rows
        down_other, rest_other = run.feed_other(self)
        down_own, rest_own = run.feed_own(self)
        far = run.far_tiles()
        far_da = run.far_rows(far)
        near = run.near_tiles(far)
        own, other, vec = run.weights(near, far)
        clean, near_da = run.near_rows(near)
        tiles = jnp.concatenate([clean.astype(BF), near_da, far_da], axis=0)
        tiles = tiles.reshape((self.leaves, rows) + tiles.shape[1:])
        order = [pick(tiles, (self.leaf - n) % self.leaves, 0) for n in range(self.leaves)]
        total = lax.psum_scatter(jnp.concatenate(order, axis=0), "leaf", scatter_dimension=0, tiled=True)
        cut = run.width // 2
        return (
            self.scatter(jnp.concatenate([down_own, down_other], axis=0)),
            self.scatter(jnp.concatenate([rest_own[:, cut:], rest_other[:, cut:]], axis=1)),
            self.scatter(jnp.concatenate([rest_own[:, :cut], rest_other[:, :cut]], axis=1)),
            self.scatter(heads_of_halves(own, other)),
            self.scatter(vec)[0],
            run.last(total.astype(F32)),
        )


class Backward:
    pass


def shards(
    leaves,
    groups,
    hidden,
    noise_mask,
    seg_blocks,
    parents,
    ln1_gain,
    w_qkv,
    w_out,
    ln2_gain,
    w_up,
    up_bias,
    w_down,
    down_bias,
    mask_embed,
    cotangent,
):
    rows = hidden.shape[1]
    width = hidden.shape[2]
    half = width // 2
    devices = leaves * groups
    net = Chain(rows) if (leaves, groups) == (8, 4) else Whole(rows, leaves, devices)
    chunk = w_down.shape[0]
    few = ln1_gain.shape[0]
    leaf = lax.axis_index("leaf")

    hid = hidden[0]
    tiles = 2 + len(net.lower(leaf))
    lanes = jnp.arange(128, dtype=jnp.int32)
    exponent = (lanes % (HEAD_DIM // 2)).astype(F32) * (-math.log(10000.0) / (HEAD_DIM // 2))

    def turns(facts):
        found = tables(net.lower, leaf, facts, parents, rows)
        angles = found[2][:, 2:3] * jnp.exp(exponent)
        sign = jnp.where((lanes % HEAD_DIM) < HEAD_DIM // 2, -1.0, 1.0)
        return jnp.cos(angles), jnp.sin(angles) * sign, found

    places = net.places()

    length = 4 * few + up_bias.shape[0]
    vectors = sum(
        jnp.pad(v[None], ((0, 0), (n * few, length - n * few - v.shape[0])))
        for n, v in enumerate((ln1_gain, ln2_gain, down_bias, mask_embed, up_bias))
    )
    lower, qkv_w, vec, coming, (cosine, sine, found) = net.first_gather(
        hid, w_qkv, w_out, w_up, w_down, vectors, seg_blocks, turns
    )
    query_cols, query_rows, key_cols, key_rows, flags = found
    gain_one, gain_two, down_b, embed = (
        vec[:, n * few : (n + 1) * few].reshape(1, width).astype(F32) for n in range(4)
    )
    up_b = jnp.concatenate(net.unit_bias(vec[:, 4 * few :].reshape(-1).astype(F32), chunk), axis=0)
    coming = net.second_start(coming)
    query, key, value = project(
        places, [hid] + lower, noise_mask, embed, gain_one, qkv_w[0], qkv_w[1], cosine, sine
    )
    coming, query = tie(coming, query)
    coming = net.second_go_on(coming)
    mixed, log_norm = attend(flags, query_cols, key_rows, query, key, value, rows)
    coming, mixed = tie(coming, mixed)
    one_w, down_w = net.second_end(coming)
    norm_rows = log_norm.T
    grad_two = cotangent[0].reshape(2 * rows, width)
    (
        output, normed_two, act, grad_pre, grad_one, grad_mixed, grad_after, grad_up_b, grad_down_b,
    ) = middle(places, mixed, hid, noise_mask, embed, grad_two, gain_two, up_b, down_b, one_w, down_w)
    output = output.reshape(1, 2, rows, width)
    units = act.shape[1] // 2

    run = Backward()
    run.chunk, run.few, run.vectors, run.grad_mixed, run.width = chunk, few, length - 2 * few, grad_mixed, width
    cut = net.near

    def feed(n, net):
        at = slice(n * units, (n + 1) * units)
        down, up = t_mm(act[:, at], grad_two).astype(BF), t_mm(normed_two, grad_pre[:, at]).astype(BF)
        return down, net.rest_pieces(t_mm(mixed, grad_one), up, n == 1)

    def far_tiles():
        return attend_back(
            cut, tiles, flags, query_rows, key_rows, query, key, value, mixed, run.grad_mixed, norm_rows, cosine, sine, rows
        )

    def far_rows(far):
        return fold_rows(places, far[1], far[2], qkv_w[0], qkv_w[1], rows)[0]

    def near_tiles(far):
        return attend_back(
            0, cut, flags, query_rows, key_rows, query, key, value, mixed, run.grad_mixed, norm_rows, cosine, sine, rows, far[0]
        )

    def weights(near, far):
        own, other, run.noisy, grad_embed = fold_weights(
            places, [hid] + lower, near, far, grad_after, noise_mask, embed, gain_one, qkv_w[0], qkv_w[1]
        )
        parts = (grad_down_b, grad_embed, net.unit_bias_back(grad_up_b[:1], grad_up_b[1:], chunk))
        return own, other, jnp.concatenate([v.reshape(devices, -1) for v in parts], axis=1)

    def near_rows(near):
        return fold_rows(places, near[1], near[2], qkv_w[0], qkv_w[1], rows, near[0])

    def last(total):
        hat, scale = normalise(hid.astype(F32))
        masked = (noise_mask[0] == 1)[:, None]
        clean = grad_after[:rows] + norm_back(hat, scale, gain_one, total)
        return (clean + jnp.where(masked, 0.0, run.noisy)).astype(BF)[None]

    run.feed_own = lambda net: feed(0, net)
    run.feed_other = lambda net: feed(1, net)
    run.far_tiles, run.far_rows, run.near_tiles, run.near_rows = far_tiles, far_rows, near_tiles, near_rows
    run.weights, run.last = weights, last
    sum_down, sum_up, sum_out, sum_qkv, sum_vec, grad_hidden = net.backward(run)
    from_weight = lambda w, g, gain: jnp.sum(w.astype(F32) * g, axis=1) / gain.astype(F32)
    return (
        output,
        grad_hidden,
        from_weight(w_qkv, sum_qkv, ln1_gain),
        sum_qkv,
        sum_out,
        from_weight(w_up, sum_up, ln2_gain),
        sum_up,
        sum_vec[2 * few :],
        sum_down,
        sum_vec[:few],
        sum_vec[few : 2 * few],
    )


def solution(mesh):
    split = ("leaf", "fsdp")
    in_specs = (
        P("fsdp", "leaf", None),
        P("fsdp", "leaf"),
        P("fsdp", None),
        P("fsdp", None),
        P(split),
        P(split, None),
        P(split, None),
        P(split),
        P(split, None),
        P(split),
        P(split, None),
        P(split),
        P(split),
        P("fsdp", None, "leaf", None),
    )
    out_specs = (
        P("fsdp", None, "leaf", None),
        P("fsdp", "leaf", None),
        P(split),
        P(split, None),
        P(split, None),
        P(split),
        P(split, None),
        P(split),
        P(split, None),
        P(split),
        P(split),
    )
    body = functools.partial(shards, mesh.shape["leaf"], mesh.shape["fsdp"])
    return jax.shard_map(body, mesh=mesh, in_specs=in_specs, out_specs=out_specs, check_vma=False)
```
